32 devices in a mesh: rep: 8 (over y, x, core), shard: 4 (over z).
Axes of the slice: x: 2, y: 2, z: 4, core: 2. Of those that a mesh axis runs over, the one named last changes fastest.
Arguments:
- layer_input: bfloat16 [16384, 2048], P(('rep', 'shard')), may hold values from -6 to 6
- gain_attn: bfloat16 [2048], P('shard'), may hold values from 0.5 to 1.5
- w_query: bfloat16 [2048, 2048], P('shard'), may hold values from -0.125 to 0.125
- w_key: bfloat16 [2048, 2048], P('shard'), may hold values from -0.125 to 0.125
- w_value: bfloat16 [2048, 2048], P('shard'), may hold values from -0.125 to 0.125
- w_out: bfloat16 [2048, 2048], P(None, 'shard'), may hold values from -0.5 to 0.5
- gain_mlp: bfloat16 [2048], P('shard'), may hold values from 0.5 to 1.5
- w_gate: bfloat16 [2048, 5632], P('shard'), may hold values from -0.125 to 0.125
- w_up: bfloat16 [2048, 5632], P('shard'), may hold values from -0.125 to 0.125
- w_down: bfloat16 [5632, 2048], P(None, 'shard'), may hold values from -0.078125 to 0.078125
- segments: int32 [32, 512], P(('rep', 'shard')), may hold values from 0 to 3, never falling along the last dimension, each value on 1 to 256 neighbouring positions
- attn_route: int32 [16384, 2], P(('rep', 'shard')), may hold values from 0 to 7, all different within a row
- attn_gate: float32 [16384, 2], P(('rep', 'shard')), may hold values from 0.2 to 1
- mlp_route: int32 [16384, 2], P(('rep', 'shard')), may hold values from 0 to 7, all different within a row
- mlp_gate: float32 [16384, 2], P(('rep', 'shard')), may hold values from 0.2 to 1
- cotangent: bfloat16 [16384, 2048], P(('rep', 'shard')), may hold values from -6 to 6
Outputs:
- output: bfloat16 [16384, 2048], P(('rep', 'shard'))
- grad_input: bfloat16 [16384, 2048], P(('rep', 'shard'))
- grad_gain_attn: float32 [2048], P('shard')
- grad_query: float32 [2048, 2048], P('shard')
- grad_key: float32 [2048, 2048], P('shard')
- grad_value: float32 [2048, 2048], P('shard')
- grad_out: float32 [2048, 2048], P(None, 'shard')
- grad_gain_mlp: float32 [2048], P('shard')
- grad_gate: float32 [2048, 5632], P('shard')
- grad_up: float32 [2048, 5632], P('shard')
- grad_down: float32 [5632, 2048], P(None, 'shard')
The draws below stay inside these ranges and needn't reach their ends.
All inputs are finite; a program needn't handle non-finite values.
Results may differ from the reference program's by a relative error of at most 0.017.
Values may be sent and summed in bfloat16 or wider, within the bound.
A program may use at most 384 MiB of HBM per device.

```python
import math
import jax
import jax.numpy as jnp
import numpy as np
from jax import lax

D = 2048
HEADS = 16
HD = 128
FF = 5632
EXPERTS = 8
WIN = 256
TOK_DEV = 512
CAP = 128
TOKENS = 16384
DEVICES = 32


def levels(stream_key, extent, split, smallest, top_value):
    factor_of, own = 1.0, jax.random.fold_in(stream_key, 6)
    for dim, parts in split:
        heights = jnp.exp(jax.random.uniform(jax.random.fold_in(own, dim), (parts,), jnp.float32, smallest / len(split), top_value / len(split)))
        factor_of = factor_of * jnp.repeat(heights, extent[dim] // parts).reshape([-1 if axis == dim else 1 for axis in range(len(extent))])
    return factor_of


def choose_distinct(rng, rows, amount, top, lift):
    sequence = jax.random.permutation(jax.random.fold_in(rng, 1), amount)
    boost = sequence
    for power in range(3):
        boost = boost * boost // amount
    boost = boost * lift // amount
    lots = jax.random.randint(jax.random.fold_in(rng, 2), (rows, amount), 0, 4096) + boost
    fixed_rows = jax.random.permutation(jax.random.fold_in(rng, 3), rows)[jnp.arange(amount) % rows]
    lots = jnp.where(jnp.arange(rows)[:, None] == fixed_rows[None, :], 1 << 14, lots)
    score = lots * amount + jnp.arange(amount)
    return lax.top_k(score.astype(jnp.int32), top)[1].astype(jnp.int32)


def profile(count, total, bound, lean):
    loads = [(1 << 20) // math.isqrt(rank ** lean) + 1 for rank in range(2, count + 1)]
    rest, holding = total - bound - (count - 1), [1] * (count - 1)
    while rest > 0:
        candidates = [i for i in range(count - 1) if holding[i] < bound]
        whole, left = sum([loads[i] for i in candidates]), rest
        for i in candidates:
            more = min(bound - holding[i], max(1, left * loads[i] // whole), rest)
            holding[i] = holding[i] + more
            rest = rest - more
    return np.array([bound] + holding)


def ragged(own_key, count, total, reach, slope):
    if count == 2:
        one = jax.random.randint(own_key, (), max(1, total - reach), min(reach, total - 1) + 1)
        return jnp.stack([one, total - one])
    tallies = jnp.asarray(profile(count, total, reach, slope), jnp.int32)
    twos = (count - 1) // 2
    source_of, receiver = tallies[1:1 + 2 * twos:2], tallies[2:2 + 2 * twos:2]
    room = jnp.minimum(source_of - 1, reach - receiver)
    shifted = jax.random.randint(jax.random.fold_in(own_key, 1), (twos,), 0, 1 << 20) % (room + 1)
    tallies = tallies.at[1:1 + 2 * twos:2].set(source_of - shifted).at[2:2 + 2 * twos:2].set(receiver + shifted)
    return tallies[jax.random.permutation(jax.random.fold_in(own_key, 2), count)]


def noise(own_key, extent, deviation, reach, cuts=(), kind=jnp.bfloat16):
    factor_of = levels(own_key, extent, cuts, -0.22, 0.18) if cuts else 1.0
    values = jax.random.normal(own_key, extent, jnp.float32) * deviation * factor_of
    return jnp.minimum(jnp.maximum(values, -reach), reach).astype(kind)


def setup_inputs(seed: int = 0) -> dict:
    key_of = jax.random.split(jax.random.key(seed), 17)
    return {
        "layer_input": noise(key_of[0], (TOKENS, D), 1.0, 6.0, ((0, 32),)),
        "gain_attn": jnp.clip(1.0 + 0.1 * jax.random.normal(key_of[1], (D,), jnp.float32), 0.5, 1.5).astype(jnp.bfloat16),
        "w_query": noise(key_of[2], (D, HEADS * HD), D ** -0.5, 0.125, ((0, 4),)),
        "w_key": noise(key_of[3], (D, HEADS * HD), D ** -0.5, 0.125, ((0, 4),)),
        "w_value": noise(key_of[4], (D, HEADS * HD), D ** -0.5, 0.125, ((0, 4),)),
        "w_out": noise(key_of[5], (HEADS * HD, D), (HEADS * HD // 16) ** -0.5, 0.5, ((1, 4),)),
        "gain_mlp": jnp.clip(1.0 + 0.1 * jax.random.normal(key_of[6], (D,), jnp.float32), 0.5, 1.5).astype(jnp.bfloat16),
        "w_gate": noise(key_of[7], (D, FF), D ** -0.5, 0.125, ((0, 4),)),
        "w_up": noise(key_of[8], (D, FF), D ** -0.5, 0.125, ((0, 4),)),
        "w_down": noise(key_of[9], (FF, D), FF ** -0.5, 0.078125, ((1, 4),)),
        "segments": jax.vmap(lambda own: jnp.searchsorted(jnp.cumsum(ragged(own, 4, TOK_DEV, TOK_DEV // 2, 2)), jnp.arange(TOK_DEV), side="right"))(jax.random.split(key_of[10], DEVICES)).reshape((DEVICES, TOK_DEV)).astype(jnp.int32),
        "attn_route": choose_distinct(key_of[11], TOKENS, EXPERTS, 2, 2048),
        "attn_gate": jnp.clip(0.2 + 0.8 * jax.random.uniform(key_of[12], (TOKENS, 2), jnp.float32) ** levels(key_of[12], (TOKENS, 2), ((0, 32),), -0.2, 0.2), 0.2, 1.0),
        "mlp_route": choose_distinct(key_of[13], TOKENS, EXPERTS, 2, 2048),
        "mlp_gate": jnp.clip(0.2 + 0.8 * jax.random.uniform(key_of[14], (TOKENS, 2), jnp.float32) ** levels(key_of[14], (TOKENS, 2), ((0, 32),), -0.2, 0.2), 0.2, 1.0),
        "cotangent": noise(key_of[15], (TOKENS, D), 1.0, 6.0, ((0, 32),)),
    }


@jax.custom_vjp
def low(v):
    return lax.optimization_barrier(v.astype(jnp.bfloat16)).astype(jnp.float32)

@jax.custom_vjp
def low_back(v):
    return v

def low_keep(v):
    return (low(v), None)

def low_pass(kept, grad):
    return (grad,)

def back_keep(v):
    return (v, None)

def back_low(kept, grad):
    return (low(grad),)
low.defvjp(low_keep, low_pass)
low_back.defvjp(back_keep, back_low)
EPSILON = 1e-05
PRECISE = lax.Precision.HIGHEST

def matmul(left, right):
    return jnp.dot(left, right, precision=PRECISE)

def rms_scaled(values, gain_row):
    root_inv = lax.rsqrt(lax.optimization_barrier(jnp.mean(values * values, axis=-1, keepdims=True)) + EPSILON)
    return values * root_inv * gain_row

def rotary_tables(length, head_width):
    half_width = head_width // 2
    positions = jnp.arange(length, dtype=jnp.float32)
    inverse = 10000.0 ** (-2.0 * jnp.arange(half_width, dtype=jnp.float32) / head_width)
    angles = positions[:, None] * inverse[None, :]
    return (jnp.cos(angles)[:, None, :], jnp.sin(angles)[:, None, :])

def rotate(values, cos_table, sin_table):
    half_width = values.shape[-1] // 2
    first_half = values[..., :half_width]
    second_half = values[..., half_width:]
    return jnp.concatenate([first_half * cos_table - second_half * sin_table, second_half * cos_table + first_half * sin_table], axis=-1)

def window_mask(segment_row):
    row_ids = jnp.arange(segment_row.shape[0], dtype=jnp.int32)
    distance = row_ids[:, None] - row_ids[None, :]
    return (segment_row[:, None] == segment_row[None, :]) & (distance >= 0) & (distance < WIN)

def attend(packed):
    queries, key_rows, values, segment_row = packed
    scores = jnp.einsum('qhd,khd->hqk', queries, key_rows, precision=PRECISE) * HD ** (-0.5)
    scores = low_back(scores)
    scores = jnp.where(window_mask(segment_row)[None], scores, -1e+30)
    row_peak = lax.optimization_barrier(jnp.max(scores, axis=-1, keepdims=True))
    weights = jnp.exp(scores - row_peak)
    weights = weights / lax.optimization_barrier(jnp.sum(weights, axis=-1, keepdims=True))
    return jnp.einsum('hqk,khd->qhd', low(weights), values, precision=PRECISE)

def slot_plan(route_ids, gate_values):
    hit_mask = route_ids == 0
    hit_count = lax.optimization_barrier(jnp.sum(hit_mask.astype(jnp.int32), axis=-1)).astype(jnp.int32)
    weight = lax.optimization_barrier(jnp.sum(jnp.where(hit_mask, gate_values, 0.0), axis=-1))
    slot_order = (jnp.cumsum(hit_count) - hit_count).astype(jnp.int32)
    kept_rows = (hit_count > 0) & (slot_order < CAP)
    slot_ids = jnp.arange(CAP, dtype=jnp.int32)
    slot_table = (slot_order[None, :] == slot_ids[:, None]) & kept_rows[None, :]
    token_ids = jnp.arange(route_ids.shape[0], dtype=jnp.int32)
    token_of = lax.optimization_barrier(jnp.sum(jnp.where(slot_table, token_ids[None, :], 0), axis=1)).astype(jnp.int32)
    filled = jnp.any(slot_table, axis=1)
    slot_of = jnp.minimum(slot_order, CAP - 1).astype(jnp.int32)
    return (token_of, filled, slot_of, jnp.where(kept_rows, weight, 0.0))

def take_rows(source_rows, indices):
    return jnp.take(source_rows, indices, axis=0)

def reference(layer_input, gain_attn, w_query, w_key, w_value, w_out, gain_mlp, w_gate, w_up, w_down, segments, attn_route, attn_gate, mlp_route, mlp_gate, cotangent):
    group_size = min(DEVICES, max(1, 4096 // TOK_DEV))
    group_count = DEVICES // group_size
    weights = (gain_attn.astype(jnp.float32), w_query.astype(jnp.float32), w_key.astype(jnp.float32), w_value.astype(jnp.float32), w_out.astype(jnp.float32), gain_mlp.astype(jnp.float32), w_gate.astype(jnp.float32), w_up.astype(jnp.float32), w_down.astype(jnp.float32))
    cos_table, sin_table = rotary_tables(TOK_DEV, HD)
    shape_heads = (group_size, TOK_DEV, HEADS, HD)

    def forward(inputs, params, segment_rows, attn_routes, attn_gates, mlp_routes, mlp_gates):
        gain_one, query_map, key_map, value_map, out_map, gain_two, gate_map, up_map, down_map = params
        tokens = group_size * TOK_DEV
        flat = inputs.reshape(tokens, D)
        normed = low(rms_scaled(flat, gain_one))
        queries = low(rotate(low_back(matmul(normed, query_map)).reshape(shape_heads), cos_table, sin_table))
        key_rows = low(rotate(low_back(matmul(normed, key_map)).reshape(shape_heads), cos_table, sin_table))
        values = low(low_back(matmul(normed, value_map))).reshape(shape_heads)
        context = lax.map(jax.checkpoint(attend), (queries, key_rows, values, segment_rows))
        context = low_back(low(context)).reshape(tokens, HEADS * HD)
        attn_weight = lax.optimization_barrier(jnp.sum(jnp.where(attn_routes == 0, attn_gates, 0.0), axis=-1)).reshape(tokens, 1)
        hidden = flat + low_back(matmul(context, out_map)) * attn_weight
        normed_two = low(rms_scaled(hidden, gain_two)).reshape(group_size, TOK_DEV, D)
        token_of, filled, slot_of, mix_weight = jax.vmap(slot_plan)(mlp_routes, mlp_gates)
        dispatched = jax.vmap(take_rows)(normed_two, token_of)
        dispatched = jnp.where(filled[..., None], dispatched, 0.0).reshape(group_size * CAP, D)
        gate_act = low_back(matmul(dispatched, gate_map))
        up_act = low_back(matmul(dispatched, up_map))
        inner_act = low(jax.nn.silu(gate_act) * up_act)
        expert_out = low_back(matmul(inner_act, down_map)).reshape(group_size, CAP, D)
        combined = jax.vmap(take_rows)(expert_out, slot_of) * mix_weight[..., None]
        return hidden.reshape(group_size, TOK_DEV, D) + combined

    def scan_step(running, pieces):
        inputs, segment_rows, attn_routes, attn_gates, mlp_routes, mlp_gates, upstream = pieces

        def closed(inputs_f, params):
            return forward(inputs_f, params, segment_rows, attn_routes, attn_gates, mlp_routes, mlp_gates)
        result, pullback = jax.vjp(closed, inputs.astype(jnp.float32), weights)
        grad_inputs, grad_params = pullback(upstream.astype(jnp.float32))
        running = jax.tree.map(jnp.add, running, grad_params)
        return (running, (result.astype(jnp.bfloat16), grad_inputs.astype(jnp.bfloat16)))

    def regroup(array):
        return array.reshape((group_count, group_size, TOK_DEV) + array.shape[1:])
    zeros = jax.tree.map(jnp.zeros_like, weights)
    totals, (outputs, grads_in) = lax.scan(scan_step, zeros, (regroup(layer_input), segments.reshape(group_count, group_size, TOK_DEV), regroup(attn_route), regroup(attn_gate), regroup(mlp_route), regroup(mlp_gate), regroup(cotangent)))
    return (outputs.reshape(TOKENS, D), grads_in.reshape(TOKENS, D), totals[0], totals[1], totals[2], totals[3], totals[4], totals[5], totals[6], totals[7], totals[8])
```

```python
import jax
import jax.numpy as jnp
from jax import lax
from jax.sharding import PartitionSpec as P

HEADS = 16
HD = 128
WIN = 256
CAP = 128
EPSILON = 1e-05
BF = jnp.bfloat16
F32 = jnp.float32


def mm(left, right):
    return jnp.dot(left, right, preferred_element_type=F32)


def mm_nt(left, right):
    return lax.dot_general(left, right, (((1,), (1,)), ((), ())), preferred_element_type=F32)


def mm_tn(left, right):
    return lax.dot_general(left, right, (((0,), (0,)), ((), ())), preferred_element_type=F32)


def swap(value, bit):
    size = lax.axis_size("rep")
    return lax.ppermute(value, "rep", [(i, i ^ bit) for i in range(size)])


def chip_bits():
    size, bits, bit = lax.axis_size("rep"), [], 2
    while bit < size:
        bits.append(bit)
        bit *= 2
    return bits


def chip_offsets():
    return list(range(0, lax.axis_size("rep"), 2))


def gather_chips(value):
    bits = chip_bits()
    if len(bits) == 2:
        one, two = bits
        half = value.shape[0] // 2
        by_one, by_two = swap(value, one), swap(value, two)
        far = jnp.concatenate([swap(by_one[:half], two), swap(by_two[half:], one)], axis=0)
        return {0: value, one: by_one, two: by_two, one ^ two: far}
    blocks = {0: value}
    for bit in bits:
        blocks.update({d ^ bit: swap(b, bit) for d, b in list(blocks.items())})
    return blocks


def add(left, right):
    return left.astype(F32) + right.astype(F32)


def scatter_chips(blocks):
    bits = chip_bits()
    if len(bits) == 2:
        one, two = bits
        half = blocks[0].shape[0] // 2
        far = blocks[one ^ two]
        near_one, near_two = blocks[one], blocks[two]
        top, bottom = swap(far[:half], one), swap(far[half:], two)
        two_bottom, one_top = swap(near_two[half:], two), swap(near_one[:half], one)
        two_top = swap(add(near_two[:half], top).astype(BF), two)
        one_bottom = swap(add(near_one[half:], bottom).astype(BF), one)
        by_one = jnp.concatenate([one_top, one_bottom], axis=0)
        by_two = jnp.concatenate([two_top, two_bottom], axis=0)
        return blocks[0].astype(F32) + by_one.astype(F32) + by_two.astype(F32)
    blocks = dict(blocks)
    for bit in reversed(bits):
        kept = {d: b for d, b in blocks.items() if not d & bit}
        blocks = {d: add(b, swap(blocks[d | bit], bit)).astype(BF) for d, b in kept.items()}
    return blocks[0].astype(F32)


def gather_plane(value):
    blocks = gather_chips(value)
    same = jnp.concatenate([blocks[d] for d in chip_offsets()], axis=0)
    return jnp.concatenate([same, swap(same, 1)], axis=0)


def scatter_plane(partial):
    half = partial.shape[0] // 2
    same = add(partial[:half], swap(partial[half:], 1)).astype(BF)
    offsets = chip_offsets()
    rows = half // len(offsets)
    return scatter_chips({d: same[i * rows : (i + 1) * rows] for i, d in enumerate(offsets)})


def rotary_tables(length):
    half = HD // 2
    positions = jnp.arange(length, dtype=F32)
    inverse = 10000.0 ** (-2.0 * jnp.arange(half, dtype=F32) / HD)
    angles = positions[:, None] * inverse[None, :]
    return jnp.cos(angles)[:, None, :], jnp.sin(angles)[:, None, :]


def rotate(values, cos_table, sin_table):
    half = values.shape[-1] // 2
    first, second = values[..., :half], values[..., half:]
    return jnp.concatenate(
        [first * cos_table - second * sin_table, second * cos_table + first * sin_table], axis=-1
    )


def plan_slots(route_ids, gate_values):
    hit_mask = route_ids == 0
    hit = jnp.any(hit_mask, axis=-1)
    weight = jnp.sum(jnp.where(hit_mask, gate_values, 0.0), axis=-1)
    ids = jnp.arange(route_ids.shape[0], dtype=jnp.int32)
    earlier = (ids[None, :] < ids[:, None]) & hit[None, :]
    order = jnp.sum(earlier.astype(jnp.int32), axis=1)
    kept = hit & (order < CAP)
    slots = jnp.arange(CAP, dtype=jnp.int32)
    table = (order[None, :] == slots[:, None]) & kept[None, :]
    return table, jnp.where(kept, weight, 0.0)


def norm_back(grad_normed, source, root, gain):
    scaled = grad_normed * gain
    grad_gain = jnp.sum(grad_normed * source * root, axis=0)
    mean = jnp.mean(scaled * source, axis=-1, keepdims=True)
    return grad_gain, root * scaled - source * (root * root * root) * mean


def gather_vector(rows):
    size, me = lax.axis_size("shard"), lax.axis_index("shard")
    parts = [rows] + [
        lax.ppermute(rows, "shard", [(i, (i - k) % size) for i in range(size)])
        for k in range(1, size)
    ]
    twice = jnp.concatenate(parts + parts, axis=1)
    own = rows.shape[1]
    return lax.dynamic_slice_in_dim(twice, ((size - me) % size) * own, size * own, 1)


def attend(qkv, tables, allowed):
    rows = qkv.shape[0]
    length = allowed.shape[-1]
    seqs = rows // length
    width = qkv.shape[1] // 3
    heads = width // HD
    shape = (seqs, length, heads, HD)
    queries = rotate(qkv[:, :width].reshape(shape), *tables).astype(BF)
    keys = rotate(qkv[:, width : 2 * width].reshape(shape), *tables).astype(BF)
    values = qkv[:, 2 * width :].astype(BF).reshape(shape)
    scores = jnp.einsum("bqhd,bkhd->bhqk", queries, keys, preferred_element_type=F32) * HD**-0.5
    scores = jnp.where(allowed[:, None], scores, -1e30)
    peak = jnp.max(scores, axis=-1, keepdims=True)
    raw = jnp.exp(scores - peak)
    total = jnp.sum(raw, axis=-1, keepdims=True)
    probs = (raw / total).astype(BF)
    context = jnp.einsum("bhqk,bkhd->bqhd", probs, values, preferred_element_type=F32).astype(BF)
    return context.reshape(rows, width), (queries, keys, values, peak + jnp.log(total))


def attend_back(saved, grad_context, tables, allowed):
    queries, keys, values, lse = saved
    shape = queries.shape
    grad_context = grad_context.reshape(shape)
    scale = HD**-0.5
    scores = jnp.einsum("bqhd,bkhd->bhqk", queries, keys, preferred_element_type=F32) * scale
    scores = jnp.where(allowed[:, None], scores, -1e30)
    probs = jnp.exp(scores - lse)
    grad_values = jnp.einsum(
        "bhqk,bqhd->bkhd", probs.astype(BF), grad_context, preferred_element_type=F32
    ).astype(BF)
    grad_probs = jnp.einsum("bqhd,bkhd->bhqk", grad_context, values, preferred_element_type=F32)
    inner = jnp.sum(probs * grad_probs, axis=-1, keepdims=True)
    grad_scores = (probs * (grad_probs - inner)).astype(BF)
    grad_queries = (
        jnp.einsum("bhqk,bkhd->bqhd", grad_scores, keys, preferred_element_type=F32) * scale
    )
    grad_keys = (
        jnp.einsum("bhqk,bqhd->bkhd", grad_scores, queries, preferred_element_type=F32) * scale
    )
    cos_table, sin_table = tables
    rows = shape[0] * shape[1]
    return jnp.concatenate(
        [
            rotate(grad_queries, cos_table, -sin_table).astype(BF).reshape(rows, -1),
            rotate(grad_keys, cos_table, -sin_table).astype(BF).reshape(rows, -1),
            grad_values.reshape(rows, -1),
        ],
        axis=1,
    )


def per_device(
    layer_input,
    gain_attn,
    w_query,
    w_key,
    w_value,
    w_out,
    gain_mlp,
    w_gate,
    w_up,
    w_down,
    segments,
    attn_route,
    attn_gate,
    mlp_route,
    mlp_gate,
    cotangent,
):
    length = layer_input.shape[0]
    size = lax.axis_size("rep")
    me = lax.axis_index("rep")
    block = w_query.shape[1] // size
    hidden_block = w_gate.shape[1] // size
    offsets = chip_offsets()

    def columns(weight, width):
        return lax.dynamic_slice_in_dim(weight, me * width, width, 1)

    def rows_of(weight, height):
        return lax.dynamic_slice_in_dim(weight, me * height, height, 0)

    own_qkv = jnp.concatenate([columns(w, block) for w in (w_query, w_key, w_value)], axis=1)
    own_qkv = lax.all_gather(own_qkv, "shard", axis=0, tiled=True)
    own_out = lax.all_gather(rows_of(w_out, block), "shard", axis=1, tiled=True)
    qkv_w = gather_chips(own_qkv)
    out_w = gather_chips(own_out)
    gate_up = jnp.concatenate([columns(w_gate, hidden_block), columns(w_up, hidden_block)], axis=1)
    gate_up = lax.all_gather(gate_up, "shard", axis=0, tiled=True)
    down = lax.all_gather(rows_of(w_down, hidden_block), "shard", axis=1, tiled=True)

    gains = gather_vector(jnp.stack([gain_attn, gain_mlp])).astype(F32)
    gain_one, gain_two = gains[0], gains[1]

    table, mix = plan_slots(mlp_route, mlp_gate)
    pick = table.astype(BF)
    upstream = cotangent.astype(F32)
    slot_weight = jnp.sum(jnp.where(table, mix[None, :], 0.0), axis=1)[:, None]
    slot_grad = (mm(pick, cotangent) * slot_weight).astype(BF)
    all_slot_grad = gather_plane(slot_grad)

    inputs = layer_input.astype(F32)
    root_one = lax.rsqrt(jnp.mean(inputs * inputs, axis=-1, keepdims=True) + EPSILON)
    normed = (inputs * root_one * gain_one).astype(BF)
    both = jnp.concatenate([normed, swap(normed, 1)], axis=0)
    seg = jnp.concatenate([segments, swap(segments, 1)], axis=0)
    ids = jnp.arange(length, dtype=jnp.int32)
    distance = ids[:, None] - ids[None, :]
    near = (distance >= 0) & (distance < WIN)
    allowed = (seg[:, :, None] == seg[:, None, :]) & near[None]
    tables = rotary_tables(length)
    context, saved = {}, {}
    for d in offsets:
        context[d], saved[d] = attend(mm(both, qkv_w[d]), tables, allowed)
    all_context = jnp.concatenate([context[d] for d in offsets], axis=1)
    all_out = jnp.concatenate([out_w[d] for d in offsets], axis=0)
    projected = mm(all_context, all_out)
    projected = projected[:length] + swap(projected[length:].astype(BF), 1).astype(F32)
    attn_weight = jnp.sum(jnp.where(attn_route == 0, attn_gate, 0.0), axis=-1)[:, None]
    hidden = inputs + projected * attn_weight
    root_two = lax.rsqrt(jnp.mean(hidden * hidden, axis=-1, keepdims=True) + EPSILON)
    normed_two = (hidden * root_two * gain_two).astype(BF)

    dispatched = gather_plane(mm(pick, normed_two).astype(BF))
    act = mm(dispatched, gate_up)
    gate_act, up_act = act[:, :hidden_block], act[:, hidden_block:]
    sigmoid = jax.nn.sigmoid(gate_act)
    silu = gate_act * sigmoid
    inner = (silu * up_act).astype(BF)
    grad_inner = mm_nt(all_slot_grad, down)
    grad_gate_act = (grad_inner * up_act * sigmoid * (1.0 + gate_act * (1.0 - sigmoid))).astype(BF)
    grad_up_act = (grad_inner * silu).astype(BF)
    grad_act = jnp.concatenate([grad_gate_act, grad_up_act], axis=1)
    grad_disp = scatter_plane(mm_nt(grad_act, gate_up).astype(BF)).astype(BF)
    expert_out = scatter_plane(mm(inner, down).astype(BF)).astype(BF)
    output = (hidden + mm_tn(pick, expert_out) * mix[:, None]).astype(BF)
    grad_gate_up = mm_tn(dispatched, grad_act).astype(BF)
    grad_down = mm_tn(inner, all_slot_grad).astype(BF)

    grad_normed_two = mm_tn(pick, grad_disp)
    grad_gain_two, through = norm_back(grad_normed_two, hidden, root_two, gain_two)
    grad_hidden = upstream + through

    grad_projected = (grad_hidden * attn_weight).astype(BF)
    both_grad = jnp.concatenate([grad_projected, swap(grad_projected, 1)], axis=0)
    grad_out_w = mm_tn(all_context, both_grad).astype(BF)
    grad_context = mm_nt(both_grad, all_out).astype(BF)
    grad_lin = {
        d: attend_back(saved[d], grad_context[:, i * block : (i + 1) * block], tables, allowed)
        for i, d in enumerate(offsets)
    }
    grad_qkv_w = {d: mm_tn(both, grad_lin[d]).astype(BF) for d in offsets}
    grad_normed = sum(mm_nt(grad_lin[d], qkv_w[d]) for d in offsets)
    grad_normed = grad_normed[:length] + swap(grad_normed[length:].astype(BF), 1).astype(F32)
    grad_gain_one, first = norm_back(grad_normed, inputs, root_one, gain_one)
    grad_input = (grad_hidden + first).astype(BF)

    def spread(value, axis):
        return lax.all_gather(value, "rep", axis=axis, tiled=True).astype(F32)

    sum_gu = lax.psum_scatter(grad_gate_up, "shard", scatter_dimension=0, tiled=True)
    sum_down = lax.psum_scatter(grad_down, "shard", scatter_dimension=1, tiled=True)
    own_grad_out = scatter_chips(
        {d: grad_out_w[i * block : (i + 1) * block] for i, d in enumerate(offsets)}
    ).astype(BF)
    sum_out = lax.psum_scatter(own_grad_out, "shard", scatter_dimension=1, tiled=True)
    own_grad_qkv = scatter_chips(grad_qkv_w).astype(BF)
    sum_qkv = lax.psum_scatter(own_grad_qkv, "shard", scatter_dimension=0, tiled=True)
    grad_gate = spread(sum_gu[:, :hidden_block], 1)
    grad_up = spread(sum_gu[:, hidden_block:], 1)
    grad_down = spread(sum_down, 0)
    grad_out = spread(sum_out, 0)
    grad_query, grad_key, grad_value = (
        spread(sum_qkv[:, i * block : (i + 1) * block], 1) for i in range(3)
    )
    gain_grads = lax.psum(jnp.stack([grad_gain_one, grad_gain_two]), ("rep", "shard"))
    own = gain_attn.shape[0]
    gain_grads = lax.dynamic_slice_in_dim(gain_grads, lax.axis_index("shard") * own, own, 1)
    return (
        output,
        grad_input,
        gain_grads[0],
        grad_query,
        grad_key,
        grad_value,
        grad_out,
        gain_grads[1],
        grad_gate,
        grad_up,
        grad_down,
    )


def solution(mesh):
    tokens = P(("rep", "shard"), None)
    tall, wide, vector = P("shard", None), P(None, "shard"), P("shard")
    weights = (vector, tall, tall, tall, wide, vector, tall, tall, wide)
    return jax.shard_map(
        per_device,
        mesh=mesh,
        in_specs=(tokens, *weights) + (tokens,) * 6,
        out_specs=(tokens, tokens, *weights),
        check_vma=False,
    )
```

```python
import functools

import jax
import jax.numpy as jnp
from jax import lax
from jax.experimental import pallas as pl
from jax.experimental.pallas import tpu as pltpu
from jax.sharding import PartitionSpec as P

HEADS = 16
HD = 128
WIN = 256
CAP = 128
EPSILON = 1e-05
BF = jnp.bfloat16
F32 = jnp.float32


def mm(left, right):
    return jnp.dot(left, right, preferred_element_type=F32)


def mm_nt(left, right):
    return lax.dot_general(left, right, (((1,), (1,)), ((), ())), preferred_element_type=F32)


def mm_tn(left, right):
    return lax.dot_general(left, right, (((0,), (0,)), ((), ())), preferred_element_type=F32)


def swap(value, bit):
    size = lax.axis_size("rep")
    return lax.ppermute(value, "rep", [(i, i ^ bit) for i in range(size)])


def chip_bits():
    size, bits, bit = lax.axis_size("rep"), [], 2
    while bit < size:
        bits.append(bit)
        bit *= 2
    return bits


def chip_offsets():
    return list(range(0, lax.axis_size("rep"), 2))


def gather_chips(value):
    bits = chip_bits()
    if len(bits) == 2:
        one, two = bits
        half = value.shape[0] // 2
        by_one, by_two = swap(value, one), swap(value, two)
        far = jnp.concatenate([swap(by_one[:half], two), swap(by_two[half:], one)], axis=0)
        return {0: value, one: by_one, two: by_two, one ^ two: far}
    blocks = {0: value}
    for bit in bits:
        blocks.update({d ^ bit: swap(b, bit) for d, b in list(blocks.items())})
    return blocks


def add(left, right):
    return left.astype(F32) + right.astype(F32)


def scatter_chips(blocks):
    bits = chip_bits()
    if len(bits) == 2:
        one, two = bits
        far = blocks[one ^ two]
        near_one, near_two = blocks[one], blocks[two]
        top, bottom = swap(far[0], one), swap(far[1], two)
        one_top, two_bottom = swap(near_one[0], one), swap(near_two[1], two)
        two_top = swap(add(near_two[0], top).astype(BF), two)
        one_bottom = swap(add(near_one[1], bottom).astype(BF), one)
        return jnp.concatenate(
            [
                blocks[0][0].astype(F32) + one_top.astype(F32) + two_top.astype(F32),
                blocks[0][1].astype(F32) + one_bottom.astype(F32) + two_bottom.astype(F32),
            ],
            axis=0,
        )
    blocks = {d: jnp.concatenate(b, axis=0) for d, b in blocks.items()}
    for bit in reversed(bits):
        kept = {d: b for d, b in blocks.items() if not d & bit}
        blocks = {d: add(b, swap(blocks[d | bit], bit)).astype(BF) for d, b in kept.items()}
    return blocks[0].astype(F32)


def halves(value):
    half = value.shape[0] // 2
    return value[:half], value[half:]


def gather_plane(value):
    blocks = gather_chips(value)
    same = jnp.concatenate([blocks[d] for d in chip_offsets()], axis=0)
    return jnp.concatenate([same, swap(same, 1)], axis=0)


def scatter_plane(partial):
    half = partial.shape[0] // 2
    same = add(partial[:half], swap(partial[half:], 1)).astype(BF)
    offsets = chip_offsets()
    rows = half // len(offsets)
    return scatter_chips({d: halves(same[i * rows : (i + 1) * rows]) for i, d in enumerate(offsets)})


def rotary_tables(length):
    half = HD // 2
    positions = jnp.arange(length, dtype=F32)
    inverse = 10000.0 ** (-2.0 * jnp.arange(half, dtype=F32) / HD)
    angles = positions[:, None] * inverse[None, :]
    cos, sin = jnp.cos(angles), jnp.sin(angles)
    return jnp.concatenate([cos, cos], axis=1), jnp.concatenate([-sin, sin], axis=1)


def rotate(values, cos, sin):
    return values * cos + pltpu.roll(values, HD // 2, 1) * sin


def window(step, seg_col, seg_row):
    low, high = max(0, step - 1) * WIN, (step + 1) * WIN
    shape = (WIN, high - low)
    row = lax.broadcasted_iota(jnp.int32, shape, 0) + step * WIN
    col = lax.broadcasted_iota(jnp.int32, shape, 1) + low
    near = (row >= col) & (row - col < WIN)
    same = seg_col[0, step * WIN : (step + 1) * WIN, :] == seg_row[0, :, low:high]
    return low, high, near & same


def attend_kernel(parts, z_ref, *refs):
    x_refs, w_refs = refs[:parts], refs[parts : 2 * parts]
    cos_ref, sin_ref, col_ref, row_ref, context_ref, qkv_ref, lse_ref, lin_ref = refs[2 * parts :]
    length, width = context_ref.shape
    tile = min(length, 256)

    @pl.loop(0, length // tile)
    def _(t):
        rows = pl.ds(pl.multiple_of(t * tile, tile), tile)
        total = mm(x_refs[0][rows, :], w_refs[0][...])
        for x, w in zip(x_refs[1:], w_refs[1:]):
            total += mm(x[rows, :], w[...])
        lin_ref[rows, :] = total

    cos, sin = cos_ref[...], sin_ref[...]
    for h in range(width // HD):
        q_at, k_at, v_at = (slice(i * width + h * HD, i * width + (h + 1) * HD) for i in range(3))
        qkv_ref[:, q_at] = rotate(lin_ref[:, q_at], cos, sin).astype(BF)
        qkv_ref[:, k_at] = rotate(lin_ref[:, k_at], cos, sin).astype(BF)
        qkv_ref[:, v_at] = lin_ref[:, v_at].astype(BF)
    for step in range(length // WIN):
        low, high, allowed = window(step, col_ref, row_ref)
        rows = slice(step * WIN, (step + 1) * WIN)
        for h in range(width // HD):
            q_at, k_at, v_at = (
                slice(i * width + h * HD, i * width + (h + 1) * HD) for i in range(3)
            )
            scores = mm_nt(qkv_ref[rows, q_at], qkv_ref[low:high, k_at]) * HD**-0.5
            scores = jnp.where(allowed, scores, -1e30)
            peak = jnp.max(scores, axis=1, keepdims=True)
            raw = jnp.exp(scores - peak)
            total = jnp.sum(raw, axis=1, keepdims=True)
            probs = (raw * (1.0 / total)).astype(BF)
            context_ref[rows, h * HD : (h + 1) * HD] = mm(probs, qkv_ref[low:high, v_at]).astype(BF)
            lse_ref[rows, h : h + 1] = peak + jnp.log(total)


def attend(shard, both, weights, tables, seg):
    parts = len(weights)
    rows, depth = both.shape
    length = tables[0].shape[0]
    wide = weights[0].shape[1]
    width = wide // 3
    piece = depth // parts
    whole = lambda *shape: pl.BlockSpec(shape, lambda s, z: (0,) * len(shape))
    take = lambda k: pl.BlockSpec((length, piece), lambda s, z: (s, (z[0] + parts - k) % parts))
    by_seq = lambda cols: pl.BlockSpec((length, cols), lambda s, z: (s, 0))
    return pl.pallas_call(
        functools.partial(attend_kernel, parts),
        grid_spec=pltpu.PrefetchScalarGridSpec(
            num_scalar_prefetch=1,
            grid=(rows // length,),
            in_specs=[take(k) for k in range(parts)]
            + [whole(piece, wide)] * parts
            + [whole(length, HD)] * 2
            + [
                pl.BlockSpec((1, length, 1), lambda s, z: (s, 0, 0)),
                pl.BlockSpec((1, 1, length), lambda s, z: (s, 0, 0)),
            ],
            out_specs=[by_seq(width), by_seq(wide), by_seq(width // HD)],
            scratch_shapes=[pltpu.VMEM((length, wide), F32)],
        ),
        out_shape=[
            jax.ShapeDtypeStruct((rows, width), BF),
            jax.ShapeDtypeStruct((rows, wide), BF),
            jax.ShapeDtypeStruct((rows, width // HD), F32),
        ],
        compiler_params=pltpu.CompilerParams(vmem_limit_bytes=40 << 20),
        cost_estimate=pl.CostEstimate(
            flops=2 * rows * depth * wide + 4 * rows * 2 * WIN * width,
            bytes_accessed=2 * (rows * depth + depth * wide + 2 * rows * wide),
            transcendentals=rows * 2 * WIN * width // HD,
        ),
        name="attend",
    )(shard, *[both] * parts, *weights, *tables, *seg)


def attend_back_kernel(
    grad_ref, out_ref, qkv_ref, lse_ref, x_ref, cos_ref, sin_ref, col_ref, row_ref,
    lin_ref, top_ref, bottom_ref, kept_ref, context_ref, keys_ref, values_ref,
):
    length, wide = qkv_ref.shape
    width = wide // 3
    seq = pl.program_id(0)
    tile = min(length, 256)

    @pl.loop(0, length // tile)
    def _(t):
        rows = pl.ds(pl.multiple_of(t * tile, tile), tile)
        context_ref[rows, :] = mm_nt(grad_ref[rows, :], out_ref[...]).astype(BF)

    cos, sin = cos_ref[...], sin_ref[...]
    scale = HD**-0.5
    for h in range(width // HD):
        q_at, k_at, v_at = (slice(i * width + h * HD, i * width + (h + 1) * HD) for i in range(3))
        head = slice(h * HD, (h + 1) * HD)
        keys_ref[...] = jnp.zeros_like(keys_ref)
        values_ref[...] = jnp.zeros_like(values_ref)
        for step in range(length // WIN):
            low, high, allowed = window(step, col_ref, row_ref)
            rows = slice(step * WIN, (step + 1) * WIN)
            queries, keys = qkv_ref[rows, q_at], qkv_ref[low:high, k_at]
            grad = context_ref[rows, head]
            scores = jnp.where(allowed, mm_nt(queries, keys) * scale, -1e30)
            probs = jnp.exp(scores - lse_ref[rows, h : h + 1])
            values_ref[low:high, :] += mm_tn(probs.astype(BF), grad)
            grad_probs = mm_nt(grad, qkv_ref[low:high, v_at])
            inner = jnp.sum(probs * grad_probs, axis=1, keepdims=True)
            grad_scores = (probs * (grad_probs - inner)).astype(BF)
            grad_queries = mm(grad_scores, keys) * scale
            keys_ref[low:high, :] += mm_tn(grad_scores, queries)
            lin_ref[rows, q_at] = rotate(grad_queries, cos[rows], -sin[rows]).astype(BF)
        lin_ref[:, k_at] = rotate(keys_ref[...] * scale, cos, -sin).astype(BF)
        lin_ref[:, v_at] = values_ref[...].astype(BF)
    kept_ref[pl.ds(pl.multiple_of(seq * length, length), length), :] = lin_ref[...]

    @pl.when(seq == pl.num_programs(0) - 1)
    def _():
        half = top_ref.shape[0]
        step = 256
        for n, ref in enumerate((top_ref, bottom_ref)):

            @pl.loop(0, half // step)
            def _(t):
                cols = pl.ds(pl.multiple_of(n * half + t * step, step), step)
                rows = pl.ds(pl.multiple_of(t * step, step), step)
                ref[rows, :] = mm_tn(x_ref[:, cols], kept_ref[...]).astype(BF)


def attend_back(grad, out_w, qkv, lse, both, tables, seg):
    rows, depth = both.shape
    length = tables[0].shape[0]
    wide = qkv.shape[1]
    width = wide // 3
    whole = lambda *shape: pl.BlockSpec(shape, lambda s: (0,) * len(shape))
    by_seq = lambda cols: pl.BlockSpec((length, cols), lambda s: (s, 0))
    return pl.pallas_call(
        attend_back_kernel,
        grid=(rows // length,),
        in_specs=[by_seq(depth), whole(width, depth), by_seq(wide), by_seq(width // HD)]
        + [whole(rows, depth), whole(length, HD), whole(length, HD)]
        + [
            pl.BlockSpec((1, length, 1), lambda s: (s, 0, 0)),
            pl.BlockSpec((1, 1, length), lambda s: (s, 0, 0)),
        ],
        out_specs=[by_seq(wide), whole(depth // 2, wide), whole(depth // 2, wide)],
        scratch_shapes=[
            pltpu.VMEM((rows, wide), BF),
            pltpu.VMEM((length, width), BF),
            pltpu.VMEM((length, HD), F32),
            pltpu.VMEM((length, HD), F32),
        ],
        out_shape=[
            jax.ShapeDtypeStruct((rows, wide), BF),
            jax.ShapeDtypeStruct((depth // 2, wide), BF),
            jax.ShapeDtypeStruct((depth // 2, wide), BF),
        ],
        compiler_params=pltpu.CompilerParams(vmem_limit_bytes=48 << 20),
        cost_estimate=pl.CostEstimate(
            flops=2 * rows * depth * (wide + width) + 10 * rows * 2 * WIN * width,
            bytes_accessed=2 * (2 * rows * depth + depth * (wide + width) + 2 * rows * wide),
            transcendentals=rows * 2 * WIN * width // HD,
        ),
        name="attend_back",
    )(grad, out_w, qkv, lse, both, *tables, *seg)


def normed_back_kernel(blocks, parts, z_ref, *refs):
    lins, weights, total_ref = refs[:blocks], refs[blocks:-1], refs[-1]
    piece = total_ref.shape[1] // parts
    for k in range(parts):
        total = mm_nt(lins[0][...], weights[k][...])
        for n in range(1, blocks):
            total += mm_nt(lins[n][...], weights[n * parts + k][...])
        at = pl.multiple_of(((z_ref[0] + parts - k) % parts) * piece, piece)
        total_ref[:, pl.ds(at, piece)] = total


def normed_back(shard, lins, weights, depth):
    parts = len(weights[0])
    rows, wide = lins[0].shape
    tile = min(rows, 256)
    flat = [w for block in weights for w in block]
    return pl.pallas_call(
        functools.partial(normed_back_kernel, len(lins), parts),
        grid_spec=pltpu.PrefetchScalarGridSpec(
            num_scalar_prefetch=1,
            grid=(rows // tile,),
            in_specs=[pl.BlockSpec((tile, wide), lambda s, z: (s, 0))] * len(lins)
            + [
                pl.BlockSpec(flat[0].shape, lambda s, z: (0, 0), pipeline_mode=pl.Buffered(1))
            ] * len(flat),
            out_specs=pl.BlockSpec((tile, depth), lambda s, z: (s, 0)),
        ),
        out_shape=jax.ShapeDtypeStruct((rows, depth), F32),
        compiler_params=pltpu.CompilerParams(vmem_limit_bytes=48 << 20),
        cost_estimate=pl.CostEstimate(
            flops=2 * rows * depth * wide * len(lins),
            bytes_accessed=2 * len(lins) * wide * (rows + depth) + 4 * rows * depth,
            transcendentals=0,
        ),
        name="normed_back",
    )(shard, *lins, *flat)


def plan_slots(route_ids, gate_values):
    hit_mask = route_ids == 0
    hit = jnp.any(hit_mask, axis=-1)
    weight = jnp.sum(jnp.where(hit_mask, gate_values, 0.0), axis=-1)
    ids = jnp.arange(route_ids.shape[0], dtype=jnp.int32)
    earlier = (ids[None, :] < ids[:, None]) & hit[None, :]
    order = jnp.sum(earlier.astype(jnp.int32), axis=1)
    kept = hit & (order < CAP)
    slots = jnp.arange(CAP, dtype=jnp.int32)
    table = (order[None, :] == slots[:, None]) & kept[None, :]
    return table, jnp.where(kept, weight, 0.0)


def norm_back(grad_normed, source, root, gain):
    scaled = grad_normed * gain
    grad_gain = jnp.sum(grad_normed * source * root, axis=0)
    mean = jnp.mean(scaled * source, axis=-1, keepdims=True)
    return grad_gain, root * scaled - source * (root * root * root) * mean


def gather_vector(rows):
    size, me = lax.axis_size("shard"), lax.axis_index("shard")
    parts = [rows] + [
        lax.ppermute(rows, "shard", [(i, (i - k) % size) for i in range(size)])
        for k in range(1, size)
    ]
    twice = jnp.concatenate(parts + parts, axis=1)
    own = rows.shape[1]
    return lax.dynamic_slice_in_dim(twice, ((size - me) % size) * own, size * own, 1)


def place_kernel(me_ref, same_ref, other_ref, out_ref):
    odd = jnp.bitwise_xor(pl.program_id(0), me_ref[0]) % 2
    out_ref[...] = jnp.where(odd == 0, same_ref[...], other_ref[...]).astype(F32)


def place(me, same, other, height, width, group, columns):
    size = lax.axis_size("rep")
    spec = pl.BlockSpec(
        (height, width), lambda j, me: (jnp.bitwise_xor(j, me[0]) // 2, group)
    )
    shape = (height, size * width) if columns else (size * height, width)
    return pl.pallas_call(
        place_kernel,
        grid_spec=pltpu.PrefetchScalarGridSpec(
            num_scalar_prefetch=1,
            grid=(size,),
            in_specs=[spec, spec],
            out_specs=pl.BlockSpec(
                (height, width), (lambda j, me: (0, j)) if columns else (lambda j, me: (j, 0))
            ),
        ),
        out_shape=jax.ShapeDtypeStruct(shape, F32),
        cost_estimate=pl.CostEstimate(
            flops=0, bytes_accessed=8 * size * height * width, transcendentals=0
        ),
        name="place",
    )(me, same, other)


def place_turned_kernel(me_ref, same_ref, other_ref, out_ref):
    odd = me_ref[0] % 2
    first = jnp.where(odd == 0, same_ref[...], other_ref[...])
    second = jnp.where(odd == 0, other_ref[...], same_ref[...])
    out_ref[...] = jnp.concatenate([first, second], axis=0).T.astype(F32)


def place_turned(me, same, other, height):
    size, width = lax.axis_size("rep"), same.shape[1]
    if 2 * height % 128:
        return place(me, same, other, height, width, 0, False).T
    spec = pl.BlockSpec((height, width), lambda j, me: (jnp.bitwise_xor(j, me[0] // 2), 0))
    return pl.pallas_call(
        place_turned_kernel,
        grid_spec=pltpu.PrefetchScalarGridSpec(
            num_scalar_prefetch=1,
            grid=(size // 2,),
            in_specs=[spec, spec],
            out_specs=pl.BlockSpec((width, 2 * height), lambda j, me: (0, j)),
        ),
        out_shape=jax.ShapeDtypeStruct((width, size * height), F32),
        compiler_params=pltpu.CompilerParams(vmem_limit_bytes=32 << 20),
        cost_estimate=pl.CostEstimate(
            flops=0, bytes_accessed=12 * same.size, transcendentals=0
        ),
        name="place_turned",
    )(me, same, other)


def gather_copies(value):
    blocks = gather_chips(value)
    same = jnp.concatenate([blocks[d] for d in chip_offsets()], axis=0)
    return same, swap(same, 1)


def sum_vectors(rows):
    size, bit = lax.axis_size("rep"), 1
    while bit < size:
        rows, bit = rows + swap(rows, bit), 2 * bit
    shards, at = lax.axis_size("shard"), lax.axis_index("shard")
    own = rows.shape[1] // shards
    total = lax.dynamic_slice_in_dim(rows, at * own, own, 1)
    for k in range(1, shards):
        part = lax.dynamic_slice_in_dim(rows, ((at + k) % shards) * own, own, 1)
        total += lax.ppermute(part, "shard", [(i, (i + k) % shards) for i in range(shards)])
    return total


def per_device(
    layer_input,
    gain_attn,
    w_query,
    w_key,
    w_value,
    w_out,
    gain_mlp,
    w_gate,
    w_up,
    w_down,
    segments,
    attn_route,
    attn_gate,
    mlp_route,
    mlp_gate,
    cotangent,
):
    length = layer_input.shape[0]
    size = lax.axis_size("rep")
    me = lax.axis_index("rep")
    block = w_query.shape[1] // size
    hidden_block = w_gate.shape[1] // size
    offsets = chip_offsets()

    def columns(weight, width):
        return lax.dynamic_slice_in_dim(weight, me * width, width, 1)

    def rows_of(weight, height):
        return lax.dynamic_slice_in_dim(weight, me * height, height, 0)

    shards = lax.axis_size("shard")
    shard = lax.axis_index("shard").astype(jnp.int32).reshape(1)
    three = (w_query, w_key, w_value)

    def local(d):
        at = jnp.bitwise_xor(me, d) * block
        return jnp.concatenate(
            [lax.dynamic_slice_in_dim(w, at, block, 1) for w in three], axis=1
        )

    piece = local(0)
    qkv_w = {d: [piece if d == 0 else local(d)] for d in offsets}
    ring = [(i, (i + 1) % shards) for i in range(shards)]
    for _ in range(1, shards):
        piece = lax.ppermute(piece, "shard", ring)
        for d, w in gather_chips(piece).items():
            qkv_w[d].append(w)
    own_out, piece = lax.optimization_barrier((rows_of(w_out, block), piece))
    qkv_w[0][-1] = piece
    own_out = lax.all_gather(own_out, "shard", axis=1, tiled=True)
    gate_up = jnp.concatenate([columns(w_gate, hidden_block), columns(w_up, hidden_block)], axis=1)
    out_w = gather_chips(own_out)
    gate_up, _ = lax.optimization_barrier((gate_up, own_out))
    gate_up = lax.all_gather(gate_up, "shard", axis=0, tiled=True)
    own_down, _ = lax.optimization_barrier((rows_of(w_down, hidden_block), gate_up))
    down = lax.all_gather(own_down, "shard", axis=1, tiled=True)

    gains = gather_vector(jnp.stack([gain_attn, gain_mlp])).astype(F32)
    gain_one, gain_two = gains[0], gains[1]

    table, mix = plan_slots(mlp_route, mlp_gate)
    pick = table.astype(BF)
    upstream = cotangent.astype(F32)
    slot_weight = jnp.sum(jnp.where(table, mix[None, :], 0.0), axis=1)[:, None]
    slot_grad = (mm(pick, cotangent) * slot_weight).astype(BF)
    all_slot_grad = gather_plane(slot_grad)

    inputs = layer_input.astype(F32)
    root_one = lax.rsqrt(jnp.mean(inputs * inputs, axis=-1, keepdims=True) + EPSILON)
    normed = (inputs * root_one * gain_one).astype(BF)
    both = jnp.concatenate([normed, swap(normed, 1)], axis=0)
    seg = jnp.concatenate([segments, swap(segments, 1)], axis=0)
    seg = (seg[:, :, None], seg[:, None, :])
    tables = rotary_tables(length)
    context, saved = {}, {}
    for d in offsets:
        context[d], *saved[d] = attend(shard, both, qkv_w[d], tables, seg)
    all_context = jnp.concatenate([context[d] for d in offsets], axis=1)
    all_out = jnp.concatenate([out_w[d] for d in offsets], axis=0)
    projected = mm(all_context, all_out)
    projected = projected[:length] + swap(projected[length:].astype(BF), 1).astype(F32)
    attn_weight = jnp.sum(jnp.where(attn_route == 0, attn_gate, 0.0), axis=-1)[:, None]
    hidden = inputs + projected * attn_weight
    root_two = lax.rsqrt(jnp.mean(hidden * hidden, axis=-1, keepdims=True) + EPSILON)
    normed_two = (hidden * root_two * gain_two).astype(BF)
    normed_two, gate_up = lax.optimization_barrier((normed_two, gate_up))

    dispatched = gather_plane(mm(pick, normed_two).astype(BF))
    act = mm(dispatched, gate_up)
    gate_act, up_act = act[:, :hidden_block], act[:, hidden_block:]
    sigmoid = jax.nn.sigmoid(gate_act)
    silu = gate_act * sigmoid
    inner = (silu * up_act).astype(BF)
    grad_inner = mm_nt(all_slot_grad, down)
    grad_gate_act = (grad_inner * up_act * sigmoid * (1.0 + gate_act * (1.0 - sigmoid))).astype(BF)
    grad_up_act = (grad_inner * silu).astype(BF)
    grad_act = jnp.concatenate([grad_gate_act, grad_up_act], axis=1)
    grad_disp = scatter_plane(mm_nt(grad_act, gate_up).astype(BF)).astype(BF)
    expert_out = scatter_plane(mm(inner, down).astype(BF)).astype(BF)
    output = (hidden + mm_tn(pick, expert_out) * mix[:, None]).astype(BF)
    grad_mlp = [
        mm_tn(grad_gate_act, dispatched).astype(BF),
        mm_tn(grad_up_act, dispatched).astype(BF),
        mm_tn(inner, all_slot_grad).astype(BF),
    ]

    grad_normed_two = mm_tn(pick, grad_disp)
    grad_gain_two, through = norm_back(grad_normed_two, hidden, root_two, gain_two)
    grad_hidden = upstream + through
    grad_hidden, grad_mlp = lax.optimization_barrier((grad_hidden, grad_mlp))

    grad_projected = (grad_hidden * attn_weight).astype(BF)
    both_grad = jnp.concatenate([grad_projected, swap(grad_projected, 1)], axis=0)
    grad_out_w = mm_tn(all_context, both_grad).astype(BF)
    lins, grad_qkv_w = {}, {}
    for d in reversed(offsets):
        lins[d], *grad_qkv_w[d] = attend_back(both_grad, out_w[d], *saved[d], both, tables, seg)
        both_grad, lins[d] = lax.optimization_barrier((both_grad, lins[d]))
    grad_normed = normed_back(
        shard, [lins[d] for d in offsets], [qkv_w[d] for d in offsets], both.shape[1]
    )
    grad_normed = grad_normed[:length] + swap(grad_normed[length:].astype(BF), 1).astype(F32)
    grad_gain_one, first = norm_back(grad_normed, inputs, root_one, gain_one)
    grad_input = (grad_hidden + first).astype(BF)

    whoami = me.astype(jnp.int32).reshape(1)
    sums = [lax.psum_scatter(g, "shard", scatter_dimension=1, tiled=True) for g in grad_mlp]
    own_grad_out = scatter_chips(
        {d: halves(grad_out_w[i * block : (i + 1) * block]) for i, d in enumerate(offsets)}
    ).astype(BF)
    own_grad_out, _ = lax.optimization_barrier((own_grad_out, sums))
    sum_out = lax.psum_scatter(own_grad_out, "shard", scatter_dimension=1, tiled=True)
    own_grad_qkv = scatter_chips(grad_qkv_w).astype(BF)
    own_grad_qkv, _ = lax.optimization_barrier((own_grad_qkv, sum_out))
    sum_qkv = lax.psum_scatter(own_grad_qkv, "shard", scatter_dimension=0, tiled=True)
    own = gain_attn.shape[0]
    grad_gate, grad_up = (
        place_turned(whoami, *gather_copies(g), hidden_block) for g in sums[:2]
    )
    grad_down = place(whoami, *gather_copies(sums[2]), hidden_block, own, 0, False)
    grad_out = place(whoami, *gather_copies(sum_out), block, own, 0, False)
    copies = gather_copies(sum_qkv)
    grad_query, grad_key, grad_value = (
        place(whoami, *copies, own, block, group, True) for group in range(3)
    )
    gain_grads = sum_vectors(jnp.stack([grad_gain_one, grad_gain_two]))
    return (
        output,
        grad_input,
        gain_grads[0],
        grad_query,
        grad_key,
        grad_value,
        grad_out,
        gain_grads[1],
        grad_gate,
        grad_up,
        grad_down,
    )


def solution(mesh):
    tokens = P(("rep", "shard"), None)
    tall, wide, vector = P("shard", None), P(None, "shard"), P("shard")
    weights = (vector, tall, tall, tall, wide, vector, tall, tall, wide)
    return jax.shard_map(
        per_device,
        mesh=mesh,
        in_specs=(tokens, *weights) + (tokens,) * 6,
        out_specs=(tokens, tokens, *weights),
        check_vma=False,
    )
```

```python
import functools

import jax
import jax.numpy as jnp
from jax import lax
from jax.experimental import pallas as pl
from jax.experimental.pallas import tpu as pltpu
from jax.sharding import PartitionSpec as P

HEADS = 16
HD = 128
WIN = 256
CAP = 128
EPSILON = 1e-05
BF = jnp.bfloat16
F32 = jnp.float32


def mm(left, right):
    return jnp.dot(left, right, preferred_element_type=F32)


def mm_nt(left, right):
    return lax.dot_general(left, right, (((1,), (1,)), ((), ())), preferred_element_type=F32)


def mm_tn(left, right):
    return lax.dot_general(left, right, (((0,), (0,)), ((), ())), preferred_element_type=F32)


def swap(value, bit):
    size = lax.axis_size("rep")
    return lax.ppermute(value, "rep", [(i, i ^ bit) for i in range(size)])


def chip_bits():
    size, bits, bit = lax.axis_size("rep"), [], 2
    while bit < size:
        bits.append(bit)
        bit *= 2
    return bits


def chip_offsets():
    return list(range(0, lax.axis_size("rep"), 2))


def add(left, right):
    return left.astype(F32) + right.astype(F32)


def halves(value):
    half = value.shape[0] // 2
    return value[:half], value[half:]


class Flow:
    def __init__(self, steps):
        self.steps, self.result, self.done = steps, None, False
        self.pending = next(steps)

    def advance(self, arrived):
        try:
            self.pending = self.steps.send(arrived)
        except StopIteration as end:
            self.pending, self.result, self.done = [], end.value, True


def stage(flows, extra=()):
    flows = [f for f in flows if not f.done]
    arrived, extra = lax.optimization_barrier(([f.pending for f in flows], extra))
    for flow, values in zip(flows, arrived):
        flow.advance(values)
    return extra


def finish(flow):
    while not flow.done:
        flow.advance(flow.pending)
    return flow.result


def gather_steps(value, sink=lambda offset, block: None):
    bits = chip_bits()
    if len(bits) == 2:
        one, two = bits
        half = value.shape[0] // 2
        by_one, by_two = yield [swap(value, one), swap(value, two)]
        sink(one, by_one)
        sink(two, by_two)
        top, bottom = yield [swap(by_one[:half], two), swap(by_two[half:], one)]
        far = jnp.concatenate([top, bottom], axis=0)
        sink(one ^ two, far)
        return {0: value, one: by_one, two: by_two, one ^ two: far}
    blocks = {0: value}
    for bit in bits:
        old = list(blocks.items())
        new = yield [swap(b, bit) for _, b in old]
        for (d, _), b in zip(old, new):
            blocks[d ^ bit] = b
            sink(d ^ bit, b)
    return blocks


def copies_steps(value):
    blocks = yield from gather_steps(value)
    same = jnp.concatenate([blocks[d] for d in chip_offsets()], axis=0)
    (other,) = yield [swap(same, 1)]
    return same, other


def scatter_steps(blocks):
    bits = chip_bits()
    if len(bits) == 2:
        one, two = bits
        far = blocks[one ^ two]
        top, bottom = yield [swap(far[0], one), swap(far[1], two)]
        near_one, near_two = blocks[one], blocks[two]
        one_top, two_bottom = yield [swap(near_one[0], one), swap(near_two[1], two)]
        two_top, one_bottom = yield [
            swap(add(near_two[0], top).astype(BF), two),
            swap(add(near_one[1], bottom).astype(BF), one),
        ]
        return jnp.concatenate(
            [
                (add(blocks[0][0], one_top) + two_top.astype(F32)).astype(BF),
                (add(blocks[0][1], one_bottom) + two_bottom.astype(F32)).astype(BF),
            ],
            axis=0,
        )
    while len(blocks) < len(chip_offsets()):
        yield []
    sums = {d: jnp.concatenate(b, axis=0) for d, b in blocks.items()}
    for bit in reversed(bits):
        kept = [d for d in sorted(sums) if not d & bit]
        new = yield [swap(sums[d | bit], bit) for d in kept]
        sums = {d: add(sums[d], n).astype(BF) for d, n in zip(kept, new)}
    return sums[0]


def plane_sum_steps(partial):
    half = partial.shape[0] // 2
    (other,) = yield [swap(partial[half:], 1)]
    same = add(partial[:half], other).astype(BF)
    offsets = chip_offsets()
    rows = half // len(offsets)
    blocks = {d: halves(same[i * rows : (i + 1) * rows]) for i, d in enumerate(offsets)}
    return (yield from scatter_steps(blocks))


def vector_sum_steps(rows):
    size, bit = lax.axis_size("rep"), 1
    while bit < size:
        (other,) = yield [swap(rows, bit)]
        rows, bit = rows + other, 2 * bit
    shards, at = lax.axis_size("shard"), lax.axis_index("shard")
    own = rows.shape[1] // shards
    parts = yield [
        lax.ppermute(
            lax.dynamic_slice_in_dim(rows, ((at + k) % shards) * own, own, 1),
            "shard",
            [(i, (i + k) % shards) for i in range(shards)],
        )
        for k in range(1, shards)
    ]
    return lax.dynamic_slice_in_dim(rows, at * own, own, 1) + sum(parts)


def vector_gather_steps(rows):
    size, me = lax.axis_size("shard"), lax.axis_index("shard")
    others = yield [
        lax.ppermute(rows, "shard", [(i, (i - k) % size) for i in range(size)])
        for k in range(1, size)
    ]
    parts = [rows, *others]
    twice = jnp.concatenate(parts + parts, axis=1)
    own = rows.shape[1]
    return lax.dynamic_slice_in_dim(twice, ((size - me) % size) * own, size * own, 1)


def rotary_tables(length):
    half = HD // 2
    positions = jnp.arange(length, dtype=F32)
    inverse = 10000.0 ** (-2.0 * jnp.arange(half, dtype=F32) / HD)
    angles = positions[:, None] * inverse[None, :]
    cos, sin = jnp.cos(angles), jnp.sin(angles)
    return jnp.concatenate([cos, cos], axis=1), jnp.concatenate([-sin, sin], axis=1)


def rotate(values, cos, sin):
    return values * cos + pltpu.roll(values, HD // 2, 1) * sin


def window(step, seg_col, seg_row):
    low, high = max(0, step - 1) * WIN, (step + 1) * WIN
    shape = (WIN, high - low)
    row = lax.broadcasted_iota(jnp.int32, shape, 0) + step * WIN
    col = lax.broadcasted_iota(jnp.int32, shape, 1) + low
    near = (row >= col) & (row - col < WIN)
    same = seg_col[0, step * WIN : (step + 1) * WIN, :] == seg_row[0, :, low:high]
    return low, high, near & same


def attend_kernel(parts, z_ref, *refs):
    x_refs, w_refs = refs[:parts], refs[parts : 2 * parts]
    cos_ref, sin_ref, col_ref, row_ref, context_ref, qkv_ref, lse_ref, lin_ref = refs[2 * parts :]
    length, width = context_ref.shape
    tile = min(length, 256)

    @pl.loop(0, length // tile)
    def _(t):
        rows = pl.ds(pl.multiple_of(t * tile, tile), tile)
        total = mm(x_refs[0][rows, :], w_refs[0][...])
        for x, w in zip(x_refs[1:], w_refs[1:]):
            total += mm(x[rows, :], w[...])
        lin_ref[rows, :] = total

    cos, sin = cos_ref[...], sin_ref[...]
    for h in range(width // HD):
        q_at, k_at, v_at = (slice(i * width + h * HD, i * width + (h + 1) * HD) for i in range(3))
        qkv_ref[:, q_at] = rotate(lin_ref[:, q_at], cos, sin).astype(BF)
        qkv_ref[:, k_at] = rotate(lin_ref[:, k_at], cos, sin).astype(BF)
        qkv_ref[:, v_at] = lin_ref[:, v_at].astype(BF)
    for step in range(length // WIN):
        low, high, allowed = window(step, col_ref, row_ref)
        rows = slice(step * WIN, (step + 1) * WIN)
        for h in range(width // HD):
            q_at, k_at, v_at = (
                slice(i * width + h * HD, i * width + (h + 1) * HD) for i in range(3)
            )
            scores = mm_nt(qkv_ref[rows, q_at], qkv_ref[low:high, k_at]) * HD**-0.5
            scores = jnp.where(allowed, scores, -1e30)
            peak = jnp.max(scores, axis=1, keepdims=True)
            raw = jnp.exp(scores - peak)
            total = jnp.sum(raw, axis=1, keepdims=True)
            probs = (raw * (1.0 / total)).astype(BF)
            context_ref[rows, h * HD : (h + 1) * HD] = mm(probs, qkv_ref[low:high, v_at]).astype(BF)
            lse_ref[rows, h : h + 1] = peak + jnp.log(total)


def attend(shard, both, weights, tables, seg):
    parts = len(weights)
    rows, depth = both.shape
    length = tables[0].shape[0]
    wide = weights[0].shape[1]
    width = wide // 3
    piece = depth // parts
    whole = lambda *shape: pl.BlockSpec(shape, lambda s, z: (0,) * len(shape))
    take = lambda k: pl.BlockSpec((length, piece), lambda s, z: (s, (z[0] + parts - k) % parts))
    by_seq = lambda cols: pl.BlockSpec((length, cols), lambda s, z: (s, 0))
    return pl.pallas_call(
        functools.partial(attend_kernel, parts),
        grid_spec=pltpu.PrefetchScalarGridSpec(
            num_scalar_prefetch=1,
            grid=(rows // length,),
            in_specs=[take(k) for k in range(parts)]
            + [whole(piece, wide)] * parts
            + [whole(length, HD)] * 2
            + [
                pl.BlockSpec((1, length, 1), lambda s, z: (s, 0, 0)),
                pl.BlockSpec((1, 1, length), lambda s, z: (s, 0, 0)),
            ],
            out_specs=[by_seq(width), by_seq(wide), by_seq(width // HD)],
            scratch_shapes=[pltpu.VMEM((length, wide), F32)],
        ),
        out_shape=[
            jax.ShapeDtypeStruct((rows, width), BF),
            jax.ShapeDtypeStruct((rows, wide), BF),
            jax.ShapeDtypeStruct((rows, width // HD), F32),
        ],
        compiler_params=pltpu.CompilerParams(vmem_limit_bytes=40 << 20),
        cost_estimate=pl.CostEstimate(
            flops=2 * rows * depth * wide + 4 * rows * 2 * WIN * width,
            bytes_accessed=2 * (rows * depth + depth * wide + 2 * rows * wide),
            transcendentals=rows * 2 * WIN * width // HD,
        ),
        name="attend",
    )(shard, *[both] * parts, *weights, *tables, *seg)


def attend_back_kernel(
    grad_ref, out_ref, qkv_ref, lse_ref, x_ref, cos_ref, sin_ref, col_ref, row_ref,
    lin_ref, top_ref, bottom_ref, kept_ref, context_ref, keys_ref, values_ref,
):
    length, wide = qkv_ref.shape
    width = wide // 3
    seq = pl.program_id(0)
    tile = min(length, 256)

    @pl.loop(0, length // tile)
    def _(t):
        rows = pl.ds(pl.multiple_of(t * tile, tile), tile)
        context_ref[rows, :] = mm_nt(grad_ref[rows, :], out_ref[...]).astype(BF)

    cos, sin = cos_ref[...], sin_ref[...]
    scale = HD**-0.5
    for h in range(width // HD):
        q_at, k_at, v_at = (slice(i * width + h * HD, i * width + (h + 1) * HD) for i in range(3))
        head = slice(h * HD, (h + 1) * HD)
        keys_ref[...] = jnp.zeros_like(keys_ref)
        values_ref[...] = jnp.zeros_like(values_ref)
        for step in range(length // WIN):
            low, high, allowed = window(step, col_ref, row_ref)
            rows = slice(step * WIN, (step + 1) * WIN)
            queries, keys = qkv_ref[rows, q_at], qkv_ref[low:high, k_at]
            grad = context_ref[rows, head]
            scores = jnp.where(allowed, mm_nt(queries, keys) * scale, -1e30)
            probs = jnp.exp(scores - lse_ref[rows, h : h + 1])
            values_ref[low:high, :] += mm_tn(probs.astype(BF), grad)
            grad_probs = mm_nt(grad, qkv_ref[low:high, v_at])
            inner = jnp.sum(probs * grad_probs, axis=1, keepdims=True)
            grad_scores = (probs * (grad_probs - inner)).astype(BF)
            grad_queries = mm(grad_scores, keys) * scale
            keys_ref[low:high, :] += mm_tn(grad_scores, queries)
            lin_ref[rows, q_at] = rotate(grad_queries, cos[rows], -sin[rows]).astype(BF)
        lin_ref[:, k_at] = rotate(keys_ref[...] * scale, cos, -sin).astype(BF)
        lin_ref[:, v_at] = values_ref[...].astype(BF)
    kept_ref[pl.ds(pl.multiple_of(seq * length, length), length), :] = lin_ref[...]

    @pl.when(seq == pl.num_programs(0) - 1)
    def _():
        half = top_ref.shape[0]
        step = 256
        for n, ref in enumerate((top_ref, bottom_ref)):

            @pl.loop(0, half // step)
            def _(t):
                cols = pl.ds(pl.multiple_of(n * half + t * step, step), step)
                rows = pl.ds(pl.multiple_of(t * step, step), step)
                ref[rows, :] = mm_tn(x_ref[:, cols], kept_ref[...]).astype(BF)


def attend_back(grad, out_w, qkv, lse, both, tables, seg):
    rows, depth = both.shape
    length = tables[0].shape[0]
    wide = qkv.shape[1]
    width = wide // 3
    whole = lambda *shape: pl.BlockSpec(shape, lambda s: (0,) * len(shape))
    by_seq = lambda cols: pl.BlockSpec((length, cols), lambda s: (s, 0))
    return pl.pallas_call(
        attend_back_kernel,
        grid=(rows // length,),
        in_specs=[by_seq(depth), whole(width, depth), by_seq(wide), by_seq(width // HD)]
        + [whole(rows, depth), whole(length, HD), whole(length, HD)]
        + [
            pl.BlockSpec((1, length, 1), lambda s: (s, 0, 0)),
            pl.BlockSpec((1, 1, length), lambda s: (s, 0, 0)),
        ],
        out_specs=[by_seq(wide), whole(depth // 2, wide), whole(depth // 2, wide)],
        scratch_shapes=[
            pltpu.VMEM((rows, wide), BF),
            pltpu.VMEM((length, width), BF),
            pltpu.VMEM((length, HD), F32),
            pltpu.VMEM((length, HD), F32),
        ],
        out_shape=[
            jax.ShapeDtypeStruct((rows, wide), BF),
            jax.ShapeDtypeStruct((depth // 2, wide), BF),
            jax.ShapeDtypeStruct((depth // 2, wide), BF),
        ],
        compiler_params=pltpu.CompilerParams(vmem_limit_bytes=48 << 20),
        cost_estimate=pl.CostEstimate(
            flops=2 * rows * depth * (wide + width) + 10 * rows * 2 * WIN * width,
            bytes_accessed=2 * (2 * rows * depth + depth * (wide + width) + 2 * rows * wide),
            transcendentals=rows * 2 * WIN * width // HD,
        ),
        name="attend_back",
    )(grad, out_w, qkv, lse, both, *tables, *seg)


def normed_back_kernel(blocks, parts, z_ref, *refs):
    lins, weights, total_ref = refs[:blocks], refs[blocks:-1], refs[-1]
    piece = total_ref.shape[1] // parts
    for k in range(parts):
        total = mm_nt(lins[0][...], weights[k][...])
        for n in range(1, blocks):
            total += mm_nt(lins[n][...], weights[n * parts + k][...])
        at = pl.multiple_of(((z_ref[0] + parts - k) % parts) * piece, piece)
        total_ref[:, pl.ds(at, piece)] = total


def normed_back(shard, lins, weights, depth):
    parts = len(weights[0])
    rows, wide = lins[0].shape
    tile = min(rows, 256)
    flat = [w for block in weights for w in block]
    return pl.pallas_call(
        functools.partial(normed_back_kernel, len(lins), parts),
        grid_spec=pltpu.PrefetchScalarGridSpec(
            num_scalar_prefetch=1,
            grid=(rows // tile,),
            in_specs=[pl.BlockSpec((tile, wide), lambda s, z: (s, 0))] * len(lins)
            + [
                pl.BlockSpec(flat[0].shape, lambda s, z: (0, 0), pipeline_mode=pl.Buffered(1))
            ] * len(flat),
            out_specs=pl.BlockSpec((tile, depth), lambda s, z: (s, 0)),
        ),
        out_shape=jax.ShapeDtypeStruct((rows, depth), F32),
        compiler_params=pltpu.CompilerParams(vmem_limit_bytes=48 << 20),
        cost_estimate=pl.CostEstimate(
            flops=2 * rows * depth * wide * len(lins),
            bytes_accessed=2 * len(lins) * wide * (rows + depth) + 4 * rows * depth,
            transcendentals=0,
        ),
        name="normed_back",
    )(shard, *lins, *flat)


def plan_slots(route_ids, gate_values):
    hit_mask = route_ids == 0
    hit = jnp.any(hit_mask, axis=-1)
    weight = jnp.sum(jnp.where(hit_mask, gate_values, 0.0), axis=-1)
    ids = jnp.arange(route_ids.shape[0], dtype=jnp.int32)
    earlier = (ids[None, :] < ids[:, None]) & hit[None, :]
    order = jnp.sum(earlier.astype(jnp.int32), axis=1)
    kept = hit & (order < CAP)
    slots = jnp.arange(CAP, dtype=jnp.int32)
    table = (order[None, :] == slots[:, None]) & kept[None, :]
    return table, jnp.where(kept, weight, 0.0)


def norm_back(grad_normed, source, root, gain):
    scaled = grad_normed * gain
    grad_gain = jnp.sum(grad_normed * source * root, axis=0)
    mean = jnp.mean(scaled * source, axis=-1, keepdims=True)
    return grad_gain, root * scaled - source * (root * root * root) * mean


def place_kernel(me_ref, same_ref, other_ref, *out_refs):
    odd = jnp.bitwise_xor(pl.program_id(0), me_ref[0]) % 2
    block = jnp.where(odd == 0, same_ref[...], other_ref[...]).astype(F32)
    width = out_refs[0].shape[1]
    for i, ref in enumerate(out_refs):
        ref[...] = block[:, i * width : (i + 1) * width]


def place(me, same, other, height, width, columns):
    size, total = lax.axis_size("rep"), same.shape[1]
    spec = pl.BlockSpec((height, total), lambda j, me: (jnp.bitwise_xor(j, me[0]) // 2, 0))
    shape = (height, size * width) if columns else (size * height, width)
    count = total // width
    return pl.pallas_call(
        place_kernel,
        grid_spec=pltpu.PrefetchScalarGridSpec(
            num_scalar_prefetch=1,
            grid=(size,),
            in_specs=[spec, spec],
            out_specs=[
                pl.BlockSpec(
                    (height, width), (lambda j, me: (0, j)) if columns else (lambda j, me: (j, 0))
                )
            ] * count,
        ),
        out_shape=[jax.ShapeDtypeStruct(shape, F32)] * count,
        cost_estimate=pl.CostEstimate(
            flops=0, bytes_accessed=8 * size * height * total, transcendentals=0
        ),
        name="place",
    )(me, same, other)


def place_turned_kernel(me_ref, same_ref, other_ref, out_ref):
    odd = me_ref[0] % 2
    first = jnp.where(odd == 0, same_ref[...], other_ref[...])
    second = jnp.where(odd == 0, other_ref[...], same_ref[...])
    out_ref[...] = jnp.concatenate([first, second], axis=0).T.astype(F32)


def place_turned(me, same, other, height):
    size, width = lax.axis_size("rep"), same.shape[1]
    if 2 * height % 128:
        return place(me, same, other, height, width, False)[0].T
    spec = pl.BlockSpec((height, width), lambda j, me: (jnp.bitwise_xor(j, me[0] // 2), 0))
    return pl.pallas_call(
        place_turned_kernel,
        grid_spec=pltpu.PrefetchScalarGridSpec(
            num_scalar_prefetch=1,
            grid=(size // 2,),
            in_specs=[spec, spec],
            out_specs=pl.BlockSpec((width, 2 * height), lambda j, me: (0, j)),
        ),
        out_shape=jax.ShapeDtypeStruct((width, size * height), F32),
        compiler_params=pltpu.CompilerParams(vmem_limit_bytes=32 << 20),
        cost_estimate=pl.CostEstimate(
            flops=0, bytes_accessed=12 * same.size, transcendentals=0
        ),
        name="place_turned",
    )(me, same, other)


def per_device(
    layer_input,
    gain_attn,
    w_query,
    w_key,
    w_value,
    w_out,
    gain_mlp,
    w_gate,
    w_up,
    w_down,
    segments,
    attn_route,
    attn_gate,
    mlp_route,
    mlp_gate,
    cotangent,
):
    length = layer_input.shape[0]
    size, shards = lax.axis_size("rep"), lax.axis_size("shard")
    me = lax.axis_index("rep")
    whoami = me.astype(jnp.int32).reshape(1)
    shard = lax.axis_index("shard").astype(jnp.int32).reshape(1)
    block = w_query.shape[1] // size
    units = w_gate.shape[1] // size
    own = gain_attn.shape[0]
    offsets = chip_offsets()
    staged = len(chip_bits()) == 2

    def columns(weight, d, width):
        return lax.dynamic_slice_in_dim(weight, jnp.bitwise_xor(me, d) * width, width, 1)

    def rows_of(weight, height):
        return lax.dynamic_slice_in_dim(weight, me * height, height, 0)

    def local(d):
        return jnp.concatenate([columns(w, d, block) for w in (w_query, w_key, w_value)], axis=1)

    inputs = layer_input.astype(F32)
    root_one = lax.rsqrt(jnp.mean(inputs * inputs, axis=-1, keepdims=True) + EPSILON)
    tables = rotary_tables(length)
    ring = [(i, (i + 1) % shards) for i in range(shards)]
    piece = local(0)
    qkv_w = {d: [local(d)] for d in offsets}
    flows, context, saved = [], {}, {}
    gain_flow = Flow(vector_gather_steps(jnp.stack([gain_attn, gain_mlp])))
    piece, seg_other, own_gate_up = stage(
        [gain_flow],
        (
            lax.ppermute(piece, "shard", ring),
            swap(segments, 1),
            jnp.concatenate([columns(w_gate, 0, units), columns(w_up, 0, units)], axis=1),
        ),
    )
    gain_one, gain_two = gain_flow.result.astype(F32)
    normed = (inputs * root_one * gain_one).astype(BF)
    seg = jnp.concatenate([segments, seg_other], axis=0)
    seg = (seg[:, :, None], seg[:, None, :])
    other = swap(normed, 1)
    for step in range(1, shards):
        qkv_w[0].append(piece)
        flows.append(Flow(gather_steps(piece, lambda d, b: qkv_w[d].append(b))))
        if step < shards - 1:
            piece, other = stage(flows, (lax.ppermute(piece, "shard", ring), other))
    own_out, own_gate_up, qkv_w[0][-1] = lax.optimization_barrier(
        (rows_of(w_out, block), own_gate_up, qkv_w[0][-1])
    )
    own_out = lax.all_gather(own_out, "shard", axis=1, tiled=True)
    both = jnp.concatenate([normed, other], axis=0)

    def run(d):
        context[d], *saved[d] = attend(shard, both, qkv_w[d], tables, seg)
        return context[d]

    context[0], own_out = stage(flows, (run(0), own_out))
    own_gate_up, own_out = lax.optimization_barrier((own_gate_up, own_out))
    gate_up = lax.all_gather(own_gate_up, "shard", axis=0, tiled=True)
    own_down, _ = lax.optimization_barrier((rows_of(w_down, units), gate_up))
    down = lax.all_gather(own_down, "shard", axis=1, tiled=True)
    early = offsets[1:2] if staged else []
    early = stage(flows, [run(d) for d in early])
    for flow in flows:
        finish(flow)
    out_flow = Flow(gather_steps(own_out))
    rest = [d for d in offsets if d not in context]
    stage([out_flow], [run(d) for d in rest])
    out_w = finish(out_flow)

    table, mix = plan_slots(mlp_route, mlp_gate)
    pick = table.astype(BF)
    upstream = cotangent.astype(F32)
    slot_weight = jnp.sum(jnp.where(table, mix[None, :], 0.0), axis=1)[:, None]
    slot_grad = (mm(pick, cotangent) * slot_weight).astype(BF)

    all_context = jnp.concatenate([context[d] for d in offsets], axis=1)
    all_out = jnp.concatenate([out_w[d] for d in offsets], axis=0)
    projected = mm(all_context, all_out)
    projected = projected[:length] + swap(projected[length:].astype(BF), 1).astype(F32)
    attn_weight = jnp.sum(jnp.where(attn_route == 0, attn_gate, 0.0), axis=-1)[:, None]
    hidden = inputs + projected * attn_weight
    root_two = lax.rsqrt(jnp.mean(hidden * hidden, axis=-1, keepdims=True) + EPSILON)
    normed_two = (hidden * root_two * gain_two).astype(BF)

    disp_flow = Flow(copies_steps(mm(pick, normed_two).astype(BF)))
    stage([disp_flow])
    slot_grad, gate_up = stage([disp_flow], (slot_grad, gate_up))
    slot_flow = Flow(copies_steps(slot_grad))
    stage([disp_flow, slot_flow])
    dispatched = jnp.concatenate(finish(disp_flow), axis=0)
    act = mm(dispatched, gate_up)
    all_slot_grad = jnp.concatenate(finish(slot_flow), axis=0)
    gate_act, up_act = act[:, :units], act[:, units:]
    sigmoid = jax.nn.sigmoid(gate_act)
    silu = gate_act * sigmoid
    inner = (silu * up_act).astype(BF)
    grad_inner = mm_nt(all_slot_grad, down)
    grad_gate_act = (grad_inner * up_act * sigmoid * (1.0 + gate_act * (1.0 - sigmoid))).astype(BF)
    grad_up_act = (grad_inner * silu).astype(BF)
    grad_act = jnp.concatenate([grad_gate_act, grad_up_act], axis=1)
    back_flow = Flow(plane_sum_steps(mm_nt(grad_act, gate_up).astype(BF)))
    grad_mlp, sums = [], []
    for left, right in (
        (grad_gate_act, dispatched),
        (grad_up_act, dispatched),
        (inner, all_slot_grad),
    ):
        grad = stage([back_flow], mm_tn(left, right).astype(BF))
        sums.append(lax.psum_scatter(grad, "shard", scatter_dimension=1, tiled=True))
    grad_normed_two = mm_tn(pick, finish(back_flow))
    grad_gain_two, through = norm_back(grad_normed_two, hidden, root_two, gain_two)
    grad_hidden = upstream + through

    grad_projected = (grad_hidden * attn_weight).astype(BF)
    both_grad = jnp.concatenate([grad_projected, swap(grad_projected, 1)], axis=0)
    lins, grad_qkv_w = {}, {}

    def run_back(*ds):
        for d in ds:
            lins[d], *grad_qkv_w[d] = attend_back(
                both_grad, out_w[d], *saved[d], both, tables, seg
            )
        return [(lins[d], grad_qkv_w[d]) for d in ds]

    def keep(ds, values):
        for d, (lin, grad) in zip(ds, values):
            lins[d], grad_qkv_w[d] = lin, grad

    far, near = offsets[-1:], offsets[1:-1]
    values, both_grad = lax.optimization_barrier((run_back(*far), both_grad))
    keep(far, values)
    qkv_flow = Flow(scatter_steps(grad_qkv_w))
    values, both_grad = stage([qkv_flow], (run_back(*near), both_grad))
    keep(near, values)
    values, grad_out_w = stage([qkv_flow], (run_back(0), mm_tn(all_context, both_grad).astype(BF)))
    keep([0], values)
    grad_normed = normed_back(
        shard, [lins[d] for d in offsets], [qkv_w[d] for d in offsets], both.shape[1]
    )
    sums[0], sums[1], grad_normed, grad_out_w = stage(
        [qkv_flow], (sums[0], sums[1], grad_normed, grad_out_w)
    )
    own_grad_qkv, sums[2] = lax.optimization_barrier((finish(qkv_flow), sums[2]))
    sum_qkv = lax.psum_scatter(own_grad_qkv, "shard", scatter_dimension=0, tiled=True)
    grad_normed = grad_normed[:length] + swap(grad_normed[length:].astype(BF), 1).astype(F32)
    grad_gain_one, first = norm_back(grad_normed, inputs, root_one, gain_one)
    grad_input = (grad_hidden + first).astype(BF)

    out_blocks = {d: halves(grad_out_w[i * block : (i + 1) * block]) for i, d in enumerate(offsets)}
    expert_out = mm(inner, down).astype(BF)
    gate_flow, expert_flow = Flow(copies_steps(sums[0])), Flow(plane_sum_steps(expert_out))
    up_flow = Flow(copies_steps(sums[1]))
    grad_input, gains, out_blocks = stage(
        [gate_flow, up_flow, expert_flow],
        (grad_input, jnp.stack([grad_gain_one, grad_gain_two]), out_blocks),
    )
    gain_flow, out_flow = Flow(vector_sum_steps(gains)), Flow(scatter_steps(out_blocks))
    stage([gate_flow, up_flow, gain_flow])
    stage([gate_flow, up_flow, out_flow, gain_flow])
    stage([out_flow, expert_flow, gain_flow])
    sums[2] = stage([out_flow, expert_flow], sums[2])
    grad_gate = place_turned(whoami, *finish(gate_flow), units)
    grad_up = place_turned(whoami, *finish(up_flow), units)
    own_grad_out, sum_qkv = lax.optimization_barrier((finish(out_flow), sum_qkv))
    sum_out = lax.psum_scatter(own_grad_out, "shard", scatter_dimension=1, tiled=True)
    down_flow, qkv_flow = Flow(copies_steps(sums[2])), Flow(copies_steps(sum_qkv))
    grad_gate, grad_up = stage([down_flow, qkv_flow], (grad_gate, grad_up))
    stage([qkv_flow, down_flow])
    stage([qkv_flow, down_flow, expert_flow])
    (grad_down,) = place(whoami, *finish(down_flow), units, own, False)
    out_flow = Flow(copies_steps(sum_out))
    grad_down = stage([out_flow, gain_flow], grad_down)
    grad_query, grad_key, grad_value = place(whoami, *finish(qkv_flow), own, block, True)
    output = (hidden + mm_tn(pick, finish(expert_flow)) * mix[:, None]).astype(BF)
    (grad_out,) = place(whoami, *finish(out_flow), block, own, False)
    gain_grads = finish(gain_flow)
    return (
        output,
        grad_input,
        gain_grads[0],
        grad_query,
        grad_key,
        grad_value,
        grad_out,
        gain_grads[1],
        grad_gate,
        grad_up,
        grad_down,
    )


def solution(mesh):
    tokens = P(("rep", "shard"), None)
    tall, wide, vector = P("shard", None), P(None, "shard"), P("shard")
    weights = (vector, tall, tall, tall, wide, vector, tall, tall, wide)
    return jax.shard_map(
        per_device,
        mesh=mesh,
        in_specs=(tokens, *weights) + (tokens,) * 6,
        out_specs=(tokens, tokens, *weights),
        check_vma=False,
    )
```

```python
import functools

import jax
import jax.numpy as jnp
from jax import lax
from jax.experimental import pallas as pl
from jax.experimental.pallas import tpu as pltpu
from jax.sharding import PartitionSpec as P

HEADS = 16
HD = 128
WIN = 256
CAP = 128
EPSILON = 1e-05
BF = jnp.bfloat16
F32 = jnp.float32


def mm(left, right):
    return jnp.dot(left, right, preferred_element_type=F32)


def mm_nt(left, right):
    return lax.dot_general(left, right, (((1,), (1,)), ((), ())), preferred_element_type=F32)


def mm_tn(left, right):
    return lax.dot_general(left, right, (((0,), (0,)), ((), ())), preferred_element_type=F32)


def swap(value, bit):
    size = lax.axis_size("rep")
    return lax.ppermute(value, "rep", [(i, i ^ bit) for i in range(size)])


def chip_bits():
    size, bits, bit = lax.axis_size("rep"), [], 2
    while bit < size:
        bits.append(bit)
        bit *= 2
    return bits


def chip_offsets():
    return list(range(0, lax.axis_size("rep"), 2))


def add(left, right):
    return left.astype(F32) + right.astype(F32)


def halves(value):
    half = value.shape[0] // 2
    return value[:half], value[half:]


class Flow:
    def __init__(self, steps):
        self.steps, self.result, self.done = steps, None, False
        self.pending = next(steps)

    def advance(self, arrived):
        try:
            self.pending = self.steps.send(arrived)
        except StopIteration as end:
            self.pending, self.result, self.done = [], end.value, True


def stage(flows, extra=()):
    flows = [f for f in flows if not f.done]
    arrived, extra = lax.optimization_barrier(([f.pending for f in flows], extra))
    for flow, values in zip(flows, arrived):
        flow.advance(values)
    return extra


def finish(flow):
    while not flow.done:
        flow.advance(flow.pending)
    return flow.result


def gather_steps(value, sink=lambda offset, block: None):
    bits = chip_bits()
    if len(bits) == 2:
        one, two = bits
        half = value.shape[0] // 2
        by_one, by_two = yield [swap(value, one), swap(value, two)]
        sink(one, by_one)
        sink(two, by_two)
        top, bottom = yield [swap(by_one[:half], two), swap(by_two[half:], one)]
        far = jnp.concatenate([top, bottom], axis=0)
        sink(one ^ two, far)
        return {0: value, one: by_one, two: by_two, one ^ two: far}
    blocks = {0: value}
    for bit in bits:
        old = list(blocks.items())
        new = yield [swap(b, bit) for _, b in old]
        for (d, _), b in zip(old, new):
            blocks[d ^ bit] = b
            sink(d ^ bit, b)
    return blocks


def copies_steps(value):
    blocks = yield from gather_steps(value)
    same = jnp.concatenate([blocks[d] for d in chip_offsets()], axis=0)
    (other,) = yield [swap(same, 1)]
    return same, other


def scatter_steps(blocks):
    bits = chip_bits()
    if len(bits) == 2:
        one, two = bits
        far = blocks[one ^ two]
        top, bottom = yield [swap(far[0], one), swap(far[1], two)]
        near_one, near_two = blocks[one], blocks[two]
        one_top, two_bottom = yield [swap(near_one[0], one), swap(near_two[1], two)]
        two_top, one_bottom = yield [
            swap(add(near_two[0], top).astype(BF), two),
            swap(add(near_one[1], bottom).astype(BF), one),
        ]
        return jnp.concatenate(
            [
                (add(blocks[0][0], one_top) + two_top.astype(F32)).astype(BF),
                (add(blocks[0][1], one_bottom) + two_bottom.astype(F32)).astype(BF),
            ],
            axis=0,
        )
    while len(blocks) < len(chip_offsets()):
        yield []
    sums = {d: jnp.concatenate(b, axis=0) for d, b in blocks.items()}
    for bit in reversed(bits):
        kept = [d for d in sorted(sums) if not d & bit]
        new = yield [swap(sums[d | bit], bit) for d in kept]
        sums = {d: add(sums[d], n).astype(BF) for d, n in zip(kept, new)}
    return sums[0]


def exchange_steps(blocks):
    bits = chip_bits()
    if len(bits) == 2:
        one, two = bits
        top, bottom = yield [swap(h, bit) for h, bit in zip(halves(blocks[one ^ two]), bits)]
        near = [swap(blocks[one], one), swap(blocks[two], two)]
        by_one, by_two, top, bottom = yield [*near, swap(top, two), swap(bottom, one)]
        both = lambda v: [(v, 0), (v, 1)]
        return {
            0: both(blocks[0]),
            one: both(by_one),
            two: both(by_two),
            one ^ two: [(top, 0), (bottom, 0)],
        }
    while len(blocks) < len(chip_offsets()):
        yield []
    size = lax.axis_size("rep")
    away = [d for d in chip_offsets() if d]
    new = yield [lax.ppermute(blocks[d], "rep", [(i, i ^ d) for i in range(size)]) for d in away]
    return {d: [(v, 0), (v, 1)] for d, v in zip([0, *away], [blocks[0], *new])}


def token_steps(own, other):
    blocks = yield from gather_steps(own)
    away = [d for d in chip_offsets() if d]
    new = yield [swap(blocks[d], 1) for d in away]
    return {0: (own, other), **{d: (blocks[d], n) for d, n in zip(away, new)}}


def plane_sum_steps(partial):
    half = partial.shape[0] // 2
    (other,) = yield [swap(partial[half:], 1)]
    same = add(partial[:half], other).astype(BF)
    offsets = chip_offsets()
    rows = half // len(offsets)
    blocks = {d: halves(same[i * rows : (i + 1) * rows]) for i, d in enumerate(offsets)}
    return (yield from scatter_steps(blocks))


def vector_sum_steps(rows):
    size, bit = lax.axis_size("rep"), 1
    while bit < size:
        (other,) = yield [swap(rows, bit)]
        rows, bit = rows + other, 2 * bit
    shards, at = lax.axis_size("shard"), lax.axis_index("shard")
    own = rows.shape[1] // shards
    parts = yield [
        lax.ppermute(
            lax.dynamic_slice_in_dim(rows, ((at + k) % shards) * own, own, 1),
            "shard",
            [(i, (i + k) % shards) for i in range(shards)],
        )
        for k in range(1, shards)
    ]
    return lax.dynamic_slice_in_dim(rows, at * own, own, 1) + sum(parts)


def vector_gather_steps(rows):
    size, me = lax.axis_size("shard"), lax.axis_index("shard")
    others = yield [
        lax.ppermute(rows, "shard", [(i, (i - k) % size) for i in range(size)])
        for k in range(1, size)
    ]
    parts = [rows, *others]
    twice = jnp.concatenate(parts + parts, axis=1)
    own = rows.shape[1]
    return lax.dynamic_slice_in_dim(twice, ((size - me) % size) * own, size * own, 1)


def rotary_tables(length):
    half = HD // 2
    positions = jnp.arange(length, dtype=F32)
    inverse = 10000.0 ** (-2.0 * jnp.arange(half, dtype=F32) / HD)
    angles = positions[:, None] * inverse[None, :]
    cos, sin = jnp.cos(angles), jnp.sin(angles)
    return jnp.concatenate([cos, cos], axis=1), jnp.concatenate([-sin, sin], axis=1)


def rotate(values, cos, sin):
    return values * cos + pltpu.roll(values, HD // 2, 1) * sin


def window(step, seg_col, seg_row):
    low, high = max(0, step - 1) * WIN, (step + 1) * WIN
    shape = (WIN, high - low)
    row = lax.broadcasted_iota(jnp.int32, shape, 0) + step * WIN
    col = lax.broadcasted_iota(jnp.int32, shape, 1) + low
    near = (row >= col) & (row - col < WIN)
    same = seg_col[0, step * WIN : (step + 1) * WIN, :] == seg_row[0, :, low:high]
    return low, high, near & same


def attend_kernel(parts, z_ref, *refs):
    x_refs, w_refs = refs[:parts], refs[parts : 2 * parts]
    cos_ref, sin_ref, col_ref, row_ref, context_ref, qkv_ref, lse_ref, lin_ref = refs[2 * parts :]
    length, width = context_ref.shape
    tile = min(length, 256)

    @pl.loop(0, length // tile)
    def _(t):
        rows = pl.ds(pl.multiple_of(t * tile, tile), tile)
        total = mm(x_refs[0][rows, :], w_refs[0][...])
        for x, w in zip(x_refs[1:], w_refs[1:]):
            total += mm(x[rows, :], w[...])
        lin_ref[rows, :] = total

    cos, sin = cos_ref[...], sin_ref[...]
    for h in range(width // HD):
        q_at, k_at, v_at = (slice(i * width + h * HD, i * width + (h + 1) * HD) for i in range(3))
        qkv_ref[:, q_at] = rotate(lin_ref[:, q_at], cos, sin).astype(BF)
        qkv_ref[:, k_at] = rotate(lin_ref[:, k_at], cos, sin).astype(BF)
        qkv_ref[:, v_at] = lin_ref[:, v_at].astype(BF)
    for step in range(length // WIN):
        low, high, allowed = window(step, col_ref, row_ref)
        rows = slice(step * WIN, (step + 1) * WIN)
        for h in range(width // HD):
            q_at, k_at, v_at = (
                slice(i * width + h * HD, i * width + (h + 1) * HD) for i in range(3)
            )
            scores = mm_nt(qkv_ref[rows, q_at], qkv_ref[low:high, k_at]) * HD**-0.5
            scores = jnp.where(allowed, scores, -1e30)
            peak = jnp.max(scores, axis=1, keepdims=True)
            raw = jnp.exp(scores - peak)
            total = jnp.sum(raw, axis=1, keepdims=True)
            probs = (raw * (1.0 / total)).astype(BF)
            context_ref[rows, h * HD : (h + 1) * HD] = mm(probs, qkv_ref[low:high, v_at]).astype(BF)
            lse_ref[rows, h : h + 1] = peak + jnp.log(total)


def attend(shard, both, weights, tables, seg):
    parts = len(weights)
    rows, depth = both.shape
    length = tables[0].shape[0]
    wide = weights[0].shape[1]
    width = wide // 3
    piece = depth // parts
    whole = lambda *shape: pl.BlockSpec(shape, lambda s, z: (0,) * len(shape))
    take = lambda k: pl.BlockSpec((length, piece), lambda s, z: (s, (z[0] + parts - k) % parts))
    by_seq = lambda cols: pl.BlockSpec((length, cols), lambda s, z: (s, 0))
    return pl.pallas_call(
        functools.partial(attend_kernel, parts),
        grid_spec=pltpu.PrefetchScalarGridSpec(
            num_scalar_prefetch=1,
            grid=(rows // length,),
            in_specs=[take(k) for k in range(parts)]
            + [whole(piece, wide)] * parts
            + [whole(length, HD)] * 2
            + [
                pl.BlockSpec((1, length, 1), lambda s, z: (s, 0, 0)),
                pl.BlockSpec((1, 1, length), lambda s, z: (s, 0, 0)),
            ],
            out_specs=[by_seq(width), by_seq(wide), by_seq(width // HD)],
            scratch_shapes=[pltpu.VMEM((length, wide), F32)],
        ),
        out_shape=[
            jax.ShapeDtypeStruct((rows, width), BF),
            jax.ShapeDtypeStruct((rows, wide), BF),
            jax.ShapeDtypeStruct((rows, width // HD), F32),
        ],
        compiler_params=pltpu.CompilerParams(vmem_limit_bytes=40 << 20),
        cost_estimate=pl.CostEstimate(
            flops=2 * rows * depth * wide + 4 * rows * 2 * WIN * width,
            bytes_accessed=2 * (rows * depth + depth * wide + 2 * rows * wide),
            transcendentals=rows * 2 * WIN * width // HD,
        ),
        name="attend",
    )(shard, *[both] * parts, *weights, *tables, *seg)


def attend_back_kernel(
    grad_ref, out_ref, qkv_ref, lse_ref, cos_ref, sin_ref, col_ref, row_ref,
    lin_ref, context_ref, keys_ref, values_ref,
):
    length, wide = qkv_ref.shape
    width = wide // 3
    tile = min(length, 256)

    @pl.loop(0, length // tile)
    def _(t):
        rows = pl.ds(pl.multiple_of(t * tile, tile), tile)
        context_ref[rows, :] = mm_nt(grad_ref[rows, :], out_ref[...]).astype(BF)

    cos, sin = cos_ref[...], sin_ref[...]
    scale = HD**-0.5
    for h in range(width // HD):
        q_at, k_at, v_at = (slice(i * width + h * HD, i * width + (h + 1) * HD) for i in range(3))
        head = slice(h * HD, (h + 1) * HD)
        keys_ref[...] = jnp.zeros_like(keys_ref)
        values_ref[...] = jnp.zeros_like(values_ref)
        for step in range(length // WIN):
            low, high, allowed = window(step, col_ref, row_ref)
            rows = slice(step * WIN, (step + 1) * WIN)
            queries, keys = qkv_ref[rows, q_at], qkv_ref[low:high, k_at]
            grad = context_ref[rows, head]
            scores = jnp.where(allowed, mm_nt(queries, keys) * scale, -1e30)
            probs = jnp.exp(scores - lse_ref[rows, h : h + 1])
            values_ref[low:high, :] += mm_tn(probs.astype(BF), grad)
            grad_probs = mm_nt(grad, qkv_ref[low:high, v_at])
            inner = jnp.sum(probs * grad_probs, axis=1, keepdims=True)
            grad_scores = (probs * (grad_probs - inner)).astype(BF)
            grad_queries = mm(grad_scores, keys) * scale
            keys_ref[low:high, :] += mm_tn(grad_scores, queries)
            lin_ref[rows, q_at] = rotate(grad_queries, cos[rows], -sin[rows]).astype(BF)
        lin_ref[:, k_at] = rotate(keys_ref[...] * scale, cos, -sin).astype(BF)
        lin_ref[:, v_at] = values_ref[...].astype(BF)


def attend_back(grad, out_w, qkv, lse, tables, seg):
    rows, depth = grad.shape
    length = tables[0].shape[0]
    wide = qkv.shape[1]
    width = wide // 3
    whole = lambda *shape: pl.BlockSpec(shape, lambda s: (0,) * len(shape))
    by_seq = lambda cols: pl.BlockSpec((length, cols), lambda s: (s, 0))
    return pl.pallas_call(
        attend_back_kernel,
        grid=(rows // length,),
        in_specs=[by_seq(depth), whole(width, depth), by_seq(wide), by_seq(width // HD)]
        + [whole(length, HD)] * 2
        + [
            pl.BlockSpec((1, length, 1), lambda s: (s, 0, 0)),
            pl.BlockSpec((1, 1, length), lambda s: (s, 0, 0)),
        ],
        out_specs=by_seq(wide),
        scratch_shapes=[
            pltpu.VMEM((length, width), BF),
            pltpu.VMEM((length, HD), F32),
            pltpu.VMEM((length, HD), F32),
        ],
        out_shape=jax.ShapeDtypeStruct((rows, wide), BF),
        compiler_params=pltpu.CompilerParams(vmem_limit_bytes=48 << 20),
        cost_estimate=pl.CostEstimate(
            flops=2 * rows * depth * width + 10 * rows * 2 * WIN * width,
            bytes_accessed=2 * (rows * depth + depth * width + 2 * rows * wide),
            transcendentals=rows * 2 * WIN * width // HD,
        ),
        name="attend_back",
    )(grad, out_w, qkv, lse, *tables, *seg)


def weight_grad_kernel(count, *refs):
    total = mm_tn(refs[0][...], refs[count][...])
    for n in range(1, count):
        total += mm_tn(refs[n][...], refs[count + n][...])
    refs[-1][...] = total.astype(BF)


def weight_grad(tokens, grads):
    rows, depth = tokens[0].shape
    wide = grads[0][0].shape[1]
    tile = min(depth, 256)

    def part(index):
        return pl.BlockSpec((rows, wide), lambda i: (index, 0), pipeline_mode=pl.Buffered(1))

    return pl.pallas_call(
        functools.partial(weight_grad_kernel, len(tokens)),
        grid=(depth // tile,),
        in_specs=[pl.BlockSpec((rows, tile), lambda i: (0, i))] * len(tokens)
        + [part(index) for _, index in grads],
        out_specs=pl.BlockSpec((tile, wide), lambda i: (i, 0)),
        out_shape=jax.ShapeDtypeStruct((depth, wide), BF),
        compiler_params=pltpu.CompilerParams(vmem_limit_bytes=40 << 20),
        cost_estimate=pl.CostEstimate(
            flops=2 * rows * len(tokens) * depth * wide,
            bytes_accessed=2 * len(tokens) * rows * (depth + wide) + 2 * depth * wide,
            transcendentals=0,
        ),
        name="weight_grad",
    )(*tokens, *[g for g, _ in grads])


def normed_back_kernel(blocks, parts, z_ref, *refs):
    lins, weights, total_ref = refs[:blocks], refs[blocks:-1], refs[-1]
    piece = total_ref.shape[1] // parts
    for k in range(parts):
        total = mm_nt(lins[0][...], weights[k][...])
        for n in range(1, blocks):
            total += mm_nt(lins[n][...], weights[n * parts + k][...])
        at = pl.multiple_of(((z_ref[0] + parts - k) % parts) * piece, piece)
        total_ref[:, pl.ds(at, piece)] = total


def normed_back(shard, lins, weights, depth):
    parts = len(weights[0])
    rows, wide = lins[0].shape
    tile = min(rows, 256)
    flat = [w for block in weights for w in block]
    return pl.pallas_call(
        functools.partial(normed_back_kernel, len(lins), parts),
        grid_spec=pltpu.PrefetchScalarGridSpec(
            num_scalar_prefetch=1,
            grid=(rows // tile,),
            in_specs=[pl.BlockSpec((tile, wide), lambda s, z: (s, 0))] * len(lins)
            + [
                pl.BlockSpec(flat[0].shape, lambda s, z: (0, 0), pipeline_mode=pl.Buffered(1))
            ] * len(flat),
            out_specs=pl.BlockSpec((tile, depth), lambda s, z: (s, 0)),
        ),
        out_shape=jax.ShapeDtypeStruct((rows, depth), F32),
        compiler_params=pltpu.CompilerParams(vmem_limit_bytes=48 << 20),
        cost_estimate=pl.CostEstimate(
            flops=2 * rows * depth * wide * len(lins),
            bytes_accessed=2 * len(lins) * wide * (rows + depth) + 4 * rows * depth,
            transcendentals=0,
        ),
        name="normed_back",
    )(shard, *lins, *flat)


def plan_slots(route_ids, gate_values):
    hit_mask = route_ids == 0
    hit = jnp.any(hit_mask, axis=-1)
    weight = jnp.sum(jnp.where(hit_mask, gate_values, 0.0), axis=-1)
    ids = jnp.arange(route_ids.shape[0], dtype=jnp.int32)
    earlier = (ids[None, :] < ids[:, None]) & hit[None, :]
    order = jnp.sum(earlier.astype(jnp.int32), axis=1)
    kept = hit & (order < CAP)
    slots = jnp.arange(CAP, dtype=jnp.int32)
    table = (order[None, :] == slots[:, None]) & kept[None, :]
    return table, jnp.where(kept, weight, 0.0)


def norm_back(grad_normed, source, root, gain):
    scaled = grad_normed * gain
    grad_gain = jnp.sum(grad_normed * source * root, axis=0)
    mean = jnp.mean(scaled * source, axis=-1, keepdims=True)
    return grad_gain, root * scaled - source * (root * root * root) * mean


def place_kernel(me_ref, same_ref, other_ref, *out_refs):
    odd = jnp.bitwise_xor(pl.program_id(0), me_ref[0]) % 2
    block = jnp.where(odd == 0, same_ref[...], other_ref[...]).astype(F32)
    width = out_refs[0].shape[1]
    for i, ref in enumerate(out_refs):
        ref[...] = block[:, i * width : (i + 1) * width]


def place(me, same, other, height, width, columns):
    size, total = lax.axis_size("rep"), same.shape[1]
    spec = pl.BlockSpec((height, total), lambda j, me: (jnp.bitwise_xor(j, me[0]) // 2, 0))
    shape = (height, size * width) if columns else (size * height, width)
    count = total // width
    return pl.pallas_call(
        place_kernel,
        grid_spec=pltpu.PrefetchScalarGridSpec(
            num_scalar_prefetch=1,
            grid=(size,),
            in_specs=[spec, spec],
            out_specs=[
                pl.BlockSpec(
                    (height, width), (lambda j, me: (0, j)) if columns else (lambda j, me: (j, 0))
                )
            ] * count,
        ),
        out_shape=[jax.ShapeDtypeStruct(shape, F32)] * count,
        cost_estimate=pl.CostEstimate(
            flops=0, bytes_accessed=8 * size * height * total, transcendentals=0
        ),
        name="place",
    )(me, same, other)


def place_turned_kernel(me_ref, same_ref, other_ref, out_ref):
    odd = me_ref[0] % 2
    first = jnp.where(odd == 0, same_ref[...], other_ref[...])
    second = jnp.where(odd == 0, other_ref[...], same_ref[...])
    out_ref[...] = jnp.concatenate([first, second], axis=0).T.astype(F32)


def place_turned(me, same, other, height):
    size, width = lax.axis_size("rep"), same.shape[1]
    if 2 * height % 128:
        return place(me, same, other, height, width, False)[0].T
    spec = pl.BlockSpec((height, width), lambda j, me: (jnp.bitwise_xor(j, me[0] // 2), 0))
    return pl.pallas_call(
        place_turned_kernel,
        grid_spec=pltpu.PrefetchScalarGridSpec(
            num_scalar_prefetch=1,
            grid=(size // 2,),
            in_specs=[spec, spec],
            out_specs=pl.BlockSpec((width, 2 * height), lambda j, me: (0, j)),
        ),
        out_shape=jax.ShapeDtypeStruct((width, size * height), F32),
        compiler_params=pltpu.CompilerParams(vmem_limit_bytes=32 << 20),
        cost_estimate=pl.CostEstimate(
            flops=0, bytes_accessed=12 * same.size, transcendentals=0
        ),
        name="place_turned",
    )(me, same, other)


def per_device(
    layer_input,
    gain_attn,
    w_query,
    w_key,
    w_value,
    w_out,
    gain_mlp,
    w_gate,
    w_up,
    w_down,
    segments,
    attn_route,
    attn_gate,
    mlp_route,
    mlp_gate,
    cotangent,
):
    length = layer_input.shape[0]
    size, shards = lax.axis_size("rep"), lax.axis_size("shard")
    me = lax.axis_index("rep")
    whoami = me.astype(jnp.int32).reshape(1)
    shard = lax.axis_index("shard").astype(jnp.int32).reshape(1)
    block = w_query.shape[1] // size
    units = w_gate.shape[1] // size
    own = gain_attn.shape[0]
    offsets = chip_offsets()
    staged = len(chip_bits()) == 2

    def columns(weight, d, width):
        return lax.dynamic_slice_in_dim(weight, jnp.bitwise_xor(me, d) * width, width, 1)

    def rows_of(weight, height):
        return lax.dynamic_slice_in_dim(weight, me * height, height, 0)

    def local(d):
        return jnp.concatenate([columns(w, d, block) for w in (w_query, w_key, w_value)], axis=1)

    inputs = layer_input.astype(F32)
    root_one = lax.rsqrt(jnp.mean(inputs * inputs, axis=-1, keepdims=True) + EPSILON)
    tables = rotary_tables(length)
    ring = [(i, (i + 1) % shards) for i in range(shards)]
    piece = local(0)
    qkv_w = {d: [local(d)] for d in offsets}
    flows, context, saved = [], {}, {}
    gain_flow = Flow(vector_gather_steps(jnp.stack([gain_attn, gain_mlp])))
    piece, seg_other, own_gate_up = stage(
        [gain_flow],
        (
            lax.ppermute(piece, "shard", ring),
            swap(segments, 1),
            jnp.concatenate([columns(w_gate, 0, units), columns(w_up, 0, units)], axis=1),
        ),
    )
    gain_one, gain_two = gain_flow.result.astype(F32)
    normed = (inputs * root_one * gain_one).astype(BF)
    seg = jnp.concatenate([segments, seg_other], axis=0)
    seg = (seg[:, :, None], seg[:, None, :])
    other = swap(normed, 1)
    for step in range(1, shards):
        qkv_w[0].append(piece)
        flows.append(Flow(gather_steps(piece, lambda d, b: qkv_w[d].append(b))))
        if step < shards - 1:
            piece, other = stage(flows, (lax.ppermute(piece, "shard", ring), other))
    own_out, own_gate_up, qkv_w[0][-1] = lax.optimization_barrier(
        (rows_of(w_out, block), own_gate_up, qkv_w[0][-1])
    )
    own_out = lax.all_gather(own_out, "shard", axis=1, tiled=True)
    both = jnp.concatenate([normed, other], axis=0)

    def run(d):
        context[d], *saved[d] = attend(shard, both, qkv_w[d], tables, seg)
        return context[d]

    context[0], own_out = stage(flows, (run(0), own_out))
    own_gate_up, own_out = lax.optimization_barrier((own_gate_up, own_out))
    gate_up = lax.all_gather(own_gate_up, "shard", axis=0, tiled=True)
    own_down, _ = lax.optimization_barrier((rows_of(w_down, units), gate_up))
    down = lax.all_gather(own_down, "shard", axis=1, tiled=True)
    early = offsets[1:2] if staged else []
    early = stage(flows, [run(d) for d in early])
    for flow in flows:
        finish(flow)
    out_flow = Flow(gather_steps(own_out))
    rest = [d for d in offsets if d not in context]
    stage([out_flow], [run(d) for d in rest])
    out_w = finish(out_flow)

    table, mix = plan_slots(mlp_route, mlp_gate)
    pick = table.astype(BF)
    upstream = cotangent.astype(F32)
    slot_weight = jnp.sum(jnp.where(table, mix[None, :], 0.0), axis=1)[:, None]
    slot_grad = (mm(pick, cotangent) * slot_weight).astype(BF)

    all_context = jnp.concatenate([context[d] for d in offsets], axis=1)
    all_out = jnp.concatenate([out_w[d] for d in offsets], axis=0)
    projected = mm(all_context, all_out)
    projected = projected[:length] + swap(projected[length:].astype(BF), 1).astype(F32)
    attn_weight = jnp.sum(jnp.where(attn_route == 0, attn_gate, 0.0), axis=-1)[:, None]
    hidden = inputs + projected * attn_weight
    root_two = lax.rsqrt(jnp.mean(hidden * hidden, axis=-1, keepdims=True) + EPSILON)
    normed_two = (hidden * root_two * gain_two).astype(BF)

    disp_flow = Flow(copies_steps(mm(pick, normed_two).astype(BF)))
    slot_grad = stage([disp_flow], slot_grad)
    slot_flow = Flow(copies_steps(slot_grad))
    gate_up, normed = stage([disp_flow, slot_flow], (gate_up, normed))
    stage([disp_flow, slot_flow])
    token_flow = Flow(token_steps(normed, other))
    dispatched = jnp.concatenate(finish(disp_flow), axis=0)
    act = stage([token_flow, slot_flow], mm(dispatched, gate_up))
    all_slot_grad = jnp.concatenate(finish(slot_flow), axis=0)
    gate_act, up_act = act[:, :units], act[:, units:]
    sigmoid = jax.nn.sigmoid(gate_act)
    silu = gate_act * sigmoid
    inner = (silu * up_act).astype(BF)
    grad_inner = mm_nt(all_slot_grad, down)
    grad_gate_act = (grad_inner * up_act * sigmoid * (1.0 + gate_act * (1.0 - sigmoid))).astype(BF)
    grad_up_act = (grad_inner * silu).astype(BF)
    grad_act = jnp.concatenate([grad_gate_act, grad_up_act], axis=1)
    back_flow = Flow(plane_sum_steps(mm_nt(grad_act, gate_up).astype(BF)))
    sums = []
    for left, right in (
        (grad_gate_act, dispatched),
        (grad_up_act, dispatched),
        (inner, all_slot_grad),
    ):
        grad = stage([back_flow, token_flow], mm_tn(left, right).astype(BF))
        sums.append(lax.psum_scatter(grad, "shard", scatter_dimension=1, tiled=True))
    grad_normed_two = mm_tn(pick, finish(back_flow))
    grad_gain_two, through = norm_back(grad_normed_two, hidden, root_two, gain_two)
    grad_hidden = upstream + through

    grad_projected = (grad_hidden * attn_weight).astype(BF)
    both_grad = jnp.concatenate([grad_projected, swap(grad_projected, 1)], axis=0)
    lins = {}

    def run_back(*ds):
        for d in ds:
            lins[d] = attend_back(both_grad, out_w[d], *saved[d], tables, seg)
        return [lins[d] for d in ds]

    far, near = offsets[-1:], offsets[1:-1]
    tokens = finish(token_flow)
    expert_flow = Flow(plane_sum_steps(mm(inner, down).astype(BF)))
    far_lin, both_grad = lax.optimization_barrier((run_back(*far), both_grad))
    lins.update(zip(far, far_lin))
    lin_flow = Flow(exchange_steps(lins))
    near_lin, both_grad = stage([lin_flow, expert_flow], (run_back(*near), both_grad))
    lins.update(zip(near, near_lin))
    own_lin, grad_out_w = (run_back(0), mm_tn(all_context, both_grad).astype(BF))
    grad_normed = normed_back(
        shard, [lins[d] for d in offsets], [qkv_w[d] for d in offsets], both.shape[1]
    )
    grad_normed, grad_out_w, sums[0] = stage([lin_flow], (grad_normed, grad_out_w, sums[0]))
    parts = finish(lin_flow)
    own_grad_qkv = weight_grad(
        [x for d in offsets for x in tokens[d]], [g for d in offsets for g in parts[d]]
    )
    own_grad_qkv, sums[2] = lax.optimization_barrier((own_grad_qkv, sums[2]))
    sum_qkv = lax.psum_scatter(own_grad_qkv, "shard", scatter_dimension=0, tiled=True)

    out_blocks = {d: halves(grad_out_w[i * block : (i + 1) * block]) for i, d in enumerate(offsets)}
    out_flow = Flow(scatter_steps(out_blocks))
    gate_flow = Flow(copies_steps(sums[0]))
    sums[1], other_normed = stage(
        [out_flow, gate_flow], (sums[1], swap(grad_normed[length:].astype(BF), 1))
    )
    grad_normed = grad_normed[:length] + other_normed.astype(F32)
    grad_gain_one, first = norm_back(grad_normed, inputs, root_one, gain_one)
    grad_input = (grad_hidden + first).astype(BF)
    grad_input, gains = stage(
        [out_flow, gate_flow], (grad_input, jnp.stack([grad_gain_one, grad_gain_two]))
    )
    up_flow = Flow(copies_steps(sums[1]))
    sums[2] = stage([out_flow, gate_flow, up_flow], sums[2])
    own_grad_out, _ = lax.optimization_barrier((finish(out_flow), sum_qkv))
    sum_out = lax.psum_scatter(own_grad_out, "shard", scatter_dimension=1, tiled=True)
    down_flow, gain_flow = Flow(copies_steps(sums[2])), Flow(vector_sum_steps(gains))
    grad_gate = place_turned(whoami, *finish(gate_flow), units)
    grad_gate, sum_qkv = stage([up_flow, down_flow, gain_flow], (grad_gate, sum_qkv))
    qkv_flow = Flow(copies_steps(sum_qkv))
    stage([qkv_flow, up_flow, down_flow])
    grad_up = place_turned(whoami, *finish(up_flow), units)
    grad_up, sum_out = stage([qkv_flow, down_flow, gain_flow], (grad_up, sum_out))
    out_flow = Flow(copies_steps(sum_out))
    (grad_down,) = place(whoami, *finish(down_flow), units, own, False)
    grad_down = stage([qkv_flow, out_flow, gain_flow], grad_down)
    grad_query, grad_key, grad_value = place(whoami, *finish(qkv_flow), own, block, True)
    grad_query = stage([out_flow, expert_flow, gain_flow], grad_query)
    stage([out_flow, expert_flow])
    output = (hidden + mm_tn(pick, finish(expert_flow)) * mix[:, None]).astype(BF)
    (grad_out,) = place(whoami, *finish(out_flow), block, own, False)
    gain_grads = finish(gain_flow)
    return (
        output,
        grad_input,
        gain_grads[0],
        grad_query,
        grad_key,
        grad_value,
        grad_out,
        gain_grads[1],
        grad_gate,
        grad_up,
        grad_down,
    )


def solution(mesh):
    tokens = P(("rep", "shard"), None)
    tall, wide, vector = P("shard", None), P(None, "shard"), P("shard")
    weights = (vector, tall, tall, tall, wide, vector, tall, tall, wide)
    return jax.shard_map(
        per_device,
        mesh=mesh,
        in_specs=(tokens, *weights) + (tokens,) * 6,
        out_specs=(tokens, tokens, *weights),
        check_vma=False,
    )
```

```python
import functools

import jax
import jax.numpy as jnp
from jax import lax
from jax.experimental import pallas as pl
from jax.experimental.pallas import tpu as pltpu
from jax.sharding import PartitionSpec as P

HEADS = 16
HD = 128
WIN = 256
CAP = 128
EPSILON = 1e-05
BF = jnp.bfloat16
F32 = jnp.float32


def mm(left, right):
    return jnp.dot(left, right, preferred_element_type=F32)


def mm_nt(left, right):
    return lax.dot_general(left, right, (((1,), (1,)), ((), ())), preferred_element_type=F32)


def mm_tn(left, right):
    return lax.dot_general(left, right, (((0,), (0,)), ((), ())), preferred_element_type=F32)


def swap(value, bit):
    size = lax.axis_size("rep")
    return lax.ppermute(value, "rep", [(i, i ^ bit) for i in range(size)])


def chip_bits():
    size, bits, bit = lax.axis_size("rep"), [], 2
    while bit < size:
        bits.append(bit)
        bit *= 2
    return bits


def chip_offsets():
    return list(range(0, lax.axis_size("rep"), 2))


def add(left, right):
    return left.astype(F32) + right.astype(F32)


def halves(value):
    half = value.shape[0] // 2
    return value[:half], value[half:]


class Flow:
    def __init__(self, steps):
        self.steps, self.result, self.done = steps, None, False
        self.pending = next(steps)

    def advance(self, arrived):
        try:
            self.pending = self.steps.send(arrived)
        except StopIteration as end:
            self.pending, self.result, self.done = [], end.value, True


def stage(flows, extra=()):
    flows = [f for f in flows if not f.done]
    arrived, extra = lax.optimization_barrier(([f.pending for f in flows], extra))
    for flow, values in zip(flows, arrived):
        flow.advance(values)
    return extra


def finish(flow):
    while not flow.done:
        flow.advance(flow.pending)
    return flow.result


def gather_steps(value, sink=lambda offset, block: None):
    bits = chip_bits()
    if len(bits) == 2:
        one, two = bits
        half = value.shape[0] // 2
        by_one, by_two = yield [swap(value, one), swap(value, two)]
        sink(one, by_one)
        sink(two, by_two)
        top, bottom = yield [swap(by_one[:half], two), swap(by_two[half:], one)]
        far = jnp.concatenate([top, bottom], axis=0)
        sink(one ^ two, far)
        return {0: value, one: by_one, two: by_two, one ^ two: far}
    blocks = {0: value}
    for bit in bits:
        old = list(blocks.items())
        new = yield [swap(b, bit) for _, b in old]
        for (d, _), b in zip(old, new):
            blocks[d ^ bit] = b
            sink(d ^ bit, b)
    return blocks


def copies_steps(value):
    blocks = yield from gather_steps(value)
    same = jnp.concatenate([blocks[d] for d in chip_offsets()], axis=0)
    (other,) = yield [swap(same, 1)]
    return same, other


def scatter_steps(blocks):
    bits = chip_bits()
    if len(bits) == 2:
        one, two = bits
        far = blocks[one ^ two]
        top, bottom = yield [swap(far[0], one), swap(far[1], two)]
        near_one, near_two = blocks[one], blocks[two]
        one_top, two_bottom = yield [swap(near_one[0], one), swap(near_two[1], two)]
        two_top, one_bottom = yield [
            swap(add(near_two[0], top).astype(BF), two),
            swap(add(near_one[1], bottom).astype(BF), one),
        ]
        return jnp.concatenate(
            [
                (add(blocks[0][0], one_top) + two_top.astype(F32)).astype(BF),
                (add(blocks[0][1], one_bottom) + two_bottom.astype(F32)).astype(BF),
            ],
            axis=0,
        )
    while len(blocks) < len(chip_offsets()):
        yield []
    sums = {d: jnp.concatenate(b, axis=0) for d, b in blocks.items()}
    for bit in reversed(bits):
        kept = [d for d in sorted(sums) if not d & bit]
        new = yield [swap(sums[d | bit], bit) for d in kept]
        sums = {d: add(sums[d], n).astype(BF) for d, n in zip(kept, new)}
    return sums[0]


def plane_sum_steps(partial):
    half = partial.shape[0] // 2
    (other,) = yield [swap(partial[half:], 1)]
    same = add(partial[:half], other).astype(BF)
    offsets = chip_offsets()
    rows = half // len(offsets)
    blocks = {d: halves(same[i * rows : (i + 1) * rows]) for i, d in enumerate(offsets)}
    return (yield from scatter_steps(blocks))


def vector_sum_steps(rows):
    size, bit = lax.axis_size("rep"), 1
    while bit < size:
        (other,) = yield [swap(rows, bit)]
        rows, bit = rows + other, 2 * bit
    shards, at = lax.axis_size("shard"), lax.axis_index("shard")
    own = rows.shape[1] // shards
    parts = yield [
        lax.ppermute(
            lax.dynamic_slice_in_dim(rows, ((at + k) % shards) * own, own, 1),
            "shard",
            [(i, (i + k) % shards) for i in range(shards)],
        )
        for k in range(1, shards)
    ]
    return lax.dynamic_slice_in_dim(rows, at * own, own, 1) + sum(parts)


def vector_gather_steps(rows):
    size, me = lax.axis_size("shard"), lax.axis_index("shard")
    others = yield [
        lax.ppermute(rows, "shard", [(i, (i - k) % size) for i in range(size)])
        for k in range(1, size)
    ]
    parts = [rows, *others]
    twice = jnp.concatenate(parts + parts, axis=1)
    own = rows.shape[1]
    return lax.dynamic_slice_in_dim(twice, ((size - me) % size) * own, size * own, 1)


def rotary_tables(length):
    half = HD // 2
    positions = jnp.arange(length, dtype=F32)
    inverse = 10000.0 ** (-2.0 * jnp.arange(half, dtype=F32) / HD)
    angles = positions[:, None] * inverse[None, :]
    cos, sin = jnp.cos(angles), jnp.sin(angles)
    return jnp.concatenate([cos, cos], axis=1), jnp.concatenate([-sin, sin], axis=1)


def rotate(values, cos, sin):
    return values * cos + pltpu.roll(values, HD // 2, 1) * sin


def window(step, seg_col, seg_row):
    low, high = max(0, step - 1) * WIN, (step + 1) * WIN
    shape = (WIN, high - low)
    row = lax.broadcasted_iota(jnp.int32, shape, 0) + step * WIN
    col = lax.broadcasted_iota(jnp.int32, shape, 1) + low
    near = (row >= col) & (row - col < WIN)
    same = seg_col[0, step * WIN : (step + 1) * WIN, :] == seg_row[0, :, low:high]
    return low, high, near & same


def attend_kernel(parts, z_ref, *refs):
    x_refs, w_refs = refs[:parts], refs[parts : 2 * parts]
    cos_ref, sin_ref, col_ref, row_ref, context_ref, qkv_ref, lse_ref, lin_ref = refs[2 * parts :]
    length, width = context_ref.shape
    tile = min(length, 256)

    @pl.loop(0, length // tile)
    def _(t):
        rows = pl.ds(pl.multiple_of(t * tile, tile), tile)
        total = mm(x_refs[0][rows, :], w_refs[0][...])
        for x, w in zip(x_refs[1:], w_refs[1:]):
            total += mm(x[rows, :], w[...])
        lin_ref[rows, :] = total

    cos, sin = cos_ref[...], sin_ref[...]
    for h in range(width // HD):
        q_at, k_at, v_at = (slice(i * width + h * HD, i * width + (h + 1) * HD) for i in range(3))
        qkv_ref[:, q_at] = rotate(lin_ref[:, q_at], cos, sin).astype(BF)
        qkv_ref[:, k_at] = rotate(lin_ref[:, k_at], cos, sin).astype(BF)
        qkv_ref[:, v_at] = lin_ref[:, v_at].astype(BF)
    for step in range(length // WIN):
        low, high, allowed = window(step, col_ref, row_ref)
        rows = slice(step * WIN, (step + 1) * WIN)
        for h in range(width // HD):
            q_at, k_at, v_at = (
                slice(i * width + h * HD, i * width + (h + 1) * HD) for i in range(3)
            )
            scores = mm_nt(qkv_ref[rows, q_at], qkv_ref[low:high, k_at]) * HD**-0.5
            scores = jnp.where(allowed, scores, -1e30)
            peak = jnp.max(scores, axis=1, keepdims=True)
            raw = jnp.exp(scores - peak)
            total = jnp.sum(raw, axis=1, keepdims=True)
            probs = (raw * (1.0 / total)).astype(BF)
            context_ref[rows, h * HD : (h + 1) * HD] = mm(probs, qkv_ref[low:high, v_at]).astype(BF)
            lse_ref[rows, h : h + 1] = peak + jnp.log(total)


def attend(shard, both, weights, tables, seg):
    parts = len(weights)
    rows, depth = both.shape
    length = tables[0].shape[0]
    wide = weights[0].shape[1]
    width = wide // 3
    piece = depth // parts
    whole = lambda *shape: pl.BlockSpec(shape, lambda s, z: (0,) * len(shape))
    take = lambda k: pl.BlockSpec((length, piece), lambda s, z: (s, (z[0] + parts - k) % parts))
    by_seq = lambda cols: pl.BlockSpec((length, cols), lambda s, z: (s, 0))
    return pl.pallas_call(
        functools.partial(attend_kernel, parts),
        grid_spec=pltpu.PrefetchScalarGridSpec(
            num_scalar_prefetch=1,
            grid=(rows // length,),
            in_specs=[take(k) for k in range(parts)]
            + [whole(piece, wide)] * parts
            + [whole(length, HD)] * 2
            + [
                pl.BlockSpec((1, length, 1), lambda s, z: (s, 0, 0)),
                pl.BlockSpec((1, 1, length), lambda s, z: (s, 0, 0)),
            ],
            out_specs=[by_seq(width), by_seq(wide), by_seq(width // HD)],
            scratch_shapes=[pltpu.VMEM((length, wide), F32)],
        ),
        out_shape=[
            jax.ShapeDtypeStruct((rows, width), BF),
            jax.ShapeDtypeStruct((rows, wide), BF),
            jax.ShapeDtypeStruct((rows, width // HD), F32),
        ],
        compiler_params=pltpu.CompilerParams(vmem_limit_bytes=40 << 20),
        cost_estimate=pl.CostEstimate(
            flops=2 * rows * depth * wide + 4 * rows * 2 * WIN * width,
            bytes_accessed=2 * (rows * depth + depth * wide + 2 * rows * wide),
            transcendentals=rows * 2 * WIN * width // HD,
        ),
        name="attend",
    )(shard, *[both] * parts, *weights, *tables, *seg)


def attend_back_kernel(
    grad_ref, out_ref, qkv_ref, lse_ref, x_ref, cos_ref, sin_ref, col_ref, row_ref,
    lin_ref, top_ref, bottom_ref, kept_ref, context_ref, keys_ref, values_ref,
):
    length, wide = qkv_ref.shape
    width = wide // 3
    seq = pl.program_id(0)
    tile = min(length, 256)

    @pl.loop(0, length // tile)
    def _(t):
        rows = pl.ds(pl.multiple_of(t * tile, tile), tile)
        context_ref[rows, :] = mm_nt(grad_ref[rows, :], out_ref[...]).astype(BF)

    cos, sin = cos_ref[...], sin_ref[...]
    scale = HD**-0.5
    for h in range(width // HD):
        q_at, k_at, v_at = (slice(i * width + h * HD, i * width + (h + 1) * HD) for i in range(3))
        head = slice(h * HD, (h + 1) * HD)
        keys_ref[...] = jnp.zeros_like(keys_ref)
        values_ref[...] = jnp.zeros_like(values_ref)
        for step in range(length // WIN):
            low, high, allowed = window(step, col_ref, row_ref)
            rows = slice(step * WIN, (step + 1) * WIN)
            queries, keys = qkv_ref[rows, q_at], qkv_ref[low:high, k_at]
            grad = context_ref[rows, head]
            scores = jnp.where(allowed, mm_nt(queries, keys) * scale, -1e30)
            probs = jnp.exp(scores - lse_ref[rows, h : h + 1])
            values_ref[low:high, :] += mm_tn(probs.astype(BF), grad)
            grad_probs = mm_nt(grad, qkv_ref[low:high, v_at])
            inner = jnp.sum(probs * grad_probs, axis=1, keepdims=True)
            grad_scores = (probs * (grad_probs - inner)).astype(BF)
            grad_queries = mm(grad_scores, keys) * scale
            keys_ref[low:high, :] += mm_tn(grad_scores, queries)
            lin_ref[rows, q_at] = rotate(grad_queries, cos[rows], -sin[rows]).astype(BF)
        lin_ref[:, k_at] = rotate(keys_ref[...] * scale, cos, -sin).astype(BF)
        lin_ref[:, v_at] = values_ref[...].astype(BF)
    kept_ref[pl.ds(pl.multiple_of(seq * length, length), length), :] = lin_ref[...]

    @pl.when(seq == pl.num_programs(0) - 1)
    def _():
        half = top_ref.shape[0]
        step = 256
        for n, ref in enumerate((top_ref, bottom_ref)):

            @pl.loop(0, half // step)
            def _(t):
                cols = pl.ds(pl.multiple_of(n * half + t * step, step), step)
                rows = pl.ds(pl.multiple_of(t * step, step), step)
                ref[rows, :] = mm_tn(x_ref[:, cols], kept_ref[...]).astype(BF)


def attend_back(grad, out_w, qkv, lse, both, tables, seg):
    rows, depth = both.shape
    length = tables[0].shape[0]
    wide = qkv.shape[1]
    width = wide // 3
    whole = lambda *shape: pl.BlockSpec(shape, lambda s: (0,) * len(shape))
    by_seq = lambda cols: pl.BlockSpec((length, cols), lambda s: (s, 0))
    return pl.pallas_call(
        attend_back_kernel,
        grid=(rows // length,),
        in_specs=[by_seq(depth), whole(width, depth), by_seq(wide), by_seq(width // HD)]
        + [whole(rows, depth), whole(length, HD), whole(length, HD)]
        + [
            pl.BlockSpec((1, length, 1), lambda s: (s, 0, 0)),
            pl.BlockSpec((1, 1, length), lambda s: (s, 0, 0)),
        ],
        out_specs=[by_seq(wide), whole(depth // 2, wide), whole(depth // 2, wide)],
        scratch_shapes=[
            pltpu.VMEM((rows, wide), BF),
            pltpu.VMEM((length, width), BF),
            pltpu.VMEM((length, HD), F32),
            pltpu.VMEM((length, HD), F32),
        ],
        out_shape=[
            jax.ShapeDtypeStruct((rows, wide), BF),
            jax.ShapeDtypeStruct((depth // 2, wide), BF),
            jax.ShapeDtypeStruct((depth // 2, wide), BF),
        ],
        compiler_params=pltpu.CompilerParams(vmem_limit_bytes=48 << 20),
        cost_estimate=pl.CostEstimate(
            flops=2 * rows * depth * (wide + width) + 10 * rows * 2 * WIN * width,
            bytes_accessed=2 * (2 * rows * depth + depth * (wide + width) + 2 * rows * wide),
            transcendentals=rows * 2 * WIN * width // HD,
        ),
        name="attend_back",
    )(grad, out_w, qkv, lse, both, *tables, *seg)


def normed_back_kernel(blocks, parts, z_ref, *refs):
    lins, weights, total_ref = refs[:blocks], refs[blocks:-1], refs[-1]
    piece = total_ref.shape[1] // parts
    for k in range(parts):
        total = mm_nt(lins[0][...], weights[k][...])
        for n in range(1, blocks):
            total += mm_nt(lins[n][...], weights[n * parts + k][...])
        at = pl.multiple_of(((z_ref[0] + parts - k) % parts) * piece, piece)
        total_ref[:, pl.ds(at, piece)] = total


def normed_back(shard, lins, weights, depth):
    parts = len(weights[0])
    rows, wide = lins[0].shape
    tile = min(rows, 256)
    flat = [w for block in weights for w in block]
    return pl.pallas_call(
        functools.partial(normed_back_kernel, len(lins), parts),
        grid_spec=pltpu.PrefetchScalarGridSpec(
            num_scalar_prefetch=1,
            grid=(rows // tile,),
            in_specs=[pl.BlockSpec((tile, wide), lambda s, z: (s, 0))] * len(lins)
            + [
                pl.BlockSpec(flat[0].shape, lambda s, z: (0, 0), pipeline_mode=pl.Buffered(1))
            ] * len(flat),
            out_specs=pl.BlockSpec((tile, depth), lambda s, z: (s, 0)),
        ),
        out_shape=jax.ShapeDtypeStruct((rows, depth), F32),
        compiler_params=pltpu.CompilerParams(vmem_limit_bytes=48 << 20),
        cost_estimate=pl.CostEstimate(
            flops=2 * rows * depth * wide * len(lins),
            bytes_accessed=2 * len(lins) * wide * (rows + depth) + 4 * rows * depth,
            transcendentals=0,
        ),
        name="normed_back",
    )(shard, *lins, *flat)


def plan_slots(route_ids, gate_values):
    hit_mask = route_ids == 0
    hit = jnp.any(hit_mask, axis=-1)
    weight = jnp.sum(jnp.where(hit_mask, gate_values, 0.0), axis=-1)
    ids = jnp.arange(route_ids.shape[0], dtype=jnp.int32)
    earlier = (ids[None, :] < ids[:, None]) & hit[None, :]
    order = jnp.sum(earlier.astype(jnp.int32), axis=1)
    kept = hit & (order < CAP)
    slots = jnp.arange(CAP, dtype=jnp.int32)
    table = (order[None, :] == slots[:, None]) & kept[None, :]
    return table, jnp.where(kept, weight, 0.0)


def norm_back(grad_normed, source, root, gain):
    scaled = grad_normed * gain
    grad_gain = jnp.sum(grad_normed * source * root, axis=0)
    mean = jnp.mean(scaled * source, axis=-1, keepdims=True)
    return grad_gain, root * scaled - source * (root * root * root) * mean


def place_kernel(me_ref, same_ref, other_ref, *out_refs):
    block = jnp.where(pl.program_id(0) % 2 == 0, same_ref[...], other_ref[...]).astype(F32)
    width = out_refs[0].shape[1]
    for i, ref in enumerate(out_refs):
        ref[...] = block[:, i * width : (i + 1) * width]


def place(me, same, other, height, width, columns):
    size, total = lax.axis_size("rep"), same.shape[1]
    spec = pl.BlockSpec((height, total), lambda d, me: (d // 2, 0))
    at = lambda d, me: jnp.bitwise_xor(d, me[0])
    shape = (height, size * width) if columns else (size * height, width)
    count = total // width
    return pl.pallas_call(
        place_kernel,
        grid_spec=pltpu.PrefetchScalarGridSpec(
            num_scalar_prefetch=1,
            grid=(size,),
            in_specs=[spec, spec],
            out_specs=[
                pl.BlockSpec(
                    (height, width),
                    (lambda d, me: (0, at(d, me))) if columns else (lambda d, me: (at(d, me), 0)),
                )
            ] * count,
        ),
        out_shape=[jax.ShapeDtypeStruct(shape, F32)] * count,
        cost_estimate=pl.CostEstimate(
            flops=0, bytes_accessed=8 * size * height * total, transcendentals=0
        ),
        name="place",
    )(me, same, other)


def place_turned_kernel(me_ref, same_ref, other_ref, out_ref):
    odd = me_ref[0] % 2
    first = jnp.where(odd == 0, same_ref[...], other_ref[...])
    second = jnp.where(odd == 0, other_ref[...], same_ref[...])
    out_ref[...] = jnp.concatenate([first, second], axis=0).T.astype(F32)


def place_turned(me, same, other, height):
    size, width = lax.axis_size("rep"), same.shape[1]
    if 2 * height % 128:
        return place(me, same, other, height, width, False)[0].T
    spec = pl.BlockSpec((height, width), lambda j, me: (jnp.bitwise_xor(j, me[0] // 2), 0))
    return pl.pallas_call(
        place_turned_kernel,
        grid_spec=pltpu.PrefetchScalarGridSpec(
            num_scalar_prefetch=1,
            grid=(size // 2,),
            in_specs=[spec, spec],
            out_specs=pl.BlockSpec((width, 2 * height), lambda j, me: (0, j)),
        ),
        out_shape=jax.ShapeDtypeStruct((width, size * height), F32),
        compiler_params=pltpu.CompilerParams(vmem_limit_bytes=32 << 20),
        cost_estimate=pl.CostEstimate(
            flops=0, bytes_accessed=12 * same.size, transcendentals=0
        ),
        name="place_turned",
    )(me, same, other)


def turn_kernel(in_ref, out_ref):
    out_ref[...] = in_ref[...].T.astype(F32)


def turn(value):
    rows, width = value.shape
    tile = 512 if rows % 512 == 0 else rows
    return pl.pallas_call(
        turn_kernel,
        grid=(rows // tile,),
        in_specs=[pl.BlockSpec((tile, width), lambda i: (i, 0))],
        out_specs=pl.BlockSpec((width, tile), lambda i: (0, i)),
        out_shape=jax.ShapeDtypeStruct((width, rows), F32),
        cost_estimate=pl.CostEstimate(flops=0, bytes_accessed=6 * value.size, transcendentals=0),
        name="turn",
    )(value)


def per_device(
    layer_input,
    gain_attn,
    w_query,
    w_key,
    w_value,
    w_out,
    gain_mlp,
    w_gate,
    w_up,
    w_down,
    segments,
    attn_route,
    attn_gate,
    mlp_route,
    mlp_gate,
    cotangent,
):
    length = layer_input.shape[0]
    size, shards = lax.axis_size("rep"), lax.axis_size("shard")
    me = lax.axis_index("rep")
    whoami = me.astype(jnp.int32).reshape(1)
    shard = lax.axis_index("shard").astype(jnp.int32).reshape(1)
    block = w_query.shape[1] // size
    units = w_gate.shape[1] // size
    own = gain_attn.shape[0]
    offsets = chip_offsets()
    staged = len(chip_bits()) == 2

    def columns(weight, d, width):
        return lax.dynamic_slice_in_dim(weight, jnp.bitwise_xor(me, d) * width, width, 1)

    def rows_of(weight, height):
        return lax.dynamic_slice_in_dim(weight, me * height, height, 0)

    def local(d):
        return jnp.concatenate([columns(w, d, block) for w in (w_query, w_key, w_value)], axis=1)

    inputs = layer_input.astype(F32)
    root_one = lax.rsqrt(jnp.mean(inputs * inputs, axis=-1, keepdims=True) + EPSILON)
    tables = rotary_tables(length)
    ring = [(i, (i + 1) % shards) for i in range(shards)]
    piece = local(0)
    qkv_w = {d: [local(d)] for d in offsets}
    flows, context, saved = [], {}, {}
    gain_flow = Flow(vector_gather_steps(jnp.stack([gain_attn, gain_mlp])))
    piece, seg_other, own_gate_up = stage(
        [gain_flow],
        (
            lax.ppermute(piece, "shard", ring),
            swap(segments, 1),
            jnp.concatenate([columns(w_gate, 0, units), columns(w_up, 0, units)], axis=1),
        ),
    )
    gain_one, gain_two = gain_flow.result.astype(F32)
    normed = (inputs * root_one * gain_one).astype(BF)
    seg = jnp.concatenate([segments, seg_other], axis=0)
    seg = (seg[:, :, None], seg[:, None, :])
    other = swap(normed, 1)
    for step in range(1, shards):
        qkv_w[0].append(piece)
        flows.append(Flow(gather_steps(piece, lambda d, b: qkv_w[d].append(b))))
        if step < shards - 1:
            piece, other = stage(flows, (lax.ppermute(piece, "shard", ring), other))
    own_out, own_gate_up, qkv_w[0][-1] = lax.optimization_barrier(
        (rows_of(w_out, block), own_gate_up, qkv_w[0][-1])
    )
    own_out = lax.all_gather(own_out, "shard", axis=1, tiled=True)
    both = jnp.concatenate([normed, other], axis=0)

    def run(d):
        context[d], *saved[d] = attend(shard, both, qkv_w[d], tables, seg)
        return context[d]

    context[0], own_out = stage(flows, (run(0), own_out))
    own_gate_up, own_out = lax.optimization_barrier((own_gate_up, own_out))
    gate_up = lax.all_gather(own_gate_up, "shard", axis=0, tiled=True)
    own_down, _ = lax.optimization_barrier((rows_of(w_down, units), gate_up))
    down = lax.all_gather(own_down, "shard", axis=1, tiled=True)
    early = offsets[1:2] if staged else []
    early = stage(flows, [run(d) for d in early])
    for flow in flows:
        finish(flow)
    out_flow = Flow(gather_steps(own_out))
    rest = [d for d in offsets if d not in context]
    stage([out_flow], [run(d) for d in rest])
    out_w = finish(out_flow)

    table, mix = plan_slots(mlp_route, mlp_gate)
    pick = table.astype(BF)
    upstream = cotangent.astype(F32)
    slot_weight = jnp.sum(jnp.where(table, mix[None, :], 0.0), axis=1)[:, None]
    slot_grad = (mm(pick, cotangent) * slot_weight).astype(BF)

    all_context = jnp.concatenate([context[d] for d in offsets], axis=1)
    all_out = jnp.concatenate([out_w[d] for d in offsets], axis=0)
    projected = mm(all_context, all_out)
    projected = projected[:length] + swap(projected[length:].astype(BF), 1).astype(F32)
    attn_weight = jnp.sum(jnp.where(attn_route == 0, attn_gate, 0.0), axis=-1)[:, None]
    hidden = inputs + projected * attn_weight
    root_two = lax.rsqrt(jnp.mean(hidden * hidden, axis=-1, keepdims=True) + EPSILON)
    normed_two = (hidden * root_two * gain_two).astype(BF)

    disp_flow = Flow(copies_steps(mm(pick, normed_two).astype(BF)))
    stage([disp_flow])
    slot_grad, gate_up = stage([disp_flow], (slot_grad, gate_up))
    slot_flow = Flow(copies_steps(slot_grad))
    stage([disp_flow, slot_flow])
    dispatched = jnp.concatenate(finish(disp_flow), axis=0)
    act = mm(dispatched, gate_up)
    all_slot_grad = jnp.concatenate(finish(slot_flow), axis=0)
    gate_act, up_act = act[:, :units], act[:, units:]
    sigmoid = jax.nn.sigmoid(gate_act)
    silu = gate_act * sigmoid
    inner = (silu * up_act).astype(BF)
    grad_inner = mm_nt(all_slot_grad, down)
    grad_gate_act = (grad_inner * up_act * sigmoid * (1.0 + gate_act * (1.0 - sigmoid))).astype(BF)
    grad_up_act = (grad_inner * silu).astype(BF)
    grad_act = jnp.concatenate([grad_gate_act, grad_up_act], axis=1)
    back_flow = Flow(plane_sum_steps(mm_nt(grad_act, gate_up).astype(BF)))
    grad_mlp, sums = [], []
    for left, right in (
        (grad_gate_act, dispatched),
        (grad_up_act, dispatched),
        (inner, all_slot_grad),
    ):
        grad = stage([back_flow], mm_tn(left, right).astype(BF))
        sums.append(lax.psum_scatter(grad, "shard", scatter_dimension=1, tiled=True))
    grad_normed_two = mm_tn(pick, finish(back_flow))
    grad_gain_two, through = norm_back(grad_normed_two, hidden, root_two, gain_two)
    grad_hidden = upstream + through

    grad_projected = (grad_hidden * attn_weight).astype(BF)
    both_grad = jnp.concatenate([grad_projected, swap(grad_projected, 1)], axis=0)
    lins, grad_qkv_w = {}, {}

    def run_back(*ds):
        for d in ds:
            lins[d], *grad_qkv_w[d] = attend_back(
                both_grad, out_w[d], *saved[d], both, tables, seg
            )
        return [(lins[d], grad_qkv_w[d]) for d in ds]

    def keep(ds, values):
        for d, (lin, grad) in zip(ds, values):
            lins[d], grad_qkv_w[d] = lin, grad

    far, near = offsets[-1:], offsets[1:-1]
    values, both_grad = lax.optimization_barrier((run_back(*far), both_grad))
    keep(far, values)
    qkv_flow = Flow(scatter_steps(grad_qkv_w))
    values, both_grad = stage([qkv_flow], (run_back(*near), both_grad))
    keep(near, values)
    values, grad_out_w = stage([qkv_flow], (run_back(0), mm_tn(all_context, both_grad).astype(BF)))
    keep([0], values)
    grad_normed = normed_back(
        shard, [lins[d] for d in offsets], [qkv_w[d] for d in offsets], both.shape[1]
    )
    own_lin, sums[1] = lax.optimization_barrier((lins[0], (sums[1], sums[2])))
    sums[1], sums[2] = sums[1]
    lins[0] = own_lin
    sums[0], grad_normed, grad_out_w = stage([qkv_flow], (sums[0], grad_normed, grad_out_w))
    all_up = lax.all_gather(sums[1], "rep", axis=0, tiled=True)
    own_grad_qkv, all_up = lax.optimization_barrier((finish(qkv_flow), all_up))
    sum_qkv = lax.psum_scatter(own_grad_qkv, "shard", scatter_dimension=0, tiled=True)

    out_blocks = {d: halves(grad_out_w[i * block : (i + 1) * block]) for i, d in enumerate(offsets)}
    out_flow, gate_flow = Flow(scatter_steps(out_blocks)), Flow(copies_steps(sums[0]))
    expert_flow = Flow(plane_sum_steps(mm(inner, down).astype(BF)))
    other_normed = stage(
        [out_flow, gate_flow, expert_flow], swap(grad_normed[length:].astype(BF), 1)
    )
    grad_normed = grad_normed[:length] + other_normed.astype(F32)
    grad_gain_one, first = norm_back(grad_normed, inputs, root_one, gain_one)
    grad_input = (grad_hidden + first).astype(BF)
    grad_input, gains = stage(
        [out_flow, gate_flow, expert_flow], (grad_input, jnp.stack([grad_gain_one, grad_gain_two]))
    )
    gain_flow = Flow(vector_sum_steps(gains))
    stage([out_flow, gate_flow, gain_flow])
    grad_gate = place_turned(whoami, *finish(gate_flow), units)
    own_grad_out, sum_qkv = lax.optimization_barrier((finish(out_flow), sum_qkv))
    sum_out = lax.psum_scatter(own_grad_out, "shard", scatter_dimension=1, tiled=True)
    grad_gate, all_up = stage([expert_flow, gain_flow], (grad_gate, all_up))
    grad_up = turn(all_up)
    qkv_flow = Flow(copies_steps(sum_qkv))
    grad_up, sum_out = stage([qkv_flow, expert_flow], (grad_up, sum_out))
    down_sum, sum_out = lax.optimization_barrier((sums[2], sum_out))
    all_down = lax.all_gather(down_sum, "rep", axis=0, tiled=True)
    stage([qkv_flow, gain_flow])
    out_flow = Flow(copies_steps(sum_out))
    output = (hidden + mm_tn(pick, finish(expert_flow)) * mix[:, None]).astype(BF)
    output = stage([qkv_flow, out_flow, gain_flow], output)
    grad_query, grad_key, grad_value = place(whoami, *finish(qkv_flow), own, block, True)
    grad_query = stage([out_flow], grad_query)
    (grad_out,) = place(whoami, *finish(out_flow), block, own, False)
    grad_down = all_down.astype(F32)
    gain_grads = finish(gain_flow)
    return (
        output,
        grad_input,
        gain_grads[0],
        grad_query,
        grad_key,
        grad_value,
        grad_out,
        gain_grads[1],
        grad_gate,
        grad_up,
        grad_down,
    )


def solution(mesh):
    tokens = P(("rep", "shard"), None)
    tall, wide, vector = P("shard", None), P(None, "shard"), P("shard")
    weights = (vector, tall, tall, tall, wide, vector, tall, tall, wide)
    return jax.shard_map(
        per_device,
        mesh=mesh,
        in_specs=(tokens, *weights) + (tokens,) * 6,
        out_specs=(tokens, tokens, *weights),
        check_vma=False,
    )
```

```python
import functools

import jax
import jax.numpy as jnp
from jax import lax
from jax.experimental import pallas as pl
from jax.experimental.pallas import tpu as pltpu
from jax.sharding import PartitionSpec as P

HEADS = 16
HD = 128
WIN = 256
CAP = 128
EPSILON = 1e-05
BF = jnp.bfloat16
F32 = jnp.float32


def mm(left, right):
    return jnp.dot(left, right, preferred_element_type=F32)


def mm_nt(left, right):
    return lax.dot_general(left, right, (((1,), (1,)), ((), ())), preferred_element_type=F32)


def mm_tn(left, right):
    return lax.dot_general(left, right, (((0,), (0,)), ((), ())), preferred_element_type=F32)


def swap(value, bit):
    size = lax.axis_size("rep")
    return lax.ppermute(value, "rep", [(i, i ^ bit) for i in range(size)])


def chip_bits():
    size, bits, bit = lax.axis_size("rep"), [], 2
    while bit < size:
        bits.append(bit)
        bit *= 2
    return bits


def chip_offsets():
    return list(range(0, lax.axis_size("rep"), 2))


def add(left, right):
    return left.astype(F32) + right.astype(F32)


def halves(value):
    half = value.shape[0] // 2
    return value[:half], value[half:]


class Flow:
    def __init__(self, steps):
        self.steps, self.result, self.done = steps, None, False
        self.pending = next(steps)

    def advance(self, arrived):
        try:
            self.pending = self.steps.send(arrived)
        except StopIteration as end:
            self.pending, self.result, self.done = [], end.value, True


def stage(flows, extra=()):
    flows = [f for f in flows if not f.done]
    arrived, extra = lax.optimization_barrier(([f.pending for f in flows], extra))
    for flow, values in zip(flows, arrived):
        flow.advance(values)
    return extra


def finish(flow):
    while not flow.done:
        flow.advance(flow.pending)
    return flow.result


def gather_steps(value, sink=lambda offset, block: None):
    bits = chip_bits()
    if len(bits) == 2:
        one, two = bits
        half = value.shape[0] // 2
        by_one, by_two = yield [swap(value, one), swap(value, two)]
        sink(one, by_one)
        sink(two, by_two)
        top, bottom = yield [swap(by_one[:half], two), swap(by_two[half:], one)]
        far = jnp.concatenate([top, bottom], axis=0)
        sink(one ^ two, far)
        return {0: value, one: by_one, two: by_two, one ^ two: far}
    blocks = {0: value}
    for bit in bits:
        old = list(blocks.items())
        new = yield [swap(b, bit) for _, b in old]
        for (d, _), b in zip(old, new):
            blocks[d ^ bit] = b
            sink(d ^ bit, b)
    return blocks


def copies_steps(value):
    blocks = yield from gather_steps(value)
    same = jnp.concatenate([blocks[d] for d in chip_offsets()], axis=0)
    (other,) = yield [swap(same, 1)]
    return same, other


def scatter_steps(blocks):
    bits = chip_bits()
    if len(bits) == 2:
        one, two = bits
        far = blocks[one ^ two]
        top, bottom = yield [swap(far[0], one), swap(far[1], two)]
        near_one, near_two = blocks[one], blocks[two]
        one_top, two_bottom = yield [swap(near_one[0], one), swap(near_two[1], two)]
        two_top, one_bottom = yield [
            swap(add(near_two[0], top).astype(BF), two),
            swap(add(near_one[1], bottom).astype(BF), one),
        ]
        return jnp.concatenate(
            [
                (add(blocks[0][0], one_top) + two_top.astype(F32)).astype(BF),
                (add(blocks[0][1], one_bottom) + two_bottom.astype(F32)).astype(BF),
            ],
            axis=0,
        )
    while len(blocks) < len(chip_offsets()):
        yield []
    sums = {d: jnp.concatenate(b, axis=0) for d, b in blocks.items()}
    for bit in reversed(bits):
        kept = [d for d in sorted(sums) if not d & bit]
        new = yield [swap(sums[d | bit], bit) for d in kept]
        sums = {d: add(sums[d], n).astype(BF) for d, n in zip(kept, new)}
    return sums[0]


def plane_sum_steps(partial):
    half = partial.shape[0] // 2
    (other,) = yield [swap(partial[half:], 1)]
    same = add(partial[:half], other).astype(BF)
    offsets = chip_offsets()
    rows = half // len(offsets)
    blocks = {d: halves(same[i * rows : (i + 1) * rows]) for i, d in enumerate(offsets)}
    return (yield from scatter_steps(blocks))


def vector_sum_steps(rows):
    size, bit = lax.axis_size("rep"), 1
    while bit < size:
        (other,) = yield [swap(rows, bit)]
        rows, bit = rows + other, 2 * bit
    shards, at = lax.axis_size("shard"), lax.axis_index("shard")
    own = rows.shape[1] // shards
    parts = yield [
        lax.ppermute(
            lax.dynamic_slice_in_dim(rows, ((at + k) % shards) * own, own, 1),
            "shard",
            [(i, (i + k) % shards) for i in range(shards)],
        )
        for k in range(1, shards)
    ]
    return lax.dynamic_slice_in_dim(rows, at * own, own, 1) + sum(parts)


def vector_gather_steps(rows):
    size, me = lax.axis_size("shard"), lax.axis_index("shard")
    others = yield [
        lax.ppermute(rows, "shard", [(i, (i - k) % size) for i in range(size)])
        for k in range(1, size)
    ]
    parts = [rows, *others]
    twice = jnp.concatenate(parts + parts, axis=1)
    own = rows.shape[1]
    return lax.dynamic_slice_in_dim(twice, ((size - me) % size) * own, size * own, 1)


def rotary_tables(length):
    half = HD // 2
    positions = jnp.arange(length, dtype=F32)
    inverse = 10000.0 ** (-2.0 * jnp.arange(half, dtype=F32) / HD)
    angles = positions[:, None] * inverse[None, :]
    cos, sin = jnp.cos(angles), jnp.sin(angles)
    return jnp.concatenate([cos, cos], axis=1), jnp.concatenate([-sin, sin], axis=1)


def rotate(values, cos, sin):
    return values * cos + pltpu.roll(values, HD // 2, 1) * sin


def window(step, seg_col, seg_row):
    low, high = max(0, step - 1) * WIN, (step + 1) * WIN
    shape = (WIN, high - low)
    row = lax.broadcasted_iota(jnp.int32, shape, 0) + step * WIN
    col = lax.broadcasted_iota(jnp.int32, shape, 1) + low
    near = (row >= col) & (row - col < WIN)
    same = seg_col[0, step * WIN : (step + 1) * WIN, :] == seg_row[0, :, low:high]
    return low, high, near & same


def attend_kernel(parts, z_ref, *refs):
    x_refs, w_refs = refs[:parts], refs[parts : 2 * parts]
    cos_ref, sin_ref, col_ref, row_ref, context_ref, qkv_ref, lse_ref, lin_ref = refs[2 * parts :]
    length, width = context_ref.shape
    tile = min(length, 256)

    @pl.loop(0, length // tile)
    def _(t):
        rows = pl.ds(pl.multiple_of(t * tile, tile), tile)
        total = mm(x_refs[0][rows, :], w_refs[0][...])
        for x, w in zip(x_refs[1:], w_refs[1:]):
            total += mm(x[rows, :], w[...])
        lin_ref[rows, :] = total

    cos, sin = cos_ref[...], sin_ref[...]
    for h in range(width // HD):
        q_at, k_at, v_at = (slice(i * width + h * HD, i * width + (h + 1) * HD) for i in range(3))
        qkv_ref[:, q_at] = rotate(lin_ref[:, q_at], cos, sin).astype(BF)
        qkv_ref[:, k_at] = rotate(lin_ref[:, k_at], cos, sin).astype(BF)
        qkv_ref[:, v_at] = lin_ref[:, v_at].astype(BF)
    for step in range(length // WIN):
        low, high, allowed = window(step, col_ref, row_ref)
        rows = slice(step * WIN, (step + 1) * WIN)
        for h in range(width // HD):
            q_at, k_at, v_at = (
                slice(i * width + h * HD, i * width + (h + 1) * HD) for i in range(3)
            )
            scores = mm_nt(qkv_ref[rows, q_at], qkv_ref[low:high, k_at]) * HD**-0.5
            scores = jnp.where(allowed, scores, -1e30)
            peak = jnp.max(scores, axis=1, keepdims=True)
            raw = jnp.exp(scores - peak)
            total = jnp.sum(raw, axis=1, keepdims=True)
            probs = (raw * (1.0 / total)).astype(BF)
            context_ref[rows, h * HD : (h + 1) * HD] = mm(probs, qkv_ref[low:high, v_at]).astype(BF)
            lse_ref[rows, h : h + 1] = peak + jnp.log(total)


def attend(shard, both, weights, tables, seg):
    parts = len(weights)
    rows, depth = both.shape
    length = tables[0].shape[0]
    wide = weights[0].shape[1]
    width = wide // 3
    piece = depth // parts
    whole = lambda *shape: pl.BlockSpec(shape, lambda s, z: (0,) * len(shape))
    take = lambda k: pl.BlockSpec((length, piece), lambda s, z: (s, (z[0] + parts - k) % parts))
    by_seq = lambda cols: pl.BlockSpec((length, cols), lambda s, z: (s, 0))
    return pl.pallas_call(
        functools.partial(attend_kernel, parts),
        grid_spec=pltpu.PrefetchScalarGridSpec(
            num_scalar_prefetch=1,
            grid=(rows // length,),
            in_specs=[take(k) for k in range(parts)]
            + [whole(piece, wide)] * parts
            + [whole(length, HD)] * 2
            + [
                pl.BlockSpec((1, length, 1), lambda s, z: (s, 0, 0)),
                pl.BlockSpec((1, 1, length), lambda s, z: (s, 0, 0)),
            ],
            out_specs=[by_seq(width), by_seq(wide), by_seq(width // HD)],
            scratch_shapes=[pltpu.VMEM((length, wide), F32)],
        ),
        out_shape=[
            jax.ShapeDtypeStruct((rows, width), BF),
            jax.ShapeDtypeStruct((rows, wide), BF),
            jax.ShapeDtypeStruct((rows, width // HD), F32),
        ],
        compiler_params=pltpu.CompilerParams(vmem_limit_bytes=40 << 20),
        cost_estimate=pl.CostEstimate(
            flops=2 * rows * depth * wide + 4 * rows * 2 * WIN * width,
            bytes_accessed=2 * (rows * depth + depth * wide + 2 * rows * wide),
            transcendentals=rows * 2 * WIN * width // HD,
        ),
        name="attend",
    )(shard, *[both] * parts, *weights, *tables, *seg)


def attend_back_kernel(
    grad_ref, out_ref, qkv_ref, lse_ref, x_ref, cos_ref, sin_ref, col_ref, row_ref,
    lin_ref, top_ref, bottom_ref, kept_ref, context_ref, keys_ref, values_ref,
):
    length, wide = qkv_ref.shape
    width = wide // 3
    seq = pl.program_id(0)
    tile = min(length, 256)

    @pl.loop(0, length // tile)
    def _(t):
        rows = pl.ds(pl.multiple_of(t * tile, tile), tile)
        context_ref[rows, :] = mm_nt(grad_ref[rows, :], out_ref[...]).astype(BF)

    cos, sin = cos_ref[...], sin_ref[...]
    scale = HD**-0.5
    for h in range(width // HD):
        q_at, k_at, v_at = (slice(i * width + h * HD, i * width + (h + 1) * HD) for i in range(3))
        head = slice(h * HD, (h + 1) * HD)
        keys_ref[...] = jnp.zeros_like(keys_ref)
        values_ref[...] = jnp.zeros_like(values_ref)
        for step in range(length // WIN):
            low, high, allowed = window(step, col_ref, row_ref)
            rows = slice(step * WIN, (step + 1) * WIN)
            queries, keys = qkv_ref[rows, q_at], qkv_ref[low:high, k_at]
            grad = context_ref[rows, head]
            scores = jnp.where(allowed, mm_nt(queries, keys) * scale, -1e30)
            probs = jnp.exp(scores - lse_ref[rows, h : h + 1])
            values_ref[low:high, :] += mm_tn(probs.astype(BF), grad)
            grad_probs = mm_nt(grad, qkv_ref[low:high, v_at])
            inner = jnp.sum(probs * grad_probs, axis=1, keepdims=True)
            grad_scores = (probs * (grad_probs - inner)).astype(BF)
            grad_queries = mm(grad_scores, keys) * scale
            keys_ref[low:high, :] += mm_tn(grad_scores, queries)
            lin_ref[rows, q_at] = rotate(grad_queries, cos[rows], -sin[rows]).astype(BF)
        lin_ref[:, k_at] = rotate(keys_ref[...] * scale, cos, -sin).astype(BF)
        lin_ref[:, v_at] = values_ref[...].astype(BF)
    kept_ref[pl.ds(pl.multiple_of(seq * length, length), length), :] = lin_ref[...]

    @pl.when(seq == pl.num_programs(0) - 1)
    def _():
        half = top_ref.shape[0]
        step = 256
        for n, ref in enumerate((top_ref, bottom_ref)):

            @pl.loop(0, half // step)
            def _(t):
                cols = pl.ds(pl.multiple_of(n * half + t * step, step), step)
                rows = pl.ds(pl.multiple_of(t * step, step), step)
                ref[rows, :] = mm_tn(x_ref[:, cols], kept_ref[...]).astype(BF)


def attend_back(grad, out_w, qkv, lse, both, tables, seg):
    rows, depth = both.shape
    length = tables[0].shape[0]
    wide = qkv.shape[1]
    width = wide // 3
    whole = lambda *shape: pl.BlockSpec(shape, lambda s: (0,) * len(shape))
    by_seq = lambda cols: pl.BlockSpec((length, cols), lambda s: (s, 0))
    return pl.pallas_call(
        attend_back_kernel,
        grid=(rows // length,),
        in_specs=[by_seq(depth), whole(width, depth), by_seq(wide), by_seq(width // HD)]
        + [whole(rows, depth), whole(length, HD), whole(length, HD)]
        + [
            pl.BlockSpec((1, length, 1), lambda s: (s, 0, 0)),
            pl.BlockSpec((1, 1, length), lambda s: (s, 0, 0)),
        ],
        out_specs=[by_seq(wide), whole(depth // 2, wide), whole(depth // 2, wide)],
        scratch_shapes=[
            pltpu.VMEM((rows, wide), BF),
            pltpu.VMEM((length, width), BF),
            pltpu.VMEM((length, HD), F32),
            pltpu.VMEM((length, HD), F32),
        ],
        out_shape=[
            jax.ShapeDtypeStruct((rows, wide), BF),
            jax.ShapeDtypeStruct((depth // 2, wide), BF),
            jax.ShapeDtypeStruct((depth // 2, wide), BF),
        ],
        compiler_params=pltpu.CompilerParams(vmem_limit_bytes=48 << 20),
        cost_estimate=pl.CostEstimate(
            flops=2 * rows * depth * (wide + width) + 10 * rows * 2 * WIN * width,
            bytes_accessed=2 * (2 * rows * depth + depth * (wide + width) + 2 * rows * wide),
            transcendentals=rows * 2 * WIN * width // HD,
        ),
        name="attend_back",
    )(grad, out_w, qkv, lse, both, *tables, *seg)


def normed_back_kernel(blocks, parts, z_ref, *refs):
    lins, weights, total_ref = refs[:blocks], refs[blocks:-1], refs[-1]
    piece = total_ref.shape[1] // parts
    for k in range(parts):
        total = mm_nt(lins[0][...], weights[k][...])
        for n in range(1, blocks):
            total += mm_nt(lins[n][...], weights[n * parts + k][...])
        at = pl.multiple_of(((z_ref[0] + parts - k) % parts) * piece, piece)
        total_ref[:, pl.ds(at, piece)] = total


def normed_back(shard, lins, weights, depth):
    parts = len(weights[0])
    rows, wide = lins[0].shape
    tile = min(rows, 256)
    flat = [w for block in weights for w in block]
    return pl.pallas_call(
        functools.partial(normed_back_kernel, len(lins), parts),
        grid_spec=pltpu.PrefetchScalarGridSpec(
            num_scalar_prefetch=1,
            grid=(rows // tile,),
            in_specs=[pl.BlockSpec((tile, wide), lambda s, z: (s, 0))] * len(lins)
            + [
                pl.BlockSpec(flat[0].shape, lambda s, z: (0, 0), pipeline_mode=pl.Buffered(1))
            ] * len(flat),
            out_specs=pl.BlockSpec((tile, depth), lambda s, z: (s, 0)),
        ),
        out_shape=jax.ShapeDtypeStruct((rows, depth), F32),
        compiler_params=pltpu.CompilerParams(vmem_limit_bytes=48 << 20),
        cost_estimate=pl.CostEstimate(
            flops=2 * rows * depth * wide * len(lins),
            bytes_accessed=2 * len(lins) * wide * (rows + depth) + 4 * rows * depth,
            transcendentals=0,
        ),
        name="normed_back",
    )(shard, *lins, *flat)


def plan_slots(route_ids, gate_values):
    hit_mask = route_ids == 0
    hit = jnp.any(hit_mask, axis=-1)
    weight = jnp.sum(jnp.where(hit_mask, gate_values, 0.0), axis=-1)
    ids = jnp.arange(route_ids.shape[0], dtype=jnp.int32)
    earlier = (ids[None, :] < ids[:, None]) & hit[None, :]
    order = jnp.sum(earlier.astype(jnp.int32), axis=1)
    kept = hit & (order < CAP)
    slots = jnp.arange(CAP, dtype=jnp.int32)
    table = (order[None, :] == slots[:, None]) & kept[None, :]
    return table, jnp.where(kept, weight, 0.0)


def norm_back(grad_normed, source, root, gain):
    scaled = grad_normed * gain
    grad_gain = jnp.sum(grad_normed * source * root, axis=0)
    mean = jnp.mean(scaled * source, axis=-1, keepdims=True)
    return grad_gain, root * scaled - source * (root * root * root) * mean


def place_kernel(me_ref, same_ref, other_ref, *out_refs):
    block = jnp.where(pl.program_id(0) % 2 == 0, same_ref[...], other_ref[...]).astype(F32)
    width = out_refs[0].shape[1]
    for i, ref in enumerate(out_refs):
        ref[...] = block[:, i * width : (i + 1) * width]


def place(me, same, other, height, width, columns):
    size, total = lax.axis_size("rep"), same.shape[1]
    spec = pl.BlockSpec((height, total), lambda d, me: (d // 2, 0))
    at = lambda d, me: jnp.bitwise_xor(d, me[0])
    shape = (height, size * width) if columns else (size * height, width)
    count = total // width
    return pl.pallas_call(
        place_kernel,
        grid_spec=pltpu.PrefetchScalarGridSpec(
            num_scalar_prefetch=1,
            grid=(size,),
            in_specs=[spec, spec],
            out_specs=[
                pl.BlockSpec(
                    (height, width),
                    (lambda d, me: (0, at(d, me))) if columns else (lambda d, me: (at(d, me), 0)),
                )
            ] * count,
        ),
        out_shape=[jax.ShapeDtypeStruct(shape, F32)] * count,
        cost_estimate=pl.CostEstimate(
            flops=0, bytes_accessed=8 * size * height * total, transcendentals=0
        ),
        name="place",
    )(me, same, other)


def place_turned_kernel(me_ref, same_ref, other_ref, out_ref):
    odd = me_ref[0] % 2
    first = jnp.where(odd == 0, same_ref[...], other_ref[...])
    second = jnp.where(odd == 0, other_ref[...], same_ref[...])
    out_ref[...] = jnp.concatenate([first, second], axis=0).T.astype(F32)


def place_turned(me, same, other, height):
    size, width = lax.axis_size("rep"), same.shape[1]
    if 2 * height % 128:
        return place(me, same, other, height, width, False)[0].T
    spec = pl.BlockSpec((height, width), lambda j, me: (jnp.bitwise_xor(j, me[0] // 2), 0))
    return pl.pallas_call(
        place_turned_kernel,
        grid_spec=pltpu.PrefetchScalarGridSpec(
            num_scalar_prefetch=1,
            grid=(size // 2,),
            in_specs=[spec, spec],
            out_specs=pl.BlockSpec((width, 2 * height), lambda j, me: (0, j)),
        ),
        out_shape=jax.ShapeDtypeStruct((width, size * height), F32),
        compiler_params=pltpu.CompilerParams(vmem_limit_bytes=32 << 20),
        cost_estimate=pl.CostEstimate(
            flops=0, bytes_accessed=12 * same.size, transcendentals=0
        ),
        name="place_turned",
    )(me, same, other)


def per_device(
    layer_input,
    gain_attn,
    w_query,
    w_key,
    w_value,
    w_out,
    gain_mlp,
    w_gate,
    w_up,
    w_down,
    segments,
    attn_route,
    attn_gate,
    mlp_route,
    mlp_gate,
    cotangent,
):
    length = layer_input.shape[0]
    size, shards = lax.axis_size("rep"), lax.axis_size("shard")
    me = lax.axis_index("rep")
    whoami = me.astype(jnp.int32).reshape(1)
    shard = lax.axis_index("shard").astype(jnp.int32).reshape(1)
    block = w_query.shape[1] // size
    units = w_gate.shape[1] // size
    own = gain_attn.shape[0]
    offsets = chip_offsets()
    staged = len(chip_bits()) == 2

    def columns(weight, d, width):
        return lax.dynamic_slice_in_dim(weight, jnp.bitwise_xor(me, d) * width, width, 1)

    def rows_of(weight, height):
        return lax.dynamic_slice_in_dim(weight, me * height, height, 0)

    def local(d):
        return jnp.concatenate([columns(w, d, block) for w in (w_query, w_key, w_value)], axis=1)

    inputs = layer_input.astype(F32)
    root_one = lax.rsqrt(jnp.mean(inputs * inputs, axis=-1, keepdims=True) + EPSILON)
    tables = rotary_tables(length)
    ring = [(i, (i + 1) % shards) for i in range(shards)]
    piece = local(0)
    qkv_w = {d: [local(d)] for d in offsets}
    flows, context, saved = [], {}, {}
    gain_flow = Flow(vector_gather_steps(jnp.stack([gain_attn, gain_mlp])))
    piece, seg_other, own_gate_up = stage(
        [gain_flow],
        (
            lax.ppermute(piece, "shard", ring),
            swap(segments, 1),
            jnp.concatenate([columns(w_gate, 0, units), columns(w_up, 0, units)], axis=1),
        ),
    )
    gain_one, gain_two = gain_flow.result.astype(F32)
    normed = (inputs * root_one * gain_one).astype(BF)
    seg = jnp.concatenate([segments, seg_other], axis=0)
    seg = (seg[:, :, None], seg[:, None, :])
    other = swap(normed, 1)
    for step in range(1, shards):
        qkv_w[0].append(piece)
        flows.append(Flow(gather_steps(piece, lambda d, b: qkv_w[d].append(b))))
        if step < shards - 1:
            piece, other = stage(flows, (lax.ppermute(piece, "shard", ring), other))
    own_out, own_gate_up, qkv_w[0][-1] = lax.optimization_barrier(
        (rows_of(w_out, block), own_gate_up, qkv_w[0][-1])
    )
    own_out = lax.all_gather(own_out, "shard", axis=1, tiled=True)
    both = jnp.concatenate([normed, other], axis=0)

    def run(d):
        context[d], *saved[d] = attend(shard, both, qkv_w[d], tables, seg)
        return context[d]

    context[0], own_out = stage(flows, (run(0), own_out))
    own_gate_up, own_out = lax.optimization_barrier((own_gate_up, own_out))
    gate_up = lax.all_gather(own_gate_up, "shard", axis=0, tiled=True)
    own_down, _ = lax.optimization_barrier((rows_of(w_down, units), gate_up))
    down = lax.all_gather(own_down, "shard", axis=1, tiled=True)
    early = offsets[1:2] if staged else []
    early = stage(flows, [run(d) for d in early])
    for flow in flows:
        finish(flow)
    out_flow = Flow(gather_steps(own_out))
    rest = [d for d in offsets if d not in context]
    stage([out_flow], [run(d) for d in rest])
    out_w = finish(out_flow)

    table, mix = plan_slots(mlp_route, mlp_gate)
    pick = table.astype(BF)
    upstream = cotangent.astype(F32)
    slot_weight = jnp.sum(jnp.where(table, mix[None, :], 0.0), axis=1)[:, None]
    slot_grad = (mm(pick, cotangent) * slot_weight).astype(BF)

    all_context = jnp.concatenate([context[d] for d in offsets], axis=1)
    all_out = jnp.concatenate([out_w[d] for d in offsets], axis=0)
    projected = mm(all_context, all_out)
    projected = projected[:length] + swap(projected[length:].astype(BF), 1).astype(F32)
    attn_weight = jnp.sum(jnp.where(attn_route == 0, attn_gate, 0.0), axis=-1)[:, None]
    hidden = inputs + projected * attn_weight
    root_two = lax.rsqrt(jnp.mean(hidden * hidden, axis=-1, keepdims=True) + EPSILON)
    normed_two = (hidden * root_two * gain_two).astype(BF)

    disp_flow = Flow(copies_steps(mm(pick, normed_two).astype(BF)))
    stage([disp_flow])
    slot_grad, gate_up = stage([disp_flow], (slot_grad, gate_up))
    slot_flow = Flow(copies_steps(slot_grad))
    stage([disp_flow, slot_flow])
    dispatched = jnp.concatenate(finish(disp_flow), axis=0)
    act = mm(dispatched, gate_up)
    all_slot_grad = jnp.concatenate(finish(slot_flow), axis=0)
    gate_act, up_act = act[:, :units], act[:, units:]
    sigmoid = jax.nn.sigmoid(gate_act)
    silu = gate_act * sigmoid
    inner = (silu * up_act).astype(BF)
    grad_inner = mm_nt(all_slot_grad, down)
    grad_gate_act = (grad_inner * up_act * sigmoid * (1.0 + gate_act * (1.0 - sigmoid))).astype(BF)
    grad_up_act = (grad_inner * silu).astype(BF)
    grad_act = jnp.concatenate([grad_gate_act, grad_up_act], axis=1)
    back_flow = Flow(plane_sum_steps(mm_nt(grad_act, gate_up).astype(BF)))
    flows, sums = [back_flow], []
    for left, right in (
        (grad_gate_act, dispatched),
        (grad_up_act, dispatched),
        (inner, all_slot_grad),
    ):
        grad = stage(flows, mm_tn(left, right).astype(BF))
        sums.append(lax.psum_scatter(grad, "shard", scatter_dimension=1, tiled=True))
        if len(flows) == 1:
            expert_flow = Flow(plane_sum_steps(mm(inner, down).astype(BF)))
            flows.append(expert_flow)
    stage(flows)
    grad_normed_two = mm_tn(pick, finish(back_flow))
    grad_gain_two, through = norm_back(grad_normed_two, hidden, root_two, gain_two)
    grad_hidden = upstream + through

    grad_projected = (grad_hidden * attn_weight).astype(BF)
    both_grad = jnp.concatenate([grad_projected, swap(grad_projected, 1)], axis=0)
    lins, grad_qkv_w = {}, {}

    def run_back(*ds):
        for d in ds:
            lins[d], *grad_qkv_w[d] = attend_back(
                both_grad, out_w[d], *saved[d], both, tables, seg
            )
        return [(lins[d], grad_qkv_w[d]) for d in ds]

    def keep(ds, values):
        for d, (lin, grad) in zip(ds, values):
            lins[d], grad_qkv_w[d] = lin, grad

    far, near = offsets[-1:], offsets[1:-1]
    values, both_grad = stage([expert_flow], (run_back(*far), both_grad))
    keep(far, values)
    qkv_flow = Flow(scatter_steps(grad_qkv_w))
    values, both_grad = stage([qkv_flow], (run_back(*near), both_grad))
    keep(near, values)
    values, grad_out_w = stage([qkv_flow], (run_back(0), mm_tn(all_context, both_grad).astype(BF)))
    keep([0], values)
    grad_normed = normed_back(
        shard, [lins[d] for d in offsets], [qkv_w[d] for d in offsets], both.shape[1]
    )
    sums[0], sums[1], grad_normed, grad_out_w = stage(
        [qkv_flow], (sums[0], sums[1], grad_normed, grad_out_w)
    )
    own_grad_qkv, sums[2] = lax.optimization_barrier((finish(qkv_flow), sums[2]))
    sum_qkv = lax.psum_scatter(own_grad_qkv, "shard", scatter_dimension=0, tiled=True)

    out_blocks = {d: halves(grad_out_w[i * block : (i + 1) * block]) for i, d in enumerate(offsets)}
    out_flow, gate_flow = Flow(scatter_steps(out_blocks)), Flow(copies_steps(sums[0]))
    other_normed, up_sum = stage(
        [out_flow, gate_flow], (swap(grad_normed[length:].astype(BF), 1), sums[1])
    )
    grad_normed = grad_normed[:length] + other_normed.astype(F32)
    grad_gain_one, first = norm_back(grad_normed, inputs, root_one, gain_one)
    grad_input = (grad_hidden + first).astype(BF)
    grad_input, gains, up_sum = stage(
        [out_flow, gate_flow],
        (grad_input, jnp.stack([grad_gain_one, grad_gain_two]), up_sum),
    )
    gain_flow, up_flow = Flow(vector_sum_steps(gains)), Flow(copies_steps(up_sum))
    sum_qkv = stage([out_flow, gate_flow, up_flow, gain_flow], sum_qkv)
    sum_out = lax.psum_scatter(finish(out_flow), "shard", scatter_dimension=1, tiled=True)
    qkv_flow = Flow(copies_steps(sum_qkv))
    grad_gate = place_turned(whoami, *finish(gate_flow), units)
    grad_gate, sum_out = stage([up_flow, qkv_flow, gain_flow], (grad_gate, sum_out))
    down_sum, sum_out = lax.optimization_barrier((sums[2], sum_out))
    all_down = lax.all_gather(down_sum, "rep", axis=0, tiled=True)
    out_flow = Flow(copies_steps(sum_out))
    output = (hidden + mm_tn(pick, finish(expert_flow)) * mix[:, None]).astype(BF)
    output = stage([up_flow, qkv_flow, out_flow, gain_flow], output)
    grad_up = place_turned(whoami, *finish(up_flow), units)
    grad_up = stage([qkv_flow, out_flow, gain_flow], grad_up)
    grad_query, grad_key, grad_value = place(whoami, *finish(qkv_flow), own, block, True)
    grad_query = stage([out_flow], grad_query)
    (grad_out,) = place(whoami, *finish(out_flow), block, own, False)
    grad_down = all_down.astype(F32)
    gain_grads = finish(gain_flow)
    return (
        output,
        grad_input,
        gain_grads[0],
        grad_query,
        grad_key,
        grad_value,
        grad_out,
        gain_grads[1],
        grad_gate,
        grad_up,
        grad_down,
    )


def solution(mesh):
    tokens = P(("rep", "shard"), None)
    tall, wide, vector = P("shard", None), P(None, "shard"), P("shard")
    weights = (vector, tall, tall, tall, wide, vector, tall, tall, wide)
    return jax.shard_map(
        per_device,
        mesh=mesh,
        in_specs=(tokens, *weights) + (tokens,) * 6,
        out_specs=(tokens, tokens, *weights),
        check_vma=False,
    )
```

```python
import functools

import jax
import jax.numpy as jnp
from jax import lax
from jax.experimental import pallas as pl
from jax.experimental.pallas import tpu as pltpu
from jax.sharding import PartitionSpec as P

HEADS = 16
HD = 128
WIN = 256
CAP = 128
EPSILON = 1e-05
BF = jnp.bfloat16
F32 = jnp.float32


def mm(left, right):
    return jnp.dot(left, right, preferred_element_type=F32)


def mm_nt(left, right):
    return lax.dot_general(left, right, (((1,), (1,)), ((), ())), preferred_element_type=F32)


def mm_tn(left, right):
    return lax.dot_general(left, right, (((0,), (0,)), ((), ())), preferred_element_type=F32)


def swap(value, bit):
    size = lax.axis_size("rep")
    return lax.ppermute(value, "rep", [(i, i ^ bit) for i in range(size)])


def chip_bits():
    size, bits, bit = lax.axis_size("rep"), [], 2
    while bit < size:
        bits.append(bit)
        bit *= 2
    return bits


def chip_offsets():
    return list(range(0, lax.axis_size("rep"), 2))


def add(left, right):
    return left.astype(F32) + right.astype(F32)


def halves(value):
    half = value.shape[0] // 2
    return value[:half], value[half:]


class Flow:
    def __init__(self, steps):
        self.steps, self.result, self.done = steps, None, False
        self.pending = next(steps)

    def advance(self, arrived):
        try:
            self.pending = self.steps.send(arrived)
        except StopIteration as end:
            self.pending, self.result, self.done = [], end.value, True


def stage(flows, extra=()):
    flows = [f for f in flows if not f.done]
    arrived, extra = lax.optimization_barrier(([f.pending for f in flows], extra))
    for flow, values in zip(flows, arrived):
        flow.advance(values)
    return extra


def finish(flow):
    while not flow.done:
        flow.advance(flow.pending)
    return flow.result


def gather_steps(value, sink=lambda offset, block: None):
    bits = chip_bits()
    if len(bits) == 2:
        one, two = bits
        half = value.shape[0] // 2
        by_one, by_two = yield [swap(value, one), swap(value, two)]
        sink(one, by_one)
        sink(two, by_two)
        top, bottom = yield [swap(by_one[:half], two), swap(by_two[half:], one)]
        far = jnp.concatenate([top, bottom], axis=0)
        sink(one ^ two, far)
        return {0: value, one: by_one, two: by_two, one ^ two: far}
    blocks = {0: value}
    for bit in bits:
        old = list(blocks.items())
        new = yield [swap(b, bit) for _, b in old]
        for (d, _), b in zip(old, new):
            blocks[d ^ bit] = b
            sink(d ^ bit, b)
    return blocks


def jump(value, offset):
    size = lax.axis_size("rep")
    return lax.ppermute(value, "rep", [(i, i ^ offset) for i in range(size)])


def straight_steps(value):
    away = [d for d in chip_offsets() if d]
    new = yield [jump(value, d) for d in away]
    return dict(zip([0, *away], [value, *new]))


def copies_steps(value, gather=gather_steps):
    blocks = yield from gather(value)
    same = jnp.concatenate([blocks[d] for d in chip_offsets()], axis=0)
    (other,) = yield [swap(same, 1)]
    return same, other


def scatter_steps(blocks):
    bits = chip_bits()
    if len(bits) == 2:
        one, two = bits
        far = blocks[one ^ two]
        top, bottom = yield [swap(far[0], one), swap(far[1], two)]
        near_one, near_two = blocks[one], blocks[two]
        one_top, two_bottom = yield [swap(near_one[0], one), swap(near_two[1], two)]
        two_top, one_bottom = yield [
            swap(add(near_two[0], top).astype(BF), two),
            swap(add(near_one[1], bottom).astype(BF), one),
        ]
        return jnp.concatenate(
            [
                (add(blocks[0][0], one_top) + two_top.astype(F32)).astype(BF),
                (add(blocks[0][1], one_bottom) + two_bottom.astype(F32)).astype(BF),
            ],
            axis=0,
        )
    while len(blocks) < len(chip_offsets()):
        yield []
    sums = {d: jnp.concatenate(b, axis=0) for d, b in blocks.items()}
    for bit in reversed(bits):
        kept = [d for d in sorted(sums) if not d & bit]
        new = yield [swap(sums[d | bit], bit) for d in kept]
        sums = {d: add(sums[d], n).astype(BF) for d, n in zip(kept, new)}
    return sums[0]


def plane_sum_steps(partial):
    half = partial.shape[0] // 2
    (other,) = yield [swap(partial[half:], 1)]
    same = add(partial[:half], other).astype(BF)
    offsets = chip_offsets()
    rows = half // len(offsets)
    blocks = {d: same[i * rows : (i + 1) * rows] for i, d in enumerate(offsets)}
    new = yield [jump(blocks[d], d) for d in offsets if d]
    return sum((n.astype(F32) for n in new), blocks[0].astype(F32)).astype(BF)


def vector_sum_steps(rows):
    size, bit = lax.axis_size("rep"), 1
    while bit < size:
        (other,) = yield [swap(rows, bit)]
        rows, bit = rows + other, 2 * bit
    shards, at = lax.axis_size("shard"), lax.axis_index("shard")
    own = rows.shape[1] // shards
    parts = yield [
        lax.ppermute(
            lax.dynamic_slice_in_dim(rows, ((at + k) % shards) * own, own, 1),
            "shard",
            [(i, (i + k) % shards) for i in range(shards)],
        )
        for k in range(1, shards)
    ]
    return lax.dynamic_slice_in_dim(rows, at * own, own, 1) + sum(parts)


def vector_gather_steps(rows):
    size, me = lax.axis_size("shard"), lax.axis_index("shard")
    others = yield [
        lax.ppermute(rows, "shard", [(i, (i - k) % size) for i in range(size)])
        for k in range(1, size)
    ]
    parts = [rows, *others]
    twice = jnp.concatenate(parts + parts, axis=1)
    own = rows.shape[1]
    return lax.dynamic_slice_in_dim(twice, ((size - me) % size) * own, size * own, 1)


def rotary_tables(length):
    half = HD // 2
    positions = jnp.arange(length, dtype=F32)
    inverse = 10000.0 ** (-2.0 * jnp.arange(half, dtype=F32) / HD)
    angles = positions[:, None] * inverse[None, :]
    cos, sin = jnp.cos(angles), jnp.sin(angles)
    return jnp.concatenate([cos, cos], axis=1), jnp.concatenate([-sin, sin], axis=1)


def rotate(values, cos, sin):
    return values * cos + pltpu.roll(values, HD // 2, 1) * sin


def window(step, seg_col, seg_row):
    low, high = max(0, step - 1) * WIN, (step + 1) * WIN
    shape = (WIN, high - low)
    row = lax.broadcasted_iota(jnp.int32, shape, 0) + step * WIN
    col = lax.broadcasted_iota(jnp.int32, shape, 1) + low
    near = (row >= col) & (row - col < WIN)
    same = seg_col[0, step * WIN : (step + 1) * WIN, :] == seg_row[0, :, low:high]
    return low, high, near & same


def attend_kernel(parts, z_ref, *refs):
    x_refs, w_refs = refs[:parts], refs[parts : 2 * parts]
    cos_ref, sin_ref, col_ref, row_ref, context_ref, qkv_ref, lse_ref, lin_ref = refs[2 * parts :]
    length, width = context_ref.shape
    tile = min(length, 256)

    @pl.loop(0, length // tile)
    def _(t):
        rows = pl.ds(pl.multiple_of(t * tile, tile), tile)
        total = mm(x_refs[0][rows, :], w_refs[0][...])
        for x, w in zip(x_refs[1:], w_refs[1:]):
            total += mm(x[rows, :], w[...])
        lin_ref[rows, :] = total

    cos, sin = cos_ref[...], sin_ref[...]
    for h in range(width // HD):
        q_at, k_at, v_at = (slice(i * width + h * HD, i * width + (h + 1) * HD) for i in range(3))
        qkv_ref[:, q_at] = rotate(lin_ref[:, q_at], cos, sin).astype(BF)
        qkv_ref[:, k_at] = rotate(lin_ref[:, k_at], cos, sin).astype(BF)
        qkv_ref[:, v_at] = lin_ref[:, v_at].astype(BF)
    for step in range(length // WIN):
        low, high, allowed = window(step, col_ref, row_ref)
        rows = slice(step * WIN, (step + 1) * WIN)
        for h in range(width // HD):
            q_at, k_at, v_at = (
                slice(i * width + h * HD, i * width + (h + 1) * HD) for i in range(3)
            )
            scores = mm_nt(qkv_ref[rows, q_at], qkv_ref[low:high, k_at]) * HD**-0.5
            scores = jnp.where(allowed, scores, -1e30)
            peak = jnp.max(scores, axis=1, keepdims=True)
            raw = jnp.exp(scores - peak)
            total = jnp.sum(raw, axis=1, keepdims=True)
            probs = (raw * (1.0 / total)).astype(BF)
            context_ref[rows, h * HD : (h + 1) * HD] = mm(probs, qkv_ref[low:high, v_at]).astype(BF)
            lse_ref[rows, h : h + 1] = peak + jnp.log(total)


def attend(shard, both, weights, tables, seg):
    parts = len(weights)
    rows, depth = both.shape
    length = tables[0].shape[0]
    wide = weights[0].shape[1]
    width = wide // 3
    piece = depth // parts
    whole = lambda *shape: pl.BlockSpec(shape, lambda s, z: (0,) * len(shape))
    take = lambda k: pl.BlockSpec((length, piece), lambda s, z: (s, (z[0] + parts - k) % parts))
    by_seq = lambda cols: pl.BlockSpec((length, cols), lambda s, z: (s, 0))
    return pl.pallas_call(
        functools.partial(attend_kernel, parts),
        grid_spec=pltpu.PrefetchScalarGridSpec(
            num_scalar_prefetch=1,
            grid=(rows // length,),
            in_specs=[take(k) for k in range(parts)]
            + [whole(piece, wide)] * parts
            + [whole(length, HD)] * 2
            + [
                pl.BlockSpec((1, length, 1), lambda s, z: (s, 0, 0)),
                pl.BlockSpec((1, 1, length), lambda s, z: (s, 0, 0)),
            ],
            out_specs=[by_seq(width), by_seq(wide), by_seq(width // HD)],
            scratch_shapes=[pltpu.VMEM((length, wide), F32)],
        ),
        out_shape=[
            jax.ShapeDtypeStruct((rows, width), BF),
            jax.ShapeDtypeStruct((rows, wide), BF),
            jax.ShapeDtypeStruct((rows, width // HD), F32),
        ],
        compiler_params=pltpu.CompilerParams(vmem_limit_bytes=40 << 20),
        cost_estimate=pl.CostEstimate(
            flops=2 * rows * depth * wide + 4 * rows * 2 * WIN * width,
            bytes_accessed=2 * (rows * depth + depth * wide + 2 * rows * wide),
            transcendentals=rows * 2 * WIN * width // HD,
        ),
        name="attend",
    )(shard, *[both] * parts, *weights, *tables, *seg)


def attend_back_kernel(
    grad_ref, out_ref, qkv_ref, lse_ref, x_ref, cos_ref, sin_ref, col_ref, row_ref,
    lin_ref, top_ref, bottom_ref, kept_ref, context_ref, keys_ref, values_ref,
):
    length, wide = qkv_ref.shape
    width = wide // 3
    seq = pl.program_id(0)
    tile = min(length, 256)

    @pl.loop(0, length // tile)
    def _(t):
        rows = pl.ds(pl.multiple_of(t * tile, tile), tile)
        context_ref[rows, :] = mm_nt(grad_ref[rows, :], out_ref[...]).astype(BF)

    cos, sin = cos_ref[...], sin_ref[...]
    scale = HD**-0.5
    for h in range(width // HD):
        q_at, k_at, v_at = (slice(i * width + h * HD, i * width + (h + 1) * HD) for i in range(3))
        head = slice(h * HD, (h + 1) * HD)
        keys_ref[...] = jnp.zeros_like(keys_ref)
        values_ref[...] = jnp.zeros_like(values_ref)
        for step in range(length // WIN):
            low, high, allowed = window(step, col_ref, row_ref)
            rows = slice(step * WIN, (step + 1) * WIN)
            queries, keys = qkv_ref[rows, q_at], qkv_ref[low:high, k_at]
            grad = context_ref[rows, head]
            scores = jnp.where(allowed, mm_nt(queries, keys) * scale, -1e30)
            probs = jnp.exp(scores - lse_ref[rows, h : h + 1])
            values_ref[low:high, :] += mm_tn(probs.astype(BF), grad)
            grad_probs = mm_nt(grad, qkv_ref[low:high, v_at])
            inner = jnp.sum(probs * grad_probs, axis=1, keepdims=True)
            grad_scores = (probs * (grad_probs - inner)).astype(BF)
            grad_queries = mm(grad_scores, keys) * scale
            keys_ref[low:high, :] += mm_tn(grad_scores, queries)
            lin_ref[rows, q_at] = rotate(grad_queries, cos[rows], -sin[rows]).astype(BF)
        lin_ref[:, k_at] = rotate(keys_ref[...] * scale, cos, -sin).astype(BF)
        lin_ref[:, v_at] = values_ref[...].astype(BF)
    kept_ref[pl.ds(pl.multiple_of(seq * length, length), length), :] = lin_ref[...]

    @pl.when(seq == pl.num_programs(0) - 1)
    def _():
        half = top_ref.shape[0]
        step = 256
        for n, ref in enumerate((top_ref, bottom_ref)):

            @pl.loop(0, half // step)
            def _(t):
                cols = pl.ds(pl.multiple_of(n * half + t * step, step), step)
                rows = pl.ds(pl.multiple_of(t * step, step), step)
                ref[rows, :] = mm_tn(x_ref[:, cols], kept_ref[...]).astype(BF)


def attend_back(grad, out_w, qkv, lse, both, tables, seg):
    rows, depth = both.shape
    length = tables[0].shape[0]
    wide = qkv.shape[1]
    width = wide // 3
    whole = lambda *shape: pl.BlockSpec(shape, lambda s: (0,) * len(shape))
    by_seq = lambda cols: pl.BlockSpec((length, cols), lambda s: (s, 0))
    return pl.pallas_call(
        attend_back_kernel,
        grid=(rows // length,),
        in_specs=[by_seq(depth), whole(width, depth), by_seq(wide), by_seq(width // HD)]
        + [whole(rows, depth), whole(length, HD), whole(length, HD)]
        + [
            pl.BlockSpec((1, length, 1), lambda s: (s, 0, 0)),
            pl.BlockSpec((1, 1, length), lambda s: (s, 0, 0)),
        ],
        out_specs=[by_seq(wide), whole(depth // 2, wide), whole(depth // 2, wide)],
        scratch_shapes=[
            pltpu.VMEM((rows, wide), BF),
            pltpu.VMEM((length, width), BF),
            pltpu.VMEM((length, HD), F32),
            pltpu.VMEM((length, HD), F32),
        ],
        out_shape=[
            jax.ShapeDtypeStruct((rows, wide), BF),
            jax.ShapeDtypeStruct((depth // 2, wide), BF),
            jax.ShapeDtypeStruct((depth // 2, wide), BF),
        ],
        compiler_params=pltpu.CompilerParams(vmem_limit_bytes=48 << 20),
        cost_estimate=pl.CostEstimate(
            flops=2 * rows * depth * (wide + width) + 10 * rows * 2 * WIN * width,
            bytes_accessed=2 * (2 * rows * depth + depth * (wide + width) + 2 * rows * wide),
            transcendentals=rows * 2 * WIN * width // HD,
        ),
        name="attend_back",
    )(grad, out_w, qkv, lse, both, *tables, *seg)


def normed_back_kernel(blocks, parts, z_ref, *refs):
    lins, weights, (own_ref, other_ref) = refs[:blocks], refs[blocks:-2], refs[-2:]
    piece = own_ref.shape[1] // parts
    own = pl.program_id(0) < pl.num_programs(0) // 2
    for k in range(parts):
        total = mm_nt(lins[0][...], weights[k][...])
        for n in range(1, blocks):
            total += mm_nt(lins[n][...], weights[n * parts + k][...])
        at = pl.multiple_of(((z_ref[0] + parts - k) % parts) * piece, piece)

        @pl.when(own)
        def _():
            own_ref[:, pl.ds(at, piece)] = total

        @pl.when(jnp.logical_not(own))
        def _():
            other_ref[:, pl.ds(at, piece)] = total.astype(BF)


def normed_back(shard, lins, weights, depth):
    parts = len(weights[0])
    rows, wide = lins[0].shape
    tile = min(rows // 2, 256)
    steps = rows // 2 // tile
    flat = [w for block in weights for w in block]
    return pl.pallas_call(
        functools.partial(normed_back_kernel, len(lins), parts),
        grid_spec=pltpu.PrefetchScalarGridSpec(
            num_scalar_prefetch=1,
            grid=(rows // tile,),
            in_specs=[pl.BlockSpec((tile, wide), lambda s, z: (s, 0))] * len(lins)
            + [
                pl.BlockSpec(flat[0].shape, lambda s, z: (0, 0), pipeline_mode=pl.Buffered(1))
            ] * len(flat),
            out_specs=[
                pl.BlockSpec((tile, depth), lambda s, z: (jnp.minimum(s, steps - 1), 0)),
                pl.BlockSpec((tile, depth), lambda s, z: (jnp.maximum(s - steps, 0), 0)),
            ],
        ),
        out_shape=[
            jax.ShapeDtypeStruct((rows // 2, depth), F32),
            jax.ShapeDtypeStruct((rows // 2, depth), BF),
        ],
        compiler_params=pltpu.CompilerParams(vmem_limit_bytes=48 << 20),
        cost_estimate=pl.CostEstimate(
            flops=2 * rows * depth * wide * len(lins),
            bytes_accessed=2 * len(lins) * wide * (rows + depth) + 4 * rows * depth,
            transcendentals=0,
        ),
        name="normed_back",
    )(shard, *lins, *flat)


def plan_slots(route_ids, gate_values):
    hit_mask = route_ids == 0
    hit = jnp.any(hit_mask, axis=-1)
    weight = jnp.sum(jnp.where(hit_mask, gate_values, 0.0), axis=-1)
    ids = jnp.arange(route_ids.shape[0], dtype=jnp.int32)
    earlier = (ids[None, :] < ids[:, None]) & hit[None, :]
    order = jnp.sum(earlier.astype(jnp.int32), axis=1)
    kept = hit & (order < CAP)
    slots = jnp.arange(CAP, dtype=jnp.int32)
    table = (order[None, :] == slots[:, None]) & kept[None, :]
    return table, jnp.where(kept, weight, 0.0)


def norm_back(grad_normed, source, root, gain):
    scaled = grad_normed * gain
    grad_gain = jnp.sum(grad_normed * source * root, axis=0)
    mean = jnp.mean(scaled * source, axis=-1, keepdims=True)
    return grad_gain, root * scaled - source * (root * root * root) * mean


def place_kernel(me_ref, same_ref, other_ref, *out_refs):
    block = jnp.where(pl.program_id(0) % 2 == 0, same_ref[...], other_ref[...]).astype(F32)
    width = out_refs[0].shape[1]
    for i, ref in enumerate(out_refs):
        ref[...] = block[:, i * width : (i + 1) * width]


def place(me, same, other, height, width, columns):
    size, total = lax.axis_size("rep"), same.shape[1]
    spec = pl.BlockSpec((height, total), lambda d, me: (d // 2, 0))
    at = lambda d, me: jnp.bitwise_xor(d, me[0])
    shape = (height, size * width) if columns else (size * height, width)
    count = total // width
    return pl.pallas_call(
        place_kernel,
        grid_spec=pltpu.PrefetchScalarGridSpec(
            num_scalar_prefetch=1,
            grid=(size,),
            in_specs=[spec, spec],
            out_specs=[
                pl.BlockSpec(
                    (height, width),
                    (lambda d, me: (0, at(d, me))) if columns else (lambda d, me: (at(d, me), 0)),
                )
            ] * count,
        ),
        out_shape=[jax.ShapeDtypeStruct(shape, F32)] * count,
        cost_estimate=pl.CostEstimate(
            flops=0, bytes_accessed=8 * size * height * total, transcendentals=0
        ),
        name="place",
    )(me, same, other)


def place_turned_kernel(me_ref, same_ref, other_ref, out_ref):
    odd = me_ref[0] % 2
    first = jnp.where(odd == 0, same_ref[...], other_ref[...])
    second = jnp.where(odd == 0, other_ref[...], same_ref[...])
    out_ref[...] = jnp.concatenate([first, second], axis=0).T.astype(F32)


def place_turned(me, same, other, height):
    size, width = lax.axis_size("rep"), same.shape[1]
    if 2 * height % 128:
        return place(me, same, other, height, width, False)[0].T
    spec = pl.BlockSpec((height, width), lambda j, me: (jnp.bitwise_xor(j, me[0] // 2), 0))
    return pl.pallas_call(
        place_turned_kernel,
        grid_spec=pltpu.PrefetchScalarGridSpec(
            num_scalar_prefetch=1,
            grid=(size // 2,),
            in_specs=[spec, spec],
            out_specs=pl.BlockSpec((width, 2 * height), lambda j, me: (0, j)),
        ),
        out_shape=jax.ShapeDtypeStruct((width, size * height), F32),
        compiler_params=pltpu.CompilerParams(vmem_limit_bytes=32 << 20),
        cost_estimate=pl.CostEstimate(
            flops=0, bytes_accessed=12 * same.size, transcendentals=0
        ),
        name="place_turned",
    )(me, same, other)


def per_device(
    layer_input,
    gain_attn,
    w_query,
    w_key,
    w_value,
    w_out,
    gain_mlp,
    w_gate,
    w_up,
    w_down,
    segments,
    attn_route,
    attn_gate,
    mlp_route,
    mlp_gate,
    cotangent,
):
    length = layer_input.shape[0]
    size, shards = lax.axis_size("rep"), lax.axis_size("shard")
    me = lax.axis_index("rep")
    whoami = me.astype(jnp.int32).reshape(1)
    shard = lax.axis_index("shard").astype(jnp.int32).reshape(1)
    block = w_query.shape[1] // size
    units = w_gate.shape[1] // size
    own = gain_attn.shape[0]
    offsets = chip_offsets()
    staged = len(chip_bits()) == 2

    def columns(weight, d, width):
        return lax.dynamic_slice_in_dim(weight, jnp.bitwise_xor(me, d) * width, width, 1)

    def rows_of(weight, height):
        return lax.dynamic_slice_in_dim(weight, me * height, height, 0)

    def local(d):
        return jnp.concatenate([columns(w, d, block) for w in (w_query, w_key, w_value)], axis=1)

    inputs = layer_input.astype(F32)
    root_one = lax.rsqrt(jnp.mean(inputs * inputs, axis=-1, keepdims=True) + EPSILON)
    tables = rotary_tables(length)
    ring = [(i, (i + 1) % shards) for i in range(shards)]
    piece = local(0)
    qkv_w = {d: [local(d)] for d in offsets}
    flows, context, saved = [], {}, {}
    gain_flow = Flow(vector_gather_steps(jnp.stack([gain_attn, gain_mlp])))
    piece, seg_other, own_gate_up = stage(
        [gain_flow],
        (
            lax.ppermute(piece, "shard", ring),
            swap(segments, 1),
            jnp.concatenate([columns(w_gate, 0, units), columns(w_up, 0, units)], axis=1),
        ),
    )
    gain_one, gain_two = gain_flow.result.astype(F32)
    normed = (inputs * root_one * gain_one).astype(BF)
    seg = jnp.concatenate([segments, seg_other], axis=0)
    seg = (seg[:, :, None], seg[:, None, :])
    other = swap(normed, 1)
    for step in range(1, shards):
        qkv_w[0].append(piece)
        flows.append(Flow(gather_steps(piece, lambda d, b: qkv_w[d].append(b))))
        if step < shards - 1:
            piece, other = stage(flows, (lax.ppermute(piece, "shard", ring), other))
    own_out, own_gate_up, own_down, qkv_w[0][-1] = lax.optimization_barrier(
        (rows_of(w_out, block), own_gate_up, rows_of(w_down, units), qkv_w[0][-1])
    )
    own_out = lax.all_gather(own_out, "shard", axis=1, tiled=True)
    both = jnp.concatenate([normed, other], axis=0)

    def run(d):
        context[d], *saved[d] = attend(shard, both, qkv_w[d], tables, seg)
        return context[d]

    context[0], own_out = stage(flows, (run(0), own_out))
    gate_up = lax.all_gather(own_gate_up, "shard", axis=0, tiled=True)
    down = lax.all_gather(own_down, "shard", axis=1, tiled=True)
    early = offsets[1:2] if staged else []
    early = stage(flows, [run(d) for d in early])
    for flow in flows:
        finish(flow)
    out_flow = Flow(gather_steps(own_out))
    rest = [d for d in offsets if d not in context]
    stage([out_flow], [run(d) for d in rest])
    out_w = finish(out_flow)

    table, mix = plan_slots(mlp_route, mlp_gate)
    pick = table.astype(BF)
    upstream = cotangent.astype(F32)
    slot_weight = jnp.sum(jnp.where(table, mix[None, :], 0.0), axis=1)[:, None]
    slot_grad = (mm(pick, cotangent) * slot_weight).astype(BF)

    all_context = jnp.concatenate([context[d] for d in offsets], axis=1)
    all_out = jnp.concatenate([out_w[d] for d in offsets], axis=0)
    projected = mm(all_context, all_out)
    projected = projected[:length] + swap(projected[length:].astype(BF), 1).astype(F32)
    attn_weight = jnp.sum(jnp.where(attn_route == 0, attn_gate, 0.0), axis=-1)[:, None]
    hidden = inputs + projected * attn_weight
    root_two = lax.rsqrt(jnp.mean(hidden * hidden, axis=-1, keepdims=True) + EPSILON)
    normed_two = (hidden * root_two * gain_two).astype(BF)

    disp_flow = Flow(copies_steps(mm(pick, normed_two).astype(BF), straight_steps))
    slot_grad, gate_up = stage([disp_flow], (slot_grad, gate_up))
    slot_flow = Flow(copies_steps(slot_grad, straight_steps))
    stage([disp_flow])
    dispatched = jnp.concatenate(finish(disp_flow), axis=0)
    act = mm(dispatched, gate_up)
    all_slot_grad = jnp.concatenate(finish(slot_flow), axis=0)
    gate_act, up_act = act[:, :units], act[:, units:]
    sigmoid = jax.nn.sigmoid(gate_act)
    silu = gate_act * sigmoid
    inner = (silu * up_act).astype(BF)
    grad_inner = mm_nt(all_slot_grad, down)
    grad_gate_act = (grad_inner * up_act * sigmoid * (1.0 + gate_act * (1.0 - sigmoid))).astype(BF)
    grad_up_act = (grad_inner * silu).astype(BF)
    grad_act = jnp.concatenate([grad_gate_act, grad_up_act], axis=1)
    back_flow = Flow(plane_sum_steps(mm_nt(grad_act, gate_up).astype(BF)))
    grad_gate = stage([back_flow], mm_tn(grad_gate_act, dispatched).astype(BF))
    expert_flow = Flow(plane_sum_steps(mm(inner, down).astype(BF)))
    grad_up, grad_down = stage(
        [back_flow, expert_flow],
        (mm_tn(grad_up_act, dispatched).astype(BF), mm_tn(inner, all_slot_grad).astype(BF)),
    )
    sums = [
        lax.psum_scatter(g, "shard", scatter_dimension=1, tiled=True)
        for g in (grad_gate, grad_up, grad_down)
    ]
    grad_normed_two = mm_tn(pick, finish(back_flow))
    grad_gain_two, through = norm_back(grad_normed_two, hidden, root_two, gain_two)
    grad_hidden = upstream + through

    grad_projected = (grad_hidden * attn_weight).astype(BF)
    both_grad = jnp.concatenate([grad_projected, swap(grad_projected, 1)], axis=0)
    lins, grad_qkv_w = {}, {}

    def run_back(*ds):
        for d in ds:
            lins[d], *grad_qkv_w[d] = attend_back(
                both_grad, out_w[d], *saved[d], both, tables, seg
            )
        return [(lins[d], grad_qkv_w[d]) for d in ds]

    def keep(ds, values):
        for d, (lin, grad) in zip(ds, values):
            lins[d], grad_qkv_w[d] = lin, grad

    far, near = offsets[-1:], offsets[1:-1]
    values, both_grad = stage([expert_flow], (run_back(*far), both_grad))
    keep(far, values)
    qkv_flow = Flow(scatter_steps(grad_qkv_w))
    values, both_grad = stage([qkv_flow], (run_back(*near), both_grad))
    keep(near, values)
    values, grad_out_w = stage([qkv_flow], (run_back(0), mm_tn(all_context, both_grad).astype(BF)))
    keep([0], values)
    grad_normed = normed_back(
        shard, [lins[d] for d in offsets], [qkv_w[d] for d in offsets], both.shape[1]
    )
    sums[0], sums[1], grad_normed, grad_out_w = stage(
        [qkv_flow], (sums[0], sums[1], grad_normed, grad_out_w)
    )
    own_grad_qkv, sums[2] = lax.optimization_barrier((finish(qkv_flow), sums[2]))
    sum_qkv = lax.psum_scatter(own_grad_qkv, "shard", scatter_dimension=0, tiled=True)

    out_blocks = {d: halves(grad_out_w[i * block : (i + 1) * block]) for i, d in enumerate(offsets)}
    out_flow, gate_flow = Flow(scatter_steps(out_blocks)), Flow(copies_steps(sums[0]))
    other_normed, up_sum = stage(
        [out_flow, gate_flow], (swap(grad_normed[1], 1), sums[1])
    )
    grad_normed = grad_normed[0] + other_normed.astype(F32)
    grad_gain_one, first = norm_back(grad_normed, inputs, root_one, gain_one)
    grad_input = (grad_hidden + first).astype(BF)
    grad_input, gains, up_sum = stage(
        [out_flow, gate_flow],
        (grad_input, jnp.stack([grad_gain_one, grad_gain_two]), up_sum),
    )
    gain_flow, up_flow = Flow(vector_sum_steps(gains)), Flow(copies_steps(up_sum))
    sum_qkv = stage([out_flow, gate_flow, up_flow, gain_flow], sum_qkv)
    sum_out = lax.psum_scatter(finish(out_flow), "shard", scatter_dimension=1, tiled=True)
    qkv_flow = Flow(copies_steps(sum_qkv, straight_steps))
    grad_gate = place_turned(whoami, *finish(gate_flow), units)
    grad_gate, sum_out = stage([up_flow, qkv_flow, gain_flow], (grad_gate, sum_out))
    down_sum, sum_out = lax.optimization_barrier((sums[2], sum_out))
    all_down = lax.all_gather(down_sum, "rep", axis=0, tiled=True)
    out_flow = Flow(copies_steps(sum_out, straight_steps))
    output = (hidden + mm_tn(pick, finish(expert_flow)) * mix[:, None]).astype(BF)
    output = stage([up_flow, qkv_flow, out_flow, gain_flow], output)
    grad_up = place_turned(whoami, *finish(up_flow), units)
    grad_query, grad_key, grad_value = place(whoami, *finish(qkv_flow), own, block, True)
    grad_up, grad_query = stage([out_flow, gain_flow], (grad_up, grad_query))
    (grad_out,) = place(whoami, *finish(out_flow), block, own, False)
    grad_down = all_down.astype(F32)
    gain_grads = finish(gain_flow)
    return (
        output,
        grad_input,
        gain_grads[0],
        grad_query,
        grad_key,
        grad_value,
        grad_out,
        gain_grads[1],
        grad_gate,
        grad_up,
        grad_down,
    )


def solution(mesh):
    tokens = P(("rep", "shard"), None)
    tall, wide, vector = P("shard", None), P(None, "shard"), P("shard")
    weights = (vector, tall, tall, tall, wide, vector, tall, tall, wide)
    return jax.shard_map(
        per_device,
        mesh=mesh,
        in_specs=(tokens, *weights) + (tokens,) * 6,
        out_specs=(tokens, tokens, *weights),
        check_vma=False,
    )
```

```python
import functools

import jax
import jax.numpy as jnp
from jax import lax
from jax.experimental import pallas as pl
from jax.experimental.pallas import tpu as pltpu
from jax.sharding import PartitionSpec as P

HEADS = 16
HD = 128
WIN = 256
CAP = 128
EPSILON = 1e-05
BF = jnp.bfloat16
F32 = jnp.float32


def mm(left, right):
    return jnp.dot(left, right, preferred_element_type=F32)


def mm_nt(left, right):
    return lax.dot_general(left, right, (((1,), (1,)), ((), ())), preferred_element_type=F32)


def mm_tn(left, right):
    return lax.dot_general(left, right, (((0,), (0,)), ((), ())), preferred_element_type=F32)


def swap(value, bit):
    size = lax.axis_size("rep")
    return lax.ppermute(value, "rep", [(i, i ^ bit) for i in range(size)])


def chip_bits():
    size, bits, bit = lax.axis_size("rep"), [], 2
    while bit < size:
        bits.append(bit)
        bit *= 2
    return bits


def chip_offsets():
    return list(range(0, lax.axis_size("rep"), 2))


def add(left, right):
    return left.astype(F32) + right.astype(F32)


def halves(value):
    half = value.shape[0] // 2
    return value[:half], value[half:]


class Flow:
    def __init__(self, steps):
        self.steps, self.result, self.done = steps, None, False
        self.pending = next(steps)

    def advance(self, arrived):
        try:
            self.pending = self.steps.send(arrived)
        except StopIteration as end:
            self.pending, self.result, self.done = [], end.value, True


def stage(flows, extra=()):
    flows = [f for f in flows if not f.done]
    arrived, extra = lax.optimization_barrier(([f.pending for f in flows], extra))
    for flow, values in zip(flows, arrived):
        flow.advance(values)
    return extra


def finish(flow):
    while not flow.done:
        flow.advance(flow.pending)
    return flow.result


def gather_steps(value, sink=lambda offset, block: None):
    bits = chip_bits()
    if len(bits) == 2:
        one, two = bits
        half = value.shape[0] // 2
        by_one, by_two = yield [swap(value, one), swap(value, two)]
        sink(one, by_one)
        sink(two, by_two)
        top, bottom = yield [swap(by_one[:half], two), swap(by_two[half:], one)]
        far = jnp.concatenate([top, bottom], axis=0)
        sink(one ^ two, far)
        return {0: value, one: by_one, two: by_two, one ^ two: far}
    blocks = {0: value}
    for bit in bits:
        old = list(blocks.items())
        new = yield [swap(b, bit) for _, b in old]
        for (d, _), b in zip(old, new):
            blocks[d ^ bit] = b
            sink(d ^ bit, b)
    return blocks


def peers():
    return [1, *[d for d in chip_offsets() if d]]


def greet(others):
    barrier = pltpu.get_barrier_semaphore()
    for device in others.values():
        pl.semaphore_signal(barrier, inc=1, device_id={"rep": device})
    pl.semaphore_wait(barrier, len(others))


def gather_kernel(offsets, in_ref, out_ref, own_sem, send_sem, recv_sem):
    me, rows = lax.axis_index("rep"), in_ref.shape[0]
    others = {d: jnp.bitwise_xor(me, d) for d in offsets}
    spot = {d: pl.ds((d // 2 + d % 2 * len(offsets)) * rows, rows) for d in range(2 * len(offsets))}
    greet(others)
    own = pltpu.make_async_copy(in_ref, out_ref.at[spot[0]], own_sem)
    own.start()

    def send(source, offset, to):
        return pltpu.make_async_remote_copy(
            src_ref=source,
            dst_ref=out_ref.at[spot[offset]],
            send_sem=send_sem.at[offset],
            recv_sem=recv_sem.at[offset],
            device_id={"rep": others[to]},
        )

    chips = [d for d in offsets if d != 1]
    first = {d: send(in_ref, d, d) for d in [*reversed(chips), 1]}
    for copy in first.values():
        copy.start()
    second = {}
    for d in chips:
        first[d].wait_recv()
        second[d] = send(out_ref.at[spot[d]], d + 1, 1)
        second[d].start()
    first[1].wait_recv()
    for copy in second.values():
        copy.wait_recv()
    own.wait()
    for copy in [*first.values(), *second.values()]:
        copy.wait_send()


def gather_rows(value, number):
    rows, width = value.shape
    size = lax.axis_size("rep")
    return pl.pallas_call(
        functools.partial(gather_kernel, peers()),
        out_shape=jax.ShapeDtypeStruct((size * rows, width), value.dtype),
        in_specs=[pl.BlockSpec(memory_space=pltpu.VMEM)],
        out_specs=pl.BlockSpec(memory_space=pltpu.VMEM),
        scratch_shapes=[
            pltpu.SemaphoreType.DMA,
            pltpu.SemaphoreType.DMA((size,)),
            pltpu.SemaphoreType.DMA((size,)),
        ],
        compiler_params=pltpu.CompilerParams(
            collective_id=number, has_side_effects=True, vmem_limit_bytes=16 << 20
        ),
        cost_estimate=pl.CostEstimate(
            flops=0, bytes_accessed=30 * value.size * size, transcendentals=0
        ),
        name="gather_rows",
    )(value)


def reduce_kernel(offsets, in_ref, out_ref, core_ref, held_ref, chip_ref, send_sem, recv_sem):
    me, rows = lax.axis_index("rep"), out_ref.shape[0]
    others = {d: jnp.bitwise_xor(me, d) for d in offsets}
    chips = [0, *[d for d in offsets if d != 1]]
    count = len(chips)
    greet(others)

    def block(ref, i):
        return ref.at[pl.ds(i * rows, rows)]

    def send(source, target, index, to):
        return pltpu.make_async_remote_copy(
            src_ref=source,
            dst_ref=target,
            send_sem=send_sem.at[index],
            recv_sem=recv_sem.at[index],
            device_id={"rep": others[to]},
        )

    order = list(reversed(range(count)))
    core = {i: send(block(in_ref, count + i), block(core_ref, i), i, 1) for i in order}
    for copy in core.values():
        copy.start()
    chip = {}
    for i in order:
        core[i].wait_recv()
        at = pl.ds(i * rows, rows)
        total = in_ref[at, :].astype(F32) + core_ref[at, :].astype(F32)
        held_ref[at, :] = total.astype(BF)
        if i:
            chip[i] = send(block(held_ref, i), block(chip_ref, i), count + i, chips[i])
            chip[i].start()
    total = held_ref[pl.ds(0, rows), :].astype(F32)
    for i in chip:
        chip[i].wait_recv()
        total += chip_ref[pl.ds(i * rows, rows), :].astype(F32)
    out_ref[...] = total.astype(BF)
    for copy in [*core.values(), *chip.values()]:
        copy.wait_send()


def reduce_rows(partial, number):
    size = lax.axis_size("rep")
    rows, width = partial.shape[0] // size, partial.shape[1]
    half = pltpu.VMEM((size // 2 * rows, width), BF)
    return pl.pallas_call(
        functools.partial(reduce_kernel, peers()),
        out_shape=jax.ShapeDtypeStruct((rows, width), BF),
        in_specs=[pl.BlockSpec(memory_space=pltpu.VMEM)],
        out_specs=pl.BlockSpec(memory_space=pltpu.VMEM),
        scratch_shapes=[
            half,
            half,
            half,
            pltpu.SemaphoreType.DMA((size,)),
            pltpu.SemaphoreType.DMA((size,)),
        ],
        compiler_params=pltpu.CompilerParams(
            collective_id=number, has_side_effects=True, vmem_limit_bytes=24 << 20
        ),
        cost_estimate=pl.CostEstimate(
            flops=0, bytes_accessed=30 * partial.size, transcendentals=0
        ),
        name="reduce_rows",
    )(partial)


def jump(value, offset):
    size = lax.axis_size("rep")
    return lax.ppermute(value, "rep", [(i, i ^ offset) for i in range(size)])


def straight_steps(value):
    away = [d for d in chip_offsets() if d]
    new = yield [jump(value, d) for d in away]
    return dict(zip([0, *away], [value, *new]))


def copies_steps(value, gather=gather_steps):
    blocks = yield from gather(value)
    same = jnp.concatenate([blocks[d] for d in chip_offsets()], axis=0)
    (other,) = yield [swap(same, 1)]
    return same, other


def scatter_steps(blocks):
    bits = chip_bits()
    if len(bits) == 2:
        one, two = bits
        far = blocks[one ^ two]
        top, bottom = yield [swap(far[0], one), swap(far[1], two)]
        near_one, near_two = blocks[one], blocks[two]
        one_top, two_bottom = yield [swap(near_one[0], one), swap(near_two[1], two)]
        two_top, one_bottom = yield [
            swap(add(near_two[0], top).astype(BF), two),
            swap(add(near_one[1], bottom).astype(BF), one),
        ]
        return jnp.concatenate(
            [
                (add(blocks[0][0], one_top) + two_top.astype(F32)).astype(BF),
                (add(blocks[0][1], one_bottom) + two_bottom.astype(F32)).astype(BF),
            ],
            axis=0,
        )
    while len(blocks) < len(chip_offsets()):
        yield []
    sums = {d: jnp.concatenate(b, axis=0) for d, b in blocks.items()}
    for bit in reversed(bits):
        kept = [d for d in sorted(sums) if not d & bit]
        new = yield [swap(sums[d | bit], bit) for d in kept]
        sums = {d: add(sums[d], n).astype(BF) for d, n in zip(kept, new)}
    return sums[0]


def plane_sum_steps(partial):
    half = partial.shape[0] // 2
    (other,) = yield [swap(partial[half:], 1)]
    same = add(partial[:half], other).astype(BF)
    offsets = chip_offsets()
    rows = half // len(offsets)
    blocks = {d: same[i * rows : (i + 1) * rows] for i, d in enumerate(offsets)}
    new = yield [jump(blocks[d], d) for d in offsets if d]
    return sum((n.astype(F32) for n in new), blocks[0].astype(F32)).astype(BF)


def vector_sum_steps(rows):
    size, bit = lax.axis_size("rep"), 1
    while bit < size:
        (other,) = yield [swap(rows, bit)]
        rows, bit = rows + other, 2 * bit
    shards, at = lax.axis_size("shard"), lax.axis_index("shard")
    own = rows.shape[1] // shards
    parts = yield [
        lax.ppermute(
            lax.dynamic_slice_in_dim(rows, ((at + k) % shards) * own, own, 1),
            "shard",
            [(i, (i + k) % shards) for i in range(shards)],
        )
        for k in range(1, shards)
    ]
    return lax.dynamic_slice_in_dim(rows, at * own, own, 1) + sum(parts)


def vector_gather_steps(rows):
    size, me = lax.axis_size("shard"), lax.axis_index("shard")
    others = yield [
        lax.ppermute(rows, "shard", [(i, (i - k) % size) for i in range(size)])
        for k in range(1, size)
    ]
    parts = [rows, *others]
    twice = jnp.concatenate(parts + parts, axis=1)
    own = rows.shape[1]
    return lax.dynamic_slice_in_dim(twice, ((size - me) % size) * own, size * own, 1)


def rotary_tables(length):
    half = HD // 2
    positions = jnp.arange(length, dtype=F32)
    inverse = 10000.0 ** (-2.0 * jnp.arange(half, dtype=F32) / HD)
    angles = positions[:, None] * inverse[None, :]
    cos, sin = jnp.cos(angles), jnp.sin(angles)
    return jnp.concatenate([cos, cos], axis=1), jnp.concatenate([-sin, sin], axis=1)


def rotate(values, cos, sin):
    return values * cos + pltpu.roll(values, HD // 2, 1) * sin


def window(step, seg_col, seg_row):
    low, high = max(0, step - 1) * WIN, (step + 1) * WIN
    shape = (WIN, high - low)
    row = lax.broadcasted_iota(jnp.int32, shape, 0) + step * WIN
    col = lax.broadcasted_iota(jnp.int32, shape, 1) + low
    near = (row >= col) & (row - col < WIN)
    same = seg_col[0, step * WIN : (step + 1) * WIN, :] == seg_row[0, :, low:high]
    return low, high, near & same


def attend_kernel(parts, z_ref, *refs):
    x_refs, w_refs = refs[:parts], refs[parts : 2 * parts]
    cos_ref, sin_ref, col_ref, row_ref, context_ref, qkv_ref, lse_ref, lin_ref = refs[2 * parts :]
    length, width = context_ref.shape
    tile = min(length, 256)

    @pl.loop(0, length // tile)
    def _(t):
        rows = pl.ds(pl.multiple_of(t * tile, tile), tile)
        total = mm(x_refs[0][rows, :], w_refs[0][...])
        for x, w in zip(x_refs[1:], w_refs[1:]):
            total += mm(x[rows, :], w[...])
        lin_ref[rows, :] = total

    cos, sin = cos_ref[...], sin_ref[...]
    for h in range(width // HD):
        q_at, k_at, v_at = (slice(i * width + h * HD, i * width + (h + 1) * HD) for i in range(3))
        qkv_ref[:, q_at] = rotate(lin_ref[:, q_at], cos, sin).astype(BF)
        qkv_ref[:, k_at] = rotate(lin_ref[:, k_at], cos, sin).astype(BF)
        qkv_ref[:, v_at] = lin_ref[:, v_at].astype(BF)
    for step in range(length // WIN):
        low, high, allowed = window(step, col_ref, row_ref)
        rows = slice(step * WIN, (step + 1) * WIN)
        for h in range(width // HD):
            q_at, k_at, v_at = (
                slice(i * width + h * HD, i * width + (h + 1) * HD) for i in range(3)
            )
            scores = mm_nt(qkv_ref[rows, q_at], qkv_ref[low:high, k_at]) * HD**-0.5
            scores = jnp.where(allowed, scores, -1e30)
            peak = jnp.max(scores, axis=1, keepdims=True)
            raw = jnp.exp(scores - peak)
            total = jnp.sum(raw, axis=1, keepdims=True)
            probs = (raw * (1.0 / total)).astype(BF)
            context_ref[rows, h * HD : (h + 1) * HD] = mm(probs, qkv_ref[low:high, v_at]).astype(BF)
            lse_ref[rows, h : h + 1] = peak + jnp.log(total)


def attend(shard, both, weights, tables, seg):
    parts = len(weights)
    rows, depth = both.shape
    length = tables[0].shape[0]
    wide = weights[0].shape[1]
    width = wide // 3
    piece = depth // parts
    whole = lambda *shape: pl.BlockSpec(shape, lambda s, z: (0,) * len(shape))
    take = lambda k: pl.BlockSpec((length, piece), lambda s, z: (s, (z[0] + parts - k) % parts))
    by_seq = lambda cols: pl.BlockSpec((length, cols), lambda s, z: (s, 0))
    return pl.pallas_call(
        functools.partial(attend_kernel, parts),
        grid_spec=pltpu.PrefetchScalarGridSpec(
            num_scalar_prefetch=1,
            grid=(rows // length,),
            in_specs=[take(k) for k in range(parts)]
            + [whole(piece, wide)] * parts
            + [whole(length, HD)] * 2
            + [
                pl.BlockSpec((1, length, 1), lambda s, z: (s, 0, 0)),
                pl.BlockSpec((1, 1, length), lambda s, z: (s, 0, 0)),
            ],
            out_specs=[by_seq(width), by_seq(wide), by_seq(width // HD)],
            scratch_shapes=[pltpu.VMEM((length, wide), F32)],
        ),
        out_shape=[
            jax.ShapeDtypeStruct((rows, width), BF),
            jax.ShapeDtypeStruct((rows, wide), BF),
            jax.ShapeDtypeStruct((rows, width // HD), F32),
        ],
        compiler_params=pltpu.CompilerParams(vmem_limit_bytes=40 << 20),
        cost_estimate=pl.CostEstimate(
            flops=2 * rows * depth * wide + 4 * rows * 2 * WIN * width,
            bytes_accessed=2 * (rows * depth + depth * wide + 2 * rows * wide),
            transcendentals=rows * 2 * WIN * width // HD,
        ),
        name="attend",
    )(shard, *[both] * parts, *weights, *tables, *seg)


def attend_back_kernel(
    grad_ref, out_ref, qkv_ref, lse_ref, x_ref, cos_ref, sin_ref, col_ref, row_ref,
    lin_ref, top_ref, bottom_ref, kept_ref, context_ref, keys_ref, values_ref,
):
    length, wide = qkv_ref.shape
    width = wide // 3
    seq = pl.program_id(0)
    tile = min(length, 256)

    @pl.loop(0, length // tile)
    def _(t):
        rows = pl.ds(pl.multiple_of(t * tile, tile), tile)
        context_ref[rows, :] = mm_nt(grad_ref[rows, :], out_ref[...]).astype(BF)

    cos, sin = cos_ref[...], sin_ref[...]
    scale = HD**-0.5
    for h in range(width // HD):
        q_at, k_at, v_at = (slice(i * width + h * HD, i * width + (h + 1) * HD) for i in range(3))
        head = slice(h * HD, (h + 1) * HD)
        keys_ref[...] = jnp.zeros_like(keys_ref)
        values_ref[...] = jnp.zeros_like(values_ref)
        for step in range(length // WIN):
            low, high, allowed = window(step, col_ref, row_ref)
            rows = slice(step * WIN, (step + 1) * WIN)
            queries, keys = qkv_ref[rows, q_at], qkv_ref[low:high, k_at]
            grad = context_ref[rows, head]
            scores = jnp.where(allowed, mm_nt(queries, keys) * scale, -1e30)
            probs = jnp.exp(scores - lse_ref[rows, h : h + 1])
            values_ref[low:high, :] += mm_tn(probs.astype(BF), grad)
            grad_probs = mm_nt(grad, qkv_ref[low:high, v_at])
            inner = jnp.sum(probs * grad_probs, axis=1, keepdims=True)
            grad_scores = (probs * (grad_probs - inner)).astype(BF)
            grad_queries = mm(grad_scores, keys) * scale
            keys_ref[low:high, :] += mm_tn(grad_scores, queries)
            lin_ref[rows, q_at] = rotate(grad_queries, cos[rows], -sin[rows]).astype(BF)
        lin_ref[:, k_at] = rotate(keys_ref[...] * scale, cos, -sin).astype(BF)
        lin_ref[:, v_at] = values_ref[...].astype(BF)
    kept_ref[pl.ds(pl.multiple_of(seq * length, length), length), :] = lin_ref[...]

    @pl.when(seq == pl.num_programs(0) - 1)
    def _():
        half = top_ref.shape[0]
        step = 256
        for n, ref in enumerate((top_ref, bottom_ref)):

            @pl.loop(0, half // step)
            def _(t):
                cols = pl.ds(pl.multiple_of(n * half + t * step, step), step)
                rows = pl.ds(pl.multiple_of(t * step, step), step)
                ref[rows, :] = mm_tn(x_ref[:, cols], kept_ref[...]).astype(BF)


def attend_back(grad, out_w, qkv, lse, both, tables, seg):
    rows, depth = both.shape
    length = tables[0].shape[0]
    wide = qkv.shape[1]
    width = wide // 3
    whole = lambda *shape: pl.BlockSpec(shape, lambda s: (0,) * len(shape))
    by_seq = lambda cols: pl.BlockSpec((length, cols), lambda s: (s, 0))
    return pl.pallas_call(
        attend_back_kernel,
        grid=(rows // length,),
        in_specs=[by_seq(depth), whole(width, depth), by_seq(wide), by_seq(width // HD)]
        + [whole(rows, depth), whole(length, HD), whole(length, HD)]
        + [
            pl.BlockSpec((1, length, 1), lambda s: (s, 0, 0)),
            pl.BlockSpec((1, 1, length), lambda s: (s, 0, 0)),
        ],
        out_specs=[by_seq(wide), whole(depth // 2, wide), whole(depth // 2, wide)],
        scratch_shapes=[
            pltpu.VMEM((rows, wide), BF),
            pltpu.VMEM((length, width), BF),
            pltpu.VMEM((length, HD), F32),
            pltpu.VMEM((length, HD), F32),
        ],
        out_shape=[
            jax.ShapeDtypeStruct((rows, wide), BF),
            jax.ShapeDtypeStruct((depth // 2, wide), BF),
            jax.ShapeDtypeStruct((depth // 2, wide), BF),
        ],
        compiler_params=pltpu.CompilerParams(vmem_limit_bytes=48 << 20),
        cost_estimate=pl.CostEstimate(
            flops=2 * rows * depth * (wide + width) + 10 * rows * 2 * WIN * width,
            bytes_accessed=2 * (2 * rows * depth + depth * (wide + width) + 2 * rows * wide),
            transcendentals=rows * 2 * WIN * width // HD,
        ),
        name="attend_back",
    )(grad, out_w, qkv, lse, both, *tables, *seg)


def normed_back_kernel(blocks, parts, z_ref, *refs):
    lins, weights, (own_ref, other_ref) = refs[:blocks], refs[blocks:-2], refs[-2:]
    piece = own_ref.shape[1] // parts
    own = pl.program_id(0) < pl.num_programs(0) // 2
    for k in range(parts):
        total = mm_nt(lins[0][...], weights[k][...])
        for n in range(1, blocks):
            total += mm_nt(lins[n][...], weights[n * parts + k][...])
        at = pl.multiple_of(((z_ref[0] + parts - k) % parts) * piece, piece)

        @pl.when(own)
        def _():
            own_ref[:, pl.ds(at, piece)] = total

        @pl.when(jnp.logical_not(own))
        def _():
            other_ref[:, pl.ds(at, piece)] = total.astype(BF)


def normed_back(shard, lins, weights, depth):
    parts = len(weights[0])
    rows, wide = lins[0].shape
    tile = min(rows // 2, 256)
    steps = rows // 2 // tile
    flat = [w for block in weights for w in block]
    return pl.pallas_call(
        functools.partial(normed_back_kernel, len(lins), parts),
        grid_spec=pltpu.PrefetchScalarGridSpec(
            num_scalar_prefetch=1,
            grid=(rows // tile,),
            in_specs=[pl.BlockSpec((tile, wide), lambda s, z: (s, 0))] * len(lins)
            + [
                pl.BlockSpec(flat[0].shape, lambda s, z: (0, 0), pipeline_mode=pl.Buffered(1))
            ] * len(flat),
            out_specs=[
                pl.BlockSpec((tile, depth), lambda s, z: (jnp.minimum(s, steps - 1), 0)),
                pl.BlockSpec((tile, depth), lambda s, z: (jnp.maximum(s - steps, 0), 0)),
            ],
        ),
        out_shape=[
            jax.ShapeDtypeStruct((rows // 2, depth), F32),
            jax.ShapeDtypeStruct((rows // 2, depth), BF),
        ],
        compiler_params=pltpu.CompilerParams(vmem_limit_bytes=48 << 20),
        cost_estimate=pl.CostEstimate(
            flops=2 * rows * depth * wide * len(lins),
            bytes_accessed=2 * len(lins) * wide * (rows + depth) + 4 * rows * depth,
            transcendentals=0,
        ),
        name="normed_back",
    )(shard, *lins, *flat)


def plan_slots(route_ids, gate_values):
    hit_mask = route_ids == 0
    hit = jnp.any(hit_mask, axis=-1)
    weight = jnp.sum(jnp.where(hit_mask, gate_values, 0.0), axis=-1)
    ids = jnp.arange(route_ids.shape[0], dtype=jnp.int32)
    earlier = (ids[None, :] < ids[:, None]) & hit[None, :]
    order = jnp.sum(earlier.astype(jnp.int32), axis=1)
    kept = hit & (order < CAP)
    slots = jnp.arange(CAP, dtype=jnp.int32)
    table = (order[None, :] == slots[:, None]) & kept[None, :]
    return table, jnp.where(kept, weight, 0.0)


def norm_back(grad_normed, source, root, gain):
    scaled = grad_normed * gain
    grad_gain = jnp.sum(grad_normed * source * root, axis=0)
    mean = jnp.mean(scaled * source, axis=-1, keepdims=True)
    return grad_gain, root * scaled - source * (root * root * root) * mean


def place_kernel(me_ref, same_ref, other_ref, *out_refs):
    block = jnp.where(pl.program_id(0) % 2 == 0, same_ref[...], other_ref[...]).astype(F32)
    width = out_refs[0].shape[1]
    for i, ref in enumerate(out_refs):
        ref[...] = block[:, i * width : (i + 1) * width]


def place(me, same, other, height, width, columns):
    size, total = lax.axis_size("rep"), same.shape[1]
    spec = pl.BlockSpec((height, total), lambda d, me: (d // 2, 0))
    at = lambda d, me: jnp.bitwise_xor(d, me[0])
    shape = (height, size * width) if columns else (size * height, width)
    count = total // width
    return pl.pallas_call(
        place_kernel,
        grid_spec=pltpu.PrefetchScalarGridSpec(
            num_scalar_prefetch=1,
            grid=(size,),
            in_specs=[spec, spec],
            out_specs=[
                pl.BlockSpec(
                    (height, width),
                    (lambda d, me: (0, at(d, me))) if columns else (lambda d, me: (at(d, me), 0)),
                )
            ] * count,
        ),
        out_shape=[jax.ShapeDtypeStruct(shape, F32)] * count,
        cost_estimate=pl.CostEstimate(
            flops=0, bytes_accessed=8 * size * height * total, transcendentals=0
        ),
        name="place",
    )(me, same, other)


def place_turned_kernel(me_ref, same_ref, other_ref, out_ref):
    odd = me_ref[0] % 2
    first = jnp.where(odd == 0, same_ref[...], other_ref[...])
    second = jnp.where(odd == 0, other_ref[...], same_ref[...])
    out_ref[...] = jnp.concatenate([first, second], axis=0).T.astype(F32)


def place_turned(me, same, other, height):
    size, width = lax.axis_size("rep"), same.shape[1]
    if 2 * height % 128:
        return place(me, same, other, height, width, False)[0].T
    spec = pl.BlockSpec((height, width), lambda j, me: (jnp.bitwise_xor(j, me[0] // 2), 0))
    return pl.pallas_call(
        place_turned_kernel,
        grid_spec=pltpu.PrefetchScalarGridSpec(
            num_scalar_prefetch=1,
            grid=(size // 2,),
            in_specs=[spec, spec],
            out_specs=pl.BlockSpec((width, 2 * height), lambda j, me: (0, j)),
        ),
        out_shape=jax.ShapeDtypeStruct((width, size * height), F32),
        compiler_params=pltpu.CompilerParams(vmem_limit_bytes=32 << 20),
        cost_estimate=pl.CostEstimate(
            flops=0, bytes_accessed=12 * same.size, transcendentals=0
        ),
        name="place_turned",
    )(me, same, other)


def per_device(
    layer_input,
    gain_attn,
    w_query,
    w_key,
    w_value,
    w_out,
    gain_mlp,
    w_gate,
    w_up,
    w_down,
    segments,
    attn_route,
    attn_gate,
    mlp_route,
    mlp_gate,
    cotangent,
):
    length = layer_input.shape[0]
    size, shards = lax.axis_size("rep"), lax.axis_size("shard")
    me = lax.axis_index("rep")
    whoami = me.astype(jnp.int32).reshape(1)
    shard = lax.axis_index("shard").astype(jnp.int32).reshape(1)
    block = w_query.shape[1] // size
    units = w_gate.shape[1] // size
    own = gain_attn.shape[0]
    offsets = chip_offsets()
    staged = len(chip_bits()) == 2

    def columns(weight, d, width):
        return lax.dynamic_slice_in_dim(weight, jnp.bitwise_xor(me, d) * width, width, 1)

    def rows_of(weight, height):
        return lax.dynamic_slice_in_dim(weight, me * height, height, 0)

    def local(d):
        return jnp.concatenate([columns(w, d, block) for w in (w_query, w_key, w_value)], axis=1)

    inputs = layer_input.astype(F32)
    root_one = lax.rsqrt(jnp.mean(inputs * inputs, axis=-1, keepdims=True) + EPSILON)
    tables = rotary_tables(length)
    ring = [(i, (i + 1) % shards) for i in range(shards)]
    piece = local(0)
    qkv_w = {d: [local(d)] for d in offsets}
    flows, context, saved = [], {}, {}
    gain_flow = Flow(vector_gather_steps(jnp.stack([gain_attn, gain_mlp])))
    piece, seg_other, own_gate_up = stage(
        [gain_flow],
        (
            lax.ppermute(piece, "shard", ring),
            swap(segments, 1),
            jnp.concatenate([columns(w_gate, 0, units), columns(w_up, 0, units)], axis=1),
        ),
    )
    gain_one, gain_two = gain_flow.result.astype(F32)
    normed = (inputs * root_one * gain_one).astype(BF)
    seg = jnp.concatenate([segments, seg_other], axis=0)
    seg = (seg[:, :, None], seg[:, None, :])
    other = swap(normed, 1)
    for step in range(1, shards):
        qkv_w[0].append(piece)
        flows.append(Flow(gather_steps(piece, lambda d, b: qkv_w[d].append(b))))
        if step < shards - 1:
            piece, other = stage(flows, (lax.ppermute(piece, "shard", ring), other))
    own_out, own_gate_up, own_down, qkv_w[0][-1] = lax.optimization_barrier(
        (rows_of(w_out, block), own_gate_up, rows_of(w_down, units), qkv_w[0][-1])
    )
    own_out = lax.all_gather(own_out, "shard", axis=1, tiled=True)
    both = jnp.concatenate([normed, other], axis=0)

    def run(d):
        context[d], *saved[d] = attend(shard, both, qkv_w[d], tables, seg)
        return context[d]

    context[0], own_out = stage(flows, (run(0), own_out))
    gate_up = lax.all_gather(own_gate_up, "shard", axis=0, tiled=True)
    down = lax.all_gather(own_down, "shard", axis=1, tiled=True)
    early = offsets[1:2] if staged else []
    early = stage(flows, [run(d) for d in early])
    for flow in flows:
        finish(flow)
    out_flow = Flow(gather_steps(own_out))
    rest = [d for d in offsets if d not in context]
    stage([out_flow], [run(d) for d in rest])
    out_w = finish(out_flow)

    table, mix = plan_slots(mlp_route, mlp_gate)
    pick = table.astype(BF)
    upstream = cotangent.astype(F32)
    slot_weight = jnp.sum(jnp.where(table, mix[None, :], 0.0), axis=1)[:, None]
    slot_grad = (mm(pick, cotangent) * slot_weight).astype(BF)

    all_context = jnp.concatenate([context[d] for d in offsets], axis=1)
    all_out = jnp.concatenate([out_w[d] for d in offsets], axis=0)
    projected = mm(all_context, all_out)
    projected = projected[:length] + swap(projected[length:].astype(BF), 1).astype(F32)
    attn_weight = jnp.sum(jnp.where(attn_route == 0, attn_gate, 0.0), axis=-1)[:, None]
    hidden = inputs + projected * attn_weight
    root_two = lax.rsqrt(jnp.mean(hidden * hidden, axis=-1, keepdims=True) + EPSILON)
    normed_two = (hidden * root_two * gain_two).astype(BF)

    dispatched = gather_rows(mm(pick, normed_two).astype(BF), 0)
    act = mm(dispatched, gate_up)
    slot_grad, act = lax.optimization_barrier((slot_grad, act))
    all_slot_grad = gather_rows(slot_grad, 0)
    gate_act, up_act = act[:, :units], act[:, units:]
    sigmoid = jax.nn.sigmoid(gate_act)
    silu = gate_act * sigmoid
    inner = (silu * up_act).astype(BF)
    grad_inner = mm_nt(all_slot_grad, down)
    grad_gate_act = (grad_inner * up_act * sigmoid * (1.0 + gate_act * (1.0 - sigmoid))).astype(BF)
    grad_up_act = (grad_inner * silu).astype(BF)
    grad_act = jnp.concatenate([grad_gate_act, grad_up_act], axis=1)
    grad_gate, back = lax.optimization_barrier(
        (mm_tn(grad_gate_act, dispatched).astype(BF), mm_nt(grad_act, gate_up).astype(BF))
    )
    grad_disp = reduce_rows(back, 1)
    expert_flow = Flow(plane_sum_steps(mm(inner, down).astype(BF)))
    grad_up, grad_down = (
        mm_tn(grad_up_act, dispatched).astype(BF),
        mm_tn(inner, all_slot_grad).astype(BF),
    )
    grad_normed_two = mm_tn(pick, grad_disp)
    grad_gain_two, through = norm_back(grad_normed_two, hidden, root_two, gain_two)
    grad_hidden = upstream + through

    grad_projected = (grad_hidden * attn_weight).astype(BF)
    both_grad = jnp.concatenate([grad_projected, swap(grad_projected, 1)], axis=0)
    lins, grad_qkv_w = {}, {}

    def run_back(*ds):
        for d in ds:
            lins[d], *grad_qkv_w[d] = attend_back(
                both_grad, out_w[d], *saved[d], both, tables, seg
            )
        return [(lins[d], grad_qkv_w[d]) for d in ds]

    def keep(ds, values):
        for d, (lin, grad) in zip(ds, values):
            lins[d], grad_qkv_w[d] = lin, grad

    far, near = offsets[-1:], offsets[1:-1]
    values, both_grad, grad_up, grad_down = stage(
        [expert_flow], (run_back(*far), both_grad, grad_up, grad_down)
    )
    keep(far, values)
    sums = [
        lax.psum_scatter(g, "shard", scatter_dimension=1, tiled=True)
        for g in (grad_gate, grad_up, grad_down)
    ]
    qkv_flow = Flow(scatter_steps(grad_qkv_w))
    values, both_grad = stage([qkv_flow], (run_back(*near), both_grad))
    keep(near, values)
    values, grad_out_w = stage([qkv_flow], (run_back(0), mm_tn(all_context, both_grad).astype(BF)))
    keep([0], values)
    grad_normed = normed_back(
        shard, [lins[d] for d in offsets], [qkv_w[d] for d in offsets], both.shape[1]
    )
    sums[0], sums[1], grad_normed, grad_out_w = stage(
        [qkv_flow], (sums[0], sums[1], grad_normed, grad_out_w)
    )
    own_grad_qkv, sums[2] = lax.optimization_barrier((finish(qkv_flow), sums[2]))
    sum_qkv = lax.psum_scatter(own_grad_qkv, "shard", scatter_dimension=0, tiled=True)

    out_blocks = {d: halves(grad_out_w[i * block : (i + 1) * block]) for i, d in enumerate(offsets)}
    out_flow, gate_flow = Flow(scatter_steps(out_blocks)), Flow(copies_steps(sums[0]))
    other_normed, up_sum = stage(
        [out_flow, gate_flow], (swap(grad_normed[1], 1), sums[1])
    )
    grad_normed = grad_normed[0] + other_normed.astype(F32)
    grad_gain_one, first = norm_back(grad_normed, inputs, root_one, gain_one)
    grad_input = (grad_hidden + first).astype(BF)
    grad_input, gains, up_sum = stage(
        [out_flow, gate_flow],
        (grad_input, jnp.stack([grad_gain_one, grad_gain_two]), up_sum),
    )
    gain_flow, up_flow = Flow(vector_sum_steps(gains)), Flow(copies_steps(up_sum))
    sum_qkv = stage([out_flow, gate_flow, up_flow, gain_flow], sum_qkv)
    sum_out = lax.psum_scatter(finish(out_flow), "shard", scatter_dimension=1, tiled=True)
    qkv_flow = Flow(copies_steps(sum_qkv, straight_steps))
    grad_gate = place_turned(whoami, *finish(gate_flow), units)
    grad_gate, sum_out = stage([up_flow, qkv_flow, gain_flow], (grad_gate, sum_out))
    down_sum, sum_out = lax.optimization_barrier((sums[2], sum_out))
    all_down = lax.all_gather(down_sum, "rep", axis=0, tiled=True)
    out_flow = Flow(copies_steps(sum_out, straight_steps))
    output = (hidden + mm_tn(pick, finish(expert_flow)) * mix[:, None]).astype(BF)
    output = stage([up_flow, qkv_flow, out_flow, gain_flow], output)
    grad_up = place_turned(whoami, *finish(up_flow), units)
    grad_query, grad_key, grad_value = place(whoami, *finish(qkv_flow), own, block, True)
    grad_up, grad_query = stage([out_flow, gain_flow], (grad_up, grad_query))
    (grad_out,) = place(whoami, *finish(out_flow), block, own, False)
    grad_down = all_down.astype(F32)
    gain_grads = finish(gain_flow)
    return (
        output,
        grad_input,
        gain_grads[0],
        grad_query,
        grad_key,
        grad_value,
        grad_out,
        gain_grads[1],
        grad_gate,
        grad_up,
        grad_down,
    )


def solution(mesh):
    tokens = P(("rep", "shard"), None)
    tall, wide, vector = P("shard", None), P(None, "shard"), P("shard")
    weights = (vector, tall, tall, tall, wide, vector, tall, tall, wide)
    return jax.shard_map(
        per_device,
        mesh=mesh,
        in_specs=(tokens, *weights) + (tokens,) * 6,
        out_specs=(tokens, tokens, *weights),
        check_vma=False,
    )
```

```python
import functools

import jax
import jax.numpy as jnp
from jax import lax
from jax.experimental import pallas as pl
from jax.experimental.pallas import tpu as pltpu
from jax.sharding import PartitionSpec as P

HEADS = 16
HD = 128
WIN = 256
CAP = 128
EPSILON = 1e-05
BF = jnp.bfloat16
F32 = jnp.float32


def mm(left, right):
    return jnp.dot(left, right, preferred_element_type=F32)


def mm_nt(left, right):
    return lax.dot_general(left, right, (((1,), (1,)), ((), ())), preferred_element_type=F32)


def mm_tn(left, right):
    return lax.dot_general(left, right, (((0,), (0,)), ((), ())), preferred_element_type=F32)


def swap(value, bit):
    size = lax.axis_size("rep")
    return lax.ppermute(value, "rep", [(i, i ^ bit) for i in range(size)])


def chip_bits():
    size, bits, bit = lax.axis_size("rep"), [], 2
    while bit < size:
        bits.append(bit)
        bit *= 2
    return bits


def chip_offsets():
    return list(range(0, lax.axis_size("rep"), 2))


def add(left, right):
    return left.astype(F32) + right.astype(F32)


def halves(value):
    half = value.shape[0] // 2
    return value[:half], value[half:]


class Flow:
    def __init__(self, steps):
        self.steps, self.result, self.done = steps, None, False
        self.pending = next(steps)

    def advance(self, arrived):
        try:
            self.pending = self.steps.send(arrived)
        except StopIteration as end:
            self.pending, self.result, self.done = [], end.value, True


def stage(flows, extra=()):
    flows = [f for f in flows if not f.done]
    arrived, extra = lax.optimization_barrier(([f.pending for f in flows], extra))
    for flow, values in zip(flows, arrived):
        flow.advance(values)
    return extra


def finish(flow):
    while not flow.done:
        flow.advance(flow.pending)
    return flow.result


def gather_steps(value, sink=lambda offset, block: None):
    bits = chip_bits()
    if len(bits) == 2:
        one, two = bits
        half = value.shape[0] // 2
        by_one, by_two = yield [swap(value, one), swap(value, two)]
        sink(one, by_one)
        sink(two, by_two)
        top, bottom = yield [swap(by_one[:half], two), swap(by_two[half:], one)]
        far = jnp.concatenate([top, bottom], axis=0)
        sink(one ^ two, far)
        return {0: value, one: by_one, two: by_two, one ^ two: far}
    blocks = {0: value}
    for bit in bits:
        old = list(blocks.items())
        new = yield [swap(b, bit) for _, b in old]
        for (d, _), b in zip(old, new):
            blocks[d ^ bit] = b
            sink(d ^ bit, b)
    return blocks


def peers():
    return [1, *[d for d in chip_offsets() if d]]


def greet(others):
    barrier = pltpu.get_barrier_semaphore()
    for device in others.values():
        pl.semaphore_signal(barrier, inc=1, device_id={"rep": device})
    pl.semaphore_wait(barrier, len(others))


def gather_kernel(offsets, in_ref, out_ref, own_sem, send_sem, recv_sem):
    me, rows = lax.axis_index("rep"), in_ref.shape[0]
    others = {d: jnp.bitwise_xor(me, d) for d in offsets}
    spot = {d: pl.ds((d // 2 + d % 2 * len(offsets)) * rows, rows) for d in range(2 * len(offsets))}
    greet(others)
    own = pltpu.make_async_copy(in_ref, out_ref.at[spot[0]], own_sem)
    own.start()

    def send(source, offset, to):
        return pltpu.make_async_remote_copy(
            src_ref=source,
            dst_ref=out_ref.at[spot[offset]],
            send_sem=send_sem.at[offset],
            recv_sem=recv_sem.at[offset],
            device_id={"rep": others[to]},
        )

    chips = [d for d in offsets if d != 1]
    first = {d: send(in_ref, d, d) for d in [*reversed(chips), 1]}
    for copy in first.values():
        copy.start()
    second = {}
    for d in chips:
        first[d].wait_recv()
        second[d] = send(out_ref.at[spot[d]], d + 1, 1)
        second[d].start()
    first[1].wait_recv()
    for copy in second.values():
        copy.wait_recv()
    own.wait()
    for copy in [*first.values(), *second.values()]:
        copy.wait_send()


def gather_rows(value, number):
    rows, width = value.shape
    size = lax.axis_size("rep")
    return pl.pallas_call(
        functools.partial(gather_kernel, peers()),
        out_shape=jax.ShapeDtypeStruct((size * rows, width), value.dtype),
        in_specs=[pl.BlockSpec(memory_space=pltpu.VMEM)],
        out_specs=pl.BlockSpec(memory_space=pltpu.VMEM),
        scratch_shapes=[
            pltpu.SemaphoreType.DMA,
            pltpu.SemaphoreType.DMA((size,)),
            pltpu.SemaphoreType.DMA((size,)),
        ],
        compiler_params=pltpu.CompilerParams(
            collective_id=number, has_side_effects=True, vmem_limit_bytes=16 << 20
        ),
        cost_estimate=pl.CostEstimate(
            flops=0, bytes_accessed=30 * value.size * size, transcendentals=0
        ),
        name="gather_rows",
    )(value)


def reduce_kernel(offsets, in_ref, out_ref, core_ref, held_ref, chip_ref, send_sem, recv_sem):
    me, rows = lax.axis_index("rep"), out_ref.shape[0]
    others = {d: jnp.bitwise_xor(me, d) for d in offsets}
    chips = [0, *[d for d in offsets if d != 1]]
    count = len(chips)
    greet(others)

    def block(ref, i):
        return ref.at[pl.ds(i * rows, rows)]

    def send(source, target, index, to):
        return pltpu.make_async_remote_copy(
            src_ref=source,
            dst_ref=target,
            send_sem=send_sem.at[index],
            recv_sem=recv_sem.at[index],
            device_id={"rep": others[to]},
        )

    order = list(reversed(range(count)))
    core = {i: send(block(in_ref, count + i), block(core_ref, i), i, 1) for i in order}
    for copy in core.values():
        copy.start()
    chip = {}
    for i in order:
        core[i].wait_recv()
        at = pl.ds(i * rows, rows)
        total = in_ref[at, :].astype(F32) + core_ref[at, :].astype(F32)
        held_ref[at, :] = total.astype(BF)
        if i:
            chip[i] = send(block(held_ref, i), block(chip_ref, i), count + i, chips[i])
            chip[i].start()
    total = held_ref[pl.ds(0, rows), :].astype(F32)
    for i in chip:
        chip[i].wait_recv()
        total += chip_ref[pl.ds(i * rows, rows), :].astype(F32)
    out_ref[...] = total.astype(BF)
    for copy in [*core.values(), *chip.values()]:
        copy.wait_send()


def reduce_rows(partial, number):
    size = lax.axis_size("rep")
    rows, width = partial.shape[0] // size, partial.shape[1]
    half = pltpu.VMEM((size // 2 * rows, width), BF)
    return pl.pallas_call(
        functools.partial(reduce_kernel, peers()),
        out_shape=jax.ShapeDtypeStruct((rows, width), BF),
        in_specs=[pl.BlockSpec(memory_space=pltpu.VMEM)],
        out_specs=pl.BlockSpec(memory_space=pltpu.VMEM),
        scratch_shapes=[
            half,
            half,
            half,
            pltpu.SemaphoreType.DMA((size,)),
            pltpu.SemaphoreType.DMA((size,)),
        ],
        compiler_params=pltpu.CompilerParams(
            collective_id=number, has_side_effects=True, vmem_limit_bytes=24 << 20
        ),
        cost_estimate=pl.CostEstimate(
            flops=0, bytes_accessed=30 * partial.size, transcendentals=0
        ),
        name="reduce_rows",
    )(partial)


def jump(value, offset):
    size = lax.axis_size("rep")
    return lax.ppermute(value, "rep", [(i, i ^ offset) for i in range(size)])


def straight_steps(value):
    away = [d for d in chip_offsets() if d]
    new = yield [jump(value, d) for d in away]
    return dict(zip([0, *away], [value, *new]))


def copies_steps(value, gather=gather_steps):
    blocks = yield from gather(value)
    same = jnp.concatenate([blocks[d] for d in chip_offsets()], axis=0)
    (other,) = yield [swap(same, 1)]
    return same, other


def scatter_steps(blocks):
    bits = chip_bits()
    if len(bits) == 2:
        one, two = bits
        far = blocks[one ^ two]
        top, bottom = yield [swap(far[0], one), swap(far[1], two)]
        near_one, near_two = blocks[one], blocks[two]
        one_top, two_bottom = yield [swap(near_one[0], one), swap(near_two[1], two)]
        two_top, one_bottom = yield [
            swap(add(near_two[0], top).astype(BF), two),
            swap(add(near_one[1], bottom).astype(BF), one),
        ]
        return jnp.concatenate(
            [
                (add(blocks[0][0], one_top) + two_top.astype(F32)).astype(BF),
                (add(blocks[0][1], one_bottom) + two_bottom.astype(F32)).astype(BF),
            ],
            axis=0,
        )
    while len(blocks) < len(chip_offsets()):
        yield []
    sums = {d: jnp.concatenate(b, axis=0) for d, b in blocks.items()}
    for bit in reversed(bits):
        kept = [d for d in sorted(sums) if not d & bit]
        new = yield [swap(sums[d | bit], bit) for d in kept]
        sums = {d: add(sums[d], n).astype(BF) for d, n in zip(kept, new)}
    return sums[0]


def plane_sum_steps(partial):
    half = partial.shape[0] // 2
    (other,) = yield [swap(partial[half:], 1)]
    same = add(partial[:half], other).astype(BF)
    offsets = chip_offsets()
    rows = half // len(offsets)
    blocks = {d: same[i * rows : (i + 1) * rows] for i, d in enumerate(offsets)}
    new = yield [jump(blocks[d], d) for d in offsets if d]
    return sum((n.astype(F32) for n in new), blocks[0].astype(F32)).astype(BF)


def vector_sum_steps(rows):
    size, bit = lax.axis_size("rep"), 1
    while bit < size:
        (other,) = yield [swap(rows, bit)]
        rows, bit = rows + other, 2 * bit
    shards, at = lax.axis_size("shard"), lax.axis_index("shard")
    own = rows.shape[1] // shards
    parts = yield [
        lax.ppermute(
            lax.dynamic_slice_in_dim(rows, ((at + k) % shards) * own, own, 1),
            "shard",
            [(i, (i + k) % shards) for i in range(shards)],
        )
        for k in range(1, shards)
    ]
    return lax.dynamic_slice_in_dim(rows, at * own, own, 1) + sum(parts)


def vector_gather_steps(rows):
    size, me = lax.axis_size("shard"), lax.axis_index("shard")
    others = yield [
        lax.ppermute(rows, "shard", [(i, (i - k) % size) for i in range(size)])
        for k in range(1, size)
    ]
    parts = [rows, *others]
    twice = jnp.concatenate(parts + parts, axis=1)
    own = rows.shape[1]
    return lax.dynamic_slice_in_dim(twice, ((size - me) % size) * own, size * own, 1)


def rotary_tables(length):
    half = HD // 2
    positions = jnp.arange(length, dtype=F32)
    inverse = 10000.0 ** (-2.0 * jnp.arange(half, dtype=F32) / HD)
    angles = positions[:, None] * inverse[None, :]
    cos, sin = jnp.cos(angles), jnp.sin(angles)
    return jnp.concatenate([cos, cos], axis=1), jnp.concatenate([-sin, sin], axis=1)


def rotate(values, cos, sin):
    return values * cos + pltpu.roll(values, HD // 2, 1) * sin


def window(step, seg_col, seg_row):
    low, high = max(0, step - 1) * WIN, (step + 1) * WIN
    shape = (WIN, high - low)
    row = lax.broadcasted_iota(jnp.int32, shape, 0) + step * WIN
    col = lax.broadcasted_iota(jnp.int32, shape, 1) + low
    near = (row >= col) & (row - col < WIN)
    same = seg_col[0, step * WIN : (step + 1) * WIN, :] == seg_row[0, :, low:high]
    return low, high, near & same


def attend_kernel(parts, z_ref, *refs):
    x_refs, w_refs = refs[:parts], refs[parts : 2 * parts]
    cos_ref, sin_ref, col_ref, row_ref, context_ref, qkv_ref, lse_ref, lin_ref = refs[2 * parts :]
    length, width = context_ref.shape
    tile = min(length, 256)

    @pl.loop(0, length // tile)
    def _(t):
        rows = pl.ds(pl.multiple_of(t * tile, tile), tile)
        total = mm(x_refs[0][rows, :], w_refs[0][...])
        for x, w in zip(x_refs[1:], w_refs[1:]):
            total += mm(x[rows, :], w[...])
        lin_ref[rows, :] = total

    cos, sin = cos_ref[...], sin_ref[...]
    for h in range(width // HD):
        q_at, k_at, v_at = (slice(i * width + h * HD, i * width + (h + 1) * HD) for i in range(3))
        qkv_ref[:, q_at] = rotate(lin_ref[:, q_at], cos, sin).astype(BF)
        qkv_ref[:, k_at] = rotate(lin_ref[:, k_at], cos, sin).astype(BF)
        qkv_ref[:, v_at] = lin_ref[:, v_at].astype(BF)
    for step in range(length // WIN):
        low, high, allowed = window(step, col_ref, row_ref)
        rows = slice(step * WIN, (step + 1) * WIN)
        for h in range(width // HD):
            q_at, k_at, v_at = (
                slice(i * width + h * HD, i * width + (h + 1) * HD) for i in range(3)
            )
            scores = mm_nt(qkv_ref[rows, q_at], qkv_ref[low:high, k_at]) * HD**-0.5
            scores = jnp.where(allowed, scores, -1e30)
            peak = jnp.max(scores, axis=1, keepdims=True)
            raw = jnp.exp(scores - peak)
            total = jnp.sum(raw, axis=1, keepdims=True)
            probs = (raw * (1.0 / total)).astype(BF)
            context_ref[rows, h * HD : (h + 1) * HD] = mm(probs, qkv_ref[low:high, v_at]).astype(BF)
            lse_ref[rows, h : h + 1] = peak + jnp.log(total)


def attend(shard, both, weights, tables, seg):
    parts = len(weights)
    rows, depth = both.shape
    length = tables[0].shape[0]
    wide = weights[0].shape[1]
    width = wide // 3
    piece = depth // parts
    whole = lambda *shape: pl.BlockSpec(shape, lambda s, z: (0,) * len(shape))
    take = lambda k: pl.BlockSpec((length, piece), lambda s, z: (s, (z[0] + parts - k) % parts))
    by_seq = lambda cols: pl.BlockSpec((length, cols), lambda s, z: (s, 0))
    return pl.pallas_call(
        functools.partial(attend_kernel, parts),
        grid_spec=pltpu.PrefetchScalarGridSpec(
            num_scalar_prefetch=1,
            grid=(rows // length,),
            in_specs=[take(k) for k in range(parts)]
            + [whole(piece, wide)] * parts
            + [whole(length, HD)] * 2
            + [
                pl.BlockSpec((1, length, 1), lambda s, z: (s, 0, 0)),
                pl.BlockSpec((1, 1, length), lambda s, z: (s, 0, 0)),
            ],
            out_specs=[by_seq(width), by_seq(wide), by_seq(width // HD)],
            scratch_shapes=[pltpu.VMEM((length, wide), F32)],
        ),
        out_shape=[
            jax.ShapeDtypeStruct((rows, width), BF),
            jax.ShapeDtypeStruct((rows, wide), BF),
            jax.ShapeDtypeStruct((rows, width // HD), F32),
        ],
        compiler_params=pltpu.CompilerParams(vmem_limit_bytes=40 << 20),
        cost_estimate=pl.CostEstimate(
            flops=2 * rows * depth * wide + 4 * rows * 2 * WIN * width,
            bytes_accessed=2 * (rows * depth + depth * wide + 2 * rows * wide),
            transcendentals=rows * 2 * WIN * width // HD,
        ),
        name="attend",
    )(shard, *[both] * parts, *weights, *tables, *seg)


def attend_back_kernel(
    grad_ref, out_ref, qkv_ref, lse_ref, x_ref, cos_ref, sin_ref, col_ref, row_ref,
    lin_ref, top_ref, bottom_ref, kept_ref, context_ref, keys_ref, values_ref,
):
    length, wide = qkv_ref.shape
    width = wide // 3
    seq = pl.program_id(0)
    tile = min(length, 256)

    @pl.loop(0, length // tile)
    def _(t):
        rows = pl.ds(pl.multiple_of(t * tile, tile), tile)
        context_ref[rows, :] = mm_nt(grad_ref[rows, :], out_ref[...]).astype(BF)

    cos, sin = cos_ref[...], sin_ref[...]
    scale = HD**-0.5
    for h in range(width // HD):
        q_at, k_at, v_at = (slice(i * width + h * HD, i * width + (h + 1) * HD) for i in range(3))
        head = slice(h * HD, (h + 1) * HD)
        keys_ref[...] = jnp.zeros_like(keys_ref)
        values_ref[...] = jnp.zeros_like(values_ref)
        for step in range(length // WIN):
            low, high, allowed = window(step, col_ref, row_ref)
            rows = slice(step * WIN, (step + 1) * WIN)
            queries, keys = qkv_ref[rows, q_at], qkv_ref[low:high, k_at]
            grad = context_ref[rows, head]
            scores = jnp.where(allowed, mm_nt(queries, keys) * scale, -1e30)
            probs = jnp.exp(scores - lse_ref[rows, h : h + 1])
            values_ref[low:high, :] += mm_tn(probs.astype(BF), grad)
            grad_probs = mm_nt(grad, qkv_ref[low:high, v_at])
            inner = jnp.sum(probs * grad_probs, axis=1, keepdims=True)
            grad_scores = (probs * (grad_probs - inner)).astype(BF)
            grad_queries = mm(grad_scores, keys) * scale
            keys_ref[low:high, :] += mm_tn(grad_scores, queries)
            lin_ref[rows, q_at] = rotate(grad_queries, cos[rows], -sin[rows]).astype(BF)
        lin_ref[:, k_at] = rotate(keys_ref[...] * scale, cos, -sin).astype(BF)
        lin_ref[:, v_at] = values_ref[...].astype(BF)
    kept_ref[pl.ds(pl.multiple_of(seq * length, length), length), :] = lin_ref[...]

    @pl.when(seq == pl.num_programs(0) - 1)
    def _():
        half = top_ref.shape[0]
        step = 256
        for n, ref in enumerate((top_ref, bottom_ref)):

            @pl.loop(0, half // step)
            def _(t):
                cols = pl.ds(pl.multiple_of(n * half + t * step, step), step)
                rows = pl.ds(pl.multiple_of(t * step, step), step)
                ref[rows, :] = mm_tn(x_ref[:, cols], kept_ref[...]).astype(BF)


def attend_back(grad, out_w, qkv, lse, both, tables, seg):
    rows, depth = both.shape
    length = tables[0].shape[0]
    wide = qkv.shape[1]
    width = wide // 3
    whole = lambda *shape: pl.BlockSpec(shape, lambda s: (0,) * len(shape))
    by_seq = lambda cols: pl.BlockSpec((length, cols), lambda s: (s, 0))
    return pl.pallas_call(
        attend_back_kernel,
        grid=(rows // length,),
        in_specs=[by_seq(depth), whole(width, depth), by_seq(wide), by_seq(width // HD)]
        + [whole(rows, depth), whole(length, HD), whole(length, HD)]
        + [
            pl.BlockSpec((1, length, 1), lambda s: (s, 0, 0)),
            pl.BlockSpec((1, 1, length), lambda s: (s, 0, 0)),
        ],
        out_specs=[by_seq(wide), whole(depth // 2, wide), whole(depth // 2, wide)],
        scratch_shapes=[
            pltpu.VMEM((rows, wide), BF),
            pltpu.VMEM((length, width), BF),
            pltpu.VMEM((length, HD), F32),
            pltpu.VMEM((length, HD), F32),
        ],
        out_shape=[
            jax.ShapeDtypeStruct((rows, wide), BF),
            jax.ShapeDtypeStruct((depth // 2, wide), BF),
            jax.ShapeDtypeStruct((depth // 2, wide), BF),
        ],
        compiler_params=pltpu.CompilerParams(vmem_limit_bytes=48 << 20),
        cost_estimate=pl.CostEstimate(
            flops=2 * rows * depth * (wide + width) + 10 * rows * 2 * WIN * width,
            bytes_accessed=2 * (2 * rows * depth + depth * (wide + width) + 2 * rows * wide),
            transcendentals=rows * 2 * WIN * width // HD,
        ),
        name="attend_back",
    )(grad, out_w, qkv, lse, both, *tables, *seg)


def normed_back_kernel(blocks, parts, z_ref, *refs):
    lins, weights, (own_ref, other_ref) = refs[:blocks], refs[blocks:-2], refs[-2:]
    piece = own_ref.shape[1] // parts
    own = pl.program_id(0) < pl.num_programs(0) // 2
    for k in range(parts):
        total = mm_nt(lins[0][...], weights[k][...])
        for n in range(1, blocks):
            total += mm_nt(lins[n][...], weights[n * parts + k][...])
        at = pl.multiple_of(((z_ref[0] + parts - k) % parts) * piece, piece)

        @pl.when(own)
        def _():
            own_ref[:, pl.ds(at, piece)] = total

        @pl.when(jnp.logical_not(own))
        def _():
            other_ref[:, pl.ds(at, piece)] = total.astype(BF)


def normed_back(shard, lins, weights, depth):
    parts = len(weights[0])
    rows, wide = lins[0].shape
    tile = min(rows // 2, 256)
    steps = rows // 2 // tile
    flat = [w for block in weights for w in block]
    return pl.pallas_call(
        functools.partial(normed_back_kernel, len(lins), parts),
        grid_spec=pltpu.PrefetchScalarGridSpec(
            num_scalar_prefetch=1,
            grid=(rows // tile,),
            in_specs=[pl.BlockSpec((tile, wide), lambda s, z: (s, 0))] * len(lins)
            + [
                pl.BlockSpec(flat[0].shape, lambda s, z: (0, 0), pipeline_mode=pl.Buffered(1))
            ] * len(flat),
            out_specs=[
                pl.BlockSpec((tile, depth), lambda s, z: (jnp.minimum(s, steps - 1), 0)),
                pl.BlockSpec((tile, depth), lambda s, z: (jnp.maximum(s - steps, 0), 0)),
            ],
        ),
        out_shape=[
            jax.ShapeDtypeStruct((rows // 2, depth), F32),
            jax.ShapeDtypeStruct((rows // 2, depth), BF),
        ],
        compiler_params=pltpu.CompilerParams(vmem_limit_bytes=48 << 20),
        cost_estimate=pl.CostEstimate(
            flops=2 * rows * depth * wide * len(lins),
            bytes_accessed=2 * len(lins) * wide * (rows + depth) + 4 * rows * depth,
            transcendentals=0,
        ),
        name="normed_back",
    )(shard, *lins, *flat)


def plan_slots(route_ids, gate_values):
    hit_mask = route_ids == 0
    hit = jnp.any(hit_mask, axis=-1)
    weight = jnp.sum(jnp.where(hit_mask, gate_values, 0.0), axis=-1)
    ids = jnp.arange(route_ids.shape[0], dtype=jnp.int32)
    earlier = (ids[None, :] < ids[:, None]) & hit[None, :]
    order = jnp.sum(earlier.astype(jnp.int32), axis=1)
    kept = hit & (order < CAP)
    slots = jnp.arange(CAP, dtype=jnp.int32)
    table = (order[None, :] == slots[:, None]) & kept[None, :]
    return table, jnp.where(kept, weight, 0.0)


def norm_back(grad_normed, source, root, gain):
    scaled = grad_normed * gain
    grad_gain = jnp.sum(grad_normed * source * root, axis=0)
    mean = jnp.mean(scaled * source, axis=-1, keepdims=True)
    return grad_gain, root * scaled - source * (root * root * root) * mean


def place_kernel(me_ref, same_ref, other_ref, *out_refs):
    block = jnp.where(pl.program_id(0) % 2 == 0, same_ref[...], other_ref[...]).astype(F32)
    width = out_refs[0].shape[1]
    for i, ref in enumerate(out_refs):
        ref[...] = block[:, i * width : (i + 1) * width]


def place(me, same, other, height, width, columns):
    size, total = lax.axis_size("rep"), same.shape[1]
    spec = pl.BlockSpec((height, total), lambda d, me: (d // 2, 0))
    at = lambda d, me: jnp.bitwise_xor(d, me[0])
    shape = (height, size * width) if columns else (size * height, width)
    count = total // width
    return pl.pallas_call(
        place_kernel,
        grid_spec=pltpu.PrefetchScalarGridSpec(
            num_scalar_prefetch=1,
            grid=(size,),
            in_specs=[spec, spec],
            out_specs=[
                pl.BlockSpec(
                    (height, width),
                    (lambda d, me: (0, at(d, me))) if columns else (lambda d, me: (at(d, me), 0)),
                )
            ] * count,
        ),
        out_shape=[jax.ShapeDtypeStruct(shape, F32)] * count,
        cost_estimate=pl.CostEstimate(
            flops=0, bytes_accessed=8 * size * height * total, transcendentals=0
        ),
        name="place",
    )(me, same, other)


def place_turned_kernel(me_ref, same_ref, other_ref, out_ref):
    odd = me_ref[0] % 2
    first = jnp.where(odd == 0, same_ref[...], other_ref[...])
    second = jnp.where(odd == 0, other_ref[...], same_ref[...])
    out_ref[...] = jnp.concatenate([first, second], axis=0).T.astype(F32)


def place_turned(me, same, other, height):
    size, width = lax.axis_size("rep"), same.shape[1]
    if 2 * height % 128:
        return place(me, same, other, height, width, False)[0].T
    spec = pl.BlockSpec((height, width), lambda j, me: (jnp.bitwise_xor(j, me[0] // 2), 0))
    return pl.pallas_call(
        place_turned_kernel,
        grid_spec=pltpu.PrefetchScalarGridSpec(
            num_scalar_prefetch=1,
            grid=(size // 2,),
            in_specs=[spec, spec],
            out_specs=pl.BlockSpec((width, 2 * height), lambda j, me: (0, j)),
        ),
        out_shape=jax.ShapeDtypeStruct((width, size * height), F32),
        compiler_params=pltpu.CompilerParams(vmem_limit_bytes=32 << 20),
        cost_estimate=pl.CostEstimate(
            flops=0, bytes_accessed=12 * same.size, transcendentals=0
        ),
        name="place_turned",
    )(me, same, other)


def per_device(
    layer_input,
    gain_attn,
    w_query,
    w_key,
    w_value,
    w_out,
    gain_mlp,
    w_gate,
    w_up,
    w_down,
    segments,
    attn_route,
    attn_gate,
    mlp_route,
    mlp_gate,
    cotangent,
):
    length = layer_input.shape[0]
    size, shards = lax.axis_size("rep"), lax.axis_size("shard")
    me = lax.axis_index("rep")
    whoami = me.astype(jnp.int32).reshape(1)
    shard = lax.axis_index("shard").astype(jnp.int32).reshape(1)
    block = w_query.shape[1] // size
    units = w_gate.shape[1] // size
    own = gain_attn.shape[0]
    offsets = chip_offsets()
    staged = len(chip_bits()) == 2

    def columns(weight, d, width):
        return lax.dynamic_slice_in_dim(weight, jnp.bitwise_xor(me, d) * width, width, 1)

    def rows_of(weight, height):
        return lax.dynamic_slice_in_dim(weight, me * height, height, 0)

    def local(d):
        return jnp.concatenate([columns(w, d, block) for w in (w_query, w_key, w_value)], axis=1)

    inputs = layer_input.astype(F32)
    root_one = lax.rsqrt(jnp.mean(inputs * inputs, axis=-1, keepdims=True) + EPSILON)
    tables = rotary_tables(length)
    ring = [(i, (i + 1) % shards) for i in range(shards)]
    piece = local(0)
    qkv_w = {d: [local(d)] for d in offsets}
    flows, context, saved = [], {}, {}
    gain_flow = Flow(vector_gather_steps(jnp.stack([gain_attn, gain_mlp])))
    piece, seg_other, own_gate_up = stage(
        [gain_flow],
        (
            lax.ppermute(piece, "shard", ring),
            swap(segments, 1),
            jnp.concatenate([columns(w_gate, 0, units), columns(w_up, 0, units)], axis=1),
        ),
    )
    gain_one, gain_two = gain_flow.result.astype(F32)
    normed = (inputs * root_one * gain_one).astype(BF)
    seg = jnp.concatenate([segments, seg_other], axis=0)
    seg = (seg[:, :, None], seg[:, None, :])
    other = swap(normed, 1)
    for step in range(1, shards):
        qkv_w[0].append(piece)
        flows.append(Flow(gather_steps(piece, lambda d, b: qkv_w[d].append(b))))
        if step < shards - 1:
            piece, other = stage(flows, (lax.ppermute(piece, "shard", ring), other))
    own_out, own_gate_up, own_down, qkv_w[0][-1] = lax.optimization_barrier(
        (rows_of(w_out, block), own_gate_up, rows_of(w_down, units), qkv_w[0][-1])
    )
    own_out = lax.all_gather(own_out, "shard", axis=1, tiled=True)
    both = jnp.concatenate([normed, other], axis=0)

    def run(d):
        context[d], *saved[d] = attend(shard, both, qkv_w[d], tables, seg)
        return context[d]

    context[0], own_out = stage(flows, (run(0), own_out))
    gate_up = lax.all_gather(own_gate_up, "shard", axis=0, tiled=True)
    down = lax.all_gather(own_down, "shard", axis=1, tiled=True)
    early = offsets[1:2] if staged else []
    early = stage(flows, [run(d) for d in early])
    for flow in flows:
        finish(flow)
    out_flow = Flow(gather_steps(own_out))
    rest = [d for d in offsets if d not in context]
    stage([out_flow], [run(d) for d in rest])
    out_w = finish(out_flow)

    table, mix = plan_slots(mlp_route, mlp_gate)
    pick = table.astype(BF)
    upstream = cotangent.astype(F32)
    slot_weight = jnp.sum(jnp.where(table, mix[None, :], 0.0), axis=1)[:, None]
    slot_grad = (mm(pick, cotangent) * slot_weight).astype(BF)

    all_context = jnp.concatenate([context[d] for d in offsets], axis=1)
    all_out = jnp.concatenate([out_w[d] for d in offsets], axis=0)
    projected = mm(all_context, all_out)
    projected = projected[:length] + swap(projected[length:].astype(BF), 1).astype(F32)
    attn_weight = jnp.sum(jnp.where(attn_route == 0, attn_gate, 0.0), axis=-1)[:, None]
    hidden = inputs + projected * attn_weight
    root_two = lax.rsqrt(jnp.mean(hidden * hidden, axis=-1, keepdims=True) + EPSILON)
    normed_two = (hidden * root_two * gain_two).astype(BF)

    dispatched = gather_rows(mm(pick, normed_two).astype(BF), 0)
    act = mm(dispatched, gate_up)
    slot_grad, act = lax.optimization_barrier((slot_grad, act))
    all_slot_grad = gather_rows(slot_grad, 0)
    gate_act, up_act = act[:, :units], act[:, units:]
    sigmoid = jax.nn.sigmoid(gate_act)
    silu = gate_act * sigmoid
    inner = (silu * up_act).astype(BF)
    expert_flow = Flow(plane_sum_steps(mm(inner, down).astype(BF)))
    grad_inner = mm_nt(all_slot_grad, down)
    grad_gate_act = (grad_inner * up_act * sigmoid * (1.0 + gate_act * (1.0 - sigmoid))).astype(BF)
    grad_up_act = (grad_inner * silu).astype(BF)
    grad_gate_act, grad_up_act = stage([expert_flow], (grad_gate_act, grad_up_act))
    grad_act = jnp.concatenate([grad_gate_act, grad_up_act], axis=1)
    grad_gate, back = lax.optimization_barrier(
        (mm_tn(grad_gate_act, dispatched).astype(BF), mm_nt(grad_act, gate_up).astype(BF))
    )
    grad_disp, grad_up_act, inner = lax.optimization_barrier(
        (reduce_rows(back, 1), grad_up_act, inner)
    )
    grad_normed_two = mm_tn(pick, grad_disp)
    grad_gain_two, through = norm_back(grad_normed_two, hidden, root_two, gain_two)
    grad_hidden = upstream + through

    grad_projected = (grad_hidden * attn_weight).astype(BF)
    both_grad = jnp.concatenate([grad_projected, swap(grad_projected, 1)], axis=0)
    lins, grad_qkv_w = {}, {}

    def run_back(*ds):
        for d in ds:
            lins[d], *grad_qkv_w[d] = attend_back(
                both_grad, out_w[d], *saved[d], both, tables, seg
            )
        return [(lins[d], grad_qkv_w[d]) for d in ds]

    def keep(ds, values):
        for d, (lin, grad) in zip(ds, values):
            lins[d], grad_qkv_w[d] = lin, grad

    far, near = offsets[-1:], offsets[1:-1]
    values, both_grad, grad_up, inner = stage(
        [expert_flow],
        (run_back(*far), both_grad, mm_tn(grad_up_act, dispatched).astype(BF), inner),
    )
    keep(far, values)
    qkv_flow = Flow(scatter_steps(grad_qkv_w))
    grad_down = mm_tn(inner, all_slot_grad).astype(BF)
    values, both_grad, grad_down, expert_out = stage(
        [qkv_flow], (run_back(*near), both_grad, grad_down, finish(expert_flow))
    )
    keep(near, values)
    sums = [
        lax.psum_scatter(g, "shard", scatter_dimension=1, tiled=True)
        for g in (grad_gate, grad_up, grad_down)
    ]
    output = (hidden + mm_tn(pick, expert_out) * mix[:, None]).astype(BF)
    values, grad_out_w, output = stage(
        [qkv_flow], (run_back(0), mm_tn(all_context, both_grad).astype(BF), output)
    )
    keep([0], values)
    grad_normed = normed_back(
        shard, [lins[d] for d in offsets], [qkv_w[d] for d in offsets], both.shape[1]
    )
    sums[0], sums[1], grad_normed, grad_out_w = stage(
        [qkv_flow], (sums[0], sums[1], grad_normed, grad_out_w)
    )
    own_grad_qkv, sums[2] = lax.optimization_barrier((finish(qkv_flow), sums[2]))
    sum_qkv = lax.psum_scatter(own_grad_qkv, "shard", scatter_dimension=0, tiled=True)

    out_blocks = {d: halves(grad_out_w[i * block : (i + 1) * block]) for i, d in enumerate(offsets)}
    out_flow, gate_flow = Flow(scatter_steps(out_blocks)), Flow(copies_steps(sums[0]))
    other_normed, up_sum = stage(
        [out_flow, gate_flow], (swap(grad_normed[1], 1), sums[1])
    )
    grad_normed = grad_normed[0] + other_normed.astype(F32)
    grad_gain_one, first = norm_back(grad_normed, inputs, root_one, gain_one)
    grad_input = (grad_hidden + first).astype(BF)
    grad_input, gains, up_sum = stage(
        [out_flow, gate_flow],
        (grad_input, jnp.stack([grad_gain_one, grad_gain_two]), up_sum),
    )
    gain_flow, up_flow = Flow(vector_sum_steps(gains)), Flow(copies_steps(up_sum))
    sum_qkv = stage([out_flow, gate_flow, up_flow, gain_flow], sum_qkv)
    sum_out = lax.psum_scatter(finish(out_flow), "shard", scatter_dimension=1, tiled=True)
    qkv_flow = Flow(copies_steps(sum_qkv))
    grad_gate = place_turned(whoami, *finish(gate_flow), units)
    grad_gate, sum_out = stage([up_flow, qkv_flow, gain_flow], (grad_gate, sum_out))
    down_sum, sum_out = lax.optimization_barrier((sums[2], sum_out))
    all_down = lax.all_gather(down_sum, "rep", axis=0, tiled=True)
    out_flow = Flow(copies_steps(sum_out, straight_steps))
    stage([up_flow, qkv_flow, out_flow, gain_flow])
    grad_up = place_turned(whoami, *finish(up_flow), units)
    grad_up = stage([qkv_flow, out_flow, gain_flow], grad_up)
    grad_query, grad_key, grad_value = place(whoami, *finish(qkv_flow), own, block, True)
    (grad_out,) = place(whoami, *finish(out_flow), block, own, False)
    grad_down = all_down.astype(F32)
    gain_grads = finish(gain_flow)
    return (
        output,
        grad_input,
        gain_grads[0],
        grad_query,
        grad_key,
        grad_value,
        grad_out,
        gain_grads[1],
        grad_gate,
        grad_up,
        grad_down,
    )


def solution(mesh):
    tokens = P(("rep", "shard"), None)
    tall, wide, vector = P("shard", None), P(None, "shard"), P("shard")
    weights = (vector, tall, tall, tall, wide, vector, tall, tall, wide)
    return jax.shard_map(
        per_device,
        mesh=mesh,
        in_specs=(tokens, *weights) + (tokens,) * 6,
        out_specs=(tokens, tokens, *weights),
        check_vma=False,
    )
```

```python
import functools

import jax
import jax.numpy as jnp
from jax import lax
from jax.experimental import pallas as pl
from jax.experimental.pallas import tpu as pltpu
from jax.sharding import PartitionSpec as P

HEADS = 16
HD = 128
WIN = 256
CAP = 128
EPSILON = 1e-05
BF = jnp.bfloat16
F32 = jnp.float32


def mm(left, right):
    return jnp.dot(left, right, preferred_element_type=F32)


def mm_nt(left, right):
    return lax.dot_general(left, right, (((1,), (1,)), ((), ())), preferred_element_type=F32)


def mm_tn(left, right):
    return lax.dot_general(left, right, (((0,), (0,)), ((), ())), preferred_element_type=F32)


def swap(value, bit):
    size = lax.axis_size("rep")
    return lax.ppermute(value, "rep", [(i, i ^ bit) for i in range(size)])


def chip_bits():
    size, bits, bit = lax.axis_size("rep"), [], 2
    while bit < size:
        bits.append(bit)
        bit *= 2
    return bits


def chip_offsets():
    return list(range(0, lax.axis_size("rep"), 2))


def add(left, right):
    return left.astype(F32) + right.astype(F32)


def halves(value):
    half = value.shape[0] // 2
    return value[:half], value[half:]


class Flow:
    def __init__(self, steps):
        self.steps, self.result, self.done = steps, None, False
        self.pending = next(steps)

    def advance(self, arrived):
        try:
            self.pending = self.steps.send(arrived)
        except StopIteration as end:
            self.pending, self.result, self.done = [], end.value, True


def stage(flows, extra=()):
    flows = [f for f in flows if not f.done]
    arrived, extra = lax.optimization_barrier(([f.pending for f in flows], extra))
    for flow, values in zip(flows, arrived):
        flow.advance(values)
    return extra


def finish(flow):
    while not flow.done:
        flow.advance(flow.pending)
    return flow.result


def gather_steps(value, sink=lambda offset, block: None):
    bits = chip_bits()
    if len(bits) == 2:
        one, two = bits
        half = value.shape[0] // 2
        by_one, by_two = yield [swap(value, one), swap(value, two)]
        sink(one, by_one)
        sink(two, by_two)
        top, bottom = yield [swap(by_one[:half], two), swap(by_two[half:], one)]
        far = jnp.concatenate([top, bottom], axis=0)
        sink(one ^ two, far)
        return {0: value, one: by_one, two: by_two, one ^ two: far}
    blocks = {0: value}
    for bit in bits:
        old = list(blocks.items())
        new = yield [swap(b, bit) for _, b in old]
        for (d, _), b in zip(old, new):
            blocks[d ^ bit] = b
            sink(d ^ bit, b)
    return blocks


def peers():
    return [1, *[d for d in chip_offsets() if d]]


def greet(others):
    barrier = pltpu.get_barrier_semaphore()
    for device in others.values():
        pl.semaphore_signal(barrier, inc=1, device_id={"rep": device})
    pl.semaphore_wait(barrier, len(others))


def gather_kernel(offsets, in_ref, out_ref, own_sem, send_sem, recv_sem):
    me, rows = lax.axis_index("rep"), in_ref.shape[0]
    others = {d: jnp.bitwise_xor(me, d) for d in offsets}
    spot = {d: pl.ds((d // 2 + d % 2 * len(offsets)) * rows, rows) for d in range(2 * len(offsets))}
    greet(others)
    own = pltpu.make_async_copy(in_ref, out_ref.at[spot[0]], own_sem)
    own.start()

    def send(source, offset, to):
        return pltpu.make_async_remote_copy(
            src_ref=source,
            dst_ref=out_ref.at[spot[offset]],
            send_sem=send_sem.at[offset],
            recv_sem=recv_sem.at[offset],
            device_id={"rep": others[to]},
        )

    chips = [d for d in offsets if d != 1]
    first = {d: send(in_ref, d, d) for d in [*reversed(chips), 1]}
    for copy in first.values():
        copy.start()
    second = {}
    for d in chips:
        first[d].wait_recv()
        second[d] = send(out_ref.at[spot[d]], d + 1, 1)
        second[d].start()
    first[1].wait_recv()
    for copy in second.values():
        copy.wait_recv()
    own.wait()
    for copy in [*first.values(), *second.values()]:
        copy.wait_send()


def gather_rows(value, number):
    rows, width = value.shape
    size = lax.axis_size("rep")
    return pl.pallas_call(
        functools.partial(gather_kernel, peers()),
        out_shape=jax.ShapeDtypeStruct((size * rows, width), value.dtype),
        in_specs=[pl.BlockSpec(memory_space=pltpu.VMEM)],
        out_specs=pl.BlockSpec(memory_space=pltpu.VMEM),
        scratch_shapes=[
            pltpu.SemaphoreType.DMA,
            pltpu.SemaphoreType.DMA((size,)),
            pltpu.SemaphoreType.DMA((size,)),
        ],
        compiler_params=pltpu.CompilerParams(
            collective_id=number, has_side_effects=True, vmem_limit_bytes=16 << 20
        ),
        cost_estimate=pl.CostEstimate(
            flops=0, bytes_accessed=30 * value.size * size, transcendentals=0
        ),
        name="gather_rows",
    )(value)


def reduce_kernel(offsets, in_ref, out_ref, core_ref, held_ref, chip_ref, send_sem, recv_sem):
    me, rows = lax.axis_index("rep"), out_ref.shape[0]
    others = {d: jnp.bitwise_xor(me, d) for d in offsets}
    chips = [0, *[d for d in offsets if d != 1]]
    count = len(chips)
    greet(others)

    def block(ref, i):
        return ref.at[pl.ds(i * rows, rows)]

    def send(source, target, index, to):
        return pltpu.make_async_remote_copy(
            src_ref=source,
            dst_ref=target,
            send_sem=send_sem.at[index],
            recv_sem=recv_sem.at[index],
            device_id={"rep": others[to]},
        )

    order = list(reversed(range(count)))
    core = {i: send(block(in_ref, count + i), block(core_ref, i), i, 1) for i in order}
    for copy in core.values():
        copy.start()
    chip = {}
    for i in order:
        core[i].wait_recv()
        at = pl.ds(i * rows, rows)
        total = in_ref[at, :].astype(F32) + core_ref[at, :].astype(F32)
        held_ref[at, :] = total.astype(BF)
        if i:
            chip[i] = send(block(held_ref, i), block(chip_ref, i), count + i, chips[i])
            chip[i].start()
    total = held_ref[pl.ds(0, rows), :].astype(F32)
    for i in chip:
        chip[i].wait_recv()
        total += chip_ref[pl.ds(i * rows, rows), :].astype(F32)
    out_ref[...] = total.astype(BF)
    for copy in [*core.values(), *chip.values()]:
        copy.wait_send()


def reduce_rows(partial, number):
    size = lax.axis_size("rep")
    rows, width = partial.shape[0] // size, partial.shape[1]
    half = pltpu.VMEM((size // 2 * rows, width), BF)
    return pl.pallas_call(
        functools.partial(reduce_kernel, peers()),
        out_shape=jax.ShapeDtypeStruct((rows, width), BF),
        in_specs=[pl.BlockSpec(memory_space=pltpu.VMEM)],
        out_specs=pl.BlockSpec(memory_space=pltpu.VMEM),
        scratch_shapes=[
            half,
            half,
            half,
            pltpu.SemaphoreType.DMA((size,)),
            pltpu.SemaphoreType.DMA((size,)),
        ],
        compiler_params=pltpu.CompilerParams(
            collective_id=number, has_side_effects=True, vmem_limit_bytes=24 << 20
        ),
        cost_estimate=pl.CostEstimate(
            flops=0, bytes_accessed=30 * partial.size, transcendentals=0
        ),
        name="reduce_rows",
    )(partial)


def jump(value, offset):
    size = lax.axis_size("rep")
    return lax.ppermute(value, "rep", [(i, i ^ offset) for i in range(size)])


def straight_steps(value):
    away = [d for d in chip_offsets() if d]
    new = yield [jump(value, d) for d in away]
    return dict(zip([0, *away], [value, *new]))


def copies_steps(value, gather=gather_steps):
    blocks = yield from gather(value)
    same = jnp.concatenate([blocks[d] for d in chip_offsets()], axis=0)
    (other,) = yield [swap(same, 1)]
    return same, other


def scatter_steps(blocks):
    bits = chip_bits()
    if len(bits) == 2:
        one, two = bits
        far = blocks[one ^ two]
        top, bottom = yield [swap(far[0], one), swap(far[1], two)]
        near_one, near_two = blocks[one], blocks[two]
        one_top, two_bottom = yield [swap(near_one[0], one), swap(near_two[1], two)]
        two_top, one_bottom = yield [
            swap(add(near_two[0], top).astype(BF), two),
            swap(add(near_one[1], bottom).astype(BF), one),
        ]
        return jnp.concatenate(
            [
                (add(blocks[0][0], one_top) + two_top.astype(F32)).astype(BF),
                (add(blocks[0][1], one_bottom) + two_bottom.astype(F32)).astype(BF),
            ],
            axis=0,
        )
    while len(blocks) < len(chip_offsets()):
        yield []
    sums = {d: jnp.concatenate(b, axis=0) for d, b in blocks.items()}
    for bit in reversed(bits):
        kept = [d for d in sorted(sums) if not d & bit]
        new = yield [swap(sums[d | bit], bit) for d in kept]
        sums = {d: add(sums[d], n).astype(BF) for d, n in zip(kept, new)}
    return sums[0]


def plane_sum_steps(partial):
    half = partial.shape[0] // 2
    (other,) = yield [swap(partial[half:], 1)]
    same = add(partial[:half], other).astype(BF)
    offsets = chip_offsets()
    rows = half // len(offsets)
    blocks = {d: same[i * rows : (i + 1) * rows] for i, d in enumerate(offsets)}
    new = yield [jump(blocks[d], d) for d in offsets if d]
    return sum((n.astype(F32) for n in new), blocks[0].astype(F32)).astype(BF)


def vector_sum_steps(rows):
    size, bit = lax.axis_size("rep"), 1
    while bit < size:
        (other,) = yield [swap(rows, bit)]
        rows, bit = rows + other, 2 * bit
    shards, at = lax.axis_size("shard"), lax.axis_index("shard")
    own = rows.shape[1] // shards
    parts = yield [
        lax.ppermute(
            lax.dynamic_slice_in_dim(rows, ((at + k) % shards) * own, own, 1),
            "shard",
            [(i, (i + k) % shards) for i in range(shards)],
        )
        for k in range(1, shards)
    ]
    return lax.dynamic_slice_in_dim(rows, at * own, own, 1) + sum(parts)


def vector_gather_steps(rows):
    size, me = lax.axis_size("shard"), lax.axis_index("shard")
    others = yield [
        lax.ppermute(rows, "shard", [(i, (i - k) % size) for i in range(size)])
        for k in range(1, size)
    ]
    parts = [rows, *others]
    twice = jnp.concatenate(parts + parts, axis=1)
    own = rows.shape[1]
    return lax.dynamic_slice_in_dim(twice, ((size - me) % size) * own, size * own, 1)


def rotary_tables(length):
    half = HD // 2
    positions = jnp.arange(length, dtype=F32)
    inverse = 10000.0 ** (-2.0 * jnp.arange(half, dtype=F32) / HD)
    angles = positions[:, None] * inverse[None, :]
    cos, sin = jnp.cos(angles), jnp.sin(angles)
    return jnp.concatenate([cos, cos], axis=1), jnp.concatenate([-sin, sin], axis=1)


def rotate(values, cos, sin):
    return values * cos + pltpu.roll(values, HD // 2, 1) * sin


def window(step, seg_col, seg_row):
    low, high = max(0, step - 1) * WIN, (step + 1) * WIN
    shape = (WIN, high - low)
    row = lax.broadcasted_iota(jnp.int32, shape, 0) + step * WIN
    col = lax.broadcasted_iota(jnp.int32, shape, 1) + low
    near = (row >= col) & (row - col < WIN)
    same = seg_col[0, step * WIN : (step + 1) * WIN, :] == seg_row[0, :, low:high]
    return low, high, near & same


def attend_kernel(parts, z_ref, *refs):
    x_refs, w_refs = refs[:parts], refs[parts : 2 * parts]
    cos_ref, sin_ref, col_ref, row_ref, context_ref, qkv_ref, lse_ref, lin_ref = refs[2 * parts :]
    length, width = context_ref.shape
    tile = min(length, 256)

    @pl.loop(0, length // tile)
    def _(t):
        rows = pl.ds(pl.multiple_of(t * tile, tile), tile)
        total = mm(x_refs[0][rows, :], w_refs[0][...])
        for x, w in zip(x_refs[1:], w_refs[1:]):
            total += mm(x[rows, :], w[...])
        lin_ref[rows, :] = total

    cos, sin = cos_ref[...], sin_ref[...]
    for h in range(width // HD):
        q_at, k_at, v_at = (slice(i * width + h * HD, i * width + (h + 1) * HD) for i in range(3))
        qkv_ref[:, q_at] = rotate(lin_ref[:, q_at], cos, sin).astype(BF)
        qkv_ref[:, k_at] = rotate(lin_ref[:, k_at], cos, sin).astype(BF)
        qkv_ref[:, v_at] = lin_ref[:, v_at].astype(BF)
    for step in range(length // WIN):
        low, high, allowed = window(step, col_ref, row_ref)
        rows = slice(step * WIN, (step + 1) * WIN)
        for h in range(width // HD):
            q_at, k_at, v_at = (
                slice(i * width + h * HD, i * width + (h + 1) * HD) for i in range(3)
            )
            scores = mm_nt(qkv_ref[rows, q_at], qkv_ref[low:high, k_at]) * HD**-0.5
            scores = jnp.where(allowed, scores, -1e30)
            peak = jnp.max(scores, axis=1, keepdims=True)
            raw = jnp.exp(scores - peak)
            total = jnp.sum(raw, axis=1, keepdims=True)
            probs = (raw * (1.0 / total)).astype(BF)
            context_ref[rows, h * HD : (h + 1) * HD] = mm(probs, qkv_ref[low:high, v_at]).astype(BF)
            lse_ref[rows, h : h + 1] = peak + jnp.log(total)


def attend(shard, both, weights, tables, seg):
    parts = len(weights)
    rows, depth = both.shape
    length = tables[0].shape[0]
    wide = weights[0].shape[1]
    width = wide // 3
    piece = depth // parts
    whole = lambda *shape: pl.BlockSpec(shape, lambda s, z: (0,) * len(shape))
    take = lambda k: pl.BlockSpec((length, piece), lambda s, z: (s, (z[0] + parts - k) % parts))
    by_seq = lambda cols: pl.BlockSpec((length, cols), lambda s, z: (s, 0))
    return pl.pallas_call(
        functools.partial(attend_kernel, parts),
        grid_spec=pltpu.PrefetchScalarGridSpec(
            num_scalar_prefetch=1,
            grid=(rows // length,),
            in_specs=[take(k) for k in range(parts)]
            + [whole(piece, wide)] * parts
            + [whole(length, HD)] * 2
            + [
                pl.BlockSpec((1, length, 1), lambda s, z: (s, 0, 0)),
                pl.BlockSpec((1, 1, length), lambda s, z: (s, 0, 0)),
            ],
            out_specs=[by_seq(width), by_seq(wide), by_seq(width // HD)],
            scratch_shapes=[pltpu.VMEM((length, wide), F32)],
        ),
        out_shape=[
            jax.ShapeDtypeStruct((rows, width), BF),
            jax.ShapeDtypeStruct((rows, wide), BF),
            jax.ShapeDtypeStruct((rows, width // HD), F32),
        ],
        compiler_params=pltpu.CompilerParams(vmem_limit_bytes=40 << 20),
        cost_estimate=pl.CostEstimate(
            flops=2 * rows * depth * wide + 4 * rows * 2 * WIN * width,
            bytes_accessed=2 * (rows * depth + depth * wide + 2 * rows * wide),
            transcendentals=rows * 2 * WIN * width // HD,
        ),
        name="attend",
    )(shard, *[both] * parts, *weights, *tables, *seg)


def attend_back_kernel(
    grad_ref, out_ref, qkv_ref, lse_ref, x_ref, cos_ref, sin_ref, col_ref, row_ref,
    lin_ref, top_ref, bottom_ref, kept_ref, context_ref, keys_ref, values_ref,
):
    length, wide = qkv_ref.shape
    width = wide // 3
    seq = pl.program_id(0)
    tile = min(length, 256)

    @pl.loop(0, length // tile)
    def _(t):
        rows = pl.ds(pl.multiple_of(t * tile, tile), tile)
        context_ref[rows, :] = mm_nt(grad_ref[rows, :], out_ref[...]).astype(BF)

    cos, sin = cos_ref[...], sin_ref[...]
    scale = HD**-0.5
    for h in range(width // HD):
        q_at, k_at, v_at = (slice(i * width + h * HD, i * width + (h + 1) * HD) for i in range(3))
        head = slice(h * HD, (h + 1) * HD)
        keys_ref[...] = jnp.zeros_like(keys_ref)
        values_ref[...] = jnp.zeros_like(values_ref)
        for step in range(length // WIN):
            low, high, allowed = window(step, col_ref, row_ref)
            rows = slice(step * WIN, (step + 1) * WIN)
            queries, keys = qkv_ref[rows, q_at], qkv_ref[low:high, k_at]
            grad = context_ref[rows, head]
            scores = jnp.where(allowed, mm_nt(queries, keys) * scale, -1e30)
            probs = jnp.exp(scores - lse_ref[rows, h : h + 1])
            values_ref[low:high, :] += mm_tn(probs.astype(BF), grad)
            grad_probs = mm_nt(grad, qkv_ref[low:high, v_at])
            inner = jnp.sum(probs * grad_probs, axis=1, keepdims=True)
            grad_scores = (probs * (grad_probs - inner)).astype(BF)
            grad_queries = mm(grad_scores, keys) * scale
            keys_ref[low:high, :] += mm_tn(grad_scores, queries)
            lin_ref[rows, q_at] = rotate(grad_queries, cos[rows], -sin[rows]).astype(BF)
        lin_ref[:, k_at] = rotate(keys_ref[...] * scale, cos, -sin).astype(BF)
        lin_ref[:, v_at] = values_ref[...].astype(BF)
    kept_ref[pl.ds(pl.multiple_of(seq * length, length), length), :] = lin_ref[...]

    @pl.when(seq == pl.num_programs(0) - 1)
    def _():
        half = top_ref.shape[0]
        step = 256
        for n, ref in enumerate((top_ref, bottom_ref)):

            @pl.loop(0, half // step)
            def _(t):
                cols = pl.ds(pl.multiple_of(n * half + t * step, step), step)
                rows = pl.ds(pl.multiple_of(t * step, step), step)
                ref[rows, :] = mm_tn(x_ref[:, cols], kept_ref[...]).astype(BF)


def attend_back(grad, out_w, qkv, lse, both, tables, seg):
    rows, depth = both.shape
    length = tables[0].shape[0]
    wide = qkv.shape[1]
    width = wide // 3
    whole = lambda *shape: pl.BlockSpec(shape, lambda s: (0,) * len(shape))
    by_seq = lambda cols: pl.BlockSpec((length, cols), lambda s: (s, 0))
    return pl.pallas_call(
        attend_back_kernel,
        grid=(rows // length,),
        in_specs=[by_seq(depth), whole(width, depth), by_seq(wide), by_seq(width // HD)]
        + [whole(rows, depth), whole(length, HD), whole(length, HD)]
        + [
            pl.BlockSpec((1, length, 1), lambda s: (s, 0, 0)),
            pl.BlockSpec((1, 1, length), lambda s: (s, 0, 0)),
        ],
        out_specs=[by_seq(wide), whole(depth // 2, wide), whole(depth // 2, wide)],
        scratch_shapes=[
            pltpu.VMEM((rows, wide), BF),
            pltpu.VMEM((length, width), BF),
            pltpu.VMEM((length, HD), F32),
            pltpu.VMEM((length, HD), F32),
        ],
        out_shape=[
            jax.ShapeDtypeStruct((rows, wide), BF),
            jax.ShapeDtypeStruct((depth // 2, wide), BF),
            jax.ShapeDtypeStruct((depth // 2, wide), BF),
        ],
        compiler_params=pltpu.CompilerParams(vmem_limit_bytes=48 << 20),
        cost_estimate=pl.CostEstimate(
            flops=2 * rows * depth * (wide + width) + 10 * rows * 2 * WIN * width,
            bytes_accessed=2 * (2 * rows * depth + depth * (wide + width) + 2 * rows * wide),
            transcendentals=rows * 2 * WIN * width // HD,
        ),
        name="attend_back",
    )(grad, out_w, qkv, lse, both, *tables, *seg)


def normed_back_kernel(blocks, parts, z_ref, *refs):
    lins, weights, (own_ref, other_ref) = refs[:blocks], refs[blocks:-2], refs[-2:]
    piece = own_ref.shape[1] // parts
    own = pl.program_id(0) < pl.num_programs(0) // 2
    for k in range(parts):
        total = mm_nt(lins[0][...], weights[k][...])
        for n in range(1, blocks):
            total += mm_nt(lins[n][...], weights[n * parts + k][...])
        at = pl.multiple_of(((z_ref[0] + parts - k) % parts) * piece, piece)

        @pl.when(own)
        def _():
            own_ref[:, pl.ds(at, piece)] = total

        @pl.when(jnp.logical_not(own))
        def _():
            other_ref[:, pl.ds(at, piece)] = total.astype(BF)


def normed_back(shard, lins, weights, depth):
    parts = len(weights[0])
    rows, wide = lins[0].shape
    tile = min(rows // 2, 256)
    steps = rows // 2 // tile
    flat = [w for block in weights for w in block]
    return pl.pallas_call(
        functools.partial(normed_back_kernel, len(lins), parts),
        grid_spec=pltpu.PrefetchScalarGridSpec(
            num_scalar_prefetch=1,
            grid=(rows // tile,),
            in_specs=[pl.BlockSpec((tile, wide), lambda s, z: (s, 0))] * len(lins)
            + [
                pl.BlockSpec(flat[0].shape, lambda s, z: (0, 0), pipeline_mode=pl.Buffered(1))
            ] * len(flat),
            out_specs=[
                pl.BlockSpec((tile, depth), lambda s, z: (jnp.minimum(s, steps - 1), 0)),
                pl.BlockSpec((tile, depth), lambda s, z: (jnp.maximum(s - steps, 0), 0)),
            ],
        ),
        out_shape=[
            jax.ShapeDtypeStruct((rows // 2, depth), F32),
            jax.ShapeDtypeStruct((rows // 2, depth), BF),
        ],
        compiler_params=pltpu.CompilerParams(vmem_limit_bytes=48 << 20),
        cost_estimate=pl.CostEstimate(
            flops=2 * rows * depth * wide * len(lins),
            bytes_accessed=2 * len(lins) * wide * (rows + depth) + 4 * rows * depth,
            transcendentals=0,
        ),
        name="normed_back",
    )(shard, *lins, *flat)


def plan_slots(route_ids, gate_values):
    hit_mask = route_ids == 0
    hit = jnp.any(hit_mask, axis=-1)
    weight = jnp.sum(jnp.where(hit_mask, gate_values, 0.0), axis=-1)
    ids = jnp.arange(route_ids.shape[0], dtype=jnp.int32)
    earlier = (ids[None, :] < ids[:, None]) & hit[None, :]
    order = jnp.sum(earlier.astype(jnp.int32), axis=1)
    kept = hit & (order < CAP)
    slots = jnp.arange(CAP, dtype=jnp.int32)
    table = (order[None, :] == slots[:, None]) & kept[None, :]
    return table, jnp.where(kept, weight, 0.0)


def norm_back(grad_normed, source, root, gain):
    scaled = grad_normed * gain
    grad_gain = jnp.sum(grad_normed * source * root, axis=0)
    mean = jnp.mean(scaled * source, axis=-1, keepdims=True)
    return grad_gain, root * scaled - source * (root * root * root) * mean


def place_kernel(me_ref, same_ref, other_ref, *out_refs):
    block = jnp.where(pl.program_id(0) % 2 == 0, same_ref[...], other_ref[...]).astype(F32)
    width = out_refs[0].shape[1]
    for i, ref in enumerate(out_refs):
        ref[...] = block[:, i * width : (i + 1) * width]


def place(me, same, other, height, width, columns):
    size, total = lax.axis_size("rep"), same.shape[1]
    spec = pl.BlockSpec((height, total), lambda d, me: (d // 2, 0))
    at = lambda d, me: jnp.bitwise_xor(d, me[0])
    shape = (height, size * width) if columns else (size * height, width)
    count = total // width
    return pl.pallas_call(
        place_kernel,
        grid_spec=pltpu.PrefetchScalarGridSpec(
            num_scalar_prefetch=1,
            grid=(size,),
            in_specs=[spec, spec],
            out_specs=[
                pl.BlockSpec(
                    (height, width),
                    (lambda d, me: (0, at(d, me))) if columns else (lambda d, me: (at(d, me), 0)),
                )
            ] * count,
        ),
        out_shape=[jax.ShapeDtypeStruct(shape, F32)] * count,
        cost_estimate=pl.CostEstimate(
            flops=0, bytes_accessed=8 * size * height * total, transcendentals=0
        ),
        name="place",
    )(me, same, other)


def place_turned_kernel(me_ref, same_ref, other_ref, out_ref):
    odd = me_ref[0] % 2
    first = jnp.where(odd == 0, same_ref[...], other_ref[...])
    second = jnp.where(odd == 0, other_ref[...], same_ref[...])
    out_ref[...] = jnp.concatenate([first, second], axis=0).T.astype(F32)


def place_turned(me, same, other, height):
    size, width = lax.axis_size("rep"), same.shape[1]
    if 2 * height % 128:
        return place(me, same, other, height, width, False)[0].T
    spec = pl.BlockSpec((height, width), lambda j, me: (jnp.bitwise_xor(j, me[0] // 2), 0))
    return pl.pallas_call(
        place_turned_kernel,
        grid_spec=pltpu.PrefetchScalarGridSpec(
            num_scalar_prefetch=1,
            grid=(size // 2,),
            in_specs=[spec, spec],
            out_specs=pl.BlockSpec((width, 2 * height), lambda j, me: (0, j)),
        ),
        out_shape=jax.ShapeDtypeStruct((width, size * height), F32),
        compiler_params=pltpu.CompilerParams(vmem_limit_bytes=32 << 20),
        cost_estimate=pl.CostEstimate(
            flops=0, bytes_accessed=12 * same.size, transcendentals=0
        ),
        name="place_turned",
    )(me, same, other)


def per_device(
    layer_input,
    gain_attn,
    w_query,
    w_key,
    w_value,
    w_out,
    gain_mlp,
    w_gate,
    w_up,
    w_down,
    segments,
    attn_route,
    attn_gate,
    mlp_route,
    mlp_gate,
    cotangent,
):
    length = layer_input.shape[0]
    size, shards = lax.axis_size("rep"), lax.axis_size("shard")
    me = lax.axis_index("rep")
    whoami = me.astype(jnp.int32).reshape(1)
    shard = lax.axis_index("shard").astype(jnp.int32).reshape(1)
    block = w_query.shape[1] // size
    units = w_gate.shape[1] // size
    own = gain_attn.shape[0]
    offsets = chip_offsets()
    staged = len(chip_bits()) == 2

    def columns(weight, d, width):
        return lax.dynamic_slice_in_dim(weight, jnp.bitwise_xor(me, d) * width, width, 1)

    def rows_of(weight, height):
        return lax.dynamic_slice_in_dim(weight, me * height, height, 0)

    def local(d):
        return jnp.concatenate([columns(w, d, block) for w in (w_query, w_key, w_value)], axis=1)

    table, mix = plan_slots(mlp_route, mlp_gate)
    pick = table.astype(BF)
    upstream = cotangent.astype(F32)
    slot_weight = jnp.sum(jnp.where(table, mix[None, :], 0.0), axis=1)[:, None]
    slot_grad = (mm(pick, cotangent) * slot_weight).astype(BF)

    inputs = layer_input.astype(F32)
    root_one = lax.rsqrt(jnp.mean(inputs * inputs, axis=-1, keepdims=True) + EPSILON)
    tables = rotary_tables(length)
    ring = [(i, (i + 1) % shards) for i in range(shards)]
    piece = local(0)
    qkv_w = {d: [local(d)] for d in offsets}
    flows, context, saved = [], {}, {}
    gain_flow = Flow(vector_gather_steps(jnp.stack([gain_attn, gain_mlp])))
    slot_flow = Flow(copies_steps(slot_grad, straight_steps))
    piece, seg_other, own_gate_up = stage(
        [gain_flow, slot_flow],
        (
            lax.ppermute(piece, "shard", ring),
            swap(segments, 1),
            jnp.concatenate([columns(w_gate, 0, units), columns(w_up, 0, units)], axis=1),
        ),
    )
    gain_one, gain_two = gain_flow.result.astype(F32)
    normed = (inputs * root_one * gain_one).astype(BF)
    seg = jnp.concatenate([segments, seg_other], axis=0)
    seg = (seg[:, :, None], seg[:, None, :])
    other = swap(normed, 1)
    own_out, piece = lax.optimization_barrier((rows_of(w_out, block), piece))
    own_out = lax.all_gather(own_out, "shard", axis=1, tiled=True)
    for step in range(1, shards):
        qkv_w[0].append(piece)
        flows.append(Flow(gather_steps(piece, lambda d, b: qkv_w[d].append(b))))
        if step < shards - 1:
            extra = (lax.ppermute(piece, "shard", ring), other)
            if step == shards - 2:
                extra = (*extra, own_out)
            piece, other, *rest = stage([*flows, slot_flow], extra)
            own_out = rest[0] if rest else own_out
    own_gate_up, own_down, qkv_w[0][-1] = lax.optimization_barrier(
        (own_gate_up, rows_of(w_down, units), qkv_w[0][-1])
    )
    both = jnp.concatenate([normed, other], axis=0)

    def run(d):
        context[d], *saved[d] = attend(shard, both, qkv_w[d], tables, seg)
        return context[d]

    context[0], own_out = stage(flows, (run(0), own_out))
    gate_up = lax.all_gather(own_gate_up, "shard", axis=0, tiled=True)
    down = lax.all_gather(own_down, "shard", axis=1, tiled=True)
    early = offsets[1:2] if staged else []
    early = stage(flows, [run(d) for d in early])
    for flow in flows:
        finish(flow)
    out_flow = Flow(gather_steps(own_out))
    rest = [d for d in offsets if d not in context]
    stage([out_flow], [run(d) for d in rest])
    out_w = finish(out_flow)

    all_context = jnp.concatenate([context[d] for d in offsets], axis=1)
    all_out = jnp.concatenate([out_w[d] for d in offsets], axis=0)
    projected = mm(all_context, all_out)
    projected = projected[:length] + swap(projected[length:].astype(BF), 1).astype(F32)
    attn_weight = jnp.sum(jnp.where(attn_route == 0, attn_gate, 0.0), axis=-1)[:, None]
    hidden = inputs + projected * attn_weight
    root_two = lax.rsqrt(jnp.mean(hidden * hidden, axis=-1, keepdims=True) + EPSILON)
    normed_two = (hidden * root_two * gain_two).astype(BF)

    dispatched = gather_rows(mm(pick, normed_two).astype(BF), 0)
    act = mm(dispatched, gate_up)
    all_slot_grad = jnp.concatenate(finish(slot_flow), axis=0)
    gate_act, up_act = act[:, :units], act[:, units:]
    sigmoid = jax.nn.sigmoid(gate_act)
    silu = gate_act * sigmoid
    inner = (silu * up_act).astype(BF)
    expert_flow = Flow(plane_sum_steps(mm(inner, down).astype(BF)))
    grad_inner = mm_nt(all_slot_grad, down)
    grad_gate_act = (grad_inner * up_act * sigmoid * (1.0 + gate_act * (1.0 - sigmoid))).astype(BF)
    grad_up_act = (grad_inner * silu).astype(BF)
    grad_gate_act, grad_up_act = stage([expert_flow], (grad_gate_act, grad_up_act))
    grad_act = jnp.concatenate([grad_gate_act, grad_up_act], axis=1)
    grad_gate, back = lax.optimization_barrier(
        (mm_tn(grad_gate_act, dispatched).astype(BF), mm_nt(grad_act, gate_up).astype(BF))
    )
    grad_disp, grad_up_act, inner = lax.optimization_barrier(
        (reduce_rows(back, 1), grad_up_act, inner)
    )
    grad_normed_two = mm_tn(pick, grad_disp)
    grad_gain_two, through = norm_back(grad_normed_two, hidden, root_two, gain_two)
    grad_hidden = upstream + through

    grad_projected = (grad_hidden * attn_weight).astype(BF)
    both_grad = jnp.concatenate([grad_projected, swap(grad_projected, 1)], axis=0)
    lins, grad_qkv_w = {}, {}

    def run_back(*ds):
        for d in ds:
            lins[d], *grad_qkv_w[d] = attend_back(
                both_grad, out_w[d], *saved[d], both, tables, seg
            )
        return [(lins[d], grad_qkv_w[d]) for d in ds]

    def keep(ds, values):
        for d, (lin, grad) in zip(ds, values):
            lins[d], grad_qkv_w[d] = lin, grad

    far, near = offsets[-1:], offsets[1:-1]
    values, both_grad, grad_up, inner = stage(
        [expert_flow],
        (run_back(*far), both_grad, mm_tn(grad_up_act, dispatched).astype(BF), inner),
    )
    keep(far, values)
    qkv_flow = Flow(scatter_steps(grad_qkv_w))
    grad_down = mm_tn(inner, all_slot_grad).astype(BF)
    values, both_grad, grad_down, expert_out = stage(
        [qkv_flow], (run_back(*near), both_grad, grad_down, finish(expert_flow))
    )
    keep(near, values)
    sums = [
        lax.psum_scatter(g, "shard", scatter_dimension=1, tiled=True)
        for g in (grad_gate, grad_up, grad_down)
    ]
    output = (hidden + mm_tn(pick, expert_out) * mix[:, None]).astype(BF)
    values, grad_out_w, output = stage(
        [qkv_flow], (run_back(0), mm_tn(all_context, both_grad).astype(BF), output)
    )
    keep([0], values)
    grad_normed = normed_back(
        shard, [lins[d] for d in offsets], [qkv_w[d] for d in offsets], both.shape[1]
    )
    sums[0], sums[1], grad_normed, grad_out_w = stage(
        [qkv_flow], (sums[0], sums[1], grad_normed, grad_out_w)
    )
    own_grad_qkv, sums[2] = lax.optimization_barrier((finish(qkv_flow), sums[2]))
    sum_qkv = lax.psum_scatter(own_grad_qkv, "shard", scatter_dimension=0, tiled=True)

    out_blocks = {d: halves(grad_out_w[i * block : (i + 1) * block]) for i, d in enumerate(offsets)}
    out_flow, gate_flow = Flow(scatter_steps(out_blocks)), Flow(copies_steps(sums[0]))
    other_normed, up_sum = stage([out_flow], (swap(grad_normed[1], 1), sums[1]))
    grad_normed = grad_normed[0] + other_normed.astype(F32)
    grad_gain_one, first = norm_back(grad_normed, inputs, root_one, gain_one)
    grad_input = (grad_hidden + first).astype(BF)
    grad_input, gains = stage(
        [out_flow, gate_flow], (grad_input, jnp.stack([grad_gain_one, grad_gain_two]))
    )
    gain_flow, up_flow = Flow(vector_sum_steps(gains)), Flow(copies_steps(up_sum))
    stage([out_flow, gate_flow, gain_flow])
    own_grad_out, sum_qkv = lax.optimization_barrier((finish(out_flow), sum_qkv))
    sum_out = lax.psum_scatter(own_grad_out, "shard", scatter_dimension=1, tiled=True)
    qkv_flow = Flow(copies_steps(sum_qkv))
    sum_out = stage([gate_flow, up_flow, gain_flow], sum_out)
    grad_gate = place_turned(whoami, *finish(gate_flow), units)
    down_sum, sum_out = lax.optimization_barrier((sums[2], sum_out))
    all_down = lax.all_gather(down_sum, "rep", axis=0, tiled=True)
    out_flow = Flow(copies_steps(sum_out, straight_steps))
    grad_gate = stage([up_flow, qkv_flow, gain_flow], grad_gate)
    stage([up_flow, qkv_flow, out_flow])
    grad_up = place_turned(whoami, *finish(up_flow), units)
    grad_up = stage([qkv_flow, out_flow, gain_flow], grad_up)
    grad_query, grad_key, grad_value = place(whoami, *finish(qkv_flow), own, block, True)
    (grad_out,) = place(whoami, *finish(out_flow), block, own, False)
    grad_down = all_down.astype(F32)
    gain_grads = finish(gain_flow)
    return (
        output,
        grad_input,
        gain_grads[0],
        grad_query,
        grad_key,
        grad_value,
        grad_out,
        gain_grads[1],
        grad_gate,
        grad_up,
        grad_down,
    )


def solution(mesh):
    tokens = P(("rep", "shard"), None)
    tall, wide, vector = P("shard", None), P(None, "shard"), P("shard")
    weights = (vector, tall, tall, tall, wide, vector, tall, tall, wide)
    return jax.shard_map(
        per_device,
        mesh=mesh,
        in_specs=(tokens, *weights) + (tokens,) * 6,
        out_specs=(tokens, tokens, *weights),
        check_vma=False,
    )
```

```python
import functools

import jax
import jax.numpy as jnp
from jax import lax
from jax.experimental import pallas as pl
from jax.experimental.pallas import tpu as pltpu
from jax.sharding import PartitionSpec as P

HEADS = 16
HD = 128
WIN = 256
CAP = 128
EPSILON = 1e-05
BF = jnp.bfloat16
F32 = jnp.float32


def mm(left, right):
    return jnp.dot(left, right, preferred_element_type=F32)


def mm_nt(left, right):
    return lax.dot_general(left, right, (((1,), (1,)), ((), ())), preferred_element_type=F32)


def mm_tn(left, right):
    return lax.dot_general(left, right, (((0,), (0,)), ((), ())), preferred_element_type=F32)


def swap(value, bit):
    size = lax.axis_size("rep")
    return lax.ppermute(value, "rep", [(i, i ^ bit) for i in range(size)])


def chip_bits():
    size, bits, bit = lax.axis_size("rep"), [], 2
    while bit < size:
        bits.append(bit)
        bit *= 2
    return bits


def chip_offsets():
    return list(range(0, lax.axis_size("rep"), 2))


def add(left, right):
    return left.astype(F32) + right.astype(F32)


def halves(value):
    half = value.shape[0] // 2
    return value[:half], value[half:]


class Flow:
    def __init__(self, steps):
        self.steps, self.result, self.done = steps, None, False
        self.pending = next(steps)

    def advance(self, arrived):
        try:
            self.pending = self.steps.send(arrived)
        except StopIteration as end:
            self.pending, self.result, self.done = [], end.value, True


def stage(flows, extra=()):
    flows = [f for f in flows if not f.done]
    arrived, extra = lax.optimization_barrier(([f.pending for f in flows], extra))
    for flow, values in zip(flows, arrived):
        flow.advance(values)
    return extra


def finish(flow):
    while not flow.done:
        flow.advance(flow.pending)
    return flow.result


def gather_steps(value, sink=lambda offset, block: None):
    bits = chip_bits()
    if len(bits) == 2:
        one, two = bits
        half = value.shape[0] // 2
        by_one, by_two = yield [swap(value, one), swap(value, two)]
        sink(one, by_one)
        sink(two, by_two)
        top, bottom = yield [swap(by_one[:half], two), swap(by_two[half:], one)]
        far = jnp.concatenate([top, bottom], axis=0)
        sink(one ^ two, far)
        return {0: value, one: by_one, two: by_two, one ^ two: far}
    blocks = {0: value}
    for bit in bits:
        old = list(blocks.items())
        new = yield [swap(b, bit) for _, b in old]
        for (d, _), b in zip(old, new):
            blocks[d ^ bit] = b
            sink(d ^ bit, b)
    return blocks


def peers():
    return [1, *[d for d in chip_offsets() if d]]


def greet(others):
    barrier = pltpu.get_barrier_semaphore()
    for device in others.values():
        pl.semaphore_signal(barrier, inc=1, device_id={"rep": device})
    pl.semaphore_wait(barrier, len(others))


def gather_kernel(offsets, in_ref, out_ref, own_sem, send_sem, recv_sem):
    me, rows = lax.axis_index("rep"), in_ref.shape[0]
    others = {d: jnp.bitwise_xor(me, d) for d in offsets}
    spot = {d: pl.ds((d // 2 + d % 2 * len(offsets)) * rows, rows) for d in range(2 * len(offsets))}
    greet(others)
    own = pltpu.make_async_copy(in_ref, out_ref.at[spot[0]], own_sem)
    own.start()

    def send(source, offset, to):
        return pltpu.make_async_remote_copy(
            src_ref=source,
            dst_ref=out_ref.at[spot[offset]],
            send_sem=send_sem.at[offset],
            recv_sem=recv_sem.at[offset],
            device_id={"rep": others[to]},
        )

    chips = [d for d in offsets if d != 1]
    first = {d: send(in_ref, d, d) for d in [*reversed(chips), 1]}
    for copy in first.values():
        copy.start()
    second = {}
    for d in chips:
        first[d].wait_recv()
        second[d] = send(out_ref.at[spot[d]], d + 1, 1)
        second[d].start()
    first[1].wait_recv()
    for copy in second.values():
        copy.wait_recv()
    own.wait()
    for copy in [*first.values(), *second.values()]:
        copy.wait_send()


def gather_rows(value, number):
    rows, width = value.shape
    size = lax.axis_size("rep")
    return pl.pallas_call(
        functools.partial(gather_kernel, peers()),
        out_shape=jax.ShapeDtypeStruct((size * rows, width), value.dtype),
        in_specs=[pl.BlockSpec(memory_space=pltpu.VMEM)],
        out_specs=pl.BlockSpec(memory_space=pltpu.VMEM),
        scratch_shapes=[
            pltpu.SemaphoreType.DMA,
            pltpu.SemaphoreType.DMA((size,)),
            pltpu.SemaphoreType.DMA((size,)),
        ],
        compiler_params=pltpu.CompilerParams(
            collective_id=number, has_side_effects=True, vmem_limit_bytes=16 << 20
        ),
        cost_estimate=pl.CostEstimate(
            flops=0, bytes_accessed=30 * value.size * size, transcendentals=0
        ),
        name="gather_rows",
    )(value)


def reduce_kernel(offsets, in_ref, out_ref, core_ref, held_ref, chip_ref, send_sem, recv_sem):
    me, rows = lax.axis_index("rep"), out_ref.shape[0]
    others = {d: jnp.bitwise_xor(me, d) for d in offsets}
    chips = [0, *[d for d in offsets if d != 1]]
    count = len(chips)
    greet(others)

    def block(ref, i):
        return ref.at[pl.ds(i * rows, rows)]

    def send(source, target, index, to):
        return pltpu.make_async_remote_copy(
            src_ref=source,
            dst_ref=target,
            send_sem=send_sem.at[index],
            recv_sem=recv_sem.at[index],
            device_id={"rep": others[to]},
        )

    order = list(reversed(range(count)))
    core = {i: send(block(in_ref, count + i), block(core_ref, i), i, 1) for i in order}
    for copy in core.values():
        copy.start()
    chip = {}
    for i in order:
        core[i].wait_recv()
        at = pl.ds(i * rows, rows)
        total = in_ref[at, :].astype(F32) + core_ref[at, :].astype(F32)
        held_ref[at, :] = total.astype(BF)
        if i:
            chip[i] = send(block(held_ref, i), block(chip_ref, i), count + i, chips[i])
            chip[i].start()
    total = held_ref[pl.ds(0, rows), :].astype(F32)
    for i in chip:
        chip[i].wait_recv()
        total += chip_ref[pl.ds(i * rows, rows), :].astype(F32)
    out_ref[...] = total.astype(BF)
    for copy in [*core.values(), *chip.values()]:
        copy.wait_send()


def reduce_rows(partial, number):
    size = lax.axis_size("rep")
    rows, width = partial.shape[0] // size, partial.shape[1]
    half = pltpu.VMEM((size // 2 * rows, width), BF)
    return pl.pallas_call(
        functools.partial(reduce_kernel, peers()),
        out_shape=jax.ShapeDtypeStruct((rows, width), BF),
        in_specs=[pl.BlockSpec(memory_space=pltpu.VMEM)],
        out_specs=pl.BlockSpec(memory_space=pltpu.VMEM),
        scratch_shapes=[
            half,
            half,
            half,
            pltpu.SemaphoreType.DMA((size,)),
            pltpu.SemaphoreType.DMA((size,)),
        ],
        compiler_params=pltpu.CompilerParams(
            collective_id=number, has_side_effects=True, vmem_limit_bytes=24 << 20
        ),
        cost_estimate=pl.CostEstimate(
            flops=0, bytes_accessed=30 * partial.size, transcendentals=0
        ),
        name="reduce_rows",
    )(partial)


def jump(value, offset):
    size = lax.axis_size("rep")
    return lax.ppermute(value, "rep", [(i, i ^ offset) for i in range(size)])


def straight_steps(value):
    away = [d for d in chip_offsets() if d]
    new = yield [jump(value, d) for d in away]
    return dict(zip([0, *away], [value, *new]))


def copies_steps(value, gather=gather_steps):
    blocks = yield from gather(value)
    same = jnp.concatenate([blocks[d] for d in chip_offsets()], axis=0)
    (other,) = yield [swap(same, 1)]
    return same, other


def scatter_steps(blocks):
    bits = chip_bits()
    if len(bits) == 2:
        one, two = bits
        far = blocks[one ^ two]
        top, bottom = yield [swap(far[0], one), swap(far[1], two)]
        near_one, near_two = blocks[one], blocks[two]
        one_top, two_bottom = yield [swap(near_one[0], one), swap(near_two[1], two)]
        two_top, one_bottom = yield [
            swap(add(near_two[0], top).astype(BF), two),
            swap(add(near_one[1], bottom).astype(BF), one),
        ]
        return jnp.concatenate(
            [
                (add(blocks[0][0], one_top) + two_top.astype(F32)).astype(BF),
                (add(blocks[0][1], one_bottom) + two_bottom.astype(F32)).astype(BF),
            ],
            axis=0,
        )
    while len(blocks) < len(chip_offsets()):
        yield []
    sums = {d: jnp.concatenate(b, axis=0) for d, b in blocks.items()}
    for bit in reversed(bits):
        kept = [d for d in sorted(sums) if not d & bit]
        new = yield [swap(sums[d | bit], bit) for d in kept]
        sums = {d: add(sums[d], n).astype(BF) for d, n in zip(kept, new)}
    return sums[0]


def plane_sum_steps(partial):
    half = partial.shape[0] // 2
    (other,) = yield [swap(partial[half:], 1)]
    same = add(partial[:half], other).astype(BF)
    offsets = chip_offsets()
    rows = half // len(offsets)
    blocks = {d: same[i * rows : (i + 1) * rows] for i, d in enumerate(offsets)}
    new = yield [jump(blocks[d], d) for d in offsets if d]
    return sum((n.astype(F32) for n in new), blocks[0].astype(F32)).astype(BF)


def vector_sum_steps(rows):
    size, bit = lax.axis_size("rep"), 1
    while bit < size:
        (other,) = yield [swap(rows, bit)]
        rows, bit = rows + other, 2 * bit
    shards, at = lax.axis_size("shard"), lax.axis_index("shard")
    own = rows.shape[1] // shards
    parts = yield [
        lax.ppermute(
            lax.dynamic_slice_in_dim(rows, ((at + k) % shards) * own, own, 1),
            "shard",
            [(i, (i + k) % shards) for i in range(shards)],
        )
        for k in range(1, shards)
    ]
    return lax.dynamic_slice_in_dim(rows, at * own, own, 1) + sum(parts)


def vector_gather_steps(rows):
    size, me = lax.axis_size("shard"), lax.axis_index("shard")
    others = yield [
        lax.ppermute(rows, "shard", [(i, (i - k) % size) for i in range(size)])
        for k in range(1, size)
    ]
    parts = [rows, *others]
    twice = jnp.concatenate(parts + parts, axis=1)
    own = rows.shape[1]
    return lax.dynamic_slice_in_dim(twice, ((size - me) % size) * own, size * own, 1)


def rotary_tables(length):
    half = HD // 2
    positions = jnp.arange(length, dtype=F32)
    inverse = 10000.0 ** (-2.0 * jnp.arange(half, dtype=F32) / HD)
    angles = positions[:, None] * inverse[None, :]
    cos, sin = jnp.cos(angles), jnp.sin(angles)
    return jnp.concatenate([cos, cos], axis=1), jnp.concatenate([-sin, sin], axis=1)


def rotate(values, cos, sin):
    return values * cos + pltpu.roll(values, HD // 2, 1) * sin


def window(step, seg_col, seg_row):
    low, high = max(0, step - 1) * WIN, (step + 1) * WIN
    shape = (WIN, high - low)
    row = lax.broadcasted_iota(jnp.int32, shape, 0) + step * WIN
    col = lax.broadcasted_iota(jnp.int32, shape, 1) + low
    near = (row >= col) & (row - col < WIN)
    same = seg_col[0, step * WIN : (step + 1) * WIN, :] == seg_row[0, :, low:high]
    return low, high, near & same


def attend_kernel(parts, z_ref, *refs):
    x_refs, w_refs = refs[:parts], refs[parts : 2 * parts]
    cos_ref, sin_ref, col_ref, row_ref, context_ref, qkv_ref, lse_ref, lin_ref = refs[2 * parts :]
    length, width = context_ref.shape
    tile = min(length, 256)

    @pl.loop(0, length // tile)
    def _(t):
        rows = pl.ds(pl.multiple_of(t * tile, tile), tile)
        total = mm(x_refs[0][rows, :], w_refs[0][...])
        for x, w in zip(x_refs[1:], w_refs[1:]):
            total += mm(x[rows, :], w[...])
        lin_ref[rows, :] = total

    cos, sin = cos_ref[...], sin_ref[...]
    for h in range(width // HD):
        q_at, k_at, v_at = (slice(i * width + h * HD, i * width + (h + 1) * HD) for i in range(3))
        qkv_ref[:, q_at] = rotate(lin_ref[:, q_at], cos, sin).astype(BF)
        qkv_ref[:, k_at] = rotate(lin_ref[:, k_at], cos, sin).astype(BF)
        qkv_ref[:, v_at] = lin_ref[:, v_at].astype(BF)
    for step in range(length // WIN):
        low, high, allowed = window(step, col_ref, row_ref)
        rows = slice(step * WIN, (step + 1) * WIN)
        for h in range(width // HD):
            q_at, k_at, v_at = (
                slice(i * width + h * HD, i * width + (h + 1) * HD) for i in range(3)
            )
            scores = mm_nt(qkv_ref[rows, q_at], qkv_ref[low:high, k_at]) * HD**-0.5
            scores = jnp.where(allowed, scores, -1e30)
            peak = jnp.max(scores, axis=1, keepdims=True)
            raw = jnp.exp(scores - peak)
            total = jnp.sum(raw, axis=1, keepdims=True)
            probs = (raw * (1.0 / total)).astype(BF)
            context_ref[rows, h * HD : (h + 1) * HD] = mm(probs, qkv_ref[low:high, v_at]).astype(BF)
            lse_ref[rows, h : h + 1] = peak + jnp.log(total)


def attend(shard, both, weights, tables, seg):
    parts = len(weights)
    rows, depth = both.shape
    length = tables[0].shape[0]
    wide = weights[0].shape[1]
    width = wide // 3
    piece = depth // parts
    whole = lambda *shape: pl.BlockSpec(shape, lambda s, z: (0,) * len(shape))
    take = lambda k: pl.BlockSpec((length, piece), lambda s, z: (s, (z[0] + parts - k) % parts))
    by_seq = lambda cols: pl.BlockSpec((length, cols), lambda s, z: (s, 0))
    return pl.pallas_call(
        functools.partial(attend_kernel, parts),
        grid_spec=pltpu.PrefetchScalarGridSpec(
            num_scalar_prefetch=1,
            grid=(rows // length,),
            in_specs=[take(k) for k in range(parts)]
            + [whole(piece, wide)] * parts
            + [whole(length, HD)] * 2
            + [
                pl.BlockSpec((1, length, 1), lambda s, z: (s, 0, 0)),
                pl.BlockSpec((1, 1, length), lambda s, z: (s, 0, 0)),
            ],
            out_specs=[by_seq(width), by_seq(wide), by_seq(width // HD)],
            scratch_shapes=[pltpu.VMEM((length, wide), F32)],
        ),
        out_shape=[
            jax.ShapeDtypeStruct((rows, width), BF),
            jax.ShapeDtypeStruct((rows, wide), BF),
            jax.ShapeDtypeStruct((rows, width // HD), F32),
        ],
        compiler_params=pltpu.CompilerParams(vmem_limit_bytes=40 << 20),
        cost_estimate=pl.CostEstimate(
            flops=2 * rows * depth * wide + 4 * rows * 2 * WIN * width,
            bytes_accessed=2 * (rows * depth + depth * wide + 2 * rows * wide),
            transcendentals=rows * 2 * WIN * width // HD,
        ),
        name="attend",
    )(shard, *[both] * parts, *weights, *tables, *seg)


def attend_back_kernel(
    own_ref, other_ref, out_ref, qkv_ref, lse_ref, x_ref, cos_ref, sin_ref, col_ref, row_ref,
    lin_ref, top_ref, bottom_ref, kept_ref, context_ref, keys_ref, values_ref,
):
    length, wide = qkv_ref.shape
    width = wide // 3
    seq = pl.program_id(0)
    tile = min(length, 256)

    @pl.loop(0, length // tile)
    def _(t):
        rows = pl.ds(pl.multiple_of(t * tile, tile), tile)

        @pl.when(seq == 0)
        def _():
            context_ref[rows, :] = mm_nt(own_ref[rows, :], out_ref[...]).astype(BF)

        @pl.when(seq > 0)
        def _():
            context_ref[rows, :] = mm_nt(other_ref[rows, :], out_ref[...]).astype(BF)

    cos, sin = cos_ref[...], sin_ref[...]
    scale = HD**-0.5
    for h in range(width // HD):
        q_at, k_at, v_at = (slice(i * width + h * HD, i * width + (h + 1) * HD) for i in range(3))
        head = slice(h * HD, (h + 1) * HD)
        keys_ref[...] = jnp.zeros_like(keys_ref)
        values_ref[...] = jnp.zeros_like(values_ref)
        for step in range(length // WIN):
            low, high, allowed = window(step, col_ref, row_ref)
            rows = slice(step * WIN, (step + 1) * WIN)
            queries, keys = qkv_ref[rows, q_at], qkv_ref[low:high, k_at]
            grad = context_ref[rows, head]
            scores = jnp.where(allowed, mm_nt(queries, keys) * scale, -1e30)
            probs = jnp.exp(scores - lse_ref[rows, h : h + 1])
            values_ref[low:high, :] += mm_tn(probs.astype(BF), grad)
            grad_probs = mm_nt(grad, qkv_ref[low:high, v_at])
            inner = jnp.sum(probs * grad_probs, axis=1, keepdims=True)
            grad_scores = (probs * (grad_probs - inner)).astype(BF)
            grad_queries = mm(grad_scores, keys) * scale
            keys_ref[low:high, :] += mm_tn(grad_scores, queries)
            lin_ref[rows, q_at] = rotate(grad_queries, cos[rows], -sin[rows]).astype(BF)
        lin_ref[:, k_at] = rotate(keys_ref[...] * scale, cos, -sin).astype(BF)
        lin_ref[:, v_at] = values_ref[...].astype(BF)
    kept_ref[pl.ds(pl.multiple_of(seq * length, length), length), :] = lin_ref[...]

    @pl.when(seq == pl.num_programs(0) - 1)
    def _():
        half = top_ref.shape[0]
        step = 256
        for n, ref in enumerate((top_ref, bottom_ref)):

            @pl.loop(0, half // step)
            def _(t):
                cols = pl.ds(pl.multiple_of(n * half + t * step, step), step)
                rows = pl.ds(pl.multiple_of(t * step, step), step)
                ref[rows, :] = mm_tn(x_ref[:, cols], kept_ref[...]).astype(BF)


def attend_back(grad, out_w, qkv, lse, both, tables, seg):
    rows, depth = both.shape
    length = tables[0].shape[0]
    wide = qkv.shape[1]
    width = wide // 3
    whole = lambda *shape: pl.BlockSpec(shape, lambda s: (0,) * len(shape))
    by_seq = lambda cols: pl.BlockSpec((length, cols), lambda s: (s, 0))
    return pl.pallas_call(
        attend_back_kernel,
        grid=(rows // length,),
        in_specs=[whole(length, depth)] * 2
        + [whole(width, depth), by_seq(wide), by_seq(width // HD)]
        + [whole(rows, depth), whole(length, HD), whole(length, HD)]
        + [
            pl.BlockSpec((1, length, 1), lambda s: (s, 0, 0)),
            pl.BlockSpec((1, 1, length), lambda s: (s, 0, 0)),
        ],
        out_specs=[by_seq(wide), whole(depth // 2, wide), whole(depth // 2, wide)],
        scratch_shapes=[
            pltpu.VMEM((rows, wide), BF),
            pltpu.VMEM((length, width), BF),
            pltpu.VMEM((length, HD), F32),
            pltpu.VMEM((length, HD), F32),
        ],
        out_shape=[
            jax.ShapeDtypeStruct((rows, wide), BF),
            jax.ShapeDtypeStruct((depth // 2, wide), BF),
            jax.ShapeDtypeStruct((depth // 2, wide), BF),
        ],
        compiler_params=pltpu.CompilerParams(vmem_limit_bytes=48 << 20),
        cost_estimate=pl.CostEstimate(
            flops=2 * rows * depth * (wide + width) + 10 * rows * 2 * WIN * width,
            bytes_accessed=2 * (2 * rows * depth + depth * (wide + width) + 2 * rows * wide),
            transcendentals=rows * 2 * WIN * width // HD,
        ),
        name="attend_back",
    )(*grad, out_w, qkv, lse, both, *tables, *seg)


def normed_back_kernel(blocks, parts, z_ref, *refs):
    lins, weights, (own_ref, other_ref) = refs[:blocks], refs[blocks:-2], refs[-2:]
    piece = own_ref.shape[1] // parts
    own = pl.program_id(0) < pl.num_programs(0) // 2
    for k in range(parts):
        total = mm_nt(lins[0][...], weights[k][...])
        for n in range(1, blocks):
            total += mm_nt(lins[n][...], weights[n * parts + k][...])
        at = pl.multiple_of(((z_ref[0] + parts - k) % parts) * piece, piece)

        @pl.when(own)
        def _():
            own_ref[:, pl.ds(at, piece)] = total

        @pl.when(jnp.logical_not(own))
        def _():
            other_ref[:, pl.ds(at, piece)] = total.astype(BF)


def normed_back(shard, lins, weights, depth):
    parts = len(weights[0])
    rows, wide = lins[0].shape
    tile = min(rows // 2, 256)
    steps = rows // 2 // tile
    flat = [w for block in weights for w in block]
    return pl.pallas_call(
        functools.partial(normed_back_kernel, len(lins), parts),
        grid_spec=pltpu.PrefetchScalarGridSpec(
            num_scalar_prefetch=1,
            grid=(rows // tile,),
            in_specs=[pl.BlockSpec((tile, wide), lambda s, z: (s, 0))] * len(lins)
            + [
                pl.BlockSpec(flat[0].shape, lambda s, z: (0, 0), pipeline_mode=pl.Buffered(1))
            ] * len(flat),
            out_specs=[
                pl.BlockSpec((tile, depth), lambda s, z: (jnp.minimum(s, steps - 1), 0)),
                pl.BlockSpec((tile, depth), lambda s, z: (jnp.maximum(s - steps, 0), 0)),
            ],
        ),
        out_shape=[
            jax.ShapeDtypeStruct((rows // 2, depth), F32),
            jax.ShapeDtypeStruct((rows // 2, depth), BF),
        ],
        compiler_params=pltpu.CompilerParams(vmem_limit_bytes=48 << 20),
        cost_estimate=pl.CostEstimate(
            flops=2 * rows * depth * wide * len(lins),
            bytes_accessed=2 * len(lins) * wide * (rows + depth) + 4 * rows * depth,
            transcendentals=0,
        ),
        name="normed_back",
    )(shard, *lins, *flat)


def plan_slots(route_ids, gate_values):
    hit_mask = route_ids == 0
    hit = jnp.any(hit_mask, axis=-1)
    weight = jnp.sum(jnp.where(hit_mask, gate_values, 0.0), axis=-1)
    ids = jnp.arange(route_ids.shape[0], dtype=jnp.int32)
    earlier = (ids[None, :] < ids[:, None]) & hit[None, :]
    order = jnp.sum(earlier.astype(jnp.int32), axis=1)
    kept = hit & (order < CAP)
    slots = jnp.arange(CAP, dtype=jnp.int32)
    table = (order[None, :] == slots[:, None]) & kept[None, :]
    return table, jnp.where(kept, weight, 0.0)


def norm_back(grad_normed, source, root, gain):
    scaled = grad_normed * gain
    grad_gain = jnp.sum(grad_normed * source * root, axis=0)
    mean = jnp.mean(scaled * source, axis=-1, keepdims=True)
    return grad_gain, root * scaled - source * (root * root * root) * mean


def place_kernel(columns, me_ref, same_ref, other_ref, *out_refs):
    even = me_ref[0] % 2 == 0
    same, other = same_ref[...], other_ref[...]
    blocks = (jnp.where(even, same, other).astype(F32), jnp.where(even, other, same).astype(F32))
    width = same.shape[1] // len(out_refs)
    for i, ref in enumerate(out_refs):
        for n, block in enumerate(blocks):
            part = block[:, i * width : (i + 1) * width]
            if columns:
                ref[:, n * width : (n + 1) * width] = part
            else:
                ref[n * same.shape[0] : (n + 1) * same.shape[0], :] = part


def place(me, same, other, height, width, columns):
    size, total = lax.axis_size("rep"), same.shape[1]
    spec = pl.BlockSpec((height, total), lambda d, me: (d, 0))
    shape = (height, size * width) if columns else (size * height, width)
    at = lambda d, me: jnp.bitwise_xor(d, me[0] // 2)
    if columns:
        out_spec = pl.BlockSpec((height, 2 * width), lambda d, me: (0, at(d, me)))
    else:
        out_spec = pl.BlockSpec((2 * height, width), lambda d, me: (at(d, me), 0))
    count = total // width
    return pl.pallas_call(
        functools.partial(place_kernel, columns),
        grid_spec=pltpu.PrefetchScalarGridSpec(
            num_scalar_prefetch=1,
            grid=(size // 2,),
            in_specs=[spec, spec],
            out_specs=[out_spec] * count,
        ),
        out_shape=[jax.ShapeDtypeStruct(shape, F32)] * count,
        compiler_params=pltpu.CompilerParams(vmem_limit_bytes=32 << 20),
        cost_estimate=pl.CostEstimate(
            flops=0, bytes_accessed=6 * size * height * total, transcendentals=0
        ),
        name="place",
    )(me, same, other)


def place_turned_kernel(me_ref, same_ref, other_ref, out_ref):
    odd = me_ref[0] % 2
    first = jnp.where(odd == 0, same_ref[...], other_ref[...])
    second = jnp.where(odd == 0, other_ref[...], same_ref[...])
    out_ref[...] = jnp.concatenate([first, second], axis=0).T.astype(F32)


def place_turned(me, same, other, height):
    size, width = lax.axis_size("rep"), same.shape[1]
    if 2 * height % 128:
        return place(me, same, other, height, width, False)[0].T
    spec = pl.BlockSpec((height, width), lambda j, me: (jnp.bitwise_xor(j, me[0] // 2), 0))
    return pl.pallas_call(
        place_turned_kernel,
        grid_spec=pltpu.PrefetchScalarGridSpec(
            num_scalar_prefetch=1,
            grid=(size // 2,),
            in_specs=[spec, spec],
            out_specs=pl.BlockSpec((width, 2 * height), lambda j, me: (0, j)),
        ),
        out_shape=jax.ShapeDtypeStruct((width, size * height), F32),
        compiler_params=pltpu.CompilerParams(vmem_limit_bytes=32 << 20),
        cost_estimate=pl.CostEstimate(
            flops=0, bytes_accessed=12 * same.size, transcendentals=0
        ),
        name="place_turned",
    )(me, same, other)


def per_device(
    layer_input,
    gain_attn,
    w_query,
    w_key,
    w_value,
    w_out,
    gain_mlp,
    w_gate,
    w_up,
    w_down,
    segments,
    attn_route,
    attn_gate,
    mlp_route,
    mlp_gate,
    cotangent,
):
    length = layer_input.shape[0]
    size, shards = lax.axis_size("rep"), lax.axis_size("shard")
    me = lax.axis_index("rep")
    whoami = me.astype(jnp.int32).reshape(1)
    shard = lax.axis_index("shard").astype(jnp.int32).reshape(1)
    block = w_query.shape[1] // size
    units = w_gate.shape[1] // size
    own = gain_attn.shape[0]
    offsets = chip_offsets()
    staged = len(chip_bits()) == 2

    def columns(weight, d, width):
        return lax.dynamic_slice_in_dim(weight, jnp.bitwise_xor(me, d) * width, width, 1)

    def rows_of(weight, height):
        return lax.dynamic_slice_in_dim(weight, me * height, height, 0)

    def local(d):
        return jnp.concatenate([columns(w, d, block) for w in (w_query, w_key, w_value)], axis=1)

    inputs = layer_input.astype(F32)
    root_one = lax.rsqrt(jnp.mean(inputs * inputs, axis=-1, keepdims=True) + EPSILON)
    tables = rotary_tables(length)
    ring = [(i, (i + 1) % shards) for i in range(shards)]
    piece = local(0)
    qkv_w = {d: [local(d)] for d in offsets}
    flows, context, saved = [], {}, {}
    gain_flow = Flow(vector_gather_steps(jnp.stack([gain_attn, gain_mlp])))
    piece, seg_other, own_gate_up = stage(
        [gain_flow],
        (
            lax.ppermute(piece, "shard", ring),
            swap(segments, 1),
            jnp.concatenate([columns(w_gate, 0, units), columns(w_up, 0, units)], axis=1),
        ),
    )
    gain_one, gain_two = gain_flow.result.astype(F32)
    normed = (inputs * root_one * gain_one).astype(BF)
    seg = jnp.concatenate([segments, seg_other], axis=0)
    seg = (seg[:, :, None], seg[:, None, :])
    other = swap(normed, 1)
    for step in range(1, shards):
        qkv_w[0].append(piece)
        flows.append(Flow(gather_steps(piece, lambda d, b: qkv_w[d].append(b))))
        if step < shards - 1:
            piece, other = stage(flows, (lax.ppermute(piece, "shard", ring), other))
    own_out, own_gate_up, own_down, qkv_w[0][-1] = lax.optimization_barrier(
        (rows_of(w_out, block), own_gate_up, rows_of(w_down, units), qkv_w[0][-1])
    )
    own_out = lax.all_gather(own_out, "shard", axis=1, tiled=True)
    both = jnp.concatenate([normed, other], axis=0)

    def run(d):
        context[d], *saved[d] = attend(shard, both, qkv_w[d], tables, seg)
        return context[d]

    context[0], own_out = stage(flows, (run(0), own_out))
    gate_up = lax.all_gather(own_gate_up, "shard", axis=0, tiled=True)
    down = lax.all_gather(own_down, "shard", axis=1, tiled=True)
    early = offsets[1:2] if staged else []
    early = stage(flows, [run(d) for d in early])
    for flow in flows:
        finish(flow)
    out_flow = Flow(gather_steps(own_out))
    rest = [d for d in offsets if d not in context]
    stage([out_flow], [run(d) for d in rest])
    out_w = finish(out_flow)

    table, mix = plan_slots(mlp_route, mlp_gate)
    pick = table.astype(BF)
    upstream = cotangent.astype(F32)
    slot_weight = jnp.sum(jnp.where(table, mix[None, :], 0.0), axis=1)[:, None]
    slot_grad = (mm(pick, cotangent) * slot_weight).astype(BF)

    all_context = jnp.concatenate([context[d] for d in offsets], axis=1)
    all_out = jnp.concatenate([out_w[d] for d in offsets], axis=0)
    projected = mm(all_context, all_out)
    projected = projected[:length] + swap(projected[length:].astype(BF), 1).astype(F32)
    attn_weight = jnp.sum(jnp.where(attn_route == 0, attn_gate, 0.0), axis=-1)[:, None]
    hidden = inputs + projected * attn_weight
    root_two = lax.rsqrt(jnp.mean(hidden * hidden, axis=-1, keepdims=True) + EPSILON)
    normed_two = (hidden * root_two * gain_two).astype(BF)

    dispatched = gather_rows(mm(pick, normed_two).astype(BF), 0)
    act = mm(dispatched, gate_up)
    slot_grad, act = lax.optimization_barrier((slot_grad, act))
    all_slot_grad = gather_rows(slot_grad, 0)
    gate_act, up_act = act[:, :units], act[:, units:]
    sigmoid = jax.nn.sigmoid(gate_act)
    silu = gate_act * sigmoid
    inner = (silu * up_act).astype(BF)
    expert_flow = Flow(plane_sum_steps(mm(inner, down).astype(BF)))
    grad_inner = mm_nt(all_slot_grad, down)
    grad_gate_act = (grad_inner * up_act * sigmoid * (1.0 + gate_act * (1.0 - sigmoid))).astype(BF)
    grad_up_act = (grad_inner * silu).astype(BF)
    grad_act = jnp.concatenate([grad_gate_act, grad_up_act], axis=1)
    grad_gate, back = lax.optimization_barrier(
        (mm_tn(grad_gate_act, dispatched).astype(BF), mm_nt(grad_act, gate_up).astype(BF))
    )
    grad_disp, grad_up_act, inner = stage([expert_flow], (reduce_rows(back, 1), grad_up_act, inner))
    grad_normed_two = mm_tn(pick, grad_disp)
    grad_gain_two, through = norm_back(grad_normed_two, hidden, root_two, gain_two)
    grad_hidden = upstream + through

    grad_projected = (grad_hidden * attn_weight).astype(BF)
    both_grad = [grad_projected, swap(grad_projected, 1)]
    lins, grad_qkv_w = {}, {}

    def run_back(*ds):
        for d in ds:
            lins[d], *grad_qkv_w[d] = attend_back(
                both_grad, out_w[d], *saved[d], both, tables, seg
            )
        return [(lins[d], grad_qkv_w[d]) for d in ds]

    def keep(ds, values):
        for d, (lin, grad) in zip(ds, values):
            lins[d], grad_qkv_w[d] = lin, grad

    far, near = offsets[-1:], offsets[1:-1]
    values, both_grad, grad_up, inner = stage(
        [expert_flow],
        (run_back(*far), both_grad, mm_tn(grad_up_act, dispatched).astype(BF), inner),
    )
    keep(far, values)
    qkv_flow = Flow(scatter_steps(grad_qkv_w))
    grad_down = mm_tn(inner, all_slot_grad).astype(BF)
    values, both_grad, grad_down, expert_out = stage(
        [qkv_flow], (run_back(*near), both_grad, grad_down, finish(expert_flow))
    )
    keep(near, values)
    sums = [
        lax.psum_scatter(g, "shard", scatter_dimension=1, tiled=True)
        for g in (grad_gate, grad_up, grad_down)
    ]
    output = (hidden + mm_tn(pick, expert_out) * mix[:, None]).astype(BF)
    values, grad_out_w, output = stage(
        [qkv_flow], (run_back(0), mm_tn(all_context, jnp.concatenate(both_grad, axis=0)).astype(BF), output)
    )
    keep([0], values)
    grad_normed = normed_back(
        shard, [lins[d] for d in offsets], [qkv_w[d] for d in offsets], both.shape[1]
    )
    sums[0], sums[1], grad_normed, grad_out_w = stage(
        [qkv_flow], (sums[0], sums[1], grad_normed, grad_out_w)
    )
    own_grad_qkv, sums[2] = lax.optimization_barrier((finish(qkv_flow), sums[2]))
    sum_qkv = lax.psum_scatter(own_grad_qkv, "shard", scatter_dimension=0, tiled=True)

    out_blocks = {d: halves(grad_out_w[i * block : (i + 1) * block]) for i, d in enumerate(offsets)}
    out_flow, gate_flow = Flow(scatter_steps(out_blocks)), Flow(copies_steps(sums[0]))
    other_normed, up_sum = stage(
        [out_flow, gate_flow], (swap(grad_normed[1], 1), sums[1])
    )
    grad_normed = grad_normed[0] + other_normed.astype(F32)
    grad_gain_one, first = norm_back(grad_normed, inputs, root_one, gain_one)
    grad_input = (grad_hidden + first).astype(BF)
    grad_input, gains, up_sum = stage(
        [out_flow, gate_flow],
        (grad_input, jnp.stack([grad_gain_one, grad_gain_two]), up_sum),
    )
    gain_flow, up_flow = Flow(vector_sum_steps(gains)), Flow(copies_steps(up_sum))
    sum_qkv = stage([out_flow, gate_flow, up_flow, gain_flow], sum_qkv)
    sum_out = lax.psum_scatter(finish(out_flow), "shard", scatter_dimension=1, tiled=True)
    qkv_flow = Flow(copies_steps(sum_qkv))
    grad_gate = place_turned(whoami, *finish(gate_flow), units)
    grad_gate, sum_out = stage([up_flow, qkv_flow, gain_flow], (grad_gate, sum_out))
    down_sum, sum_out = lax.optimization_barrier((sums[2], sum_out))
    all_down = lax.all_gather(down_sum, "rep", axis=0, tiled=True)
    out_flow = Flow(copies_steps(sum_out, straight_steps))
    stage([up_flow, qkv_flow, out_flow, gain_flow])
    grad_up = place_turned(whoami, *finish(up_flow), units)
    grad_up = stage([qkv_flow, out_flow, gain_flow], grad_up)
    grad_query, grad_key, grad_value = place(whoami, *finish(qkv_flow), own, block, True)
    (grad_out,) = place(whoami, *finish(out_flow), block, own, False)
    grad_down = all_down.astype(F32)
    gain_grads = finish(gain_flow)
    return (
        output,
        grad_input,
        gain_grads[0],
        grad_query,
        grad_key,
        grad_value,
        grad_out,
        gain_grads[1],
        grad_gate,
        grad_up,
        grad_down,
    )


def solution(mesh):
    tokens = P(("rep", "shard"), None)
    tall, wide, vector = P("shard", None), P(None, "shard"), P("shard")
    weights = (vector, tall, tall, tall, wide, vector, tall, tall, wide)
    return jax.shard_map(
        per_device,
        mesh=mesh,
        in_specs=(tokens, *weights) + (tokens,) * 6,
        out_specs=(tokens, tokens, *weights),
        check_vma=False,
    )
```

```python
import functools

import jax
import jax.numpy as jnp
from jax import lax
from jax.experimental import pallas as pl
from jax.experimental.pallas import tpu as pltpu
from jax.sharding import PartitionSpec as P

HEADS = 16
HD = 128
WIN = 256
CAP = 128
EPSILON = 1e-05
BF = jnp.bfloat16
F32 = jnp.float32


def mm(left, right):
    return jnp.dot(left, right, preferred_element_type=F32)


def mm_nt(left, right):
    return lax.dot_general(left, right, (((1,), (1,)), ((), ())), preferred_element_type=F32)


def mm_tn(left, right):
    return lax.dot_general(left, right, (((0,), (0,)), ((), ())), preferred_element_type=F32)


def swap(value, bit):
    size = lax.axis_size("rep")
    return lax.ppermute(value, "rep", [(i, i ^ bit) for i in range(size)])


def chip_bits():
    size, bits, bit = lax.axis_size("rep"), [], 2
    while bit < size:
        bits.append(bit)
        bit *= 2
    return bits


def chip_offsets():
    return list(range(0, lax.axis_size("rep"), 2))


def add(left, right):
    return left.astype(F32) + right.astype(F32)


def halves(value):
    half = value.shape[0] // 2
    return value[:half], value[half:]


class Flow:
    def __init__(self, steps):
        self.steps, self.result, self.done = steps, None, False
        self.pending = next(steps)

    def advance(self, arrived):
        try:
            self.pending = self.steps.send(arrived)
        except StopIteration as end:
            self.pending, self.result, self.done = [], end.value, True


def stage(flows, extra=()):
    flows = [f for f in flows if not f.done]
    arrived, extra = lax.optimization_barrier(([f.pending for f in flows], extra))
    for flow, values in zip(flows, arrived):
        flow.advance(values)
    return extra


def finish(flow):
    while not flow.done:
        flow.advance(flow.pending)
    return flow.result


def gather_steps(value, sink=lambda offset, block: None):
    bits = chip_bits()
    if len(bits) == 2:
        one, two = bits
        half = value.shape[0] // 2
        by_one, by_two = yield [swap(value, one), swap(value, two)]
        sink(one, by_one)
        sink(two, by_two)
        top, bottom = yield [swap(by_one[:half], two), swap(by_two[half:], one)]
        far = jnp.concatenate([top, bottom], axis=0)
        sink(one ^ two, far)
        return {0: value, one: by_one, two: by_two, one ^ two: far}
    blocks = {0: value}
    for bit in bits:
        old = list(blocks.items())
        new = yield [swap(b, bit) for _, b in old]
        for (d, _), b in zip(old, new):
            blocks[d ^ bit] = b
            sink(d ^ bit, b)
    return blocks


def peers():
    return [1, *[d for d in chip_offsets() if d]]


def greet(others):
    barrier = pltpu.get_barrier_semaphore()
    for device in others.values():
        pl.semaphore_signal(barrier, inc=1, device_id={"rep": device})
    pl.semaphore_wait(barrier, len(others))


def gather_kernel(offsets, in_ref, out_ref, own_sem, send_sem, recv_sem):
    me, rows = lax.axis_index("rep"), in_ref.shape[0]
    others = {d: jnp.bitwise_xor(me, d) for d in offsets}
    spot = {d: pl.ds((d // 2 + d % 2 * len(offsets)) * rows, rows) for d in range(2 * len(offsets))}
    greet(others)
    own = pltpu.make_async_copy(in_ref, out_ref.at[spot[0]], own_sem)
    own.start()

    def send(source, offset, to):
        return pltpu.make_async_remote_copy(
            src_ref=source,
            dst_ref=out_ref.at[spot[offset]],
            send_sem=send_sem.at[offset],
            recv_sem=recv_sem.at[offset],
            device_id={"rep": others[to]},
        )

    chips = [d for d in offsets if d != 1]
    first = {d: send(in_ref, d, d) for d in [*reversed(chips), 1]}
    for copy in first.values():
        copy.start()
    second = {}
    for d in chips:
        first[d].wait_recv()
        second[d] = send(out_ref.at[spot[d]], d + 1, 1)
        second[d].start()
    first[1].wait_recv()
    for copy in second.values():
        copy.wait_recv()
    own.wait()
    for copy in [*first.values(), *second.values()]:
        copy.wait_send()


def gather_rows(value, number):
    rows, width = value.shape
    size = lax.axis_size("rep")
    return pl.pallas_call(
        functools.partial(gather_kernel, peers()),
        out_shape=jax.ShapeDtypeStruct((size * rows, width), value.dtype),
        in_specs=[pl.BlockSpec(memory_space=pltpu.VMEM)],
        out_specs=pl.BlockSpec(memory_space=pltpu.VMEM),
        scratch_shapes=[
            pltpu.SemaphoreType.DMA,
            pltpu.SemaphoreType.DMA((size,)),
            pltpu.SemaphoreType.DMA((size,)),
        ],
        compiler_params=pltpu.CompilerParams(
            collective_id=number, has_side_effects=True, vmem_limit_bytes=16 << 20
        ),
        cost_estimate=pl.CostEstimate(
            flops=0, bytes_accessed=30 * value.size * size, transcendentals=0
        ),
        name="gather_rows",
    )(value)


def reduce_kernel(offsets, in_ref, out_ref, core_ref, held_ref, chip_ref, send_sem, recv_sem):
    me, rows = lax.axis_index("rep"), out_ref.shape[0]
    others = {d: jnp.bitwise_xor(me, d) for d in offsets}
    chips = [0, *[d for d in offsets if d != 1]]
    count = len(chips)
    greet(others)

    def block(ref, i):
        return ref.at[pl.ds(i * rows, rows)]

    def send(source, target, index, to):
        return pltpu.make_async_remote_copy(
            src_ref=source,
            dst_ref=target,
            send_sem=send_sem.at[index],
            recv_sem=recv_sem.at[index],
            device_id={"rep": others[to]},
        )

    order = list(reversed(range(count)))
    core = {i: send(block(in_ref, count + i), block(core_ref, i), i, 1) for i in order}
    for copy in core.values():
        copy.start()
    chip, half = [], rows // 2

    def part(ref, i, n):
        return ref.at[pl.ds(i * rows + n * half, half)]

    def pass_on(i, n, index, to):
        chip.append(send(part(held_ref, i, n), part(chip_ref, i, n), index, to))
        chip[-1].start()
        return chip[-1]

    relay = count == 4
    for i in order:
        core[i].wait_recv()
        at = pl.ds(i * rows, rows)
        total = in_ref[at, :].astype(F32) + core_ref[at, :].astype(F32)
        held_ref[at, :] = total.astype(BF)
        if relay and i == 3:
            far = [pass_on(3, 0, count, chips[1]), pass_on(3, 1, count + 1, chips[2])]
        elif relay and i:
            pass_on(i, i - 1, count + 1 + i, chips[i])
        elif i:
            chip.append(send(block(held_ref, i), block(chip_ref, i), count + i, chips[i]))
            chip[-1].start()
    if relay:
        for i, n in ((2, 0), (1, 1)):
            far[n].wait_recv()
            at, moved = pl.ds(i * rows + n * half, half), pl.ds(3 * rows + n * half, half)
            total = held_ref[at, :].astype(F32) + chip_ref[moved, :].astype(F32)
            held_ref[at, :] = total.astype(BF)
            pass_on(i, n, count + 4 + n, chips[i])
        chip, sent = chip[2:], chip[:2]
    else:
        sent = []
    total = held_ref[pl.ds(0, rows), :].astype(F32)
    for copy in chip:
        copy.wait_recv()
    for i in range(1, 3 if relay else count):
        total += chip_ref[pl.ds(i * rows, rows), :].astype(F32)
    out_ref[...] = total.astype(BF)
    for copy in [*core.values(), *sent, *chip]:
        copy.wait_send()


def reduce_rows(partial, number):
    size = lax.axis_size("rep")
    rows, width = partial.shape[0] // size, partial.shape[1]
    half = pltpu.VMEM((size // 2 * rows, width), BF)
    return pl.pallas_call(
        functools.partial(reduce_kernel, peers()),
        out_shape=jax.ShapeDtypeStruct((rows, width), BF),
        in_specs=[pl.BlockSpec(memory_space=pltpu.VMEM)],
        out_specs=pl.BlockSpec(memory_space=pltpu.VMEM),
        scratch_shapes=[
            half,
            half,
            half,
            pltpu.SemaphoreType.DMA((size + 2,)),
            pltpu.SemaphoreType.DMA((size + 2,)),
        ],
        compiler_params=pltpu.CompilerParams(
            collective_id=number, has_side_effects=True, vmem_limit_bytes=24 << 20
        ),
        cost_estimate=pl.CostEstimate(
            flops=0, bytes_accessed=30 * partial.size, transcendentals=0
        ),
        name="reduce_rows",
    )(partial)


def jump(value, offset):
    size = lax.axis_size("rep")
    return lax.ppermute(value, "rep", [(i, i ^ offset) for i in range(size)])


def straight_steps(value):
    away = [d for d in chip_offsets() if d]
    new = yield [jump(value, d) for d in away]
    return dict(zip([0, *away], [value, *new]))


def copies_steps(value, gather=gather_steps):
    blocks = yield from gather(value)
    same = jnp.concatenate([blocks[d] for d in chip_offsets()], axis=0)
    (other,) = yield [swap(same, 1)]
    return same, other


def scatter_steps(blocks):
    bits = chip_bits()
    if len(bits) == 2:
        one, two = bits
        far = blocks[one ^ two]
        top, bottom = yield [swap(far[0], one), swap(far[1], two)]
        near_one, near_two = blocks[one], blocks[two]
        one_top, two_bottom = yield [swap(near_one[0], one), swap(near_two[1], two)]
        two_top, one_bottom = yield [
            swap(add(near_two[0], top).astype(BF), two),
            swap(add(near_one[1], bottom).astype(BF), one),
        ]
        return jnp.concatenate(
            [
                (add(blocks[0][0], one_top) + two_top.astype(F32)).astype(BF),
                (add(blocks[0][1], one_bottom) + two_bottom.astype(F32)).astype(BF),
            ],
            axis=0,
        )
    while len(blocks) < len(chip_offsets()):
        yield []
    sums = {d: jnp.concatenate(b, axis=0) for d, b in blocks.items()}
    for bit in reversed(bits):
        kept = [d for d in sorted(sums) if not d & bit]
        new = yield [swap(sums[d | bit], bit) for d in kept]
        sums = {d: add(sums[d], n).astype(BF) for d, n in zip(kept, new)}
    return sums[0]


def plane_sum_steps(partial):
    half = partial.shape[0] // 2
    (other,) = yield [swap(partial[half:], 1)]
    same = add(partial[:half], other).astype(BF)
    offsets = chip_offsets()
    rows = half // len(offsets)
    blocks = {d: same[i * rows : (i + 1) * rows] for i, d in enumerate(offsets)}
    new = yield [jump(blocks[d], d) for d in offsets if d]
    return sum((n.astype(F32) for n in new), blocks[0].astype(F32)).astype(BF)


def vector_sum_steps(rows):
    size, bit = lax.axis_size("rep"), 1
    while bit < size:
        (other,) = yield [swap(rows, bit)]
        rows, bit = rows + other, 2 * bit
    shards, at = lax.axis_size("shard"), lax.axis_index("shard")
    own = rows.shape[1] // shards
    parts = yield [
        lax.ppermute(
            lax.dynamic_slice_in_dim(rows, ((at + k) % shards) * own, own, 1),
            "shard",
            [(i, (i + k) % shards) for i in range(shards)],
        )
        for k in range(1, shards)
    ]
    return lax.dynamic_slice_in_dim(rows, at * own, own, 1) + sum(parts)


def vector_gather_steps(rows):
    size, me = lax.axis_size("shard"), lax.axis_index("shard")
    others = yield [
        lax.ppermute(rows, "shard", [(i, (i - k) % size) for i in range(size)])
        for k in range(1, size)
    ]
    parts = [rows, *others]
    twice = jnp.concatenate(parts + parts, axis=1)
    own = rows.shape[1]
    return lax.dynamic_slice_in_dim(twice, ((size - me) % size) * own, size * own, 1)


def rotary_tables(length):
    half = HD // 2
    positions = jnp.arange(length, dtype=F32)
    inverse = 10000.0 ** (-2.0 * jnp.arange(half, dtype=F32) / HD)
    angles = positions[:, None] * inverse[None, :]
    cos, sin = jnp.cos(angles), jnp.sin(angles)
    return jnp.concatenate([cos, cos], axis=1), jnp.concatenate([-sin, sin], axis=1)


def rotate(values, cos, sin):
    return values * cos + pltpu.roll(values, HD // 2, 1) * sin


def window(step, seg_col, seg_row):
    low, high = max(0, step - 1) * WIN, (step + 1) * WIN
    shape = (WIN, high - low)
    row = lax.broadcasted_iota(jnp.int32, shape, 0) + step * WIN
    col = lax.broadcasted_iota(jnp.int32, shape, 1) + low
    near = (row >= col) & (row - col < WIN)
    same = seg_col[0, step * WIN : (step + 1) * WIN, :] == seg_row[0, :, low:high]
    return low, high, near & same


def attend_kernel(parts, z_ref, *refs):
    x_refs, w_refs = refs[:parts], refs[parts : 2 * parts]
    cos_ref, sin_ref, col_ref, row_ref, context_ref, qkv_ref, lse_ref, lin_ref = refs[2 * parts :]
    length, width = context_ref.shape
    tile = min(length, 256)

    @pl.loop(0, length // tile)
    def _(t):
        rows = pl.ds(pl.multiple_of(t * tile, tile), tile)
        total = mm(x_refs[0][rows, :], w_refs[0][...])
        for x, w in zip(x_refs[1:], w_refs[1:]):
            total += mm(x[rows, :], w[...])
        lin_ref[rows, :] = total

    cos, sin = cos_ref[...], sin_ref[...]
    for h in range(width // HD):
        q_at, k_at, v_at = (slice(i * width + h * HD, i * width + (h + 1) * HD) for i in range(3))
        qkv_ref[:, q_at] = rotate(lin_ref[:, q_at], cos, sin).astype(BF)
        qkv_ref[:, k_at] = rotate(lin_ref[:, k_at], cos, sin).astype(BF)
        qkv_ref[:, v_at] = lin_ref[:, v_at].astype(BF)
    for step in range(length // WIN):
        low, high, allowed = window(step, col_ref, row_ref)
        rows = slice(step * WIN, (step + 1) * WIN)
        for h in range(width // HD):
            q_at, k_at, v_at = (
                slice(i * width + h * HD, i * width + (h + 1) * HD) for i in range(3)
            )
            scores = mm_nt(qkv_ref[rows, q_at], qkv_ref[low:high, k_at]) * HD**-0.5
            scores = jnp.where(allowed, scores, -1e30)
            peak = jnp.max(scores, axis=1, keepdims=True)
            raw = jnp.exp(scores - peak)
            total = jnp.sum(raw, axis=1, keepdims=True)
            probs = (raw * (1.0 / total)).astype(BF)
            context_ref[rows, h * HD : (h + 1) * HD] = mm(probs, qkv_ref[low:high, v_at]).astype(BF)
            lse_ref[rows, h : h + 1] = peak + jnp.log(total)


def attend(shard, both, weights, tables, seg):
    parts = len(weights)
    rows, depth = both.shape
    length = tables[0].shape[0]
    wide = weights[0].shape[1]
    width = wide // 3
    piece = depth // parts
    whole = lambda *shape: pl.BlockSpec(shape, lambda s, z: (0,) * len(shape))
    take = lambda k: pl.BlockSpec((length, piece), lambda s, z: (s, (z[0] + parts - k) % parts))
    by_seq = lambda cols: pl.BlockSpec((length, cols), lambda s, z: (s, 0))
    return pl.pallas_call(
        functools.partial(attend_kernel, parts),
        grid_spec=pltpu.PrefetchScalarGridSpec(
            num_scalar_prefetch=1,
            grid=(rows // length,),
            in_specs=[take(k) for k in range(parts)]
            + [whole(piece, wide)] * parts
            + [whole(length, HD)] * 2
            + [
                pl.BlockSpec((1, length, 1), lambda s, z: (s, 0, 0)),
                pl.BlockSpec((1, 1, length), lambda s, z: (s, 0, 0)),
            ],
            out_specs=[by_seq(width), by_seq(wide), by_seq(width // HD)],
            scratch_shapes=[pltpu.VMEM((length, wide), F32)],
        ),
        out_shape=[
            jax.ShapeDtypeStruct((rows, width), BF),
            jax.ShapeDtypeStruct((rows, wide), BF),
            jax.ShapeDtypeStruct((rows, width // HD), F32),
        ],
        compiler_params=pltpu.CompilerParams(vmem_limit_bytes=40 << 20),
        cost_estimate=pl.CostEstimate(
            flops=2 * rows * depth * wide + 4 * rows * 2 * WIN * width,
            bytes_accessed=2 * (rows * depth + depth * wide + 2 * rows * wide),
            transcendentals=rows * 2 * WIN * width // HD,
        ),
        name="attend",
    )(shard, *[both] * parts, *weights, *tables, *seg)


def attend_back_kernel(
    own_ref, other_ref, out_ref, qkv_ref, lse_ref, x_ref, cos_ref, sin_ref, col_ref, row_ref,
    lin_ref, top_ref, bottom_ref, kept_ref, context_ref, keys_ref, values_ref,
):
    length, wide = qkv_ref.shape
    width = wide // 3
    seq = pl.program_id(0)
    tile = min(length, 256)

    @pl.loop(0, length // tile)
    def _(t):
        rows = pl.ds(pl.multiple_of(t * tile, tile), tile)

        @pl.when(seq == 0)
        def _():
            context_ref[rows, :] = mm_nt(own_ref[rows, :], out_ref[...]).astype(BF)

        @pl.when(seq > 0)
        def _():
            context_ref[rows, :] = mm_nt(other_ref[rows, :], out_ref[...]).astype(BF)

    cos, sin = cos_ref[...], sin_ref[...]
    scale = HD**-0.5
    for h in range(width // HD):
        q_at, k_at, v_at = (slice(i * width + h * HD, i * width + (h + 1) * HD) for i in range(3))
        head = slice(h * HD, (h + 1) * HD)
        keys_ref[...] = jnp.zeros_like(keys_ref)
        values_ref[...] = jnp.zeros_like(values_ref)
        for step in range(length // WIN):
            low, high, allowed = window(step, col_ref, row_ref)
            rows = slice(step * WIN, (step + 1) * WIN)
            queries, keys = qkv_ref[rows, q_at], qkv_ref[low:high, k_at]
            grad = context_ref[rows, head]
            scores = jnp.where(allowed, mm_nt(queries, keys) * scale, -1e30)
            probs = jnp.exp(scores - lse_ref[rows, h : h + 1])
            values_ref[low:high, :] += mm_tn(probs.astype(BF), grad)
            grad_probs = mm_nt(grad, qkv_ref[low:high, v_at])
            inner = jnp.sum(probs * grad_probs, axis=1, keepdims=True)
            grad_scores = (probs * (grad_probs - inner)).astype(BF)
            grad_queries = mm(grad_scores, keys) * scale
            keys_ref[low:high, :] += mm_tn(grad_scores, queries)
            lin_ref[rows, q_at] = rotate(grad_queries, cos[rows], -sin[rows]).astype(BF)
        lin_ref[:, k_at] = rotate(keys_ref[...] * scale, cos, -sin).astype(BF)
        lin_ref[:, v_at] = values_ref[...].astype(BF)
    kept_ref[pl.ds(pl.multiple_of(seq * length, length), length), :] = lin_ref[...]

    @pl.when(seq == pl.num_programs(0) - 1)
    def _():
        half = top_ref.shape[0]
        step = 256
        for n, ref in enumerate((top_ref, bottom_ref)):

            @pl.loop(0, half // step)
            def _(t):
                cols = pl.ds(pl.multiple_of(n * half + t * step, step), step)
                rows = pl.ds(pl.multiple_of(t * step, step), step)
                ref[rows, :] = mm_tn(x_ref[:, cols], kept_ref[...]).astype(BF)


def attend_back(grad, out_w, qkv, lse, both, tables, seg):
    rows, depth = both.shape
    length = tables[0].shape[0]
    wide = qkv.shape[1]
    width = wide // 3
    whole = lambda *shape: pl.BlockSpec(shape, lambda s: (0,) * len(shape))
    by_seq = lambda cols: pl.BlockSpec((length, cols), lambda s: (s, 0))
    return pl.pallas_call(
        attend_back_kernel,
        grid=(rows // length,),
        in_specs=[whole(length, depth)] * 2
        + [whole(width, depth), by_seq(wide), by_seq(width // HD)]
        + [whole(rows, depth), whole(length, HD), whole(length, HD)]
        + [
            pl.BlockSpec((1, length, 1), lambda s: (s, 0, 0)),
            pl.BlockSpec((1, 1, length), lambda s: (s, 0, 0)),
        ],
        out_specs=[by_seq(wide), whole(depth // 2, wide), whole(depth // 2, wide)],
        scratch_shapes=[
            pltpu.VMEM((rows, wide), BF),
            pltpu.VMEM((length, width), BF),
            pltpu.VMEM((length, HD), F32),
            pltpu.VMEM((length, HD), F32),
        ],
        out_shape=[
            jax.ShapeDtypeStruct((rows, wide), BF),
            jax.ShapeDtypeStruct((depth // 2, wide), BF),
            jax.ShapeDtypeStruct((depth // 2, wide), BF),
        ],
        compiler_params=pltpu.CompilerParams(vmem_limit_bytes=48 << 20),
        cost_estimate=pl.CostEstimate(
            flops=2 * rows * depth * (wide + width) + 10 * rows * 2 * WIN * width,
            bytes_accessed=2 * (2 * rows * depth + depth * (wide + width) + 2 * rows * wide),
            transcendentals=rows * 2 * WIN * width // HD,
        ),
        name="attend_back",
    )(*grad, out_w, qkv, lse, both, *tables, *seg)


def normed_back_kernel(blocks, parts, z_ref, *refs):
    lins, weights, (own_ref, other_ref) = refs[:blocks], refs[blocks:-2], refs[-2:]
    piece = own_ref.shape[1] // parts
    own = pl.program_id(0) < pl.num_programs(0) // 2
    for k in range(parts):
        total = mm_nt(lins[0][...], weights[k][...])
        for n in range(1, blocks):
            total += mm_nt(lins[n][...], weights[n * parts + k][...])
        at = pl.multiple_of(((z_ref[0] + parts - k) % parts) * piece, piece)

        @pl.when(own)
        def _():
            own_ref[:, pl.ds(at, piece)] = total

        @pl.when(jnp.logical_not(own))
        def _():
            other_ref[:, pl.ds(at, piece)] = total.astype(BF)


def normed_back(shard, lins, weights, depth):
    parts = len(weights[0])
    rows, wide = lins[0].shape
    tile = min(rows // 2, 256)
    steps = rows // 2 // tile
    flat = [w for block in weights for w in block]
    return pl.pallas_call(
        functools.partial(normed_back_kernel, len(lins), parts),
        grid_spec=pltpu.PrefetchScalarGridSpec(
            num_scalar_prefetch=1,
            grid=(rows // tile,),
            in_specs=[pl.BlockSpec((tile, wide), lambda s, z: (s, 0))] * len(lins)
            + [
                pl.BlockSpec(flat[0].shape, lambda s, z: (0, 0), pipeline_mode=pl.Buffered(1))
            ] * len(flat),
            out_specs=[
                pl.BlockSpec((tile, depth), lambda s, z: (jnp.minimum(s, steps - 1), 0)),
                pl.BlockSpec((tile, depth), lambda s, z: (jnp.maximum(s - steps, 0), 0)),
            ],
        ),
        out_shape=[
            jax.ShapeDtypeStruct((rows // 2, depth), F32),
            jax.ShapeDtypeStruct((rows // 2, depth), BF),
        ],
        compiler_params=pltpu.CompilerParams(vmem_limit_bytes=48 << 20),
        cost_estimate=pl.CostEstimate(
            flops=2 * rows * depth * wide * len(lins),
            bytes_accessed=2 * len(lins) * wide * (rows + depth) + 4 * rows * depth,
            transcendentals=0,
        ),
        name="normed_back",
    )(shard, *lins, *flat)


def plan_slots(route_ids, gate_values):
    hit_mask = route_ids == 0
    hit = jnp.any(hit_mask, axis=-1)
    weight = jnp.sum(jnp.where(hit_mask, gate_values, 0.0), axis=-1)
    ids = jnp.arange(route_ids.shape[0], dtype=jnp.int32)
    earlier = (ids[None, :] < ids[:, None]) & hit[None, :]
    order = jnp.sum(earlier.astype(jnp.int32), axis=1)
    kept = hit & (order < CAP)
    slots = jnp.arange(CAP, dtype=jnp.int32)
    table = (order[None, :] == slots[:, None]) & kept[None, :]
    return table, jnp.where(kept, weight, 0.0)


def norm_back(grad_normed, source, root, gain):
    scaled = grad_normed * gain
    grad_gain = jnp.sum(grad_normed * source * root, axis=0)
    mean = jnp.mean(scaled * source, axis=-1, keepdims=True)
    return grad_gain, root * scaled - source * (root * root * root) * mean


def place_kernel(columns, me_ref, same_ref, other_ref, *out_refs):
    even = me_ref[0] % 2 == 0
    same, other = same_ref[...], other_ref[...]
    blocks = (jnp.where(even, same, other).astype(F32), jnp.where(even, other, same).astype(F32))
    width = same.shape[1] // len(out_refs)
    for i, ref in enumerate(out_refs):
        for n, block in enumerate(blocks):
            part = block[:, i * width : (i + 1) * width]
            if columns:
                ref[:, n * width : (n + 1) * width] = part
            else:
                ref[n * same.shape[0] : (n + 1) * same.shape[0], :] = part


def place(me, same, other, height, width, columns):
    size, total = lax.axis_size("rep"), same.shape[1]
    spec = pl.BlockSpec((height, total), lambda d, me: (d, 0))
    shape = (height, size * width) if columns else (size * height, width)
    at = lambda d, me: jnp.bitwise_xor(d, me[0] // 2)
    if columns:
        out_spec = pl.BlockSpec((height, 2 * width), lambda d, me: (0, at(d, me)))
    else:
        out_spec = pl.BlockSpec((2 * height, width), lambda d, me: (at(d, me), 0))
    count = total // width
    return pl.pallas_call(
        functools.partial(place_kernel, columns),
        grid_spec=pltpu.PrefetchScalarGridSpec(
            num_scalar_prefetch=1,
            grid=(size // 2,),
            in_specs=[spec, spec],
            out_specs=[out_spec] * count,
        ),
        out_shape=[jax.ShapeDtypeStruct(shape, F32)] * count,
        compiler_params=pltpu.CompilerParams(vmem_limit_bytes=32 << 20),
        cost_estimate=pl.CostEstimate(
            flops=0, bytes_accessed=6 * size * height * total, transcendentals=0
        ),
        name="place",
    )(me, same, other)


def place_turned_kernel(me_ref, same_ref, other_ref, out_ref):
    odd = me_ref[0] % 2
    first = jnp.where(odd == 0, same_ref[...], other_ref[...])
    second = jnp.where(odd == 0, other_ref[...], same_ref[...])
    out_ref[...] = jnp.concatenate([first, second], axis=0).T.astype(F32)


def place_turned(me, same, other, height):
    size, width = lax.axis_size("rep"), same.shape[1]
    if 2 * height % 128:
        return place(me, same, other, height, width, False)[0].T
    spec = pl.BlockSpec((height, width), lambda j, me: (jnp.bitwise_xor(j, me[0] // 2), 0))
    return pl.pallas_call(
        place_turned_kernel,
        grid_spec=pltpu.PrefetchScalarGridSpec(
            num_scalar_prefetch=1,
            grid=(size // 2,),
            in_specs=[spec, spec],
            out_specs=pl.BlockSpec((width, 2 * height), lambda j, me: (0, j)),
        ),
        out_shape=jax.ShapeDtypeStruct((width, size * height), F32),
        compiler_params=pltpu.CompilerParams(vmem_limit_bytes=32 << 20),
        cost_estimate=pl.CostEstimate(
            flops=0, bytes_accessed=12 * same.size, transcendentals=0
        ),
        name="place_turned",
    )(me, same, other)


def per_device(
    layer_input,
    gain_attn,
    w_query,
    w_key,
    w_value,
    w_out,
    gain_mlp,
    w_gate,
    w_up,
    w_down,
    segments,
    attn_route,
    attn_gate,
    mlp_route,
    mlp_gate,
    cotangent,
):
    length = layer_input.shape[0]
    size, shards = lax.axis_size("rep"), lax.axis_size("shard")
    me = lax.axis_index("rep")
    whoami = me.astype(jnp.int32).reshape(1)
    shard = lax.axis_index("shard").astype(jnp.int32).reshape(1)
    block = w_query.shape[1] // size
    units = w_gate.shape[1] // size
    own = gain_attn.shape[0]
    offsets = chip_offsets()
    staged = len(chip_bits()) == 2

    def columns(weight, d, width):
        return lax.dynamic_slice_in_dim(weight, jnp.bitwise_xor(me, d) * width, width, 1)

    def rows_of(weight, height):
        return lax.dynamic_slice_in_dim(weight, me * height, height, 0)

    def local(d):
        return jnp.concatenate([columns(w, d, block) for w in (w_query, w_key, w_value)], axis=1)

    inputs = layer_input.astype(F32)
    root_one = lax.rsqrt(jnp.mean(inputs * inputs, axis=-1, keepdims=True) + EPSILON)
    tables = rotary_tables(length)
    ring = [(i, (i + 1) % shards) for i in range(shards)]
    piece = local(0)
    qkv_w = {d: [local(d)] for d in offsets}
    flows, context, saved = [], {}, {}
    gain_flow = Flow(vector_gather_steps(jnp.stack([gain_attn, gain_mlp])))
    piece, seg_other, own_gate_up = stage(
        [gain_flow],
        (
            lax.ppermute(piece, "shard", ring),
            swap(segments, 1),
            jnp.concatenate([columns(w_gate, 0, units), columns(w_up, 0, units)], axis=1),
        ),
    )
    gain_one, gain_two = gain_flow.result.astype(F32)
    normed = (inputs * root_one * gain_one).astype(BF)
    seg = jnp.concatenate([segments, seg_other], axis=0)
    seg = (seg[:, :, None], seg[:, None, :])
    other = swap(normed, 1)
    for step in range(1, shards):
        qkv_w[0].append(piece)
        flows.append(Flow(gather_steps(piece, lambda d, b: qkv_w[d].append(b))))
        if step < shards - 1:
            piece, other = stage(flows, (lax.ppermute(piece, "shard", ring), other))
    own_out, own_gate_up, own_down, qkv_w[0][-1] = lax.optimization_barrier(
        (rows_of(w_out, block), own_gate_up, rows_of(w_down, units), qkv_w[0][-1])
    )
    own_out = lax.all_gather(own_out, "shard", axis=1, tiled=True)
    both = jnp.concatenate([normed, other], axis=0)

    def run(d):
        context[d], *saved[d] = attend(shard, both, qkv_w[d], tables, seg)
        return context[d]

    context[0], own_out = stage(flows, (run(0), own_out))
    gate_up = lax.all_gather(own_gate_up, "shard", axis=0, tiled=True)
    down = lax.all_gather(own_down, "shard", axis=1, tiled=True)
    early = offsets[1:2] if staged else []
    early = stage(flows, [run(d) for d in early])
    for flow in flows:
        finish(flow)
    out_flow = Flow(gather_steps(own_out))
    rest = [d for d in offsets if d not in context]
    stage([out_flow], [run(d) for d in rest])
    out_w = finish(out_flow)

    table, mix = plan_slots(mlp_route, mlp_gate)
    pick = table.astype(BF)
    upstream = cotangent.astype(F32)
    slot_weight = jnp.sum(jnp.where(table, mix[None, :], 0.0), axis=1)[:, None]
    slot_grad = (mm(pick, cotangent) * slot_weight).astype(BF)

    all_context = jnp.concatenate([context[d] for d in offsets], axis=1)
    all_out = jnp.concatenate([out_w[d] for d in offsets], axis=0)
    projected = mm(all_context, all_out)
    projected = projected[:length] + swap(projected[length:].astype(BF), 1).astype(F32)
    attn_weight = jnp.sum(jnp.where(attn_route == 0, attn_gate, 0.0), axis=-1)[:, None]
    hidden = inputs + projected * attn_weight
    root_two = lax.rsqrt(jnp.mean(hidden * hidden, axis=-1, keepdims=True) + EPSILON)
    normed_two = (hidden * root_two * gain_two).astype(BF)

    dispatched = gather_rows(mm(pick, normed_two).astype(BF), 0)
    act = mm(dispatched, gate_up)
    slot_grad, act = lax.optimization_barrier((slot_grad, act))
    all_slot_grad = gather_rows(slot_grad, 0)
    gate_act, up_act = act[:, :units], act[:, units:]
    sigmoid = jax.nn.sigmoid(gate_act)
    silu = gate_act * sigmoid
    inner = (silu * up_act).astype(BF)
    expert_flow = Flow(plane_sum_steps(mm(inner, down).astype(BF)))
    grad_inner = mm_nt(all_slot_grad, down)
    grad_gate_act = (grad_inner * up_act * sigmoid * (1.0 + gate_act * (1.0 - sigmoid))).astype(BF)
    grad_up_act = (grad_inner * silu).astype(BF)
    grad_act = jnp.concatenate([grad_gate_act, grad_up_act], axis=1)
    grad_gate, back = lax.optimization_barrier(
        (mm_tn(grad_gate_act, dispatched).astype(BF), mm_nt(grad_act, gate_up).astype(BF))
    )
    grad_disp, grad_up_act, inner = stage([expert_flow], (reduce_rows(back, 1), grad_up_act, inner))
    grad_normed_two = mm_tn(pick, grad_disp)
    grad_gain_two, through = norm_back(grad_normed_two, hidden, root_two, gain_two)
    grad_hidden = upstream + through

    grad_projected = (grad_hidden * attn_weight).astype(BF)
    both_grad = [grad_projected, swap(grad_projected, 1)]
    lins, grad_qkv_w = {}, {}

    def run_back(*ds):
        for d in ds:
            lins[d], *grad_qkv_w[d] = attend_back(
                both_grad, out_w[d], *saved[d], both, tables, seg
            )
        return [(lins[d], grad_qkv_w[d]) for d in ds]

    def keep(ds, values):
        for d, (lin, grad) in zip(ds, values):
            lins[d], grad_qkv_w[d] = lin, grad

    far, near = offsets[-1:], offsets[1:-1]
    values, both_grad, grad_up_act, inner = stage(
        [expert_flow], (run_back(*far), both_grad, grad_up_act, inner)
    )
    keep(far, values)
    grad_up, both_grad = lax.optimization_barrier(
        (mm_tn(grad_up_act, dispatched).astype(BF), both_grad)
    )
    qkv_flow = Flow(scatter_steps(grad_qkv_w))
    grad_down = mm_tn(inner, all_slot_grad).astype(BF)
    values, both_grad, grad_down, expert_out = stage(
        [qkv_flow], (run_back(*near), both_grad, grad_down, finish(expert_flow))
    )
    keep(near, values)
    sums = [
        lax.psum_scatter(g, "shard", scatter_dimension=1, tiled=True)
        for g in (grad_gate, grad_up, grad_down)
    ]
    output = (hidden + mm_tn(pick, expert_out) * mix[:, None]).astype(BF)
    values, grad_out_w, output = stage(
        [qkv_flow], (run_back(0), mm_tn(all_context, jnp.concatenate(both_grad, axis=0)).astype(BF), output)
    )
    keep([0], values)
    grad_normed = normed_back(
        shard, [lins[d] for d in offsets], [qkv_w[d] for d in offsets], both.shape[1]
    )
    sums[0], sums[1], grad_normed, grad_out_w = stage(
        [qkv_flow], (sums[0], sums[1], grad_normed, grad_out_w)
    )
    own_grad_qkv, sums[2] = lax.optimization_barrier((finish(qkv_flow), sums[2]))
    sum_qkv = lax.psum_scatter(own_grad_qkv, "shard", scatter_dimension=0, tiled=True)

    out_blocks = {d: halves(grad_out_w[i * block : (i + 1) * block]) for i, d in enumerate(offsets)}
    out_flow, gate_flow = Flow(scatter_steps(out_blocks)), Flow(copies_steps(sums[0]))
    other_normed, up_sum = stage(
        [out_flow, gate_flow], (swap(grad_normed[1], 1), sums[1])
    )
    grad_normed = grad_normed[0] + other_normed.astype(F32)
    grad_gain_one, first = norm_back(grad_normed, inputs, root_one, gain_one)
    grad_input = (grad_hidden + first).astype(BF)
    grad_input, gains, up_sum = stage(
        [out_flow, gate_flow],
        (grad_input, jnp.stack([grad_gain_one, grad_gain_two]), up_sum),
    )
    gain_flow, up_flow = Flow(vector_sum_steps(gains)), Flow(copies_steps(up_sum))
    sum_qkv = stage([out_flow, gate_flow, up_flow, gain_flow], sum_qkv)
    sum_out = lax.psum_scatter(finish(out_flow), "shard", scatter_dimension=1, tiled=True)
    qkv_flow = Flow(copies_steps(sum_qkv))
    grad_gate = place_turned(whoami, *finish(gate_flow), units)
    grad_gate, sum_out = stage([up_flow, qkv_flow, gain_flow], (grad_gate, sum_out))
    down_sum, sum_out = lax.optimization_barrier((sums[2], sum_out))
    all_down = lax.all_gather(down_sum, "rep", axis=0, tiled=True)
    out_flow = Flow(copies_steps(sum_out, straight_steps))
    stage([up_flow, qkv_flow, out_flow, gain_flow])
    grad_up = place_turned(whoami, *finish(up_flow), units)
    grad_up = stage([qkv_flow, out_flow, gain_flow], grad_up)
    grad_query, grad_key, grad_value = place(whoami, *finish(qkv_flow), own, block, True)
    (grad_out,) = place(whoami, *finish(out_flow), block, own, False)
    grad_down = all_down.astype(F32)
    gain_grads = finish(gain_flow)
    return (
        output,
        grad_input,
        gain_grads[0],
        grad_query,
        grad_key,
        grad_value,
        grad_out,
        gain_grads[1],
        grad_gate,
        grad_up,
        grad_down,
    )


def solution(mesh):
    tokens = P(("rep", "shard"), None)
    tall, wide, vector = P("shard", None), P(None, "shard"), P("shard")
    weights = (vector, tall, tall, tall, wide, vector, tall, tall, wide)
    return jax.shard_map(
        per_device,
        mesh=mesh,
        in_specs=(tokens, *weights) + (tokens,) * 6,
        out_specs=(tokens, tokens, *weights),
        check_vma=False,
    )
```

```python
import functools

import jax
import jax.numpy as jnp
from jax import lax
from jax.experimental import pallas as pl
from jax.experimental.pallas import tpu as pltpu
from jax.sharding import PartitionSpec as P

HEADS = 16
HD = 128
WIN = 256
CAP = 128
EPSILON = 1e-05
BF = jnp.bfloat16
F32 = jnp.float32


def mm(left, right):
    return jnp.dot(left, right, preferred_element_type=F32)


def mm_nt(left, right):
    return lax.dot_general(left, right, (((1,), (1,)), ((), ())), preferred_element_type=F32)


def mm_tn(left, right):
    return lax.dot_general(left, right, (((0,), (0,)), ((), ())), preferred_element_type=F32)


def swap(value, bit):
    size = lax.axis_size("rep")
    return lax.ppermute(value, "rep", [(i, i ^ bit) for i in range(size)])


def chip_bits():
    size, bits, bit = lax.axis_size("rep"), [], 2
    while bit < size:
        bits.append(bit)
        bit *= 2
    return bits


def chip_offsets():
    return list(range(0, lax.axis_size("rep"), 2))


def add(left, right):
    return left.astype(F32) + right.astype(F32)


def halves(value):
    half = value.shape[0] // 2
    return value[:half], value[half:]


class Flow:
    def __init__(self, steps):
        self.steps, self.result, self.done = steps, None, False
        self.pending = next(steps)

    def advance(self, arrived):
        try:
            self.pending = self.steps.send(arrived)
        except StopIteration as end:
            self.pending, self.result, self.done = [], end.value, True


def stage(flows, extra=()):
    flows = [f for f in flows if not f.done]
    arrived, extra = lax.optimization_barrier(([f.pending for f in flows], extra))
    for flow, values in zip(flows, arrived):
        flow.advance(values)
    return extra


def finish(flow):
    while not flow.done:
        flow.advance(flow.pending)
    return flow.result


def gather_steps(value, sink=lambda offset, block: None):
    bits = chip_bits()
    if len(bits) == 2:
        one, two = bits
        half = value.shape[0] // 2
        by_one, by_two = yield [swap(value, one), swap(value, two)]
        sink(one, by_one)
        sink(two, by_two)
        top, bottom = yield [swap(by_one[:half], two), swap(by_two[half:], one)]
        far = jnp.concatenate([top, bottom], axis=0)
        sink(one ^ two, far)
        return {0: value, one: by_one, two: by_two, one ^ two: far}
    blocks = {0: value}
    for bit in bits:
        old = list(blocks.items())
        new = yield [swap(b, bit) for _, b in old]
        for (d, _), b in zip(old, new):
            blocks[d ^ bit] = b
            sink(d ^ bit, b)
    return blocks


def peers():
    return [1, *[d for d in chip_offsets() if d]]


def greet(others):
    barrier = pltpu.get_barrier_semaphore()
    for device in others.values():
        pl.semaphore_signal(barrier, inc=1, device_id={"rep": device})
    pl.semaphore_wait(barrier, len(others))


def gather_kernel(offsets, in_ref, out_ref, own_sem, send_sem, recv_sem):
    me, rows = lax.axis_index("rep"), in_ref.shape[0]
    others = {d: jnp.bitwise_xor(me, d) for d in offsets}
    spot = {d: pl.ds((d // 2 + d % 2 * len(offsets)) * rows, rows) for d in range(2 * len(offsets))}
    greet(others)
    own = pltpu.make_async_copy(in_ref, out_ref.at[spot[0]], own_sem)
    own.start()

    def send(source, offset, to):
        return pltpu.make_async_remote_copy(
            src_ref=source,
            dst_ref=out_ref.at[spot[offset]],
            send_sem=send_sem.at[offset],
            recv_sem=recv_sem.at[offset],
            device_id={"rep": others[to]},
        )

    chips = [d for d in offsets if d != 1]
    first = {d: send(in_ref, d, d) for d in [*reversed(chips), 1]}
    for copy in first.values():
        copy.start()
    second = {}
    for d in chips:
        first[d].wait_recv()
        second[d] = send(out_ref.at[spot[d]], d + 1, 1)
        second[d].start()
    first[1].wait_recv()
    for copy in second.values():
        copy.wait_recv()
    own.wait()
    for copy in [*first.values(), *second.values()]:
        copy.wait_send()


def gather_rows(value, number):
    rows, width = value.shape
    size = lax.axis_size("rep")
    return pl.pallas_call(
        functools.partial(gather_kernel, peers()),
        out_shape=jax.ShapeDtypeStruct((size * rows, width), value.dtype),
        in_specs=[pl.BlockSpec(memory_space=pltpu.VMEM)],
        out_specs=pl.BlockSpec(memory_space=pltpu.VMEM),
        scratch_shapes=[
            pltpu.SemaphoreType.DMA,
            pltpu.SemaphoreType.DMA((size,)),
            pltpu.SemaphoreType.DMA((size,)),
        ],
        compiler_params=pltpu.CompilerParams(
            collective_id=number, has_side_effects=True, vmem_limit_bytes=16 << 20
        ),
        cost_estimate=pl.CostEstimate(
            flops=0, bytes_accessed=30 * value.size * size, transcendentals=0
        ),
        name="gather_rows",
    )(value)


def reduce_kernel(offsets, in_ref, out_ref, core_ref, held_ref, chip_ref, send_sem, recv_sem):
    me, rows = lax.axis_index("rep"), out_ref.shape[0]
    others = {d: jnp.bitwise_xor(me, d) for d in offsets}
    chips = [0, *[d for d in offsets if d != 1]]
    count = len(chips)
    greet(others)

    def block(ref, i):
        return ref.at[pl.ds(i * rows, rows)]

    def send(source, target, index, to):
        return pltpu.make_async_remote_copy(
            src_ref=source,
            dst_ref=target,
            send_sem=send_sem.at[index],
            recv_sem=recv_sem.at[index],
            device_id={"rep": others[to]},
        )

    order = list(reversed(range(count)))
    core = {i: send(block(in_ref, count + i), block(core_ref, i), i, 1) for i in order}
    for copy in core.values():
        copy.start()
    chip, half = [], rows // 2

    def part(ref, i, n):
        return ref.at[pl.ds(i * rows + n * half, half)]

    def pass_on(i, n, index, to):
        chip.append(send(part(held_ref, i, n), part(chip_ref, i, n), index, to))
        chip[-1].start()
        return chip[-1]

    relay = count == 4
    for i in order:
        core[i].wait_recv()
        at = pl.ds(i * rows, rows)
        total = in_ref[at, :].astype(F32) + core_ref[at, :].astype(F32)
        held_ref[at, :] = total.astype(BF)
        if relay and i == 3:
            far = [pass_on(3, 0, count, chips[1]), pass_on(3, 1, count + 1, chips[2])]
        elif relay and i:
            pass_on(i, i - 1, count + 1 + i, chips[i])
        elif i:
            chip.append(send(block(held_ref, i), block(chip_ref, i), count + i, chips[i]))
            chip[-1].start()
    if relay:
        for i, n in ((2, 0), (1, 1)):
            far[n].wait_recv()
            at, moved = pl.ds(i * rows + n * half, half), pl.ds(3 * rows + n * half, half)
            total = held_ref[at, :].astype(F32) + chip_ref[moved, :].astype(F32)
            held_ref[at, :] = total.astype(BF)
            pass_on(i, n, count + 4 + n, chips[i])
        chip, sent = chip[2:], chip[:2]
    else:
        sent = []
    total = held_ref[pl.ds(0, rows), :].astype(F32)
    for copy in chip:
        copy.wait_recv()
    for i in range(1, 3 if relay else count):
        total += chip_ref[pl.ds(i * rows, rows), :].astype(F32)
    out_ref[...] = total.astype(BF)
    for copy in [*core.values(), *sent, *chip]:
        copy.wait_send()


def reduce_rows(partial, number):
    size = lax.axis_size("rep")
    rows, width = partial.shape[0] // size, partial.shape[1]
    half = pltpu.VMEM((size // 2 * rows, width), BF)
    return pl.pallas_call(
        functools.partial(reduce_kernel, peers()),
        out_shape=jax.ShapeDtypeStruct((rows, width), BF),
        in_specs=[pl.BlockSpec(memory_space=pltpu.VMEM)],
        out_specs=pl.BlockSpec(memory_space=pltpu.VMEM),
        scratch_shapes=[
            half,
            half,
            half,
            pltpu.SemaphoreType.DMA((size + 2,)),
            pltpu.SemaphoreType.DMA((size + 2,)),
        ],
        compiler_params=pltpu.CompilerParams(
            collective_id=number, has_side_effects=True, vmem_limit_bytes=24 << 20
        ),
        cost_estimate=pl.CostEstimate(
            flops=0, bytes_accessed=30 * partial.size, transcendentals=0
        ),
        name="reduce_rows",
    )(partial)


def jump(value, offset):
    size = lax.axis_size("rep")
    return lax.ppermute(value, "rep", [(i, i ^ offset) for i in range(size)])


def straight_steps(value):
    away = [d for d in chip_offsets() if d]
    new = yield [jump(value, d) for d in away]
    return dict(zip([0, *away], [value, *new]))


def copies_steps(value, gather=gather_steps):
    blocks = yield from gather(value)
    same = jnp.concatenate([blocks[d] for d in chip_offsets()], axis=0)
    (other,) = yield [swap(same, 1)]
    return same, other


def scatter_steps(blocks):
    bits = chip_bits()
    if len(bits) == 2:
        one, two = bits
        far = blocks[one ^ two]
        top, bottom = yield [swap(far[0], one), swap(far[1], two)]
        near_one, near_two = blocks[one], blocks[two]
        one_top, two_bottom = yield [swap(near_one[0], one), swap(near_two[1], two)]
        two_top, one_bottom = yield [
            swap(add(near_two[0], top).astype(BF), two),
            swap(add(near_one[1], bottom).astype(BF), one),
        ]
        return jnp.concatenate(
            [
                (add(blocks[0][0], one_top) + two_top.astype(F32)).astype(BF),
                (add(blocks[0][1], one_bottom) + two_bottom.astype(F32)).astype(BF),
            ],
            axis=0,
        )
    while len(blocks) < len(chip_offsets()):
        yield []
    sums = {d: jnp.concatenate(b, axis=0) for d, b in blocks.items()}
    for bit in reversed(bits):
        kept = [d for d in sorted(sums) if not d & bit]
        new = yield [swap(sums[d | bit], bit) for d in kept]
        sums = {d: add(sums[d], n).astype(BF) for d, n in zip(kept, new)}
    return sums[0]


def plane_sum_steps(partial):
    half = partial.shape[0] // 2
    (other,) = yield [swap(partial[half:], 1)]
    same = add(partial[:half], other).astype(BF)
    offsets = chip_offsets()
    rows = half // len(offsets)
    blocks = {d: same[i * rows : (i + 1) * rows] for i, d in enumerate(offsets)}
    new = yield [jump(blocks[d], d) for d in offsets if d]
    return sum((n.astype(F32) for n in new), blocks[0].astype(F32)).astype(BF)


def vector_sum_steps(rows):
    size, bit = lax.axis_size("rep"), 1
    while bit < size:
        (other,) = yield [swap(rows, bit)]
        rows, bit = rows + other, 2 * bit
    shards, at = lax.axis_size("shard"), lax.axis_index("shard")
    own = rows.shape[1] // shards
    parts = yield [
        lax.ppermute(
            lax.dynamic_slice_in_dim(rows, ((at + k) % shards) * own, own, 1),
            "shard",
            [(i, (i + k) % shards) for i in range(shards)],
        )
        for k in range(1, shards)
    ]
    return lax.dynamic_slice_in_dim(rows, at * own, own, 1) + sum(parts)


def vector_gather_steps(rows):
    size, me = lax.axis_size("shard"), lax.axis_index("shard")
    others = yield [
        lax.ppermute(rows, "shard", [(i, (i - k) % size) for i in range(size)])
        for k in range(1, size)
    ]
    parts = [rows, *others]
    twice = jnp.concatenate(parts + parts, axis=1)
    own = rows.shape[1]
    return lax.dynamic_slice_in_dim(twice, ((size - me) % size) * own, size * own, 1)


def rotary_tables(length):
    half = HD // 2
    positions = jnp.arange(length, dtype=F32)
    inverse = 10000.0 ** (-2.0 * jnp.arange(half, dtype=F32) / HD)
    angles = positions[:, None] * inverse[None, :]
    cos, sin = jnp.cos(angles), jnp.sin(angles)
    return jnp.concatenate([cos, cos], axis=1), jnp.concatenate([-sin, sin], axis=1)


def rotate(values, cos, sin):
    return values * cos + pltpu.roll(values, HD // 2, 1) * sin


def window(step, seg_col, seg_row):
    low, high = max(0, step - 1) * WIN, (step + 1) * WIN
    shape = (WIN, high - low)
    row = lax.broadcasted_iota(jnp.int32, shape, 0) + step * WIN
    col = lax.broadcasted_iota(jnp.int32, shape, 1) + low
    near = (row >= col) & (row - col < WIN)
    same = seg_col[0, step * WIN : (step + 1) * WIN, :] == seg_row[0, :, low:high]
    return low, high, near & same


def attend_kernel(parts, z_ref, *refs):
    x_refs, w_refs = refs[:parts], refs[parts : 2 * parts]
    cos_ref, sin_ref, col_ref, row_ref, context_ref, qkv_ref, lse_ref, lin_ref = refs[2 * parts :]
    length, width = context_ref.shape
    tile = min(length, 256)

    @pl.loop(0, length // tile)
    def _(t):
        rows = pl.ds(pl.multiple_of(t * tile, tile), tile)
        total = mm(x_refs[0][rows, :], w_refs[0][...])
        for x, w in zip(x_refs[1:], w_refs[1:]):
            total += mm(x[rows, :], w[...])
        lin_ref[rows, :] = total

    cos, sin = cos_ref[...], sin_ref[...]
    for h in range(width // HD):
        q_at, k_at, v_at = (slice(i * width + h * HD, i * width + (h + 1) * HD) for i in range(3))
        qkv_ref[:, q_at] = rotate(lin_ref[:, q_at], cos, sin).astype(BF)
        qkv_ref[:, k_at] = rotate(lin_ref[:, k_at], cos, sin).astype(BF)
        qkv_ref[:, v_at] = lin_ref[:, v_at].astype(BF)
    for step in range(length // WIN):
        low, high, allowed = window(step, col_ref, row_ref)
        rows = slice(step * WIN, (step + 1) * WIN)
        for h in range(width // HD):
            q_at, k_at, v_at = (
                slice(i * width + h * HD, i * width + (h + 1) * HD) for i in range(3)
            )
            scores = mm_nt(qkv_ref[rows, q_at], qkv_ref[low:high, k_at]) * HD**-0.5
            scores = jnp.where(allowed, scores, -1e30)
            peak = jnp.max(scores, axis=1, keepdims=True)
            raw = jnp.exp(scores - peak)
            total = jnp.sum(raw, axis=1, keepdims=True)
            probs = (raw * (1.0 / total)).astype(BF)
            context_ref[rows, h * HD : (h + 1) * HD] = mm(probs, qkv_ref[low:high, v_at]).astype(BF)
            lse_ref[rows, h : h + 1] = peak + jnp.log(total)


def attend(shard, both, weights, tables, seg):
    parts = len(weights)
    rows, depth = both.shape
    length = tables[0].shape[0]
    wide = weights[0].shape[1]
    width = wide // 3
    piece = depth // parts
    whole = lambda *shape: pl.BlockSpec(shape, lambda s, z: (0,) * len(shape))
    take = lambda k: pl.BlockSpec((length, piece), lambda s, z: (s, (z[0] + parts - k) % parts))
    by_seq = lambda cols: pl.BlockSpec((length, cols), lambda s, z: (s, 0))
    return pl.pallas_call(
        functools.partial(attend_kernel, parts),
        grid_spec=pltpu.PrefetchScalarGridSpec(
            num_scalar_prefetch=1,
            grid=(rows // length,),
            in_specs=[take(k) for k in range(parts)]
            + [whole(piece, wide)] * parts
            + [whole(length, HD)] * 2
            + [
                pl.BlockSpec((1, length, 1), lambda s, z: (s, 0, 0)),
                pl.BlockSpec((1, 1, length), lambda s, z: (s, 0, 0)),
            ],
            out_specs=[by_seq(width), by_seq(wide), by_seq(width // HD)],
            scratch_shapes=[pltpu.VMEM((length, wide), F32)],
        ),
        out_shape=[
            jax.ShapeDtypeStruct((rows, width), BF),
            jax.ShapeDtypeStruct((rows, wide), BF),
            jax.ShapeDtypeStruct((rows, width // HD), F32),
        ],
        compiler_params=pltpu.CompilerParams(vmem_limit_bytes=40 << 20),
        cost_estimate=pl.CostEstimate(
            flops=2 * rows * depth * wide + 4 * rows * 2 * WIN * width,
            bytes_accessed=2 * (rows * depth + depth * wide + 2 * rows * wide),
            transcendentals=rows * 2 * WIN * width // HD,
        ),
        name="attend",
    )(shard, *[both] * parts, *weights, *tables, *seg)


def attend_back_kernel(
    own_ref, other_ref, out_ref, qkv_ref, lse_ref, x_ref, cos_ref, sin_ref, col_ref, row_ref,
    lin_ref, top_ref, bottom_ref, kept_ref, context_ref, keys_ref, values_ref,
):
    length, wide = qkv_ref.shape
    width = wide // 3
    seq = pl.program_id(0)
    tile = min(length, 256)

    @pl.loop(0, length // tile)
    def _(t):
        rows = pl.ds(pl.multiple_of(t * tile, tile), tile)

        @pl.when(seq == 0)
        def _():
            context_ref[rows, :] = mm_nt(own_ref[rows, :], out_ref[...]).astype(BF)

        @pl.when(seq > 0)
        def _():
            context_ref[rows, :] = mm_nt(other_ref[rows, :], out_ref[...]).astype(BF)

    cos, sin = cos_ref[...], sin_ref[...]
    scale = HD**-0.5
    for h in range(width // HD):
        q_at, k_at, v_at = (slice(i * width + h * HD, i * width + (h + 1) * HD) for i in range(3))
        head = slice(h * HD, (h + 1) * HD)
        keys_ref[...] = jnp.zeros_like(keys_ref)
        values_ref[...] = jnp.zeros_like(values_ref)
        for step in range(length // WIN):
            low, high, allowed = window(step, col_ref, row_ref)
            rows = slice(step * WIN, (step + 1) * WIN)
            queries, keys = qkv_ref[rows, q_at], qkv_ref[low:high, k_at]
            grad = context_ref[rows, head]
            scores = jnp.where(allowed, mm_nt(queries, keys) * scale, -1e30)
            probs = jnp.exp(scores - lse_ref[rows, h : h + 1])
            values_ref[low:high, :] += mm_tn(probs.astype(BF), grad)
            grad_probs = mm_nt(grad, qkv_ref[low:high, v_at])
            inner = jnp.sum(probs * grad_probs, axis=1, keepdims=True)
            grad_scores = (probs * (grad_probs - inner)).astype(BF)
            grad_queries = mm(grad_scores, keys) * scale
            keys_ref[low:high, :] += mm_tn(grad_scores, queries)
            lin_ref[rows, q_at] = rotate(grad_queries, cos[rows], -sin[rows]).astype(BF)
        lin_ref[:, k_at] = rotate(keys_ref[...] * scale, cos, -sin).astype(BF)
        lin_ref[:, v_at] = values_ref[...].astype(BF)
    kept_ref[pl.ds(pl.multiple_of(seq * length, length), length), :] = lin_ref[...]

    @pl.when(seq == pl.num_programs(0) - 1)
    def _():
        half = top_ref.shape[0]
        step = 256
        for n, ref in enumerate((top_ref, bottom_ref)):

            @pl.loop(0, half // step)
            def _(t):
                cols = pl.ds(pl.multiple_of(n * half + t * step, step), step)
                rows = pl.ds(pl.multiple_of(t * step, step), step)
                ref[rows, :] = mm(x_ref[cols, :], kept_ref[...]).astype(BF)


def attend_back(grad, out_w, qkv, lse, turned, tables, seg):
    depth, rows = turned.shape
    length = tables[0].shape[0]
    wide = qkv.shape[1]
    width = wide // 3
    whole = lambda *shape: pl.BlockSpec(shape, lambda s: (0,) * len(shape))
    by_seq = lambda cols: pl.BlockSpec((length, cols), lambda s: (s, 0))
    return pl.pallas_call(
        attend_back_kernel,
        grid=(rows // length,),
        in_specs=[whole(length, depth)] * 2
        + [whole(width, depth), by_seq(wide), by_seq(width // HD)]
        + [whole(depth, rows), whole(length, HD), whole(length, HD)]
        + [
            pl.BlockSpec((1, length, 1), lambda s: (s, 0, 0)),
            pl.BlockSpec((1, 1, length), lambda s: (s, 0, 0)),
        ],
        out_specs=[by_seq(wide), whole(depth // 2, wide), whole(depth // 2, wide)],
        scratch_shapes=[
            pltpu.VMEM((rows, wide), BF),
            pltpu.VMEM((length, width), BF),
            pltpu.VMEM((length, HD), F32),
            pltpu.VMEM((length, HD), F32),
        ],
        out_shape=[
            jax.ShapeDtypeStruct((rows, wide), BF),
            jax.ShapeDtypeStruct((depth // 2, wide), BF),
            jax.ShapeDtypeStruct((depth // 2, wide), BF),
        ],
        compiler_params=pltpu.CompilerParams(vmem_limit_bytes=48 << 20),
        cost_estimate=pl.CostEstimate(
            flops=2 * rows * depth * (wide + width) + 10 * rows * 2 * WIN * width,
            bytes_accessed=2 * (2 * rows * depth + depth * (wide + width) + 2 * rows * wide),
            transcendentals=rows * 2 * WIN * width // HD,
        ),
        name="attend_back",
    )(*grad, out_w, qkv, lse, turned, *tables, *seg)


def normed_back_kernel(blocks, parts, z_ref, *refs):
    lins, weights, (own_ref, other_ref) = refs[:blocks], refs[blocks:-2], refs[-2:]
    piece = own_ref.shape[1] // parts
    own = pl.program_id(0) < pl.num_programs(0) // 2
    for k in range(parts):
        total = mm_nt(lins[0][...], weights[k][...])
        for n in range(1, blocks):
            total += mm_nt(lins[n][...], weights[n * parts + k][...])
        at = pl.multiple_of(((z_ref[0] + parts - k) % parts) * piece, piece)

        @pl.when(own)
        def _():
            own_ref[:, pl.ds(at, piece)] = total

        @pl.when(jnp.logical_not(own))
        def _():
            other_ref[:, pl.ds(at, piece)] = total.astype(BF)


def normed_back(shard, lins, weights, depth):
    parts = len(weights[0])
    rows, wide = lins[0].shape
    tile = min(rows // 2, 256)
    steps = rows // 2 // tile
    flat = [w for block in weights for w in block]
    return pl.pallas_call(
        functools.partial(normed_back_kernel, len(lins), parts),
        grid_spec=pltpu.PrefetchScalarGridSpec(
            num_scalar_prefetch=1,
            grid=(rows // tile,),
            in_specs=[pl.BlockSpec((tile, wide), lambda s, z: (s, 0))] * len(lins)
            + [
                pl.BlockSpec(flat[0].shape, lambda s, z: (0, 0), pipeline_mode=pl.Buffered(1))
            ] * len(flat),
            out_specs=[
                pl.BlockSpec((tile, depth), lambda s, z: (jnp.minimum(s, steps - 1), 0)),
                pl.BlockSpec((tile, depth), lambda s, z: (jnp.maximum(s - steps, 0), 0)),
            ],
        ),
        out_shape=[
            jax.ShapeDtypeStruct((rows // 2, depth), F32),
            jax.ShapeDtypeStruct((rows // 2, depth), BF),
        ],
        compiler_params=pltpu.CompilerParams(vmem_limit_bytes=48 << 20),
        cost_estimate=pl.CostEstimate(
            flops=2 * rows * depth * wide * len(lins),
            bytes_accessed=2 * len(lins) * wide * (rows + depth) + 4 * rows * depth,
            transcendentals=0,
        ),
        name="normed_back",
    )(shard, *lins, *flat)


def plan_slots(route_ids, gate_values):
    hit_mask = route_ids == 0
    hit = jnp.any(hit_mask, axis=-1)
    weight = jnp.sum(jnp.where(hit_mask, gate_values, 0.0), axis=-1)
    ids = jnp.arange(route_ids.shape[0], dtype=jnp.int32)
    earlier = (ids[None, :] < ids[:, None]) & hit[None, :]
    order = jnp.sum(earlier.astype(jnp.int32), axis=1)
    kept = hit & (order < CAP)
    slots = jnp.arange(CAP, dtype=jnp.int32)
    table = (order[None, :] == slots[:, None]) & kept[None, :]
    return table, jnp.where(kept, weight, 0.0)


def norm_back(grad_normed, source, root, gain):
    scaled = grad_normed * gain
    grad_gain = jnp.sum(grad_normed * source * root, axis=0)
    mean = jnp.mean(scaled * source, axis=-1, keepdims=True)
    return grad_gain, root * scaled - source * (root * root * root) * mean


def place_kernel(columns, me_ref, same_ref, other_ref, *out_refs):
    even = me_ref[0] % 2 == 0
    same, other = same_ref[...], other_ref[...]
    blocks = (jnp.where(even, same, other).astype(F32), jnp.where(even, other, same).astype(F32))
    width = same.shape[1] // len(out_refs)
    for i, ref in enumerate(out_refs):
        for n, block in enumerate(blocks):
            part = block[:, i * width : (i + 1) * width]
            if columns:
                ref[:, n * width : (n + 1) * width] = part
            else:
                ref[n * same.shape[0] : (n + 1) * same.shape[0], :] = part


def place(me, same, other, height, width, columns):
    size, total = lax.axis_size("rep"), same.shape[1]
    spec = pl.BlockSpec((height, total), lambda d, me: (d, 0))
    shape = (height, size * width) if columns else (size * height, width)
    at = lambda d, me: jnp.bitwise_xor(d, me[0] // 2)
    if columns:
        out_spec = pl.BlockSpec((height, 2 * width), lambda d, me: (0, at(d, me)))
    else:
        out_spec = pl.BlockSpec((2 * height, width), lambda d, me: (at(d, me), 0))
    count = total // width
    return pl.pallas_call(
        functools.partial(place_kernel, columns),
        grid_spec=pltpu.PrefetchScalarGridSpec(
            num_scalar_prefetch=1,
            grid=(size // 2,),
            in_specs=[spec, spec],
            out_specs=[out_spec] * count,
        ),
        out_shape=[jax.ShapeDtypeStruct(shape, F32)] * count,
        compiler_params=pltpu.CompilerParams(vmem_limit_bytes=32 << 20),
        cost_estimate=pl.CostEstimate(
            flops=0, bytes_accessed=6 * size * height * total, transcendentals=0
        ),
        name="place",
    )(me, same, other)


def place_turned_kernel(me_ref, same_ref, other_ref, out_ref):
    odd = me_ref[0] % 2
    first = jnp.where(odd == 0, same_ref[...], other_ref[...])
    second = jnp.where(odd == 0, other_ref[...], same_ref[...])
    out_ref[...] = jnp.concatenate([first, second], axis=0).T.astype(F32)


def place_turned(me, same, other, height):
    size, width = lax.axis_size("rep"), same.shape[1]
    if 2 * height % 128:
        return place(me, same, other, height, width, False)[0].T
    spec = pl.BlockSpec((height, width), lambda j, me: (jnp.bitwise_xor(j, me[0] // 2), 0))
    return pl.pallas_call(
        place_turned_kernel,
        grid_spec=pltpu.PrefetchScalarGridSpec(
            num_scalar_prefetch=1,
            grid=(size // 2,),
            in_specs=[spec, spec],
            out_specs=pl.BlockSpec((width, 2 * height), lambda j, me: (0, j)),
        ),
        out_shape=jax.ShapeDtypeStruct((width, size * height), F32),
        compiler_params=pltpu.CompilerParams(vmem_limit_bytes=32 << 20),
        cost_estimate=pl.CostEstimate(
            flops=0, bytes_accessed=12 * same.size, transcendentals=0
        ),
        name="place_turned",
    )(me, same, other)


def turn_kernel(in_ref, out_ref):
    out_ref[...] = in_ref[...].T


def turn(value):
    rows, width = value.shape
    tile = min(width, 512)
    return pl.pallas_call(
        turn_kernel,
        grid=(width // tile,),
        in_specs=[pl.BlockSpec((rows, tile), lambda i: (0, i))],
        out_specs=pl.BlockSpec((tile, rows), lambda i: (i, 0)),
        out_shape=jax.ShapeDtypeStruct((width, rows), value.dtype),
        cost_estimate=pl.CostEstimate(flops=0, bytes_accessed=4 * value.size, transcendentals=0),
        name="turn",
    )(value)


def widen_kernel(in_ref, out_ref):
    out_ref[...] = in_ref[...].astype(F32)


def widen(value):
    rows, width = value.shape
    tile = rows // 4
    spec = pl.BlockSpec((tile, width), lambda i: (i, 0))
    return pl.pallas_call(
        widen_kernel,
        grid=(4,),
        in_specs=[spec],
        out_specs=spec,
        out_shape=jax.ShapeDtypeStruct(value.shape, F32),
        compiler_params=pltpu.CompilerParams(vmem_limit_bytes=32 << 20),
        cost_estimate=pl.CostEstimate(flops=0, bytes_accessed=6 * value.size, transcendentals=0),
        name="widen",
    )(value)


def per_device(
    layer_input,
    gain_attn,
    w_query,
    w_key,
    w_value,
    w_out,
    gain_mlp,
    w_gate,
    w_up,
    w_down,
    segments,
    attn_route,
    attn_gate,
    mlp_route,
    mlp_gate,
    cotangent,
):
    length = layer_input.shape[0]
    size, shards = lax.axis_size("rep"), lax.axis_size("shard")
    me = lax.axis_index("rep")
    whoami = me.astype(jnp.int32).reshape(1)
    shard = lax.axis_index("shard").astype(jnp.int32).reshape(1)
    block = w_query.shape[1] // size
    units = w_gate.shape[1] // size
    own = gain_attn.shape[0]
    offsets = chip_offsets()
    staged = len(chip_bits()) == 2

    def columns(weight, d, width):
        return lax.dynamic_slice_in_dim(weight, jnp.bitwise_xor(me, d) * width, width, 1)

    def rows_of(weight, height):
        return lax.dynamic_slice_in_dim(weight, me * height, height, 0)

    def local(d):
        return jnp.concatenate([columns(w, d, block) for w in (w_query, w_key, w_value)], axis=1)

    inputs = layer_input.astype(F32)
    root_one = lax.rsqrt(jnp.mean(inputs * inputs, axis=-1, keepdims=True) + EPSILON)
    tables = rotary_tables(length)
    ring = [(i, (i + 1) % shards) for i in range(shards)]
    piece = local(0)
    qkv_w = {d: [local(d)] for d in offsets}
    flows, context, saved = [], {}, {}
    gain_flow = Flow(vector_gather_steps(jnp.stack([gain_attn, gain_mlp])))
    piece, seg_other, own_gate_up = stage(
        [gain_flow],
        (
            lax.ppermute(piece, "shard", ring),
            swap(segments, 1),
            jnp.concatenate([columns(w_gate, 0, units), columns(w_up, 0, units)], axis=1),
        ),
    )
    gain_one, gain_two = gain_flow.result.astype(F32)
    normed = (inputs * root_one * gain_one).astype(BF)
    seg = jnp.concatenate([segments, seg_other], axis=0)
    seg = (seg[:, :, None], seg[:, None, :])
    other = swap(normed, 1)
    for step in range(1, shards):
        qkv_w[0].append(piece)
        flows.append(Flow(gather_steps(piece, lambda d, b: qkv_w[d].append(b))))
        if step < shards - 1:
            piece, other = stage(flows, (lax.ppermute(piece, "shard", ring), other))
    own_out, own_gate_up, own_down, qkv_w[0][-1] = lax.optimization_barrier(
        (rows_of(w_out, block), own_gate_up, rows_of(w_down, units), qkv_w[0][-1])
    )
    own_out = lax.all_gather(own_out, "shard", axis=1, tiled=True)
    both = jnp.concatenate([normed, other], axis=0)

    def run(d):
        context[d], *saved[d] = attend(shard, both, qkv_w[d], tables, seg)
        return context[d]

    context[0], own_out, turned = stage(flows, (run(0), own_out, turn(both)))
    gate_up = lax.all_gather(own_gate_up, "shard", axis=0, tiled=True)
    down = lax.all_gather(own_down, "shard", axis=1, tiled=True)
    early = offsets[1:2] if staged else []
    early = stage(flows, [run(d) for d in early])
    for flow in flows:
        finish(flow)
    out_flow = Flow(gather_steps(own_out))
    rest = [d for d in offsets if d not in context]
    stage([out_flow], [run(d) for d in rest])
    out_w = finish(out_flow)

    table, mix = plan_slots(mlp_route, mlp_gate)
    pick = table.astype(BF)
    upstream = cotangent.astype(F32)
    slot_weight = jnp.sum(jnp.where(table, mix[None, :], 0.0), axis=1)[:, None]
    slot_grad = (mm(pick, cotangent) * slot_weight).astype(BF)

    all_context = jnp.concatenate([context[d] for d in offsets], axis=1)
    all_out = jnp.concatenate([out_w[d] for d in offsets], axis=0)
    projected = mm(all_context, all_out)
    projected = projected[:length] + swap(projected[length:].astype(BF), 1).astype(F32)
    attn_weight = jnp.sum(jnp.where(attn_route == 0, attn_gate, 0.0), axis=-1)[:, None]
    hidden = inputs + projected * attn_weight
    root_two = lax.rsqrt(jnp.mean(hidden * hidden, axis=-1, keepdims=True) + EPSILON)
    normed_two = (hidden * root_two * gain_two).astype(BF)

    dispatched = gather_rows(mm(pick, normed_two).astype(BF), 0)
    act = mm(dispatched, gate_up)
    slot_grad, act = lax.optimization_barrier((slot_grad, act))
    all_slot_grad = gather_rows(slot_grad, 0)
    gate_act, up_act = act[:, :units], act[:, units:]
    sigmoid = jax.nn.sigmoid(gate_act)
    silu = gate_act * sigmoid
    inner = (silu * up_act).astype(BF)
    expert_flow = Flow(plane_sum_steps(mm(inner, down).astype(BF)))
    grad_inner = mm_nt(all_slot_grad, down)
    grad_gate_act = (grad_inner * up_act * sigmoid * (1.0 + gate_act * (1.0 - sigmoid))).astype(BF)
    grad_up_act = (grad_inner * silu).astype(BF)
    grad_act = jnp.concatenate([grad_gate_act, grad_up_act], axis=1)
    grad_gate, back = lax.optimization_barrier(
        (mm_tn(grad_gate_act, dispatched).astype(BF), mm_nt(grad_act, gate_up).astype(BF))
    )
    grad_disp, grad_up_act, inner = stage([expert_flow], (reduce_rows(back, 1), grad_up_act, inner))
    grad_normed_two = mm_tn(pick, grad_disp)
    grad_gain_two, through = norm_back(grad_normed_two, hidden, root_two, gain_two)
    grad_hidden = upstream + through

    grad_projected = (grad_hidden * attn_weight).astype(BF)
    both_grad = [grad_projected, swap(grad_projected, 1)]
    lins, grad_qkv_w = {}, {}

    def run_back(*ds):
        for d in ds:
            lins[d], *grad_qkv_w[d] = attend_back(
                both_grad, out_w[d], *saved[d], turned, tables, seg
            )
        return [(lins[d], grad_qkv_w[d]) for d in ds]

    def keep(ds, values):
        for d, (lin, grad) in zip(ds, values):
            lins[d], grad_qkv_w[d] = lin, grad

    far, near = offsets[-1:], offsets[1:-1]
    values, both_grad, grad_up_act, inner = stage(
        [expert_flow], (run_back(*far), both_grad, grad_up_act, inner)
    )
    keep(far, values)
    grad_up, both_grad = lax.optimization_barrier(
        (mm_tn(grad_up_act, dispatched).astype(BF), both_grad)
    )
    qkv_flow = Flow(scatter_steps(grad_qkv_w))
    grad_down = mm_tn(inner, all_slot_grad).astype(BF)
    values, both_grad, grad_down, expert_out = stage(
        [qkv_flow], (run_back(*near), both_grad, grad_down, finish(expert_flow))
    )
    keep(near, values)
    sums = [
        lax.psum_scatter(g, "shard", scatter_dimension=1, tiled=True)
        for g in (grad_gate, grad_up, grad_down)
    ]
    output = (hidden + mm_tn(pick, expert_out) * mix[:, None]).astype(BF)
    values, grad_out_w, output = stage(
        [qkv_flow], (run_back(0), mm_tn(all_context, jnp.concatenate(both_grad, axis=0)).astype(BF), output)
    )
    keep([0], values)
    grad_normed = normed_back(
        shard, [lins[d] for d in offsets], [qkv_w[d] for d in offsets], both.shape[1]
    )
    sums[0], sums[1], grad_normed, grad_out_w = stage(
        [qkv_flow], (sums[0], sums[1], grad_normed, grad_out_w)
    )
    own_grad_qkv, sums[2] = lax.optimization_barrier((finish(qkv_flow), sums[2]))
    sum_qkv = lax.psum_scatter(own_grad_qkv, "shard", scatter_dimension=0, tiled=True)

    out_blocks = {d: halves(grad_out_w[i * block : (i + 1) * block]) for i, d in enumerate(offsets)}
    out_flow, gate_flow = Flow(scatter_steps(out_blocks)), Flow(copies_steps(sums[0]))
    other_normed, up_sum = stage(
        [out_flow, gate_flow], (swap(grad_normed[1], 1), sums[1])
    )
    grad_normed = grad_normed[0] + other_normed.astype(F32)
    grad_gain_one, first = norm_back(grad_normed, inputs, root_one, gain_one)
    grad_input = (grad_hidden + first).astype(BF)
    grad_input, gains, up_sum = stage(
        [out_flow, gate_flow],
        (grad_input, jnp.stack([grad_gain_one, grad_gain_two]), up_sum),
    )
    gain_flow, up_flow = Flow(vector_sum_steps(gains)), Flow(copies_steps(up_sum))
    sum_qkv = stage([out_flow, gate_flow, up_flow, gain_flow], sum_qkv)
    sum_out = lax.psum_scatter(finish(out_flow), "shard", scatter_dimension=1, tiled=True)
    qkv_flow = Flow(copies_steps(sum_qkv))
    grad_gate = place_turned(whoami, *finish(gate_flow), units)
    grad_gate, sum_out = stage([up_flow, qkv_flow, gain_flow], (grad_gate, sum_out))
    down_sum, sum_out = lax.optimization_barrier((sums[2], sum_out))
    all_down = lax.all_gather(down_sum, "rep", axis=0, tiled=True)
    out_flow = Flow(copies_steps(sum_out, straight_steps))
    stage([up_flow, qkv_flow, out_flow, gain_flow])
    grad_up = place_turned(whoami, *finish(up_flow), units)
    grad_up = stage([qkv_flow, out_flow, gain_flow], grad_up)
    grad_query, grad_key, grad_value = place(whoami, *finish(qkv_flow), own, block, True)
    (grad_out,) = place(whoami, *finish(out_flow), block, own, False)
    grad_down = widen(all_down)
    gain_grads = finish(gain_flow)
    return (
        output,
        grad_input,
        gain_grads[0],
        grad_query,
        grad_key,
        grad_value,
        grad_out,
        gain_grads[1],
        grad_gate,
        grad_up,
        grad_down,
    )


def solution(mesh):
    tokens = P(("rep", "shard"), None)
    tall, wide, vector = P("shard", None), P(None, "shard"), P("shard")
    weights = (vector, tall, tall, tall, wide, vector, tall, tall, wide)
    return jax.shard_map(
        per_device,
        mesh=mesh,
        in_specs=(tokens, *weights) + (tokens,) * 6,
        out_specs=(tokens, tokens, *weights),
        check_vma=False,
    )
```

```python
import functools

import jax
import jax.numpy as jnp
from jax import lax
from jax.experimental import pallas as pl
from jax.experimental.pallas import tpu as pltpu
from jax.sharding import PartitionSpec as P

HEADS = 16
HD = 128
WIN = 256
CAP = 128
EPSILON = 1e-05
BF = jnp.bfloat16
F32 = jnp.float32


def mm(left, right):
    return jnp.dot(left, right, preferred_element_type=F32)


def mm_nt(left, right):
    return lax.dot_general(left, right, (((1,), (1,)), ((), ())), preferred_element_type=F32)


def mm_tn(left, right):
    return lax.dot_general(left, right, (((0,), (0,)), ((), ())), preferred_element_type=F32)


def swap(value, bit):
    size = lax.axis_size("rep")
    return lax.ppermute(value, "rep", [(i, i ^ bit) for i in range(size)])


def chip_bits():
    size, bits, bit = lax.axis_size("rep"), [], 2
    while bit < size:
        bits.append(bit)
        bit *= 2
    return bits


def chip_offsets():
    return list(range(0, lax.axis_size("rep"), 2))


def add(left, right):
    return left.astype(F32) + right.astype(F32)


def halves(value):
    half = value.shape[0] // 2
    return value[:half], value[half:]


class Flow:
    def __init__(self, steps):
        self.steps, self.result, self.done = steps, None, False
        self.pending = next(steps)

    def advance(self, arrived):
        try:
            self.pending = self.steps.send(arrived)
        except StopIteration as end:
            self.pending, self.result, self.done = [], end.value, True


def stage(flows, extra=()):
    flows = [f for f in flows if not f.done]
    arrived, extra = lax.optimization_barrier(([f.pending for f in flows], extra))
    for flow, values in zip(flows, arrived):
        flow.advance(values)
    return extra


def finish(flow):
    while not flow.done:
        flow.advance(flow.pending)
    return flow.result


def gather_steps(value, sink=lambda offset, block: None):
    bits = chip_bits()
    if len(bits) == 2:
        one, two = bits
        half = value.shape[0] // 2
        by_one, by_two = yield [swap(value, one), swap(value, two)]
        sink(one, by_one)
        sink(two, by_two)
        top, bottom = yield [swap(by_one[:half], two), swap(by_two[half:], one)]
        far = jnp.concatenate([top, bottom], axis=0)
        sink(one ^ two, far)
        return {0: value, one: by_one, two: by_two, one ^ two: far}
    blocks = {0: value}
    for bit in bits:
        old = list(blocks.items())
        new = yield [swap(b, bit) for _, b in old]
        for (d, _), b in zip(old, new):
            blocks[d ^ bit] = b
            sink(d ^ bit, b)
    return blocks


def peers():
    return [1, *[d for d in chip_offsets() if d]]


def greet(others):
    barrier = pltpu.get_barrier_semaphore()
    for device in others.values():
        pl.semaphore_signal(barrier, inc=1, device_id={"rep": device})
    pl.semaphore_wait(barrier, len(others))


def gather_kernel(offsets, in_ref, out_ref, own_sem, send_sem, recv_sem):
    me, rows = lax.axis_index("rep"), in_ref.shape[0]
    others = {d: jnp.bitwise_xor(me, d) for d in offsets}
    spot = {d: pl.ds((d // 2 + d % 2 * len(offsets)) * rows, rows) for d in range(2 * len(offsets))}
    greet(others)
    own = pltpu.make_async_copy(in_ref, out_ref.at[spot[0]], own_sem)
    own.start()

    def send(source, offset, to):
        return pltpu.make_async_remote_copy(
            src_ref=source,
            dst_ref=out_ref.at[spot[offset]],
            send_sem=send_sem.at[offset],
            recv_sem=recv_sem.at[offset],
            device_id={"rep": others[to]},
        )

    chips = [d for d in offsets if d != 1]
    first = {d: send(in_ref, d, d) for d in [*reversed(chips), 1]}
    for copy in first.values():
        copy.start()
    second = {}
    for d in chips:
        first[d].wait_recv()
        second[d] = send(out_ref.at[spot[d]], d + 1, 1)
        second[d].start()
    first[1].wait_recv()
    for copy in second.values():
        copy.wait_recv()
    own.wait()
    for copy in [*first.values(), *second.values()]:
        copy.wait_send()


def gather_rows(value, number):
    rows, width = value.shape
    size = lax.axis_size("rep")
    return pl.pallas_call(
        functools.partial(gather_kernel, peers()),
        out_shape=jax.ShapeDtypeStruct((size * rows, width), value.dtype),
        in_specs=[pl.BlockSpec(memory_space=pltpu.VMEM)],
        out_specs=pl.BlockSpec(memory_space=pltpu.VMEM),
        scratch_shapes=[
            pltpu.SemaphoreType.DMA,
            pltpu.SemaphoreType.DMA((size,)),
            pltpu.SemaphoreType.DMA((size,)),
        ],
        compiler_params=pltpu.CompilerParams(
            collective_id=number, has_side_effects=True, vmem_limit_bytes=16 << 20
        ),
        cost_estimate=pl.CostEstimate(
            flops=0, bytes_accessed=30 * value.size * size, transcendentals=0
        ),
        name="gather_rows",
    )(value)


def reduce_kernel(offsets, in_ref, out_ref, core_ref, held_ref, chip_ref, send_sem, recv_sem):
    me, rows = lax.axis_index("rep"), out_ref.shape[0]
    others = {d: jnp.bitwise_xor(me, d) for d in offsets}
    chips = [0, *[d for d in offsets if d != 1]]
    count = len(chips)
    greet(others)

    def block(ref, i):
        return ref.at[pl.ds(i * rows, rows)]

    def send(source, target, index, to):
        return pltpu.make_async_remote_copy(
            src_ref=source,
            dst_ref=target,
            send_sem=send_sem.at[index],
            recv_sem=recv_sem.at[index],
            device_id={"rep": others[to]},
        )

    order = list(reversed(range(count)))
    core = {i: send(block(in_ref, count + i), block(core_ref, i), i, 1) for i in order}
    for copy in core.values():
        copy.start()
    chip, half = [], rows // 2

    def part(ref, i, n):
        return ref.at[pl.ds(i * rows + n * half, half)]

    def pass_on(i, n, index, to):
        chip.append(send(part(held_ref, i, n), part(chip_ref, i, n), index, to))
        chip[-1].start()
        return chip[-1]

    relay = count == 4
    for i in order:
        core[i].wait_recv()
        at = pl.ds(i * rows, rows)
        total = in_ref[at, :].astype(F32) + core_ref[at, :].astype(F32)
        held_ref[at, :] = total.astype(BF)
        if relay and i == 3:
            far = [pass_on(3, 0, count, chips[1]), pass_on(3, 1, count + 1, chips[2])]
        elif relay and i:
            pass_on(i, i - 1, count + 1 + i, chips[i])
        elif i:
            chip.append(send(block(held_ref, i), block(chip_ref, i), count + i, chips[i]))
            chip[-1].start()
    if relay:
        for i, n in ((2, 0), (1, 1)):
            far[n].wait_recv()
            at, moved = pl.ds(i * rows + n * half, half), pl.ds(3 * rows + n * half, half)
            total = held_ref[at, :].astype(F32) + chip_ref[moved, :].astype(F32)
            held_ref[at, :] = total.astype(BF)
            pass_on(i, n, count + 4 + n, chips[i])
        chip, sent = chip[2:], chip[:2]
    else:
        sent = []
    total = held_ref[pl.ds(0, rows), :].astype(F32)
    for copy in chip:
        copy.wait_recv()
    for i in range(1, 3 if relay else count):
        total += chip_ref[pl.ds(i * rows, rows), :].astype(F32)
    out_ref[...] = total.astype(BF)
    for copy in [*core.values(), *sent, *chip]:
        copy.wait_send()


def reduce_rows(partial, number):
    size = lax.axis_size("rep")
    rows, width = partial.shape[0] // size, partial.shape[1]
    half = pltpu.VMEM((size // 2 * rows, width), BF)
    return pl.pallas_call(
        functools.partial(reduce_kernel, peers()),
        out_shape=jax.ShapeDtypeStruct((rows, width), BF),
        in_specs=[pl.BlockSpec(memory_space=pltpu.VMEM)],
        out_specs=pl.BlockSpec(memory_space=pltpu.VMEM),
        scratch_shapes=[
            half,
            half,
            half,
            pltpu.SemaphoreType.DMA((size + 2,)),
            pltpu.SemaphoreType.DMA((size + 2,)),
        ],
        compiler_params=pltpu.CompilerParams(
            collective_id=number, has_side_effects=True, vmem_limit_bytes=24 << 20
        ),
        cost_estimate=pl.CostEstimate(
            flops=0, bytes_accessed=30 * partial.size, transcendentals=0
        ),
        name="reduce_rows",
    )(partial)


def jump(value, offset):
    size = lax.axis_size("rep")
    return lax.ppermute(value, "rep", [(i, i ^ offset) for i in range(size)])


def straight_steps(value):
    away = [d for d in chip_offsets() if d]
    new = yield [jump(value, d) for d in away]
    return dict(zip([0, *away], [value, *new]))


def copies_steps(value, gather=gather_steps):
    blocks = yield from gather(value)
    same = jnp.concatenate([blocks[d] for d in chip_offsets()], axis=0)
    (other,) = yield [swap(same, 1)]
    return same, other


def scatter_steps(blocks):
    bits = chip_bits()
    if len(bits) == 2:
        one, two = bits
        far = blocks[one ^ two]
        top, bottom = yield [swap(far[0], one), swap(far[1], two)]
        near_one, near_two = blocks[one], blocks[two]
        one_top, two_bottom = yield [swap(near_one[0], one), swap(near_two[1], two)]
        two_top, one_bottom = yield [
            swap(add(near_two[0], top).astype(BF), two),
            swap(add(near_one[1], bottom).astype(BF), one),
        ]
        return jnp.concatenate(
            [
                (add(blocks[0][0], one_top) + two_top.astype(F32)).astype(BF),
                (add(blocks[0][1], one_bottom) + two_bottom.astype(F32)).astype(BF),
            ],
            axis=0,
        )
    while len(blocks) < len(chip_offsets()):
        yield []
    sums = {d: jnp.concatenate(b, axis=0) for d, b in blocks.items()}
    for bit in reversed(bits):
        kept = [d for d in sorted(sums) if not d & bit]
        new = yield [swap(sums[d | bit], bit) for d in kept]
        sums = {d: add(sums[d], n).astype(BF) for d, n in zip(kept, new)}
    return sums[0]


def plane_sum_steps(partial):
    half = partial.shape[0] // 2
    (other,) = yield [swap(partial[half:], 1)]
    same = add(partial[:half], other).astype(BF)
    offsets = chip_offsets()
    rows = half // len(offsets)
    blocks = {d: same[i * rows : (i + 1) * rows] for i, d in enumerate(offsets)}
    new = yield [jump(blocks[d], d) for d in offsets if d]
    return sum((n.astype(F32) for n in new), blocks[0].astype(F32)).astype(BF)


def vector_sum_steps(rows):
    size, bit = lax.axis_size("rep"), 1
    while bit < size:
        (other,) = yield [swap(rows, bit)]
        rows, bit = rows + other, 2 * bit
    shards, at = lax.axis_size("shard"), lax.axis_index("shard")
    own = rows.shape[1] // shards
    parts = yield [
        lax.ppermute(
            lax.dynamic_slice_in_dim(rows, ((at + k) % shards) * own, own, 1),
            "shard",
            [(i, (i + k) % shards) for i in range(shards)],
        )
        for k in range(1, shards)
    ]
    return lax.dynamic_slice_in_dim(rows, at * own, own, 1) + sum(parts)


def vector_gather_steps(rows):
    size, me = lax.axis_size("shard"), lax.axis_index("shard")
    others = yield [
        lax.ppermute(rows, "shard", [(i, (i - k) % size) for i in range(size)])
        for k in range(1, size)
    ]
    parts = [rows, *others]
    twice = jnp.concatenate(parts + parts, axis=1)
    own = rows.shape[1]
    return lax.dynamic_slice_in_dim(twice, ((size - me) % size) * own, size * own, 1)


def rotary_tables(length):
    half = HD // 2
    positions = jnp.arange(length, dtype=F32)
    inverse = 10000.0 ** (-2.0 * jnp.arange(half, dtype=F32) / HD)
    angles = positions[:, None] * inverse[None, :]
    cos, sin = jnp.cos(angles), jnp.sin(angles)
    return jnp.concatenate([cos, cos], axis=1), jnp.concatenate([-sin, sin], axis=1)


def rotate(values, cos, sin):
    return values * cos + pltpu.roll(values, HD // 2, 1) * sin


def window(step, seg_col, seg_row):
    low, high = max(0, step - 1) * WIN, (step + 1) * WIN
    shape = (WIN, high - low)
    row = lax.broadcasted_iota(jnp.int32, shape, 0) + step * WIN
    col = lax.broadcasted_iota(jnp.int32, shape, 1) + low
    near = (row >= col) & (row - col < WIN)
    same = seg_col[0, step * WIN : (step + 1) * WIN, :] == seg_row[0, :, low:high]
    return low, high, near & same


def attend_kernel(parts, z_ref, *refs):
    x_refs, w_refs = refs[:parts], refs[parts : 2 * parts]
    cos_ref, sin_ref, col_ref, row_ref, context_ref, qkv_ref, lse_ref, lin_ref = refs[2 * parts :]
    length, width = context_ref.shape
    tile = min(length, 256)

    @pl.loop(0, length // tile)
    def _(t):
        rows = pl.ds(pl.multiple_of(t * tile, tile), tile)
        total = mm(x_refs[0][rows, :], w_refs[0][...])
        for x, w in zip(x_refs[1:], w_refs[1:]):
            total += mm(x[rows, :], w[...])
        lin_ref[rows, :] = total

    cos, sin = cos_ref[...], sin_ref[...]
    for h in range(width // HD):
        q_at, k_at, v_at = (slice(i * width + h * HD, i * width + (h + 1) * HD) for i in range(3))
        qkv_ref[:, q_at] = rotate(lin_ref[:, q_at], cos, sin).astype(BF)
        qkv_ref[:, k_at] = rotate(lin_ref[:, k_at], cos, sin).astype(BF)
        qkv_ref[:, v_at] = lin_ref[:, v_at].astype(BF)
    for step in range(length // WIN):
        low, high, allowed = window(step, col_ref, row_ref)
        rows = slice(step * WIN, (step + 1) * WIN)
        for h in range(width // HD):
            q_at, k_at, v_at = (
                slice(i * width + h * HD, i * width + (h + 1) * HD) for i in range(3)
            )
            scores = mm_nt(qkv_ref[rows, q_at], qkv_ref[low:high, k_at]) * HD**-0.5
            scores = jnp.where(allowed, scores, -1e30)
            peak = jnp.max(scores, axis=1, keepdims=True)
            raw = jnp.exp(scores - peak)
            total = jnp.sum(raw, axis=1, keepdims=True)
            probs = (raw * (1.0 / total)).astype(BF)
            context_ref[rows, h * HD : (h + 1) * HD] = mm(probs, qkv_ref[low:high, v_at]).astype(BF)
            lse_ref[rows, h : h + 1] = peak + jnp.log(total)


def attend(shard, both, weights, tables, seg):
    parts = len(weights)
    rows, depth = both.shape
    length = tables[0].shape[0]
    wide = weights[0].shape[1]
    width = wide // 3
    piece = depth // parts
    whole = lambda *shape: pl.BlockSpec(shape, lambda s, z: (0,) * len(shape))
    take = lambda k: pl.BlockSpec((length, piece), lambda s, z: (s, (z[0] + parts - k) % parts))
    by_seq = lambda cols: pl.BlockSpec((length, cols), lambda s, z: (s, 0))
    return pl.pallas_call(
        functools.partial(attend_kernel, parts),
        grid_spec=pltpu.PrefetchScalarGridSpec(
            num_scalar_prefetch=1,
            grid=(rows // length,),
            in_specs=[take(k) for k in range(parts)]
            + [whole(piece, wide)] * parts
            + [whole(length, HD)] * 2
            + [
                pl.BlockSpec((1, length, 1), lambda s, z: (s, 0, 0)),
                pl.BlockSpec((1, 1, length), lambda s, z: (s, 0, 0)),
            ],
            out_specs=[by_seq(width), by_seq(wide), by_seq(width // HD)],
            scratch_shapes=[pltpu.VMEM((length, wide), F32)],
        ),
        out_shape=[
            jax.ShapeDtypeStruct((rows, width), BF),
            jax.ShapeDtypeStruct((rows, wide), BF),
            jax.ShapeDtypeStruct((rows, width // HD), F32),
        ],
        compiler_params=pltpu.CompilerParams(vmem_limit_bytes=40 << 20),
        cost_estimate=pl.CostEstimate(
            flops=2 * rows * depth * wide + 4 * rows * 2 * WIN * width,
            bytes_accessed=2 * (rows * depth + depth * wide + 2 * rows * wide),
            transcendentals=rows * 2 * WIN * width // HD,
        ),
        name="attend",
    )(shard, *[both] * parts, *weights, *tables, *seg)


def attend_back_kernel(
    own_ref, other_ref, out_ref, qkv_ref, lse_ref, x_ref, cos_ref, sin_ref, col_ref, row_ref,
    lin_ref, top_ref, bottom_ref, kept_ref, context_ref, keys_ref, values_ref,
):
    length, wide = qkv_ref.shape
    width = wide // 3
    seq = pl.program_id(0)
    tile = min(length, 256)

    @pl.loop(0, length // tile)
    def _(t):
        rows = pl.ds(pl.multiple_of(t * tile, tile), tile)

        @pl.when(seq == 0)
        def _():
            context_ref[rows, :] = mm_nt(own_ref[rows, :], out_ref[...]).astype(BF)

        @pl.when(seq > 0)
        def _():
            context_ref[rows, :] = mm_nt(other_ref[rows, :], out_ref[...]).astype(BF)

    cos, sin = cos_ref[...], sin_ref[...]
    scale = HD**-0.5
    for h in range(width // HD):
        q_at, k_at, v_at = (slice(i * width + h * HD, i * width + (h + 1) * HD) for i in range(3))
        head = slice(h * HD, (h + 1) * HD)
        keys_ref[...] = jnp.zeros_like(keys_ref)
        values_ref[...] = jnp.zeros_like(values_ref)
        for step in range(length // WIN):
            low, high, allowed = window(step, col_ref, row_ref)
            rows = slice(step * WIN, (step + 1) * WIN)
            queries, keys = qkv_ref[rows, q_at], qkv_ref[low:high, k_at]
            grad = context_ref[rows, head]
            scores = jnp.where(allowed, mm_nt(queries, keys) * scale, -1e30)
            probs = jnp.exp(scores - lse_ref[rows, h : h + 1])
            values_ref[low:high, :] += mm_tn(probs.astype(BF), grad)
            grad_probs = mm_nt(grad, qkv_ref[low:high, v_at])
            inner = jnp.sum(probs * grad_probs, axis=1, keepdims=True)
            grad_scores = (probs * (grad_probs - inner)).astype(BF)
            grad_queries = mm(grad_scores, keys) * scale
            keys_ref[low:high, :] += mm_tn(grad_scores, queries)
            lin_ref[rows, q_at] = rotate(grad_queries, cos[rows], -sin[rows]).astype(BF)
        lin_ref[:, k_at] = rotate(keys_ref[...] * scale, cos, -sin).astype(BF)
        lin_ref[:, v_at] = values_ref[...].astype(BF)
    kept_ref[pl.ds(pl.multiple_of(seq * length, length), length), :] = lin_ref[...]

    @pl.when(seq == pl.num_programs(0) - 1)
    def _():
        half = top_ref.shape[0]
        step = 256
        for n, ref in enumerate((top_ref, bottom_ref)):

            @pl.loop(0, half // step)
            def _(t):
                cols = pl.ds(pl.multiple_of(n * half + t * step, step), step)
                rows = pl.ds(pl.multiple_of(t * step, step), step)
                ref[rows, :] = mm_tn(x_ref[:, cols], kept_ref[...]).astype(BF)


def attend_back(grad, out_w, qkv, lse, both, tables, seg):
    rows, depth = both.shape
    length = tables[0].shape[0]
    wide = qkv.shape[1]
    width = wide // 3
    whole = lambda *shape: pl.BlockSpec(shape, lambda s: (0,) * len(shape))
    by_seq = lambda cols: pl.BlockSpec((length, cols), lambda s: (s, 0))
    return pl.pallas_call(
        attend_back_kernel,
        grid=(rows // length,),
        in_specs=[whole(length, depth)] * 2
        + [whole(width, depth), by_seq(wide), by_seq(width // HD)]
        + [whole(rows, depth), whole(length, HD), whole(length, HD)]
        + [
            pl.BlockSpec((1, length, 1), lambda s: (s, 0, 0)),
            pl.BlockSpec((1, 1, length), lambda s: (s, 0, 0)),
        ],
        out_specs=[by_seq(wide), whole(depth // 2, wide), whole(depth // 2, wide)],
        scratch_shapes=[
            pltpu.VMEM((rows, wide), BF),
            pltpu.VMEM((length, width), BF),
            pltpu.VMEM((length, HD), F32),
            pltpu.VMEM((length, HD), F32),
        ],
        out_shape=[
            jax.ShapeDtypeStruct((rows, wide), BF),
            jax.ShapeDtypeStruct((depth // 2, wide), BF),
            jax.ShapeDtypeStruct((depth // 2, wide), BF),
        ],
        compiler_params=pltpu.CompilerParams(vmem_limit_bytes=48 << 20),
        cost_estimate=pl.CostEstimate(
            flops=2 * rows * depth * (wide + width) + 10 * rows * 2 * WIN * width,
            bytes_accessed=2 * (2 * rows * depth + depth * (wide + width) + 2 * rows * wide),
            transcendentals=rows * 2 * WIN * width // HD,
        ),
        name="attend_back",
    )(*grad, out_w, qkv, lse, both, *tables, *seg)


def normed_back_kernel(blocks, parts, z_ref, *refs):
    lins, weights, (own_ref, other_ref) = refs[:blocks], refs[blocks:-2], refs[-2:]
    piece = own_ref.shape[1] // parts
    own = pl.program_id(0) < pl.num_programs(0) // 2
    for k in range(parts):
        total = mm_nt(lins[0][...], weights[k][...])
        for n in range(1, blocks):
            total += mm_nt(lins[n][...], weights[n * parts + k][...])
        at = pl.multiple_of(((z_ref[0] + parts - k) % parts) * piece, piece)

        @pl.when(own)
        def _():
            own_ref[:, pl.ds(at, piece)] = total

        @pl.when(jnp.logical_not(own))
        def _():
            other_ref[:, pl.ds(at, piece)] = total.astype(BF)


def normed_back(shard, lins, weights, depth):
    parts = len(weights[0])
    rows, wide = lins[0].shape
    tile = min(rows // 2, 256)
    steps = rows // 2 // tile
    flat = [w for block in weights for w in block]
    return pl.pallas_call(
        functools.partial(normed_back_kernel, len(lins), parts),
        grid_spec=pltpu.PrefetchScalarGridSpec(
            num_scalar_prefetch=1,
            grid=(rows // tile,),
            in_specs=[pl.BlockSpec((tile, wide), lambda s, z: (s, 0))] * len(lins)
            + [
                pl.BlockSpec(flat[0].shape, lambda s, z: (0, 0), pipeline_mode=pl.Buffered(1))
            ] * len(flat),
            out_specs=[
                pl.BlockSpec((tile, depth), lambda s, z: (jnp.minimum(s, steps - 1), 0)),
                pl.BlockSpec((tile, depth), lambda s, z: (jnp.maximum(s - steps, 0), 0)),
            ],
        ),
        out_shape=[
            jax.ShapeDtypeStruct((rows // 2, depth), F32),
            jax.ShapeDtypeStruct((rows // 2, depth), BF),
        ],
        compiler_params=pltpu.CompilerParams(vmem_limit_bytes=48 << 20),
        cost_estimate=pl.CostEstimate(
            flops=2 * rows * depth * wide * len(lins),
            bytes_accessed=2 * len(lins) * wide * (rows + depth) + 4 * rows * depth,
            transcendentals=0,
        ),
        name="normed_back",
    )(shard, *lins, *flat)


def plan_slots(route_ids, gate_values):
    hit_mask = route_ids == 0
    hit = jnp.any(hit_mask, axis=-1)
    weight = jnp.sum(jnp.where(hit_mask, gate_values, 0.0), axis=-1)
    ids = jnp.arange(route_ids.shape[0], dtype=jnp.int32)
    earlier = (ids[None, :] < ids[:, None]) & hit[None, :]
    order = jnp.sum(earlier.astype(jnp.int32), axis=1)
    kept = hit & (order < CAP)
    slots = jnp.arange(CAP, dtype=jnp.int32)
    table = (order[None, :] == slots[:, None]) & kept[None, :]
    return table, jnp.where(kept, weight, 0.0)


def norm_back(grad_normed, source, root, gain):
    scaled = grad_normed * gain
    grad_gain = jnp.sum(grad_normed * source * root, axis=0)
    mean = jnp.mean(scaled * source, axis=-1, keepdims=True)
    return grad_gain, root * scaled - source * (root * root * root) * mean


def place_kernel(columns, me_ref, same_ref, other_ref, *out_refs):
    even = me_ref[0] % 2 == 0
    same, other = same_ref[...], other_ref[...]
    blocks = (jnp.where(even, same, other).astype(F32), jnp.where(even, other, same).astype(F32))
    width = same.shape[1] // len(out_refs)
    for i, ref in enumerate(out_refs):
        for n, block in enumerate(blocks):
            part = block[:, i * width : (i + 1) * width]
            if columns:
                ref[:, n * width : (n + 1) * width] = part
            else:
                ref[n * same.shape[0] : (n + 1) * same.shape[0], :] = part


def place(me, same, other, height, width, columns):
    size, total = lax.axis_size("rep"), same.shape[1]
    spec = pl.BlockSpec((height, total), lambda d, me: (d, 0))
    shape = (height, size * width) if columns else (size * height, width)
    at = lambda d, me: jnp.bitwise_xor(d, me[0] // 2)
    if columns:
        out_spec = pl.BlockSpec((height, 2 * width), lambda d, me: (0, at(d, me)))
    else:
        out_spec = pl.BlockSpec((2 * height, width), lambda d, me: (at(d, me), 0))
    count = total // width
    return pl.pallas_call(
        functools.partial(place_kernel, columns),
        grid_spec=pltpu.PrefetchScalarGridSpec(
            num_scalar_prefetch=1,
            grid=(size // 2,),
            in_specs=[spec, spec],
            out_specs=[out_spec] * count,
        ),
        out_shape=[jax.ShapeDtypeStruct(shape, F32)] * count,
        compiler_params=pltpu.CompilerParams(vmem_limit_bytes=32 << 20),
        cost_estimate=pl.CostEstimate(
            flops=0, bytes_accessed=6 * size * height * total, transcendentals=0
        ),
        name="place",
    )(me, same, other)


def place_turned_kernel(me_ref, same_ref, other_ref, out_ref):
    odd = me_ref[0] % 2
    first = jnp.where(odd == 0, same_ref[...], other_ref[...])
    second = jnp.where(odd == 0, other_ref[...], same_ref[...])
    out_ref[...] = jnp.concatenate([first, second], axis=0).T.astype(F32)


def place_turned(me, same, other, height):
    size, width = lax.axis_size("rep"), same.shape[1]
    if 2 * height % 128:
        return place(me, same, other, height, width, False)[0].T
    spec = pl.BlockSpec((height, width), lambda j, me: (jnp.bitwise_xor(j, me[0] // 2), 0))
    return pl.pallas_call(
        place_turned_kernel,
        grid_spec=pltpu.PrefetchScalarGridSpec(
            num_scalar_prefetch=1,
            grid=(size // 2,),
            in_specs=[spec, spec],
            out_specs=pl.BlockSpec((width, 2 * height), lambda j, me: (0, j)),
        ),
        out_shape=jax.ShapeDtypeStruct((width, size * height), F32),
        compiler_params=pltpu.CompilerParams(vmem_limit_bytes=32 << 20),
        cost_estimate=pl.CostEstimate(
            flops=0, bytes_accessed=12 * same.size, transcendentals=0
        ),
        name="place_turned",
    )(me, same, other)


def widen_kernel(in_ref, out_ref):
    out_ref[...] = in_ref[...].astype(F32)


def widen(value):
    rows, width = value.shape
    tile = rows // 4
    spec = pl.BlockSpec((tile, width), lambda i: (i, 0))
    return pl.pallas_call(
        widen_kernel,
        grid=(4,),
        in_specs=[spec],
        out_specs=spec,
        out_shape=jax.ShapeDtypeStruct(value.shape, F32),
        compiler_params=pltpu.CompilerParams(vmem_limit_bytes=32 << 20),
        cost_estimate=pl.CostEstimate(flops=0, bytes_accessed=6 * value.size, transcendentals=0),
        name="widen",
    )(value)


def per_device(
    layer_input,
    gain_attn,
    w_query,
    w_key,
    w_value,
    w_out,
    gain_mlp,
    w_gate,
    w_up,
    w_down,
    segments,
    attn_route,
    attn_gate,
    mlp_route,
    mlp_gate,
    cotangent,
):
    length = layer_input.shape[0]
    size, shards = lax.axis_size("rep"), lax.axis_size("shard")
    me = lax.axis_index("rep")
    whoami = me.astype(jnp.int32).reshape(1)
    shard = lax.axis_index("shard").astype(jnp.int32).reshape(1)
    block = w_query.shape[1] // size
    units = w_gate.shape[1] // size
    own = gain_attn.shape[0]
    offsets = chip_offsets()
    staged = len(chip_bits()) == 2

    def columns(weight, d, width):
        return lax.dynamic_slice_in_dim(weight, jnp.bitwise_xor(me, d) * width, width, 1)

    def rows_of(weight, height):
        return lax.dynamic_slice_in_dim(weight, me * height, height, 0)

    def local(d):
        return jnp.concatenate([columns(w, d, block) for w in (w_query, w_key, w_value)], axis=1)

    inputs = layer_input.astype(F32)
    root_one = lax.rsqrt(jnp.mean(inputs * inputs, axis=-1, keepdims=True) + EPSILON)
    tables = rotary_tables(length)
    ring = [(i, (i + 1) % shards) for i in range(shards)]
    piece = local(0)
    qkv_w = {d: [local(d)] for d in offsets}
    flows, context, saved = [], {}, {}
    gain_flow = Flow(vector_gather_steps(jnp.stack([gain_attn, gain_mlp])))
    piece, seg_other, own_gate_up = stage(
        [gain_flow],
        (
            lax.ppermute(piece, "shard", ring),
            swap(segments, 1),
            jnp.concatenate([columns(w_gate, 0, units), columns(w_up, 0, units)], axis=1),
        ),
    )
    gain_one, gain_two = gain_flow.result.astype(F32)
    normed = (inputs * root_one * gain_one).astype(BF)
    seg = jnp.concatenate([segments, seg_other], axis=0)
    seg = (seg[:, :, None], seg[:, None, :])
    other = swap(normed, 1)
    for step in range(1, shards):
        qkv_w[0].append(piece)
        flows.append(Flow(gather_steps(piece, lambda d, b: qkv_w[d].append(b))))
        if step < shards - 1:
            piece, other = stage(flows, (lax.ppermute(piece, "shard", ring), other))
    own_out, own_gate_up, own_down, qkv_w[0][-1] = lax.optimization_barrier(
        (rows_of(w_out, block), own_gate_up, rows_of(w_down, units), qkv_w[0][-1])
    )
    own_out = lax.all_gather(own_out, "shard", axis=1, tiled=True)
    both = jnp.concatenate([normed, other], axis=0)

    def run(d):
        context[d], *saved[d] = attend(shard, both, qkv_w[d], tables, seg)
        return context[d]

    context[0], own_out = stage(flows, (run(0), own_out))
    gate_up = lax.all_gather(own_gate_up, "shard", axis=0, tiled=True)
    down = lax.all_gather(own_down, "shard", axis=1, tiled=True)
    early = offsets[1:2] if staged else []
    early = stage(flows, [run(d) for d in early])
    for flow in flows:
        finish(flow)
    out_flow = Flow(gather_steps(own_out))
    rest = [d for d in offsets if d not in context]
    stage([out_flow], [run(d) for d in rest])
    out_w = finish(out_flow)

    table, mix = plan_slots(mlp_route, mlp_gate)
    pick = table.astype(BF)
    upstream = cotangent.astype(F32)
    slot_weight = jnp.sum(jnp.where(table, mix[None, :], 0.0), axis=1)[:, None]
    slot_grad = (mm(pick, cotangent) * slot_weight).astype(BF)

    all_context = jnp.concatenate([context[d] for d in offsets], axis=1)
    all_out = jnp.concatenate([out_w[d] for d in offsets], axis=0)
    projected = mm(all_context, all_out)
    projected = projected[:length] + swap(projected[length:].astype(BF), 1).astype(F32)
    attn_weight = jnp.sum(jnp.where(attn_route == 0, attn_gate, 0.0), axis=-1)[:, None]
    hidden = inputs + projected * attn_weight
    root_two = lax.rsqrt(jnp.mean(hidden * hidden, axis=-1, keepdims=True) + EPSILON)
    normed_two = (hidden * root_two * gain_two).astype(BF)

    dispatched = gather_rows(mm(pick, normed_two).astype(BF), 0)
    act = mm(dispatched, gate_up)
    slot_grad, act = lax.optimization_barrier((slot_grad, act))
    all_slot_grad = gather_rows(slot_grad, 0)
    gate_act, up_act = act[:, :units], act[:, units:]
    sigmoid = jax.nn.sigmoid(gate_act)
    silu = gate_act * sigmoid
    inner = (silu * up_act).astype(BF)
    expert_flow = Flow(plane_sum_steps(mm(inner, down).astype(BF)))
    grad_inner = mm_nt(all_slot_grad, down)
    grad_gate_act = (grad_inner * up_act * sigmoid * (1.0 + gate_act * (1.0 - sigmoid))).astype(BF)
    grad_up_act = (grad_inner * silu).astype(BF)
    grad_act = jnp.concatenate([grad_gate_act, grad_up_act], axis=1)
    grad_gate, back = lax.optimization_barrier(
        (mm_tn(grad_gate_act, dispatched).astype(BF), mm_nt(grad_act, gate_up).astype(BF))
    )
    grad_disp, grad_up_act, inner = stage([expert_flow], (reduce_rows(back, 1), grad_up_act, inner))
    grad_normed_two = mm_tn(pick, grad_disp)
    grad_gain_two, through = norm_back(grad_normed_two, hidden, root_two, gain_two)
    grad_hidden = upstream + through

    grad_projected = (grad_hidden * attn_weight).astype(BF)
    both_grad = [grad_projected, swap(grad_projected, 1)]
    lins, grad_qkv_w = {}, {}

    def run_back(*ds):
        for d in ds:
            lins[d], *grad_qkv_w[d] = attend_back(
                both_grad, out_w[d], *saved[d], both, tables, seg
            )
        return [(lins[d], grad_qkv_w[d]) for d in ds]

    def keep(ds, values):
        for d, (lin, grad) in zip(ds, values):
            lins[d], grad_qkv_w[d] = lin, grad

    far, near = offsets[-1:], offsets[1:-1]
    values, both_grad, grad_up_act, inner = stage(
        [expert_flow], (run_back(*far), both_grad, grad_up_act, inner)
    )
    keep(far, values)
    grad_up, both_grad = lax.optimization_barrier(
        (mm_tn(grad_up_act, dispatched).astype(BF), both_grad)
    )
    qkv_flow = Flow(scatter_steps(grad_qkv_w))
    grad_down = mm_tn(inner, all_slot_grad).astype(BF)
    values, both_grad, grad_down, expert_out = stage(
        [qkv_flow], (run_back(*near), both_grad, grad_down, finish(expert_flow))
    )
    keep(near, values)
    sums = [
        lax.psum_scatter(g, "shard", scatter_dimension=1, tiled=True)
        for g in (grad_gate, grad_up, grad_down)
    ]
    output = (hidden + mm_tn(pick, expert_out) * mix[:, None]).astype(BF)
    values, grad_out_w, output = stage(
        [qkv_flow], (run_back(0), mm_tn(all_context, jnp.concatenate(both_grad, axis=0)).astype(BF), output)
    )
    keep([0], values)
    grad_normed = normed_back(
        shard, [lins[d] for d in offsets], [qkv_w[d] for d in offsets], both.shape[1]
    )
    sums[0], sums[1], grad_normed, grad_out_w = stage(
        [qkv_flow], (sums[0], sums[1], grad_normed, grad_out_w)
    )
    own_grad_qkv, sums[2] = lax.optimization_barrier((finish(qkv_flow), sums[2]))
    sum_qkv = lax.psum_scatter(own_grad_qkv, "shard", scatter_dimension=0, tiled=True)

    out_blocks = {d: halves(grad_out_w[i * block : (i + 1) * block]) for i, d in enumerate(offsets)}
    out_flow, gate_flow = Flow(scatter_steps(out_blocks)), Flow(copies_steps(sums[0]))
    other_normed, up_sum = stage(
        [out_flow, gate_flow], (swap(grad_normed[1], 1), sums[1])
    )
    grad_normed = grad_normed[0] + other_normed.astype(F32)
    grad_gain_one, first = norm_back(grad_normed, inputs, root_one, gain_one)
    grad_input = (grad_hidden + first).astype(BF)
    grad_input, gains, up_sum, sum_qkv, down_sum = stage(
        [out_flow, gate_flow],
        (grad_input, jnp.stack([grad_gain_one, grad_gain_two]), up_sum, sum_qkv, sums[2]),
    )
    all_down = lax.all_gather(down_sum, "rep", axis=0, tiled=True)
    gain_flow, up_flow = Flow(vector_sum_steps(gains)), Flow(copies_steps(up_sum))
    stage([out_flow, gate_flow, up_flow, gain_flow])
    sum_out = lax.psum_scatter(finish(out_flow), "shard", scatter_dimension=1, tiled=True)
    qkv_flow = Flow(copies_steps(sum_qkv))
    grad_gate = place_turned(whoami, *finish(gate_flow), units)
    grad_gate, all_down = stage([up_flow, qkv_flow, gain_flow], (grad_gate, all_down))
    sum_out = stage([up_flow, qkv_flow, gain_flow], sum_out)
    out_flow = Flow(copies_steps(sum_out, straight_steps))
    grad_up, grad_down = stage(
        [qkv_flow, out_flow, gain_flow],
        (place_turned(whoami, *finish(up_flow), units), widen(all_down)),
    )
    grad_query, grad_key, grad_value = place(whoami, *finish(qkv_flow), own, block, True)
    grad_query = stage([out_flow], grad_query)
    (grad_out,) = place(whoami, *finish(out_flow), block, own, False)
    gain_grads = finish(gain_flow)
    return (
        output,
        grad_input,
        gain_grads[0],
        grad_query,
        grad_key,
        grad_value,
        grad_out,
        gain_grads[1],
        grad_gate,
        grad_up,
        grad_down,
    )


def solution(mesh):
    tokens = P(("rep", "shard"), None)
    tall, wide, vector = P("shard", None), P(None, "shard"), P("shard")
    weights = (vector, tall, tall, tall, wide, vector, tall, tall, wide)
    return jax.shard_map(
        per_device,
        mesh=mesh,
        in_specs=(tokens, *weights) + (tokens,) * 6,
        out_specs=(tokens, tokens, *weights),
        check_vma=False,
    )
```

```python
import functools

import jax
import jax.numpy as jnp
from jax import lax
from jax.experimental import pallas as pl
from jax.experimental.pallas import tpu as pltpu
from jax.sharding import PartitionSpec as P

HEADS = 16
HD = 128
WIN = 256
CAP = 128
EPSILON = 1e-05
BF = jnp.bfloat16
F32 = jnp.float32


def mm(left, right):
    return jnp.dot(left, right, preferred_element_type=F32)


def mm_nt(left, right):
    return lax.dot_general(left, right, (((1,), (1,)), ((), ())), preferred_element_type=F32)


def mm_tn(left, right):
    return lax.dot_general(left, right, (((0,), (0,)), ((), ())), preferred_element_type=F32)


def swap(value, bit):
    size = lax.axis_size("rep")
    return lax.ppermute(value, "rep", [(i, i ^ bit) for i in range(size)])


def chip_bits():
    size, bits, bit = lax.axis_size("rep"), [], 2
    while bit < size:
        bits.append(bit)
        bit *= 2
    return bits


def chip_offsets():
    return list(range(0, lax.axis_size("rep"), 2))


def add(left, right):
    return left.astype(F32) + right.astype(F32)


def halves(value):
    half = value.shape[0] // 2
    return value[:half], value[half:]


class Flow:
    def __init__(self, steps):
        self.steps, self.result, self.done = steps, None, False
        self.pending = next(steps)

    def advance(self, arrived):
        try:
            self.pending = self.steps.send(arrived)
        except StopIteration as end:
            self.pending, self.result, self.done = [], end.value, True


def stage(flows, extra=()):
    flows = [f for f in flows if not f.done]
    arrived, extra = lax.optimization_barrier(([f.pending for f in flows], extra))
    for flow, values in zip(flows, arrived):
        flow.advance(values)
    return extra


def finish(flow):
    while not flow.done:
        flow.advance(flow.pending)
    return flow.result


def gather_steps(value, sink=lambda offset, block: None):
    bits = chip_bits()
    if len(bits) == 2:
        one, two = bits
        half = value.shape[0] // 2
        by_one, by_two = yield [swap(value, one), swap(value, two)]
        sink(one, by_one)
        sink(two, by_two)
        top, bottom = yield [swap(by_one[:half], two), swap(by_two[half:], one)]
        far = jnp.concatenate([top, bottom], axis=0)
        sink(one ^ two, far)
        return {0: value, one: by_one, two: by_two, one ^ two: far}
    blocks = {0: value}
    for bit in bits:
        old = list(blocks.items())
        new = yield [swap(b, bit) for _, b in old]
        for (d, _), b in zip(old, new):
            blocks[d ^ bit] = b
            sink(d ^ bit, b)
    return blocks


def peers():
    return [1, *[d for d in chip_offsets() if d]]


def greet(others):
    barrier = pltpu.get_barrier_semaphore()
    for device in others.values():
        pl.semaphore_signal(barrier, inc=1, device_id={"rep": device})
    pl.semaphore_wait(barrier, len(others))


def gather_kernel(offsets, in_ref, out_ref, own_sem, send_sem, recv_sem):
    me, rows = lax.axis_index("rep"), in_ref.shape[0]
    others = {d: jnp.bitwise_xor(me, d) for d in offsets}
    spot = {d: pl.ds((d // 2 + d % 2 * len(offsets)) * rows, rows) for d in range(2 * len(offsets))}
    greet(others)
    own = pltpu.make_async_copy(in_ref, out_ref.at[spot[0]], own_sem)
    own.start()

    def send(source, offset, to):
        return pltpu.make_async_remote_copy(
            src_ref=source,
            dst_ref=out_ref.at[spot[offset]],
            send_sem=send_sem.at[offset],
            recv_sem=recv_sem.at[offset],
            device_id={"rep": others[to]},
        )

    chips = [d for d in offsets if d != 1]
    first = {d: send(in_ref, d, d) for d in [*reversed(chips), 1]}
    for copy in first.values():
        copy.start()
    second = {}
    for d in chips:
        first[d].wait_recv()
        second[d] = send(out_ref.at[spot[d]], d + 1, 1)
        second[d].start()
    first[1].wait_recv()
    for copy in second.values():
        copy.wait_recv()
    own.wait()
    for copy in [*first.values(), *second.values()]:
        copy.wait_send()


def gather_rows(value, number):
    rows, width = value.shape
    size = lax.axis_size("rep")
    return pl.pallas_call(
        functools.partial(gather_kernel, peers()),
        out_shape=jax.ShapeDtypeStruct((size * rows, width), value.dtype),
        in_specs=[pl.BlockSpec(memory_space=pltpu.VMEM)],
        out_specs=pl.BlockSpec(memory_space=pltpu.VMEM),
        scratch_shapes=[
            pltpu.SemaphoreType.DMA,
            pltpu.SemaphoreType.DMA((size,)),
            pltpu.SemaphoreType.DMA((size,)),
        ],
        compiler_params=pltpu.CompilerParams(
            collective_id=number, has_side_effects=True, vmem_limit_bytes=16 << 20
        ),
        cost_estimate=pl.CostEstimate(
            flops=0, bytes_accessed=30 * value.size * size, transcendentals=0
        ),
        name="gather_rows",
    )(value)


def reduce_kernel(offsets, in_ref, out_ref, core_ref, held_ref, chip_ref, send_sem, recv_sem):
    me, rows = lax.axis_index("rep"), out_ref.shape[0]
    others = {d: jnp.bitwise_xor(me, d) for d in offsets}
    chips = [0, *[d for d in offsets if d != 1]]
    count = len(chips)
    greet(others)

    def block(ref, i):
        return ref.at[pl.ds(i * rows, rows)]

    def send(source, target, index, to):
        return pltpu.make_async_remote_copy(
            src_ref=source,
            dst_ref=target,
            send_sem=send_sem.at[index],
            recv_sem=recv_sem.at[index],
            device_id={"rep": others[to]},
        )

    order = list(reversed(range(count)))
    core = {i: send(block(in_ref, count + i), block(core_ref, i), i, 1) for i in order}
    for copy in core.values():
        copy.start()
    chip, half = [], rows // 2

    def part(ref, i, n):
        return ref.at[pl.ds(i * rows + n * half, half)]

    def pass_on(i, n, index, to):
        chip.append(send(part(held_ref, i, n), part(chip_ref, i, n), index, to))
        chip[-1].start()
        return chip[-1]

    relay = count == 4
    for i in order:
        core[i].wait_recv()
        at = pl.ds(i * rows, rows)
        total = in_ref[at, :].astype(F32) + core_ref[at, :].astype(F32)
        held_ref[at, :] = total.astype(BF)
        if relay and i == 3:
            far = [pass_on(3, 0, count, chips[1]), pass_on(3, 1, count + 1, chips[2])]
        elif relay and i:
            pass_on(i, i - 1, count + 1 + i, chips[i])
        elif i:
            chip.append(send(block(held_ref, i), block(chip_ref, i), count + i, chips[i]))
            chip[-1].start()
    if relay:
        for i, n in ((2, 0), (1, 1)):
            far[n].wait_recv()
            at, moved = pl.ds(i * rows + n * half, half), pl.ds(3 * rows + n * half, half)
            total = held_ref[at, :].astype(F32) + chip_ref[moved, :].astype(F32)
            held_ref[at, :] = total.astype(BF)
            pass_on(i, n, count + 4 + n, chips[i])
        chip, sent = chip[2:], chip[:2]
    else:
        sent = []
    total = held_ref[pl.ds(0, rows), :].astype(F32)
    for copy in chip:
        copy.wait_recv()
    for i in range(1, 3 if relay else count):
        total += chip_ref[pl.ds(i * rows, rows), :].astype(F32)
    out_ref[...] = total.astype(BF)
    for copy in [*core.values(), *sent, *chip]:
        copy.wait_send()


def reduce_rows(partial, number):
    size = lax.axis_size("rep")
    rows, width = partial.shape[0] // size, partial.shape[1]
    half = pltpu.VMEM((size // 2 * rows, width), BF)
    return pl.pallas_call(
        functools.partial(reduce_kernel, peers()),
        out_shape=jax.ShapeDtypeStruct((rows, width), BF),
        in_specs=[pl.BlockSpec(memory_space=pltpu.VMEM)],
        out_specs=pl.BlockSpec(memory_space=pltpu.VMEM),
        scratch_shapes=[
            half,
            half,
            half,
            pltpu.SemaphoreType.DMA((size + 2,)),
            pltpu.SemaphoreType.DMA((size + 2,)),
        ],
        compiler_params=pltpu.CompilerParams(
            collective_id=number, has_side_effects=True, vmem_limit_bytes=24 << 20
        ),
        cost_estimate=pl.CostEstimate(
            flops=0, bytes_accessed=30 * partial.size, transcendentals=0
        ),
        name="reduce_rows",
    )(partial)


def jump(value, offset):
    size = lax.axis_size("rep")
    return lax.ppermute(value, "rep", [(i, i ^ offset) for i in range(size)])


def straight_steps(value):
    away = [d for d in chip_offsets() if d]
    new = yield [jump(value, d) for d in away]
    return dict(zip([0, *away], [value, *new]))


def copies_steps(value, gather=gather_steps):
    blocks = yield from gather(value)
    same = jnp.concatenate([blocks[d] for d in chip_offsets()], axis=0)
    (other,) = yield [swap(same, 1)]
    return same, other


def scatter_steps(blocks):
    bits = chip_bits()
    if len(bits) == 2:
        one, two = bits
        far = blocks[one ^ two]
        top, bottom = yield [swap(far[0], one), swap(far[1], two)]
        near_one, near_two = blocks[one], blocks[two]
        one_top, two_bottom = yield [swap(near_one[0], one), swap(near_two[1], two)]
        two_top, one_bottom = yield [
            swap(add(near_two[0], top).astype(BF), two),
            swap(add(near_one[1], bottom).astype(BF), one),
        ]
        return jnp.concatenate(
            [
                (add(blocks[0][0], one_top) + two_top.astype(F32)).astype(BF),
                (add(blocks[0][1], one_bottom) + two_bottom.astype(F32)).astype(BF),
            ],
            axis=0,
        )
    while len(blocks) < len(chip_offsets()):
        yield []
    sums = {d: jnp.concatenate(b, axis=0) for d, b in blocks.items()}
    for bit in reversed(bits):
        kept = [d for d in sorted(sums) if not d & bit]
        new = yield [swap(sums[d | bit], bit) for d in kept]
        sums = {d: add(sums[d], n).astype(BF) for d, n in zip(kept, new)}
    return sums[0]


def plane_sum_steps(partial):
    half = partial.shape[0] // 2
    (other,) = yield [swap(partial[half:], 1)]
    same = add(partial[:half], other).astype(BF)
    offsets = chip_offsets()
    rows = half // len(offsets)
    blocks = {d: same[i * rows : (i + 1) * rows] for i, d in enumerate(offsets)}
    new = yield [jump(blocks[d], d) for d in offsets if d]
    return sum((n.astype(F32) for n in new), blocks[0].astype(F32)).astype(BF)


def vector_sum_steps(rows):
    size, bit = lax.axis_size("rep"), 1
    while bit < size:
        (other,) = yield [swap(rows, bit)]
        rows, bit = rows + other, 2 * bit
    shards, at = lax.axis_size("shard"), lax.axis_index("shard")
    own = rows.shape[1] // shards
    parts = yield [
        lax.ppermute(
            lax.dynamic_slice_in_dim(rows, ((at + k) % shards) * own, own, 1),
            "shard",
            [(i, (i + k) % shards) for i in range(shards)],
        )
        for k in range(1, shards)
    ]
    return lax.dynamic_slice_in_dim(rows, at * own, own, 1) + sum(parts)


def vector_gather_steps(rows):
    size, me = lax.axis_size("shard"), lax.axis_index("shard")
    others = yield [
        lax.ppermute(rows, "shard", [(i, (i - k) % size) for i in range(size)])
        for k in range(1, size)
    ]
    parts = [rows, *others]
    twice = jnp.concatenate(parts + parts, axis=1)
    own = rows.shape[1]
    return lax.dynamic_slice_in_dim(twice, ((size - me) % size) * own, size * own, 1)


def rotary_tables(length):
    half = HD // 2
    positions = jnp.arange(length, dtype=F32)
    inverse = 10000.0 ** (-2.0 * jnp.arange(half, dtype=F32) / HD)
    angles = positions[:, None] * inverse[None, :]
    cos, sin = jnp.cos(angles), jnp.sin(angles)
    return jnp.concatenate([cos, cos], axis=1), jnp.concatenate([-sin, sin], axis=1)


def rotate(values, cos, sin):
    return values * cos + pltpu.roll(values, HD // 2, 1) * sin


def window(step, seg_col, seg_row):
    low, high = max(0, step - 1) * WIN, (step + 1) * WIN
    shape = (WIN, high - low)
    row = lax.broadcasted_iota(jnp.int32, shape, 0) + step * WIN
    col = lax.broadcasted_iota(jnp.int32, shape, 1) + low
    near = (row >= col) & (row - col < WIN)
    same = seg_col[0, step * WIN : (step + 1) * WIN, :] == seg_row[0, :, low:high]
    return low, high, near & same


def attend_kernel(parts, z_ref, *refs):
    x_refs, w_refs = refs[:parts], refs[parts : 2 * parts]
    cos_ref, sin_ref, col_ref, row_ref, context_ref, qkv_ref, lse_ref, lin_ref = refs[2 * parts :]
    length, width = context_ref.shape
    tile = min(length, 256)

    @pl.loop(0, length // tile)
    def _(t):
        rows = pl.ds(pl.multiple_of(t * tile, tile), tile)
        total = mm(x_refs[0][rows, :], w_refs[0][...])
        for x, w in zip(x_refs[1:], w_refs[1:]):
            total += mm(x[rows, :], w[...])
        lin_ref[rows, :] = total

    cos, sin = cos_ref[...], sin_ref[...]
    for h in range(width // HD):
        q_at, k_at, v_at = (slice(i * width + h * HD, i * width + (h + 1) * HD) for i in range(3))
        qkv_ref[:, q_at] = rotate(lin_ref[:, q_at], cos, sin).astype(BF)
        qkv_ref[:, k_at] = rotate(lin_ref[:, k_at], cos, sin).astype(BF)
        qkv_ref[:, v_at] = lin_ref[:, v_at].astype(BF)
    for step in range(length // WIN):
        low, high, allowed = window(step, col_ref, row_ref)
        rows = slice(step * WIN, (step + 1) * WIN)
        for h in range(width // HD):
            q_at, k_at, v_at = (
                slice(i * width + h * HD, i * width + (h + 1) * HD) for i in range(3)
            )
            scores = mm_nt(qkv_ref[rows, q_at], qkv_ref[low:high, k_at]) * HD**-0.5
            scores = jnp.where(allowed, scores, -1e30)
            peak = jnp.max(scores, axis=1, keepdims=True)
            raw = jnp.exp(scores - peak)
            total = jnp.sum(raw, axis=1, keepdims=True)
            probs = (raw * (1.0 / total)).astype(BF)
            context_ref[rows, h * HD : (h + 1) * HD] = mm(probs, qkv_ref[low:high, v_at]).astype(BF)
            lse_ref[rows, h : h + 1] = peak + jnp.log(total)


def attend(shard, both, weights, tables, seg):
    parts = len(weights)
    rows, depth = both.shape
    length = tables[0].shape[0]
    wide = weights[0].shape[1]
    width = wide // 3
    piece = depth // parts
    whole = lambda *shape: pl.BlockSpec(shape, lambda s, z: (0,) * len(shape))
    take = lambda k: pl.BlockSpec((length, piece), lambda s, z: (s, (z[0] + parts - k) % parts))
    by_seq = lambda cols: pl.BlockSpec((length, cols), lambda s, z: (s, 0))
    return pl.pallas_call(
        functools.partial(attend_kernel, parts),
        grid_spec=pltpu.PrefetchScalarGridSpec(
            num_scalar_prefetch=1,
            grid=(rows // length,),
            in_specs=[take(k) for k in range(parts)]
            + [whole(piece, wide)] * parts
            + [whole(length, HD)] * 2
            + [
                pl.BlockSpec((1, length, 1), lambda s, z: (s, 0, 0)),
                pl.BlockSpec((1, 1, length), lambda s, z: (s, 0, 0)),
            ],
            out_specs=[by_seq(width), by_seq(wide), by_seq(width // HD)],
            scratch_shapes=[pltpu.VMEM((length, wide), F32)],
        ),
        out_shape=[
            jax.ShapeDtypeStruct((rows, width), BF),
            jax.ShapeDtypeStruct((rows, wide), BF),
            jax.ShapeDtypeStruct((rows, width // HD), F32),
        ],
        compiler_params=pltpu.CompilerParams(vmem_limit_bytes=40 << 20),
        cost_estimate=pl.CostEstimate(
            flops=2 * rows * depth * wide + 4 * rows * 2 * WIN * width,
            bytes_accessed=2 * (rows * depth + depth * wide + 2 * rows * wide),
            transcendentals=rows * 2 * WIN * width // HD,
        ),
        name="attend",
    )(shard, *[both] * parts, *weights, *tables, *seg)


def attend_back_kernel(
    own_ref, other_ref, out_ref, qkv_ref, lse_ref, x_ref, cos_ref, sin_ref, col_ref, row_ref,
    lin_ref, top_ref, bottom_ref, kept_ref, context_ref, keys_ref, values_ref,
):
    length, wide = qkv_ref.shape
    width = wide // 3
    seq = pl.program_id(0)
    tile = min(length, 256)

    @pl.loop(0, length // tile)
    def _(t):
        rows = pl.ds(pl.multiple_of(t * tile, tile), tile)

        @pl.when(seq == 0)
        def _():
            context_ref[rows, :] = mm_nt(own_ref[rows, :], out_ref[...]).astype(BF)

        @pl.when(seq > 0)
        def _():
            context_ref[rows, :] = mm_nt(other_ref[rows, :], out_ref[...]).astype(BF)

    cos, sin = cos_ref[...], sin_ref[...]
    scale = HD**-0.5
    for h in range(width // HD):
        q_at, k_at, v_at = (slice(i * width + h * HD, i * width + (h + 1) * HD) for i in range(3))
        head = slice(h * HD, (h + 1) * HD)
        keys_ref[...] = jnp.zeros_like(keys_ref)
        values_ref[...] = jnp.zeros_like(values_ref)
        for step in range(length // WIN):
            low, high, allowed = window(step, col_ref, row_ref)
            rows = slice(step * WIN, (step + 1) * WIN)
            queries, keys = qkv_ref[rows, q_at], qkv_ref[low:high, k_at]
            grad = context_ref[rows, head]
            scores = jnp.where(allowed, mm_nt(queries, keys) * scale, -1e30)
            probs = jnp.exp(scores - lse_ref[rows, h : h + 1])
            values_ref[low:high, :] += mm_tn(probs.astype(BF), grad)
            grad_probs = mm_nt(grad, qkv_ref[low:high, v_at])
            inner = jnp.sum(probs * grad_probs, axis=1, keepdims=True)
            grad_scores = (probs * (grad_probs - inner)).astype(BF)
            grad_queries = mm(grad_scores, keys) * scale
            keys_ref[low:high, :] += mm_tn(grad_scores, queries)
            lin_ref[rows, q_at] = rotate(grad_queries, cos[rows], -sin[rows]).astype(BF)
        lin_ref[:, k_at] = rotate(keys_ref[...] * scale, cos, -sin).astype(BF)
        lin_ref[:, v_at] = values_ref[...].astype(BF)
    kept_ref[pl.ds(pl.multiple_of(seq * length, length), length), :] = lin_ref[...]

    @pl.when(seq == pl.num_programs(0) - 1)
    def _():
        half = top_ref.shape[0]
        step = 256
        for n, ref in enumerate((top_ref, bottom_ref)):

            @pl.loop(0, half // step)
            def _(t):
                cols = pl.ds(pl.multiple_of(n * half + t * step, step), step)
                rows = pl.ds(pl.multiple_of(t * step, step), step)
                ref[rows, :] = mm_tn(x_ref[:, cols], kept_ref[...]).astype(BF)


def attend_back(grad, out_w, qkv, lse, both, tables, seg):
    rows, depth = both.shape
    length = tables[0].shape[0]
    wide = qkv.shape[1]
    width = wide // 3
    whole = lambda *shape: pl.BlockSpec(shape, lambda s: (0,) * len(shape))
    by_seq = lambda cols: pl.BlockSpec((length, cols), lambda s: (s, 0))
    return pl.pallas_call(
        attend_back_kernel,
        grid=(rows // length,),
        in_specs=[whole(length, depth)] * 2
        + [whole(width, depth), by_seq(wide), by_seq(width // HD)]
        + [whole(rows, depth), whole(length, HD), whole(length, HD)]
        + [
            pl.BlockSpec((1, length, 1), lambda s: (s, 0, 0)),
            pl.BlockSpec((1, 1, length), lambda s: (s, 0, 0)),
        ],
        out_specs=[by_seq(wide), whole(depth // 2, wide), whole(depth // 2, wide)],
        scratch_shapes=[
            pltpu.VMEM((rows, wide), BF),
            pltpu.VMEM((length, width), BF),
            pltpu.VMEM((length, HD), F32),
            pltpu.VMEM((length, HD), F32),
        ],
        out_shape=[
            jax.ShapeDtypeStruct((rows, wide), BF),
            jax.ShapeDtypeStruct((depth // 2, wide), BF),
            jax.ShapeDtypeStruct((depth // 2, wide), BF),
        ],
        compiler_params=pltpu.CompilerParams(vmem_limit_bytes=48 << 20),
        cost_estimate=pl.CostEstimate(
            flops=2 * rows * depth * (wide + width) + 10 * rows * 2 * WIN * width,
            bytes_accessed=2 * (2 * rows * depth + depth * (wide + width) + 2 * rows * wide),
            transcendentals=rows * 2 * WIN * width // HD,
        ),
        name="attend_back",
    )(*grad, out_w, qkv, lse, both, *tables, *seg)


def normed_back_kernel(blocks, parts, z_ref, *refs):
    lins, weights, (own_ref, other_ref) = refs[:blocks], refs[blocks:-2], refs[-2:]
    piece = own_ref.shape[1] // parts
    own = pl.program_id(0) < pl.num_programs(0) // 2
    for k in range(parts):
        total = mm_nt(lins[0][...], weights[k][...])
        for n in range(1, blocks):
            total += mm_nt(lins[n][...], weights[n * parts + k][...])
        at = pl.multiple_of(((z_ref[0] + parts - k) % parts) * piece, piece)

        @pl.when(own)
        def _():
            own_ref[:, pl.ds(at, piece)] = total

        @pl.when(jnp.logical_not(own))
        def _():
            other_ref[:, pl.ds(at, piece)] = total.astype(BF)


def normed_back(shard, lins, weights, depth):
    parts = len(weights[0])
    rows, wide = lins[0].shape
    tile = min(rows // 2, 256)
    steps = rows // 2 // tile
    flat = [w for block in weights for w in block]
    return pl.pallas_call(
        functools.partial(normed_back_kernel, len(lins), parts),
        grid_spec=pltpu.PrefetchScalarGridSpec(
            num_scalar_prefetch=1,
            grid=(rows // tile,),
            in_specs=[pl.BlockSpec((tile, wide), lambda s, z: (s, 0))] * len(lins)
            + [
                pl.BlockSpec(flat[0].shape, lambda s, z: (0, 0), pipeline_mode=pl.Buffered(1))
            ] * len(flat),
            out_specs=[
                pl.BlockSpec((tile, depth), lambda s, z: (jnp.minimum(s, steps - 1), 0)),
                pl.BlockSpec((tile, depth), lambda s, z: (jnp.maximum(s - steps, 0), 0)),
            ],
        ),
        out_shape=[
            jax.ShapeDtypeStruct((rows // 2, depth), F32),
            jax.ShapeDtypeStruct((rows // 2, depth), BF),
        ],
        compiler_params=pltpu.CompilerParams(vmem_limit_bytes=48 << 20),
        cost_estimate=pl.CostEstimate(
            flops=2 * rows * depth * wide * len(lins),
            bytes_accessed=2 * len(lins) * wide * (rows + depth) + 4 * rows * depth,
            transcendentals=0,
        ),
        name="normed_back",
    )(shard, *lins, *flat)


def plan_slots(route_ids, gate_values):
    hit_mask = route_ids == 0
    hit = jnp.any(hit_mask, axis=-1)
    weight = jnp.sum(jnp.where(hit_mask, gate_values, 0.0), axis=-1)
    ids = jnp.arange(route_ids.shape[0], dtype=jnp.int32)
    earlier = (ids[None, :] < ids[:, None]) & hit[None, :]
    order = jnp.sum(earlier.astype(jnp.int32), axis=1)
    kept = hit & (order < CAP)
    slots = jnp.arange(CAP, dtype=jnp.int32)
    table = (order[None, :] == slots[:, None]) & kept[None, :]
    return table, jnp.where(kept, weight, 0.0)


def norm_back(grad_normed, source, root, gain):
    scaled = grad_normed * gain
    grad_gain = jnp.sum(grad_normed * source * root, axis=0)
    mean = jnp.mean(scaled * source, axis=-1, keepdims=True)
    return grad_gain, root * scaled - source * (root * root * root) * mean


def place_kernel(columns, me_ref, same_ref, other_ref, *out_refs):
    even = me_ref[0] % 2 == 0
    same, other = same_ref[...], other_ref[...]
    blocks = (jnp.where(even, same, other).astype(F32), jnp.where(even, other, same).astype(F32))
    width = same.shape[1] // len(out_refs)
    for i, ref in enumerate(out_refs):
        for n, block in enumerate(blocks):
            part = block[:, i * width : (i + 1) * width]
            if columns:
                ref[:, n * width : (n + 1) * width] = part
            else:
                ref[n * same.shape[0] : (n + 1) * same.shape[0], :] = part


def place(me, same, other, height, width, columns):
    size, total = lax.axis_size("rep"), same.shape[1]
    spec = pl.BlockSpec((height, total), lambda d, me: (d, 0))
    shape = (height, size * width) if columns else (size * height, width)
    at = lambda d, me: jnp.bitwise_xor(d, me[0] // 2)
    if columns:
        out_spec = pl.BlockSpec((height, 2 * width), lambda d, me: (0, at(d, me)))
    else:
        out_spec = pl.BlockSpec((2 * height, width), lambda d, me: (at(d, me), 0))
    count = total // width
    return pl.pallas_call(
        functools.partial(place_kernel, columns),
        grid_spec=pltpu.PrefetchScalarGridSpec(
            num_scalar_prefetch=1,
            grid=(size // 2,),
            in_specs=[spec, spec],
            out_specs=[out_spec] * count,
        ),
        out_shape=[jax.ShapeDtypeStruct(shape, F32)] * count,
        compiler_params=pltpu.CompilerParams(vmem_limit_bytes=32 << 20),
        cost_estimate=pl.CostEstimate(
            flops=0, bytes_accessed=6 * size * height * total, transcendentals=0
        ),
        name="place",
    )(me, same, other)


def place_turned_kernel(me_ref, same_ref, other_ref, out_ref):
    odd = me_ref[0] % 2
    first = jnp.where(odd == 0, same_ref[...], other_ref[...])
    second = jnp.where(odd == 0, other_ref[...], same_ref[...])
    out_ref[...] = jnp.concatenate([first, second], axis=0).T.astype(F32)


def place_turned(me, same, other, height):
    size, width = lax.axis_size("rep"), same.shape[1]
    if 2 * height % 128:
        return place(me, same, other, height, width, False)[0].T
    spec = pl.BlockSpec((height, width), lambda j, me: (jnp.bitwise_xor(j, me[0] // 2), 0))
    return pl.pallas_call(
        place_turned_kernel,
        grid_spec=pltpu.PrefetchScalarGridSpec(
            num_scalar_prefetch=1,
            grid=(size // 2,),
            in_specs=[spec, spec],
            out_specs=pl.BlockSpec((width, 2 * height), lambda j, me: (0, j)),
        ),
        out_shape=jax.ShapeDtypeStruct((width, size * height), F32),
        compiler_params=pltpu.CompilerParams(vmem_limit_bytes=32 << 20),
        cost_estimate=pl.CostEstimate(
            flops=0, bytes_accessed=12 * same.size, transcendentals=0
        ),
        name="place_turned",
    )(me, same, other)


def widen_kernel(in_ref, out_ref):
    out_ref[...] = in_ref[...].astype(F32)


def widen(value):
    rows, width = value.shape
    tile = rows // 4
    spec = pl.BlockSpec((tile, width), lambda i: (i, 0))
    return pl.pallas_call(
        widen_kernel,
        grid=(4,),
        in_specs=[spec],
        out_specs=spec,
        out_shape=jax.ShapeDtypeStruct(value.shape, F32),
        compiler_params=pltpu.CompilerParams(vmem_limit_bytes=32 << 20),
        cost_estimate=pl.CostEstimate(flops=0, bytes_accessed=6 * value.size, transcendentals=0),
        name="widen",
    )(value)


def per_device(
    layer_input,
    gain_attn,
    w_query,
    w_key,
    w_value,
    w_out,
    gain_mlp,
    w_gate,
    w_up,
    w_down,
    segments,
    attn_route,
    attn_gate,
    mlp_route,
    mlp_gate,
    cotangent,
):
    length = layer_input.shape[0]
    size, shards = lax.axis_size("rep"), lax.axis_size("shard")
    me = lax.axis_index("rep")
    whoami = me.astype(jnp.int32).reshape(1)
    shard = lax.axis_index("shard").astype(jnp.int32).reshape(1)
    block = w_query.shape[1] // size
    units = w_gate.shape[1] // size
    own = gain_attn.shape[0]
    offsets = chip_offsets()
    staged = len(chip_bits()) == 2

    def columns(weight, d, width):
        return lax.dynamic_slice_in_dim(weight, jnp.bitwise_xor(me, d) * width, width, 1)

    def rows_of(weight, height):
        return lax.dynamic_slice_in_dim(weight, me * height, height, 0)

    def local(d):
        return jnp.concatenate([columns(w, d, block) for w in (w_query, w_key, w_value)], axis=1)

    inputs = layer_input.astype(F32)
    root_one = lax.rsqrt(jnp.mean(inputs * inputs, axis=-1, keepdims=True) + EPSILON)
    tables = rotary_tables(length)
    ring = [(i, (i + 1) % shards) for i in range(shards)]
    piece = local(0)
    qkv_w = {d: [local(d)] for d in offsets}
    flows, context, saved = [], {}, {}
    gain_flow = Flow(vector_gather_steps(jnp.stack([gain_attn, gain_mlp])))
    piece, seg_other, own_gate_up = stage(
        [gain_flow],
        (
            lax.ppermute(piece, "shard", ring),
            swap(segments, 1),
            jnp.concatenate([columns(w_gate, 0, units), columns(w_up, 0, units)], axis=1),
        ),
    )
    gain_one, gain_two = gain_flow.result.astype(F32)
    normed = (inputs * root_one * gain_one).astype(BF)
    seg = jnp.concatenate([segments, seg_other], axis=0)
    seg = (seg[:, :, None], seg[:, None, :])
    other = swap(normed, 1)
    for step in range(1, shards):
        qkv_w[0].append(piece)
        flows.append(Flow(gather_steps(piece, lambda d, b: qkv_w[d].append(b))))
        if step < shards - 1:
            piece, other = stage(flows, (lax.ppermute(piece, "shard", ring), other))
    own_out, own_gate_up, own_down, qkv_w[0][-1] = lax.optimization_barrier(
        (rows_of(w_out, block), own_gate_up, rows_of(w_down, units), qkv_w[0][-1])
    )
    own_out = lax.all_gather(own_out, "shard", axis=1, tiled=True)
    both = jnp.concatenate([normed, other], axis=0)

    def run(d):
        context[d], *saved[d] = attend(shard, both, qkv_w[d], tables, seg)
        return context[d]

    context[0], own_out = stage(flows, (run(0), own_out))
    gate_up = lax.all_gather(own_gate_up, "shard", axis=0, tiled=True)
    down = lax.all_gather(own_down, "shard", axis=1, tiled=True)
    early = offsets[1:2] if staged else []
    early = stage(flows, [run(d) for d in early])
    for flow in flows:
        finish(flow)
    out_flow = Flow(gather_steps(own_out))
    rest = [d for d in offsets if d not in context]
    stage([out_flow], [run(d) for d in rest])
    out_w = finish(out_flow)

    table, mix = plan_slots(mlp_route, mlp_gate)
    pick = table.astype(BF)
    upstream = cotangent.astype(F32)
    slot_weight = jnp.sum(jnp.where(table, mix[None, :], 0.0), axis=1)[:, None]
    slot_grad = (mm(pick, cotangent) * slot_weight).astype(BF)

    all_context = jnp.concatenate([context[d] for d in offsets], axis=1)
    all_out = jnp.concatenate([out_w[d] for d in offsets], axis=0)
    projected = mm(all_context, all_out)
    projected = projected[:length] + swap(projected[length:].astype(BF), 1).astype(F32)
    attn_weight = jnp.sum(jnp.where(attn_route == 0, attn_gate, 0.0), axis=-1)[:, None]
    hidden = inputs + projected * attn_weight
    root_two = lax.rsqrt(jnp.mean(hidden * hidden, axis=-1, keepdims=True) + EPSILON)
    normed_two = (hidden * root_two * gain_two).astype(BF)

    dispatched = gather_rows(mm(pick, normed_two).astype(BF), 0)
    act = mm(dispatched, gate_up)
    slot_grad, act = lax.optimization_barrier((slot_grad, act))
    all_slot_grad = gather_rows(slot_grad, 0)
    gate_act, up_act = act[:, :units], act[:, units:]
    sigmoid = jax.nn.sigmoid(gate_act)
    silu = gate_act * sigmoid
    inner = (silu * up_act).astype(BF)
    expert_flow = Flow(plane_sum_steps(mm(inner, down).astype(BF)))
    grad_inner = mm_nt(all_slot_grad, down)
    grad_gate_act = (grad_inner * up_act * sigmoid * (1.0 + gate_act * (1.0 - sigmoid))).astype(BF)
    grad_up_act = (grad_inner * silu).astype(BF)
    grad_act = jnp.concatenate([grad_gate_act, grad_up_act], axis=1)
    grad_gate, back = lax.optimization_barrier(
        (mm_tn(grad_gate_act, dispatched).astype(BF), mm_nt(grad_act, gate_up).astype(BF))
    )
    grad_disp, grad_up_act, inner = stage([expert_flow], (reduce_rows(back, 1), grad_up_act, inner))
    grad_normed_two = mm_tn(pick, grad_disp)
    grad_gain_two, through = norm_back(grad_normed_two, hidden, root_two, gain_two)
    grad_hidden = upstream + through

    grad_projected = (grad_hidden * attn_weight).astype(BF)
    both_grad = [grad_projected, swap(grad_projected, 1)]
    lins, grad_qkv_w = {}, {}

    def run_back(*ds):
        for d in ds:
            lins[d], *grad_qkv_w[d] = attend_back(
                both_grad, out_w[d], *saved[d], both, tables, seg
            )
        return [(lins[d], grad_qkv_w[d]) for d in ds]

    def keep(ds, values):
        for d, (lin, grad) in zip(ds, values):
            lins[d], grad_qkv_w[d] = lin, grad

    far, near = offsets[-1:], offsets[1:-1]
    values, both_grad, grad_up_act, inner = stage(
        [expert_flow], (run_back(*far), both_grad, grad_up_act, inner)
    )
    keep(far, values)
    grad_up, both_grad = lax.optimization_barrier(
        (mm_tn(grad_up_act, dispatched).astype(BF), both_grad)
    )
    qkv_flow = Flow(scatter_steps(grad_qkv_w))
    grad_down = mm_tn(inner, all_slot_grad).astype(BF)
    values, both_grad, grad_down, expert_out = stage(
        [qkv_flow], (run_back(*near), both_grad, grad_down, finish(expert_flow))
    )
    keep(near, values)
    sums = [
        lax.psum_scatter(g, "shard", scatter_dimension=1, tiled=True)
        for g in (grad_gate, grad_up, grad_down)
    ]
    output = (hidden + mm_tn(pick, expert_out) * mix[:, None]).astype(BF)
    values, grad_out_w, output = stage(
        [qkv_flow], (run_back(0), mm_tn(all_context, jnp.concatenate(both_grad, axis=0)).astype(BF), output)
    )
    keep([0], values)
    grad_normed = normed_back(
        shard, [lins[d] for d in offsets], [qkv_w[d] for d in offsets], both.shape[1]
    )
    sums[0], sums[1], grad_normed, grad_out_w = stage(
        [qkv_flow], (sums[0], sums[1], grad_normed, grad_out_w)
    )
    own_grad_qkv, sums[2] = lax.optimization_barrier((finish(qkv_flow), sums[2]))
    sum_qkv = lax.psum_scatter(own_grad_qkv, "shard", scatter_dimension=0, tiled=True)

    out_blocks = {d: halves(grad_out_w[i * block : (i + 1) * block]) for i, d in enumerate(offsets)}
    out_flow, gate_flow = Flow(scatter_steps(out_blocks)), Flow(copies_steps(sums[0]))
    other_normed, up_sum = stage(
        [out_flow, gate_flow], (swap(grad_normed[1], 1), sums[1])
    )
    grad_normed = grad_normed[0] + other_normed.astype(F32)
    grad_gain_one, first = norm_back(grad_normed, inputs, root_one, gain_one)
    grad_input = (grad_hidden + first).astype(BF)
    grad_input, gains, up_sum = stage(
        [out_flow, gate_flow],
        (grad_input, jnp.stack([grad_gain_one, grad_gain_two]), up_sum),
    )
    gain_flow, up_flow = Flow(vector_sum_steps(gains)), Flow(copies_steps(up_sum))
    sum_qkv = stage([out_flow, gate_flow, up_flow, gain_flow], sum_qkv)
    sum_out = lax.psum_scatter(finish(out_flow), "shard", scatter_dimension=1, tiled=True)
    qkv_flow = Flow(copies_steps(sum_qkv))
    grad_gate = place_turned(whoami, *finish(gate_flow), units)
    grad_gate, sum_out = stage([up_flow, qkv_flow, gain_flow], (grad_gate, sum_out))
    down_sum, sum_out = lax.optimization_barrier((sums[2], sum_out))
    all_down = lax.all_gather(down_sum, "rep", axis=0, tiled=True)
    out_flow = Flow(copies_steps(sum_out, straight_steps))
    stage([up_flow, qkv_flow, out_flow, gain_flow])
    grad_up = place_turned(whoami, *finish(up_flow), units)
    grad_up = stage([qkv_flow, out_flow, gain_flow], grad_up)
    grad_query, grad_key, grad_value = place(whoami, *finish(qkv_flow), own, block, True)
    (grad_out,) = place(whoami, *finish(out_flow), block, own, False)
    grad_down = widen(all_down)
    gain_grads = finish(gain_flow)
    return (
        output,
        grad_input,
        gain_grads[0],
        grad_query,
        grad_key,
        grad_value,
        grad_out,
        gain_grads[1],
        grad_gate,
        grad_up,
        grad_down,
    )


def solution(mesh):
    tokens = P(("rep", "shard"), None)
    tall, wide, vector = P("shard", None), P(None, "shard"), P("shard")
    weights = (vector, tall, tall, tall, wide, vector, tall, tall, wide)
    return jax.shard_map(
        per_device,
        mesh=mesh,
        in_specs=(tokens, *weights) + (tokens,) * 6,
        out_specs=(tokens, tokens, *weights),
        check_vma=False,
    )
```
